32 devices in a mesh: pts: 8 (over z, y), grp: 4 (over x, core).
Axes of the slice: x: 2, y: 2, z: 4, core: 2. Of those that a mesh axis runs over, the one named last changes fastest.
Arguments:
- input_positions: float32 [2, 32, 2, 1024], P(None, 'grp', None, 'pts'), may hold values from -6 to 6
- flow_labels: float32 [2, 32, 3, 1024], P(None, 'grp', None, 'pts'), may hold values from -6 to 6
- airfoil_boundary: int32 [2, 32, 1024], P(None, 'grp', 'pts'), may hold values 0 or 1
- valid_sizes: int32 [2, 32], P(None, 'grp'), may hold values from 768 to 1024, as said below
- lifting_readout_rows: float32 [5, 256], replicated, may hold values from -0.375 to 0.375
- block_projections: float32 [2, 5, 256, 256], replicated, may hold values from -0.375 to 0.375
- partition_maps: float32 [2, 32, 64], replicated, may hold values from -1 to 1
- triple_maps_rows: float32 [2, 32, 96], replicated, may hold values from -12 to 12
- sharpness_factors: float32 [2, 8], replicated, may hold values from 0.3 to 1
- gain_bias_rows: float32 [20, 256], replicated, may hold values from -4 to 4
- lifting_readout_mean: float32 [5, 256], replicated, may hold values from -6.1035156e-05 to 6.1035156e-05
- projection_running_mean: float32 [2, 5, 256, 256], replicated, may hold values from -1.5258789e-05 to 1.5258789e-05
- partition_map_mean: float32 [2, 32, 64], replicated, may hold values from -6.1035156e-05 to 6.1035156e-05
- triple_maps_mean: float32 [2, 32, 96], replicated, may hold values from -6.1035156e-05 to 6.1035156e-05
- sharpness_mean: float32 [2, 8], replicated, may hold values from -6.1035156e-05 to 6.1035156e-05
- gain_bias_mean: float32 [20, 256], replicated, may hold values from -6.1035156e-05 to 6.1035156e-05
- lifting_readout_square: float32 [5, 256], replicated, may hold values from 9.5235824e-12 to 3.809433e-11
- projection_running_square: float32 [2, 5, 256, 256], replicated, may hold values from 5.952239e-13 to 2.3808956e-12
- partition_map_square: float32 [2, 32, 64], replicated, may hold values from 9.5235824e-12 to 3.809433e-11
- triple_maps_square: float32 [2, 32, 96], replicated, may hold values from 9.5235824e-12 to 3.809433e-11
- sharpness_square: float32 [2, 8], replicated, may hold values from 9.5235824e-12 to 3.809433e-11
- gain_bias_square: float32 [20, 256], replicated, may hold values from 9.5235824e-12 to 3.809433e-11
Outputs:
- loss_value: float32 [], replicated
- grad_norm: float32 [], replicated
- io_first_new: float32 [5, 256], replicated
- io_second_new: float32 [5, 256], replicated
- io_weights_new: float32 [5, 256], replicated
- matrices_first_new: float32 [2, 5, 256, 256], replicated
- matrices_second_new: float32 [2, 5, 256, 256], replicated
- matrices_new: float32 [2, 5, 256, 256], replicated
- slicers_first_new: float32 [2, 32, 64], replicated
- slicers_second_new: float32 [2, 32, 64], replicated
- slicers_new: float32 [2, 32, 64], replicated
- qkv_first_new: float32 [2, 32, 96], replicated
- qkv_second_new: float32 [2, 32, 96], replicated
- qkv_new: float32 [2, 32, 96], replicated
- temperatures_first_new: float32 [2, 8], replicated
- temperatures_second_new: float32 [2, 8], replicated
- temperatures_new: float32 [2, 8], replicated
- vectors_first_new: float32 [20, 256], replicated
- vectors_second_new: float32 [20, 256], replicated
- vectors_new: float32 [20, 256], replicated
The draws below stay inside these ranges and needn't reach their ends.
Inputs may be any that keep to these rules, and one draw needn't show every extreme that they name: `valid_sizes`: the valid points of a grid are its first counts slots; in every draw some grid has all 1024 slots valid.
All inputs are finite; a program needn't handle non-finite values. No bound on the sum of `airfoil_boundary` on one device may be relied on, other than what follows from the above.
Results may differ from the reference program's by a relative error of at most 0.0003.
Values sent between devices are 32-bit elements; how exact they have to be, the bound alone decides.
A program may use at most 256 MiB of HBM per device.

```python
import math
import jax
import jax.numpy as jnp
from jax import lax

MODEL_WIDTH = 256
FOCUS_GROUPS = 8
GROUP_BREADTH = 32
SLICES = 64
FIN = 2
OUTC = 3
DEPTH_TOTAL = 2
MB = 2
STEP = 10
GRIDS_CH = 32
GPTS = 1024
LEARNABLE_TOTAL = 672016


def draw_valid_sizes(key, part):
    base = jax.random.randint(jax.random.fold_in(key, 11), (MB * GRIDS_CH,), GPTS - GPTS // 4, GPTS + 1, dtype=jnp.int32)
    chosen = jax.random.randint(jax.random.fold_in(key, 12), (), 0, MB * GRIDS_CH, dtype=jnp.int32)
    filled = jnp.where(jnp.arange(MB * GRIDS_CH, dtype=jnp.int32) == chosen, jnp.int32(GPTS), base)
    return filled.reshape(MB, GRIDS_CH).astype(jnp.int32)


def with_ends(drawn, own_key, low, high):
    extent = drawn.shape
    index_at = [jax.random.randint(jax.random.fold_in(own_key, axis), (), 0, extent[axis]) for axis in range(len(extent))]
    drawn = drawn.at[tuple(index_at)].set(low)
    longest = extent.index(max(extent))
    index_at[longest] = (index_at[longest] + 1) % extent[longest]
    return drawn.at[tuple(index_at)].set(high)


def shard_levels(own_key, dims, pieces, smallest, largest):
    level, own = 1.0, jax.random.fold_in(own_key, 6)
    for position, blocks in pieces:
        heights = jnp.exp(jax.random.uniform(jax.random.fold_in(own, position), (blocks,), jnp.float32, smallest / len(pieces), largest / len(pieces)))
        level = level * jnp.repeat(heights, dims[position] // blocks).reshape([-1 if axis == position else 1 for axis in range(len(dims))])
    return level


def noise(rng, shape, width, reach, split=(), kind=jnp.bfloat16):
    loudness = shard_levels(rng, shape, split, -0.22, 0.18) if split else 1.0
    result = jax.random.normal(rng, shape, jnp.float32) * width * loudness
    return jnp.minimum(jnp.maximum(result, -reach), reach).astype(kind)


def setup_inputs(seed: int = 0) -> dict:
    key_of = jax.random.split(jax.random.key(seed), 23)
    input_positions = noise(key_of[0], (MB, GRIDS_CH, FIN, GPTS), 1.0, 6.0, ((1, 4), (3, 8)), jnp.float32)
    flow_labels = noise(key_of[1], (MB, GRIDS_CH, OUTC, GPTS), 1.0, 6.0, ((1, 4), (3, 8)), jnp.float32)
    airfoil_boundary = with_ends((jax.random.randint(key_of[2], (MB, GRIDS_CH, GPTS), 0, 4) < 1).astype(jnp.int32), jax.random.fold_in(key_of[2], 1), 0, 1)
    valid_sizes = draw_valid_sizes(jax.random.fold_in(key_of[22], 71), 0)
    lifting_readout_rows = noise(key_of[4], (FIN + OUTC, MODEL_WIDTH), MODEL_WIDTH ** -0.5, 0.375, (), jnp.float32)
    block_projections = noise(key_of[5], (DEPTH_TOTAL, 5, MODEL_WIDTH, MODEL_WIDTH), MODEL_WIDTH ** -0.5, 0.375, (), jnp.float32)
    partition_maps = noise(key_of[6], (DEPTH_TOTAL, GROUP_BREADTH, SLICES), GROUP_BREADTH ** -0.5, 1.0, (), jnp.float32)
    triple_maps_rows = noise(key_of[7], (DEPTH_TOTAL, GROUP_BREADTH, 3 * GROUP_BREADTH), 2.0, 12.0, (), jnp.float32)
    sharpness_factors = jnp.clip(jnp.exp(jax.random.uniform(key_of[8], (DEPTH_TOTAL, FOCUS_GROUPS), jnp.float32, math.log(0.3), math.log(1.0))), 0.3, 1.0)
    gain_bias_rows = noise(key_of[9], (9 * DEPTH_TOTAL + 2, MODEL_WIDTH), 0.6, 4.0, (), jnp.float32)
    lifting_readout_mean = noise(key_of[10], (FIN + OUTC, MODEL_WIDTH), (0.0088 * LEARNABLE_TOTAL ** -0.5), 6.103515625e-05, (), jnp.float32)
    projection_running_mean = noise(key_of[11], (DEPTH_TOTAL, 5, MODEL_WIDTH, MODEL_WIDTH), (0.0022 * LEARNABLE_TOTAL ** -0.5), 1.52587890625e-05, (), jnp.float32)
    partition_map_mean = noise(key_of[12], (DEPTH_TOTAL, GROUP_BREADTH, SLICES), (0.0088 * LEARNABLE_TOTAL ** -0.5), 6.103515625e-05, (), jnp.float32)
    triple_maps_mean = noise(key_of[13], (DEPTH_TOTAL, GROUP_BREADTH, 3 * GROUP_BREADTH), (0.0088 * LEARNABLE_TOTAL ** -0.5), 6.103515625e-05, (), jnp.float32)
    sharpness_mean = noise(key_of[14], (DEPTH_TOTAL, FOCUS_GROUPS), (0.0088 * LEARNABLE_TOTAL ** -0.5), 6.103515625e-05, (), jnp.float32)
    gain_bias_mean = noise(key_of[15], (9 * DEPTH_TOTAL + 2, MODEL_WIDTH), (0.0088 * LEARNABLE_TOTAL ** -0.5), 6.103515625e-05, (), jnp.float32)
    lifting_readout_square = jnp.clip(jnp.exp(jax.random.uniform(key_of[16], (FIN + OUTC, MODEL_WIDTH), jnp.float32, math.log(9.523582443493606e-12), math.log(3.809432977397442e-11))), 9.523582443493606e-12, 3.809432977397442e-11)
    projection_running_square = jnp.clip(jnp.exp(jax.random.uniform(key_of[17], (DEPTH_TOTAL, 5, MODEL_WIDTH, MODEL_WIDTH), jnp.float32, math.log(5.952239027183504e-13), math.log(2.3808956108734014e-12))), 5.952239027183504e-13, 2.3808956108734014e-12)
    partition_map_square = jnp.clip(jnp.exp(jax.random.uniform(key_of[18], (DEPTH_TOTAL, GROUP_BREADTH, SLICES), jnp.float32, math.log(9.523582443493606e-12), math.log(3.809432977397442e-11))), 9.523582443493606e-12, 3.809432977397442e-11)
    triple_maps_square = jnp.clip(jnp.exp(jax.random.uniform(key_of[19], (DEPTH_TOTAL, GROUP_BREADTH, 3 * GROUP_BREADTH), jnp.float32, math.log(9.523582443493606e-12), math.log(3.809432977397442e-11))), 9.523582443493606e-12, 3.809432977397442e-11)
    sharpness_square = jnp.clip(jnp.exp(jax.random.uniform(key_of[20], (DEPTH_TOTAL, FOCUS_GROUPS), jnp.float32, math.log(9.523582443493606e-12), math.log(3.809432977397442e-11))), 9.523582443493606e-12, 3.809432977397442e-11)
    gain_bias_square = jnp.clip(jnp.exp(jax.random.uniform(key_of[21], (9 * DEPTH_TOTAL + 2, MODEL_WIDTH), jnp.float32, math.log(9.523582443493606e-12), math.log(3.809432977397442e-11))), 9.523582443493606e-12, 3.809432977397442e-11)
    return dict(input_positions=input_positions, flow_labels=flow_labels, airfoil_boundary=airfoil_boundary, valid_sizes=valid_sizes, lifting_readout_rows=lifting_readout_rows, block_projections=block_projections, partition_maps=partition_maps, triple_maps_rows=triple_maps_rows, sharpness_factors=sharpness_factors, gain_bias_rows=gain_bias_rows, lifting_readout_mean=lifting_readout_mean, projection_running_mean=projection_running_mean, partition_map_mean=partition_map_mean, triple_maps_mean=triple_maps_mean, sharpness_mean=sharpness_mean, gain_bias_mean=gain_bias_mean, lifting_readout_square=lifting_readout_square, projection_running_square=projection_running_square, partition_map_square=partition_map_square, triple_maps_square=triple_maps_square, sharpness_square=sharpness_square, gain_bias_square=gain_bias_square)


exact_arithmetic = lax.Precision.HIGHEST
clip_limit = 0.02
learn_rate = 0.1
beta_one = 0.9
beta_two = 0.999
adam_epsilon = 1e-08
weight_decay = 0.01

@jax.custom_vjp
def low(v):
    return lax.optimization_barrier(v.astype(jnp.bfloat16)).astype(jnp.float32)

@jax.custom_vjp
def low_back(v):
    return v

def low_keep(v):
    return (low(v), None)

def low_pass(kept, grad):
    return (grad,)

def back_keep(v):
    return (v, None)

def back_low(kept, grad):
    return (low(grad),)
low.defvjp(low_keep, low_pass)
low_back.defvjp(back_keep, back_low)

def layer_norm(values, gain, shift):
    center = values - lax.optimization_barrier(jnp.mean(values, -1, keepdims=True))
    spread_tokens = lax.optimization_barrier(jnp.mean(center * center, -1, keepdims=True))
    return center * lax.rsqrt(spread_tokens + 1e-05) * gain + shift

def slice_attend(weighted_points, masses, triple_maps_rows):
    head_size = triple_maps_rows.shape[0]
    tokens = weighted_points / (masses[..., None] + 1e-05)
    joined = jnp.einsum('imd,de->ime', tokens, triple_maps_rows, precision=exact_arithmetic)
    queries = joined[..., :head_size]
    keys = joined[..., head_size:2 * head_size]
    values = joined[..., 2 * head_size:]
    scores = jnp.einsum('imd,ind->imn', queries, keys, precision=exact_arithmetic) * head_size ** (-0.5)
    probs = jax.nn.softmax(scores, -1)
    return jnp.einsum('imn,ind->imd', probs, values, precision=exact_arithmetic)

def grid_loss(network_state, coords, valid, on_surface, off_surface, goals, inv_surf, inv_vol):
    lifting_readout_rows, block_projections, partition_maps, triple_maps_rows, sharpness_factors, gain_bias_rows = network_state
    mesh_nodes = coords.shape[-1]
    stream = jnp.einsum('fp,fc->pc', coords, lifting_readout_rows[:FIN], precision=exact_arithmetic)
    for block_number in range(DEPTH_TOTAL):
        vec_rows = gain_bias_rows[9 * block_number:9 * block_number + 9]
        weight_set = block_projections[block_number]
        normed = layer_norm(stream, vec_rows[0], vec_rows[1])
        features = jnp.dot(normed, weight_set[0], precision=exact_arithmetic) + vec_rows[2]
        chip_placement_list = jnp.dot(normed, weight_set[1], precision=exact_arithmetic) + vec_rows[3]
        partition_scores = jnp.einsum('sdj,ja->sda', chip_placement_list.reshape(mesh_nodes, FOCUS_GROUPS, GROUP_BREADTH), partition_maps[block_number], precision=exact_arithmetic) / sharpness_factors[block_number][:, None]
        slice_weights = jax.nn.softmax(partition_scores, -1) * valid[:, None, None]
        point_features = features.reshape(mesh_nodes, FOCUS_GROUPS, GROUP_BREADTH)
        weighted_points = jnp.einsum('eiw,eil->iwl', slice_weights, point_features, precision=exact_arithmetic)
        masses = lax.optimization_barrier(jnp.sum(slice_weights, 0))
        mixed_tokens = slice_attend(weighted_points, masses, triple_maps_rows[block_number])
        spread_tokens = jnp.einsum('acn,cnv->acv', slice_weights, mixed_tokens, precision=exact_arithmetic).reshape(mesh_nodes, MODEL_WIDTH)
        stream = stream + jnp.dot(spread_tokens, weight_set[2], precision=exact_arithmetic) + vec_rows[4]
        inner = jnp.dot(layer_norm(stream, vec_rows[5], vec_rows[6]), weight_set[3], precision=exact_arithmetic) + vec_rows[7]
        hidden = jax.nn.gelu(inner, approximate=False)
        stream = stream + jnp.dot(hidden, weight_set[4], precision=exact_arithmetic) + vec_rows[8]
    final = layer_norm(stream, gain_bias_rows[9 * DEPTH_TOTAL], gain_bias_rows[9 * DEPTH_TOTAL + 1])
    pred = jnp.einsum('oc,pc->op', lifting_readout_rows[FIN:], final, precision=exact_arithmetic)
    errors = (pred - goals) ** 2
    return inv_surf * jnp.sum(on_surface * errors[0]) + inv_vol * jnp.sum(off_surface * (errors[1] + errors[2]))

def adamw_update(weight, grad, first, second):
    first_new = beta_one * first + (1.0 - beta_one) * grad
    second_new = beta_two * second + (1.0 - beta_two) * grad * grad
    first_hat = first_new / (1.0 - beta_one ** STEP)
    second_hat = second_new / (1.0 - beta_two ** STEP)
    weight_new = weight - learn_rate * (first_hat / (jnp.sqrt(second_hat) + adam_epsilon) + weight_decay * weight)
    return (first_new, second_new, weight_new)

def reference(input_positions, flow_labels, airfoil_boundary, valid_sizes, lifting_readout_rows, block_projections, partition_maps, triple_maps_rows, sharpness_factors, gain_bias_rows, lifting_readout_mean, projection_running_mean, partition_map_mean, triple_maps_mean, sharpness_mean, gain_bias_mean, lifting_readout_square, projection_running_square, partition_map_square, triple_maps_square, sharpness_square, gain_bias_square):
    grids = MB * GRIDS_CH
    slots = jnp.arange(GPTS, dtype=jnp.int32)
    valid = (slots[None, None, :] < valid_sizes[:, :, None]).astype(jnp.float32).reshape(grids, GPTS)
    on_surface = valid * airfoil_boundary.astype(jnp.float32).reshape(grids, GPTS)
    off_surface = valid - on_surface
    inv_surf = 1.0 / jnp.maximum(jnp.sum(on_surface), 1.0)
    inv_vol = 1.0 / jnp.maximum(jnp.sum(off_surface), 1.0)
    network_state = (lifting_readout_rows, block_projections, partition_maps, triple_maps_rows, sharpness_factors, gain_bias_rows)

    def one_grid(carry, item):
        total, grads = carry
        coords, goals, valid_g, on_g, off_g = item
        value, pullback = jax.vjp(lambda p: grid_loss(p, coords, valid_g, on_g, off_g, goals, inv_surf, inv_vol), network_state)
        grad_set, = pullback(jnp.ones_like(value))
        return ((total + value, jax.tree.map(jnp.add, grads, grad_set)), None)
    start = (jnp.zeros((), jnp.float32), jax.tree.map(jnp.zeros_like, network_state))
    items = (input_positions.reshape(grids, FIN, GPTS), flow_labels.reshape(grids, OUTC, GPTS), valid, on_surface, off_surface)
    (loss_value, grads), _ = lax.scan(one_grid, start, items)
    grad_norm = jnp.sqrt(sum((jnp.sum(g * g) for g in grads)))
    factor = jnp.minimum(1.0, clip_limit / grad_norm)
    running_means = (lifting_readout_mean, projection_running_mean, partition_map_mean, triple_maps_mean, sharpness_mean, gain_bias_mean)
    running_squares = (lifting_readout_square, projection_running_square, partition_map_square, triple_maps_square, sharpness_square, gain_bias_square)
    results = []
    for weight, grad, first, second in zip(network_state, grads, running_means, running_squares):
        results.extend(adamw_update(weight, grad * factor, first, second))
    return tuple([loss_value, grad_norm] + results)
```

```python
import functools
import math

import jax
import jax.numpy as jnp
from jax import lax
from jax.experimental import pallas as pl
from jax.experimental.pallas import tpu as pltpu
from jax.sharding import PartitionSpec as P

STEP = 10
LANES = 128
FIN = 2
TILE = 256
VMEM_BYTES = 63 << 20
f32, bf16 = jnp.float32, jnp.bfloat16
NN, NT, TN = ((1,), (0,)), ((1,), (1,)), ((0,), (0,))


exact_arithmetic = lax.Precision.HIGHEST
clip_limit = 0.02
learn_rate = 0.1
beta_one = 0.9
beta_two = 0.999
adam_epsilon = 1e-08
weight_decay = 0.01


def layer_norm(values, gain, shift):
    center = values - jnp.mean(values, -1, keepdims=True)
    spread_tokens = jnp.mean(center * center, -1, keepdims=True)
    return center * lax.rsqrt(spread_tokens + 1e-05) * gain + shift


def slice_attend(weighted_points, masses, triple_maps_rows):
    head_size = triple_maps_rows.shape[0]
    tokens = weighted_points / (masses[..., None] + 1e-05)
    joined = jnp.einsum("imd,de->ime", tokens, triple_maps_rows, precision=exact_arithmetic)
    queries = joined[..., :head_size]
    keys = joined[..., head_size : 2 * head_size]
    values = joined[..., 2 * head_size :]
    scores = jnp.einsum("imd,ind->imn", queries, keys, precision=exact_arithmetic) * head_size ** (
        -0.5
    )
    probs = jax.nn.softmax(scores, -1)
    return jnp.einsum("imn,ind->imd", probs, values, precision=exact_arithmetic)


def slice_front(weight_set, slicer, temper, vec_rows, stream, valid):
    grids_n, points_n, width = stream.shape
    heads = temper.shape[0]
    normed = layer_norm(stream, vec_rows[0], vec_rows[1])
    features = (
        jnp.einsum("gpc,ce->gpe", normed, weight_set[0], precision=exact_arithmetic) + vec_rows[2]
    )
    chip_placement_list = (
        jnp.einsum("gpc,ce->gpe", normed, weight_set[1], precision=exact_arithmetic) + vec_rows[3]
    )
    partition_scores = (
        jnp.einsum(
            "gphd,dm->gphm",
            chip_placement_list.reshape(grids_n, points_n, heads, -1),
            slicer,
            precision=exact_arithmetic,
        )
        / temper[:, None]
    )
    slice_weights = jax.nn.softmax(partition_scores, -1) * valid[:, :, None, None]
    return (slice_weights, features.reshape(grids_n, points_n, heads, -1))


def slice_rest(weight_set, vec_rows, stream, spread_tokens):
    stream = (
        stream
        + jnp.einsum("gpc,ce->gpe", spread_tokens, weight_set[2], precision=exact_arithmetic)
        + vec_rows[4]
    )
    inner = (
        jnp.einsum(
            "gpc,ce->gpe",
            layer_norm(stream, vec_rows[5], vec_rows[6]),
            weight_set[3],
            precision=exact_arithmetic,
        )
        + vec_rows[7]
    )
    hidden = jax.nn.gelu(inner, approximate=False)
    return (
        stream
        + jnp.einsum("gpc,ce->gpe", hidden, weight_set[4], precision=exact_arithmetic)
        + vec_rows[8]
    )


def slice_mix(weighted_points, masses, qkv):
    grids_n, heads, slices, head_size = weighted_points.shape
    items = grids_n * heads
    flat_weighted = weighted_points.reshape(items, slices, head_size)
    flat_masses = masses.reshape(items, slices)
    own_weighted, own_masses = (
        lax.psum_scatter(flat_weighted, "pts", scatter_dimension=0, tiled=True),
        lax.psum_scatter(flat_masses, "pts", scatter_dimension=0, tiled=True),
    )
    mixed_tokens = lax.all_gather(
        slice_attend(own_weighted, own_masses, qkv), "pts", axis=0, tiled=True
    )
    kept = (own_weighted, own_masses)
    return (mixed_tokens.reshape(weighted_points.shape), kept)


def slice_mix_back(grad_mixed, kept, qkv):
    grids_n, heads, slices, head_size = grad_mixed.shape
    flat = grad_mixed.reshape(grids_n * heads, slices, head_size)
    _, pullback = jax.vjp(slice_attend, kept[0], kept[1], qkv)
    own_grad = lax.psum_scatter(flat, "pts", scatter_dimension=0, tiled=True)
    grad_weighted, grad_masses, grad_qkv = pullback(own_grad)
    grad_weighted, grad_masses = (
        lax.all_gather(grad_weighted, "pts", axis=0, tiled=True),
        lax.all_gather(grad_masses, "pts", axis=0, tiled=True),
    )
    return (
        grad_weighted.reshape(grad_mixed.shape),
        grad_masses.reshape(grids_n, heads, slices),
        grad_qkv,
    )


def layer_forward(stream, layer_set, valid):
    weight_set, slicer, qkv, temper, vec_rows = layer_set
    slice_weights, features = slice_front(weight_set, slicer, temper, vec_rows, stream, valid)
    weighted_points = jnp.einsum(
        "gphm,gphd->ghmd", slice_weights, features, precision=exact_arithmetic
    )
    masses = jnp.sum(slice_weights, 1)
    mixed_tokens, kept = slice_mix(weighted_points, masses, qkv)
    spread_tokens = jnp.einsum(
        "gphm,ghmd->gphd", slice_weights, mixed_tokens, precision=exact_arithmetic
    ).reshape(stream.shape)
    return (slice_rest(weight_set, vec_rows, stream, spread_tokens), (stream, mixed_tokens, kept))


def layer_backward(grad_out, layer_set, saved, valid):
    weight_set, slicer, qkv, temper, vec_rows = layer_set
    stream, mixed_tokens, kept = saved
    (slice_weights, features), pull_front = jax.vjp(
        lambda w_set, s_set, t_set, v_set, s_in: slice_front(
            w_set, s_set, t_set, v_set, s_in, valid
        ),
        weight_set,
        slicer,
        temper,
        vec_rows,
        stream,
    )
    spread_tokens = jnp.einsum(
        "gphm,ghmd->gphd", slice_weights, mixed_tokens, precision=exact_arithmetic
    ).reshape(stream.shape)
    _, pull_rest = jax.vjp(slice_rest, weight_set, vec_rows, stream, spread_tokens)
    grad_set_rest, grad_vec_rest, grad_stream, grad_spread = pull_rest(grad_out)
    grad_spread = grad_spread.reshape(features.shape)
    grad_weights = jnp.einsum(
        "gphd,ghmd->gphm", grad_spread, mixed_tokens, precision=exact_arithmetic
    )
    grad_mixed = jnp.einsum(
        "gphm,gphd->ghmd", slice_weights, grad_spread, precision=exact_arithmetic
    )
    grad_weighted, grad_masses, grad_qkv = slice_mix_back(grad_mixed, kept, qkv)
    grad_weights = (
        grad_weights
        + jnp.einsum("ghmd,gphd->gphm", grad_weighted, features, precision=exact_arithmetic)
        + grad_masses[:, None]
    )
    grad_features = jnp.einsum(
        "gphm,ghmd->gphd", slice_weights, grad_weighted, precision=exact_arithmetic
    )
    grad_set_front, grad_slicer, grad_temper, grad_vec_front, grad_stream_front = pull_front(
        (grad_weights, grad_features)
    )
    grads = (
        grad_set_rest + grad_set_front,
        grad_slicer,
        grad_qkv,
        grad_temper,
        grad_vec_rest + grad_vec_front,
    )
    return (grad_stream + grad_stream_front, grads)


def head_loss(head_rows, tail_rows, stream, goals, on_surface, off_surface, inv_surf, inv_vol):
    final = layer_norm(stream, tail_rows[0], tail_rows[1])
    pred = jnp.einsum("oc,gpc->gop", head_rows, final, precision=exact_arithmetic)
    errors = (pred - goals) ** 2
    return inv_surf * jnp.sum(on_surface * errors[:, 0]) + inv_vol * jnp.sum(
        off_surface * (errors[:, 1] + errors[:, 2])
    )


def layer_params(network_state, block_number):
    (
        lifting_readout_rows,
        block_projections,
        partition_maps,
        triple_maps_rows,
        sharpness_factors,
        gain_bias_rows,
    ) = network_state
    return (
        block_projections[block_number],
        partition_maps[block_number],
        triple_maps_rows[block_number],
        sharpness_factors[block_number],
        gain_bias_rows[9 * block_number : 9 * block_number + 9],
    )


def one_batch(network_state, coords, goals, valid, on_surface, off_surface, inv_surf, inv_vol):
    (
        lifting_readout_rows,
        block_projections,
        partition_maps,
        triple_maps_rows,
        sharpness_factors,
        gain_bias_rows,
    ) = network_state
    fin = coords.shape[1]
    layers_n = block_projections.shape[0]
    stream = jnp.einsum(
        "gfp,fc->gpc", coords, lifting_readout_rows[:fin], precision=exact_arithmetic
    )
    saved = []
    for block_number in range(layers_n):
        stream, keep_set = layer_forward(stream, layer_params(network_state, block_number), valid)
        saved.append(keep_set)
    batch_loss, pull_head = jax.vjp(
        lambda h_rows, t_rows, s_in: head_loss(
            h_rows, t_rows, s_in, goals, on_surface, off_surface, inv_surf, inv_vol
        ),
        lifting_readout_rows[fin:],
        gain_bias_rows[9 * layers_n :],
        stream,
    )
    grad_head, grad_tail, grad_stream = pull_head(jnp.ones_like(batch_loss))
    layer_grads = [None] * layers_n
    for block_number in reversed(range(layers_n)):
        grad_stream, layer_grads[block_number] = layer_backward(
            grad_stream, layer_params(network_state, block_number), saved[block_number], valid
        )
    grad_embed = jnp.einsum("gfp,gpc->fc", coords, grad_stream, precision=exact_arithmetic)
    grads = (
        jnp.concatenate([grad_embed, grad_head], 0),
        jnp.stack([entry[0] for entry in layer_grads]),
        jnp.stack([entry[1] for entry in layer_grads]),
        jnp.stack([entry[2] for entry in layer_grads]),
        jnp.stack([entry[3] for entry in layer_grads]),
        jnp.concatenate([entry[4] for entry in layer_grads] + [grad_tail], 0),
    )
    return (batch_loss, grads)


def adamw_update(weight, grad, first, second):
    first_new = beta_one * first + (1.0 - beta_one) * grad
    second_new = beta_two * second + (1.0 - beta_two) * grad * grad
    first_hat = first_new / (1.0 - beta_one**STEP)
    second_hat = second_new / (1.0 - beta_two**STEP)
    weight_new = weight - learn_rate * (
        first_hat / (jnp.sqrt(second_hat) + adam_epsilon) + weight_decay * weight
    )
    return (first_new, second_new, weight_new)


def body_points(
    input_positions,
    flow_labels,
    airfoil_boundary,
    valid_sizes,
    lifting_readout_rows,
    block_projections,
    partition_maps,
    triple_maps_rows,
    sharpness_factors,
    gain_bias_rows,
    lifting_readout_mean,
    projection_running_mean,
    partition_map_mean,
    triple_maps_mean,
    sharpness_mean,
    gain_bias_mean,
    lifting_readout_square,
    projection_running_square,
    partition_map_square,
    triple_maps_square,
    sharpness_square,
    gain_bias_square,
):
    batches = input_positions.shape[0]
    points_n = input_positions.shape[3]
    slots = lax.axis_index("pts") * points_n + jnp.arange(points_n, dtype=jnp.int32)
    valid = (slots[None, None, :] < valid_sizes[:, :, None]).astype(jnp.float32)
    on_surface = valid * airfoil_boundary.astype(jnp.float32)
    off_surface = valid - on_surface
    count_surf, count_vol = lax.psum((jnp.sum(on_surface), jnp.sum(off_surface)), ("pts", "grp"))
    inv_surf = 1.0 / jnp.maximum(count_surf, 1.0)
    inv_vol = 1.0 / jnp.maximum(count_vol, 1.0)
    network_state = (
        lifting_readout_rows,
        block_projections,
        partition_maps,
        triple_maps_rows,
        sharpness_factors,
        gain_bias_rows,
    )
    loss_value = jnp.zeros((), jnp.float32)
    grads = tuple((jnp.zeros_like(entry) for entry in network_state))
    for batch in range(batches):
        batch_loss, batch_set = one_batch(
            network_state,
            input_positions[batch],
            flow_labels[batch],
            valid[batch],
            on_surface[batch],
            off_surface[batch],
            inv_surf,
            inv_vol,
        )
        loss_value = loss_value + batch_loss
        grads = tuple((total + entry for total, entry in zip(grads, batch_set)))
    running_means = (
        lifting_readout_mean,
        projection_running_mean,
        partition_map_mean,
        triple_maps_mean,
        sharpness_mean,
        gain_bias_mean,
    )
    running_squares = (
        lifting_readout_square,
        projection_running_square,
        partition_map_square,
        triple_maps_square,
        sharpness_square,
        gain_bias_square,
    )
    return finish(loss_value, grads, network_state, running_means, running_squares)


def finish(loss_value, grads, network_state, running_means, running_squares):
    summed = lax.psum((loss_value,) + grads, ("pts", "grp"))
    loss_value = summed[0]
    grads = summed[1:]
    grad_norm = jnp.sqrt(sum((jnp.sum(entry * entry) for entry in grads)))
    factor = jnp.minimum(1.0, clip_limit / grad_norm)
    results = []
    for weight, grad, first, second in zip(network_state, grads, running_means, running_squares):
        results.extend(adamw_update(weight, grad * factor, first, second))
    return tuple([loss_value, grad_norm] + results)


def _split(x):
    high = x.astype(bf16)
    return high, (x - high.astype(f32)).astype(bf16)


def _dot(a, b, dims, precision=None):
    return lax.dot_general(a, b, (dims, ((), ())), precision=precision, preferred_element_type=f32)


def _dot3(a, b, dims):
    return _dot(a[0], b[0], dims) + _dot(a[0], b[1], dims) + _dot(a[1], b[0], dims)


def _dotx(a, b, dims):
    return _dot(a, b, dims, lax.Precision.HIGHEST)


def _wide(col, lanes):
    return jnp.concatenate([col] * (lanes // LANES), 1) if lanes > LANES else col


def _fold(x):
    total = x[:, :LANES]
    for start in range(LANES, x.shape[1], LANES):
        total = total + x[:, start : start + LANES]
    return total


def _lockstep(makers):
    running = list(makers)
    while running:
        alive = []
        for entry in running:
            try:
                next(entry)
                alive.append(entry)
            except StopIteration:
                pass
        running = alive


def _diag_heads(full, depth, slices):
    heads = full.shape[0] // depth
    lane = lax.broadcasted_iota(jnp.int32, (depth, full.shape[1]), 1)
    picked = full[:depth]
    for head in range(1, heads):
        picked = jnp.where(lane >= head * slices, full[head * depth : (head + 1) * depth], picked)
    return picked


def _block_heads(flat, heads, slices):
    lane = lax.broadcasted_iota(jnp.int32, flat.shape, 1)
    return jnp.concatenate(
        [
            jnp.where((lane >= head * slices) & (lane < (head + 1) * slices), flat, 0.0)
            for head in range(heads)
        ],
        0,
    )


def _norm(x):
    inv_width = 1.0 / x.shape[0]
    center = x - jnp.sum(x, 0, keepdims=True) * inv_width
    rstd = lax.rsqrt(jnp.sum(center * center, 0, keepdims=True) * inv_width + 1e-05)
    return center * rstd, rstd


def _norm_back(grad, xhat, rstd):
    inv_width = 1.0 / grad.shape[0]
    mean_grad = jnp.sum(grad, 0, keepdims=True) * inv_width
    mean_proj = jnp.sum(grad * xhat, 0, keepdims=True) * inv_width
    return (grad - mean_grad - xhat * mean_proj) * rstd


def grids_kernel(dims, *refs):
    (grids, points, width, heads, head_size, slices, layers, fin, outc, tile) = dims
    (
        sizes_ref,
        sharp_ref,
        inv_ref,
        points_ref,
        io_ref,
        mats_ref,
        maps_ref,
        qkv_ref,
        vecs_ref,
        loss_out,
        io_out,
        mats_out,
        maps_out,
        qkv_out,
        sharp_out,
        vecs_out,
        stream,
        xh1h,
        xh1l,
        rs1,
        feath,
        featl,
        placeh,
        placel,
        wgth,
        wgtl,
        sprh,
        sprl,
        xh2h,
        xh2l,
        rs2,
        hidh,
        hidl,
        gslope,
        upmh,
        upml,
        cols,
        bdmh,
        bdml,
        bdth,
        bdtl,
        accw,
        accf,
        tok,
        rmass,
        qkvs,
        probs,
        mbdh,
        mbdl,
        dbdh,
        dbdl,
        cmbh,
        cmbl,
        dmcol,
        vacc,
        gmacc,
        headacc,
        embacc,
        lossacc,
    ) = refs
    half = heads // 2
    span = half * slices
    group = half * head_size
    pairs = heads // 2
    all_slices = heads * slices
    steps = points // tile
    scale = head_size ** (-0.5)
    ones_rows = jnp.ones((8, LANES), f32)

    def split_to(high_ref, low_ref, index, value):
        high, low = _split(value)
        high_ref[index] = high
        low_ref[index] = low
        return high, low

    vecs = vecs_ref[...]
    row_id = lax.broadcasted_iota(jnp.int32, (vecs.shape[0], LANES), 0)

    def column(row):
        return _dotx(vecs, jnp.where(row_id == row, 1.0, 0.0), TN)

    for layer in range(layers):
        base = 9 * layer
        gain_a, shift_a = column(base), column(base + 1)
        gain_b, shift_b = column(base + 5), column(base + 6)
        cols[layer, 0] = gain_a
        cols[layer, 1] = shift_a
        cols[layer, 2] = gain_b
        cols[layer, 3] = shift_b
        for slot in range(5):
            flipped = mats_ref[layer, slot].T
            bias = column(base + (2, 3, 4, 7, 8)[slot])
            if slot in (0, 1, 3):
                gain, shift, row = (gain_b, shift_b, 5) if slot == 3 else (gain_a, shift_a, 0)
                bias = bias + _dotx(flipped, shift, NN)
                flipped = flipped * vecs[base + row : base + row + 1]
            cols[layer, 4 + slot] = bias
            split_to(upmh, upml, (layer, slot), flipped)
        tiled = jnp.concatenate([maps_ref[layer]] * half, 1)
        for part in range(2):
            lane = lax.broadcasted_iota(jnp.int32, (1, span), 1)
            sharp = jnp.full((1, span), 0.0, f32) + sharp_ref[layer, part * half]
            for head in range(1, half):
                sharp = jnp.where(lane >= head * slices, sharp_ref[layer, part * half + head], sharp)
            block = _block_heads(tiled / sharp, half, slices)
            split_to(bdth, bdtl, (layer, part), block)
            split_to(bdmh, bdml, (layer, part), block.T)

    vacc[...] = jnp.zeros_like(vacc)
    gmacc[...] = jnp.zeros_like(gmacc)
    headacc[...] = jnp.zeros_like(headacc)
    embacc[...] = jnp.zeros_like(embacc)
    lossacc[...] = jnp.zeros_like(lossacc)
    mats_out[...] = jnp.zeros_like(mats_out)
    qkv_out[...] = jnp.zeros_like(qkv_out)

    io_all = io_ref[...]
    io_id = lax.broadcasted_iota(jnp.int32, (io_all.shape[0], LANES), 0)
    lift = [_dotx(io_all, jnp.where(io_id == row, 1.0, 0.0), TN) for row in range(fin)]

    def window(step):
        return pl.ds(pl.multiple_of(step * tile, tile), tile)

    def pair_of(high_ref, low_ref, index):
        return high_ref[index], low_ref[index]

    @pl.loop(0, steps)
    def _(step):
        at = window(step)
        for grid in range(grids):
            x = jnp.zeros((width, tile), f32)
            for row in range(fin):
                x = x + _wide(lift[row], tile) * points_ref[grid, row : row + 1, at]
            stream[grid, :, at] = x

    def front(layer, grid, at, step):
        xhat, rstd = _norm(stream[grid, :, at])
        xhat = split_to(xh1h, xh1l, (layer, grid, slice(None), at), xhat)
        rs1[layer, grid, :, at] = rstd
        yield
        feat = _dot3(pair_of(upmh, upml, (layer, 0)), xhat, NN) + _wide(cols[layer, 4], tile)
        place = _dot3(pair_of(upmh, upml, (layer, 1)), xhat, NN) + _wide(cols[layer, 5], tile)
        feat = split_to(feath, featl, (layer, grid, slice(None), at), feat)
        place = split_to(placeh, placel, (layer, grid, slice(None), at), place)
        yield
        slots = lax.broadcasted_iota(jnp.int32, (1, tile), 1) + step * tile
        valid = jnp.where(slots < sizes_ref[grid], 1.0, 0.0)
        for part in range(2):
            rows = slice(part * group, (part + 1) * group)
            scores = _dot3(
                pair_of(bdmh, bdml, (layer, part)), (place[0][rows], place[1][rows]), NN
            ).reshape(half, slices, tile)
            expo = jnp.exp(scores - jnp.max(scores, 1, keepdims=True))
            ratio = valid[None] / jnp.sum(expo, 1, keepdims=True)
            weight = (expo * ratio).reshape(span, tile)
            wrows = slice(part * span, (part + 1) * span)
            weight = split_to(wgth, wgtl, (layer, grid, wrows, at), weight)
            yield
            lead = jnp.concatenate([feat[0][rows], jnp.ones((16, tile), bf16)], 0)
            accw[grid, part] += _dot(lead, weight[0], NT) + _dot(lead, weight[1], NT)
            accf[grid, part] += _dot(feat[1][rows], weight[0], NT)
            yield

    def attend(layer, grid):
        parts, masses = [], []
        for part in range(2):
            total = accw[grid, part]
            parts.append(_diag_heads(total[:group] + accf[grid, part], head_size, slices))
            masses.append(total[group : group + 1])
        rate = 1.0 / (jnp.concatenate(masses, 1) + 1e-05)
        tokens = jnp.concatenate(parts, 1) * rate
        tok[layer, grid] = tokens
        rmass[layer, grid] = rate
        yield
        joined = _dotx(qkv_ref[layer], tokens, TN)
        qkvs[layer, grid] = joined
        yield
        lane = lax.broadcasted_iota(jnp.int32, (slices, 2 * slices), 1)
        mixed = []
        for pair in range(pairs):
            at = slice(pair * 2 * slices, (pair + 1) * 2 * slices)
            query = joined[:head_size, at]
            key = joined[head_size : 2 * head_size, at]
            value = joined[2 * head_size :, at]
            full = _dotx(key, query, TN)
            scores = jnp.where(lane < slices, full[:slices], full[slices:]) * scale
            expo = jnp.exp(scores - jnp.max(scores, 0, keepdims=True))
            prob = expo / jnp.sum(expo, 0, keepdims=True)
            probs[layer, grid, pair] = prob
            mixed.append(_dotx(value, _block_heads(prob, 2, slices), NN))
        for part in range(2):
            flat = jnp.concatenate(mixed[part * (pairs // 2) : (part + 1) * (pairs // 2)], 1)
            block = _block_heads(flat, half, slices)
            split_to(mbdh, mbdl, (layer, grid, part), block)
        yield

    def rest(layer, grid, at):
        spread = []
        for part in range(2):
            wrows = slice(part * span, (part + 1) * span)
            weight = pair_of(wgth, wgtl, (layer, grid, wrows, at))
            spread.append(_dot3(pair_of(mbdh, mbdl, (layer, grid, part)), weight, NN))
        spread = split_to(
            sprh, sprl, (layer, grid, slice(None), at), jnp.concatenate(spread, 0)
        )
        yield
        x = (
            stream[grid, :, at]
            + _dot3(pair_of(upmh, upml, (layer, 2)), spread, NN)
            + _wide(cols[layer, 6], tile)
        )
        xhat, rstd = _norm(x)
        xhat = split_to(xh2h, xh2l, (layer, grid, slice(None), at), xhat)
        rs2[layer, grid, :, at] = rstd
        yield
        inner = _dot3(pair_of(upmh, upml, (layer, 3)), xhat, NN) + _wide(cols[layer, 7], tile)
        cdf = 0.5 + 0.5 * lax.erf(inner * (0.5**0.5))
        gslope[layer, grid, :, at] = cdf + inner * jnp.exp(-0.5 * inner * inner) * (
            (2.0 * math.pi) ** -0.5
        )
        hidden = split_to(hidh, hidl, (layer, grid, slice(None), at), inner * cdf)
        yield
        stream[grid, :, at] = (
            x
            + _dot3(pair_of(upmh, upml, (layer, 4)), hidden, NN)
            + _wide(cols[layer, 8], tile)
        )
        yield

    @pl.loop(0, layers)
    def _(layer):
        accw[...] = jnp.zeros_like(accw)
        accf[...] = jnp.zeros_like(accf)

        @pl.loop(0, steps)
        def _(step):
            at = window(step)
            _lockstep([front(layer, grid, at, step) for grid in range(grids)])

        _lockstep([attend(layer, grid) for grid in range(grids)])

        @pl.loop(0, steps)
        def _(step):
            at = window(step)
            _lockstep([rest(layer, grid, at) for grid in range(grids)])

    tail = 9 * layers
    head_rows = jnp.concatenate(
        [io_ref[fin:, :], jnp.zeros((8 - outc, width), f32)], 0
    )
    head_gain = head_rows * vecs[tail : tail + 1]
    head_pair = _split(head_gain)
    head_bias = _dotx(head_rows, column(tail + 1), NN)
    inv_surf, inv_vol = inv_ref[0], inv_ref[1]

    def crown(grid, at, step):
        xhat, rstd = _norm(stream[grid, :, at])
        halves = _split(xhat)
        pred = _dot3(head_pair, halves, NN) + _wide(head_bias, tile)
        slots = lax.broadcasted_iota(jnp.int32, (1, tile), 1) + step * tile
        valid = jnp.where(slots < sizes_ref[grid], 1.0, 0.0)
        surf = valid * points_ref[grid, fin + outc : fin + outc + 1, at]
        vol = (valid - surf) * inv_vol
        surf = surf * inv_surf
        row = lax.broadcasted_iota(jnp.int32, (8, tile), 0)
        factor = jnp.where(row == 0, surf, jnp.where(row < outc, vol, 0.0))
        goals = jnp.concatenate(
            [points_ref[grid, fin : fin + outc, at], jnp.zeros((8 - outc, tile), f32)], 0
        )
        error = pred - goals
        scaled = factor * error
        lossacc[...] += _fold(scaled * error)
        dpred = scaled + scaled
        headacc[0] += _fold(dpred)
        dhalves = _split(dpred)
        headacc_rows = _dot3(dhalves, halves, NT)
        for start in range(0, width, LANES):
            headacc[1 + start // LANES] += headacc_rows[:, start : start + LANES]
        yield
        grad = _dot3(head_pair, dhalves, TN)
        stream[grid, :, at] = _norm_back(grad, xhat, rstd)
        yield

    @pl.loop(0, steps)
    def _(step):
        at = window(step)
        _lockstep([crown(grid, at, step) for grid in range(grids)])

    for layer in range(layers):
        for slot in range(5):
            mat = mats_ref[layer, slot]
            if slot in (0, 1, 3):
                mat = mat * _wide(cols[layer, 2 if slot == 3 else 0], width)
            split_to(upmh, upml, (layer, slot), mat)

    def back_rest(layer, grid, at):
        grad = stream[grid, :, at]
        vacc[layer, 4] += _fold(grad)
        pieces = _split(grad)
        dhid = _dot3(pair_of(upmh, upml, (layer, 4)), pieces, NN)
        hidden = pair_of(hidh, hidl, (layer, grid, slice(None), at))
        mats_out[layer, 4] += _dot3(hidden, pieces, NT)
        yield
        dinner = dhid * gslope[layer, grid, :, at]
        vacc[layer, 3] += _fold(dinner)
        pieces = _split(dinner)
        xhat = pair_of(xh2h, xh2l, (layer, grid, slice(None), at))
        dxhat = _dot3(pair_of(upmh, upml, (layer, 3)), pieces, NN)
        mats_out[layer, 3] += _dot3(xhat, pieces, NT)
        yield
        grad = grad + _norm_back(
            dxhat, xhat[0].astype(f32) + xhat[1].astype(f32), rs2[layer, grid, :, at]
        )
        stream[grid, :, at] = grad
        vacc[layer, 2] += _fold(grad)
        pieces = _split(grad)
        dspread = _dot3(pair_of(upmh, upml, (layer, 2)), pieces, NN)
        mats_out[layer, 2] += _dot3(
            pair_of(sprh, sprl, (layer, grid, slice(None), at)), pieces, NT
        )
        dspread = split_to(sprh, sprl, (layer, grid, slice(None), at), dspread)
        yield
        for part in range(2):
            rows = slice(part * group, (part + 1) * group)
            wrows = slice(part * span, (part + 1) * span)
            weight = pair_of(wgth, wgtl, (layer, grid, wrows, at))
            accf[grid, part] += _dot3((dspread[0][rows], dspread[1][rows]), weight, NT)
        yield

    def back_attend(layer, grid):
        joined = qkvs[layer, grid]
        tokens = tok[layer, grid]
        rate = rmass[layer, grid]
        lane = lax.broadcasted_iota(jnp.int32, (slices, 2 * slices), 1)
        dmixed = jnp.concatenate(
            [_diag_heads(accf[grid, part], head_size, slices) for part in range(2)], 1
        )
        yield
        dqs, dks, dvs = [], [], []
        for pair in range(pairs):
            at = slice(pair * 2 * slices, (pair + 1) * 2 * slices)
            query = joined[:head_size, at]
            key = joined[head_size : 2 * head_size, at]
            value = joined[2 * head_size :, at]
            prob = probs[layer, grid, pair]
            dmix = dmixed[:, at]
            full = _dotx(value, dmix, TN)
            dprob = jnp.where(lane < slices, full[:slices], full[slices:])
            dscore = (
                prob * (dprob - jnp.sum(prob * dprob, 0, keepdims=True)) * scale
            )
            dblock = _block_heads(dscore, 2, slices)
            dvs.append(_dotx(dmix, _block_heads(prob, 2, slices), NT))
            dqs.append(_dotx(key, dblock, NN))
            dks.append(_dotx(query, dblock, NT))
        dqkv = jnp.concatenate(
            [jnp.concatenate(part, 1) for part in (dqs, dks, dvs)], 0
        )
        yield
        dtok = _dotx(qkv_ref[layer], dqkv, NN)
        qkv_out[layer] += _dotx(tokens, dqkv, NT)
        dweighted = dtok * rate
        dmass = -jnp.sum(dweighted * tokens, 0, keepdims=True)
        yield
        dmass = jnp.broadcast_to(dmass, (8, all_slices))
        row_one = jnp.where(
            lax.broadcasted_iota(jnp.int32, (8, LANES), 0) == 0, 1.0, 0.0
        )
        dmcol[grid] = _dotx(dmass, row_one, TN)
        for part in range(2):
            block = _block_heads(dweighted[:, part * span : (part + 1) * span], half, slices)
            split_to(dbdh, dbdl, (grid, part), block)
            mix = mbdh[layer, grid, part].astype(f32) + mbdl[layer, grid, part].astype(f32)
            both = jnp.concatenate([mix, block], 0)
            split_to(cmbh, cmbl, (grid, part), both.T)
        yield

    def back_front(layer, grid, at):
        feat = pair_of(feath, featl, (layer, grid, slice(None), at))
        place = pair_of(placeh, placel, (layer, grid, slice(None), at))
        dfeats, dplaces = [], []
        for part in range(2):
            rows = slice(part * group, (part + 1) * group)
            wrows = slice(part * span, (part + 1) * span)
            weight = pair_of(wgth, wgtl, (layer, grid, wrows, at))
            dspread = pair_of(sprh, sprl, (layer, grid, rows, at))
            both = tuple(
                jnp.concatenate([one, two[rows]], 0) for one, two in zip(dspread, feat)
            )
            dweight = _dot3(pair_of(cmbh, cmbl, (grid, part)), both, NN)
            dweight = dweight + _wide(dmcol[grid, wrows], tile)
            full = weight[0].astype(f32) + weight[1].astype(f32)
            prod = full * dweight
            total = jnp.sum(prod.reshape(half, slices, tile), 1, keepdims=True)
            dscore = (
                prod.reshape(half, slices, tile) - full.reshape(half, slices, tile) * total
            ).reshape(span, tile)
            pieces = _split(dscore)
            yield
            dplaces.append(_dot3(pair_of(bdth, bdtl, (layer, part)), pieces, NN))
            gmacc[layer, part] += _dot3((place[0][rows], place[1][rows]), pieces, NT)
            dfeats.append(_dot3(pair_of(dbdh, dbdl, (grid, part)), weight, NN))
            yield
        dfeat = jnp.concatenate(dfeats, 0)
        dplace = jnp.concatenate(dplaces, 0)
        vacc[layer, 0] += _fold(dfeat)
        vacc[layer, 1] += _fold(dplace)
        dfeat, dplace = _split(dfeat), _split(dplace)
        xhat = pair_of(xh1h, xh1l, (layer, grid, slice(None), at))
        dxhat = _dot3(pair_of(upmh, upml, (layer, 0)), dfeat, NN) + _dot3(
            pair_of(upmh, upml, (layer, 1)), dplace, NN
        )
        mats_out[layer, 0] += _dot3(xhat, dfeat, NT)
        mats_out[layer, 1] += _dot3(xhat, dplace, NT)
        yield
        grad = stream[grid, :, at] + _norm_back(
            dxhat, xhat[0].astype(f32) + xhat[1].astype(f32), rs1[layer, grid, :, at]
        )
        stream[grid, :, at] = grad
        yield

    @pl.loop(0, layers)
    def _(index):
        layer = layers - 1 - index
        accf[...] = jnp.zeros_like(accf)

        @pl.loop(0, steps)
        def _(step):
            at = window(step)
            _lockstep([back_rest(layer, grid, at) for grid in range(grids)])

        _lockstep([back_attend(layer, grid) for grid in range(grids)])

        @pl.loop(0, steps)
        def _(step):
            at = window(step)
            _lockstep([back_front(layer, grid, at) for grid in range(grids)])

    @pl.loop(0, steps)
    def _(step):
        at = window(step)
        for grid in range(grids):
            coords = jnp.concatenate(
                [points_ref[grid, :fin, at], jnp.zeros((8 - fin, tile), f32)], 0
            )
            embacc[...] += _dot3(_split(coords), _split(stream[grid, :, at]), NT)

    def to_row(folded):
        return _dotx(ones_rows, folded, NT)[:1]

    ones_wide = jnp.ones((8, width), f32)
    for layer in range(layers):
        base = 9 * layer
        sums = [to_row(vacc[layer, slot]) for slot in range(5)]
        gain_rows = []
        for slot in (0, 1, 3):
            gain, shift = (2, 3) if slot == 3 else (0, 1)
            gram = mats_out[layer, slot]
            mat = mats_ref[layer, slot]
            gain_rows.append(_dotx(ones_wide, gram * mat, NT)[:1])
            mats_out[layer, slot] = (
                _wide(cols[layer, gain], width) * gram + _wide(cols[layer, shift], width) * sums[slot]
            )
        def shift_row(slot):
            return _dotx(jnp.broadcast_to(sums[slot], (8, width)), mats_ref[layer, slot], NT)[:1]
        rows = [
            gain_rows[0] + gain_rows[1],
            shift_row(0) + shift_row(1),
            sums[0],
            sums[1],
            sums[2],
            gain_rows[2],
            shift_row(3),
            sums[3],
            sums[4],
        ]
        for slot, row in enumerate(rows):
            vecs_out[base + slot : base + slot + 1, :] = row
        tiled = jnp.concatenate([maps_ref[layer]] * half, 1)
        total = None
        sharp_total = None
        for part in range(2):
            lane = lax.broadcasted_iota(jnp.int32, (1, span), 1)
            sharp = jnp.full((1, span), 0.0, f32) + sharp_ref[layer, part * half]
            for head in range(1, half):
                sharp = jnp.where(lane >= head * slices, sharp_ref[layer, part * half + head], sharp)
            picked = _diag_heads(gmacc[layer, part], head_size, slices) / sharp
            total = picked if total is None else total + picked
            share = -jnp.sum(picked * tiled, 0, keepdims=True) / sharp
            chosen = jnp.where(
                lax.broadcasted_iota(jnp.int32, (span, LANES), 0) // slices + part * half
                == lax.broadcasted_iota(jnp.int32, (span, LANES), 1),
                1.0,
                0.0,
            )
            share = _dotx(jnp.broadcast_to(share, (8, span)), chosen, NN)
            sharp_total = share if sharp_total is None else sharp_total + share
        sharp_out[layer : layer + 1, :] = sharp_total[:1, :heads]
        total = _fold(total)
        total = total + pltpu.roll(total, slices, 1)
        maps_out[layer] = total[:, :slices]

    spread_dpred = _dotx(headacc[0], jnp.ones((LANES, LANES), f32), NN)
    gram = jnp.concatenate([headacc[1 + k] for k in range(width // LANES)], 1)
    gain_row, shift_row = vecs[tail : tail + 1], vecs[tail + 1 : tail + 2]
    io_out[fin:, :] = (gram * gain_row + _wide(spread_dpred, width) * shift_row)[:outc]
    io_out[:fin, :] = embacc[:fin, :]
    vecs_out[tail : tail + 1, :] = jnp.sum(gram * head_rows, 0, keepdims=True)
    vecs_out[tail + 1 : tail + 2, :] = jnp.sum(
        _wide(spread_dpred, width) * head_rows, 0, keepdims=True
    )
    loss_out[...] = jnp.broadcast_to(
        jnp.sum(jnp.sum(lossacc[...], 0, keepdims=True), 1, keepdims=True), (1, LANES)
    )


def whole_grid_grads(network_state, sizes, packed, inverse):
    io_rows, mats, maps, qkv, sharp, vecs = network_state
    grids, _, points = packed.shape
    layers, _, width, _ = mats.shape
    heads = sharp.shape[1]
    head_size, slices = maps.shape[1:]
    outc = io_rows.shape[0] - FIN
    tile = TILE
    half, span, group = heads // 2, heads // 2 * slices, heads // 2 * head_size
    dims = (grids, points, width, heads, head_size, slices, layers, FIN, outc, tile)

    def both(*shape):
        return [pltpu.VMEM(shape, bf16), pltpu.VMEM(shape, bf16)]

    def single(*shape):
        return [pltpu.VMEM(shape, f32)]

    kept = (layers, grids, width, points)
    scratch = (
        single(grids, width, points)
        + both(*kept)
        + single(layers, grids, 1, points)
        + both(*kept)
        + both(*kept)
        + both(layers, grids, 2 * span, points)
        + both(*kept)
        + both(*kept)
        + single(layers, grids, 1, points)
        + both(*kept)
        + single(*kept)
        + both(layers, 5, width, width)
        + single(layers, 9, width, LANES)
        + both(layers, 2, span, group)
        + both(layers, 2, group, span)
        + single(grids, 2, group + 16, span)
        + single(grids, 2, group, span)
        + single(layers, grids, head_size, 2 * span)
        + single(layers, grids, 1, 2 * span)
        + single(layers, grids, 3 * head_size, 2 * span)
        + single(layers, grids, half, slices, 2 * slices)
        + both(layers, grids, 2, group, span)
        + both(grids, 2, group, span)
        + both(grids, 2, span, 2 * group)
        + single(grids, 2 * span, LANES)
        + single(layers, 5, width, LANES)
        + single(layers, 2, group, span)
        + single(1 + width // LANES, 8, LANES)
        + single(8, width)
        + single(8, LANES)
    )
    vmem = pl.BlockSpec(memory_space=pltpu.VMEM)
    smem = pl.BlockSpec(memory_space=pltpu.SMEM)
    shapes = [(1, LANES)] + [entry.shape for entry in network_state]
    results = pl.pallas_call(
        functools.partial(grids_kernel, dims),
        out_shape=[jax.ShapeDtypeStruct(shape, f32) for shape in shapes],
        in_specs=[smem] * 3 + [vmem] * 6,
        out_specs=[vmem] * 7,
        scratch_shapes=scratch,
        compiler_params=pltpu.CompilerParams(vmem_limit_bytes=VMEM_BYTES),
    )(sizes, sharp, inverse, packed, io_rows, mats, maps, qkv, vecs)
    return (results[0][0, 0], tuple(results[1:]))


def body_grids(*arrays):
    input_positions, flow_labels, airfoil_boundary, valid_sizes = arrays[:4]
    network_state = arrays[4:10]
    batches, own, _, points_n = input_positions.shape
    members = lax.axis_size("pts")
    share = own // members
    packed = jnp.concatenate(
        [input_positions, flow_labels, airfoil_boundary.astype(f32)[:, :, None]], 2
    )
    packed = lax.all_to_all(packed, "pts", split_axis=1, concat_axis=3, tiled=True)
    packed = packed.reshape(batches * share, packed.shape[2], packed.shape[3])
    sizes = lax.dynamic_slice_in_dim(valid_sizes, lax.axis_index("pts") * share, share, 1)
    sizes = sizes.reshape(-1)
    slots = jnp.arange(packed.shape[2], dtype=jnp.int32)
    valid = (slots[None] < sizes[:, None]).astype(f32)
    on_surface = valid * packed[:, -1]
    counts = lax.psum(
        jnp.stack([jnp.sum(on_surface), jnp.sum(valid - on_surface)]), ("pts", "grp")
    )
    inverse = 1.0 / jnp.maximum(counts, 1.0)
    loss_value, grads = whole_grid_grads(network_state, sizes, packed, inverse)
    return finish(loss_value, grads, network_state, arrays[10:16], arrays[16:22])


def solution(mesh):
    in_specs = (
        P(None, "grp", None, "pts"),
        P(None, "grp", None, "pts"),
        P(None, "grp", "pts"),
        P(None, "grp"),
        P(),
        P(),
        P(),
        P(),
        P(),
        P(),
        P(),
        P(),
        P(),
        P(),
        P(),
        P(),
        P(),
        P(),
        P(),
        P(),
        P(),
        P(),
    )
    out_specs = (
        P(),
        P(),
        P(),
        P(),
        P(),
        P(),
        P(),
        P(),
        P(),
        P(),
        P(),
        P(),
        P(),
        P(),
        P(),
        P(),
        P(),
        P(),
        P(),
        P(),
    )
    members = mesh.shape["pts"]

    def body(*arrays):
        batches, own, _, points_n = arrays[0].shape
        grids = batches * own // members
        fits = own % members == 0 and grids * points_n * members <= 2048
        return (body_grids if fits else body_points)(*arrays)

    return jax.shard_map(body, mesh=mesh, in_specs=in_specs, out_specs=out_specs, check_vma=False)
```

```python
import functools
import math

import jax
import jax.numpy as jnp
from jax import lax
from jax.experimental import pallas as pl
from jax.experimental.pallas import tpu as pltpu
from jax.sharding import PartitionSpec as P

STEP = 10
LANES = 128
FIN = 2
TILE = 256
VMEM_BYTES = 63 << 20
f32, bf16 = jnp.float32, jnp.bfloat16
MESH = pl.DeviceIdType.MESH
NN, NT, TN = ((1,), (0,)), ((1,), (1,)), ((0,), (0,))


exact_arithmetic = lax.Precision.HIGHEST
clip_limit = 0.02
learn_rate = 0.1
beta_one = 0.9
beta_two = 0.999
adam_epsilon = 1e-08
weight_decay = 0.01


def layer_norm(values, gain, shift):
    center = values - jnp.mean(values, -1, keepdims=True)
    spread_tokens = jnp.mean(center * center, -1, keepdims=True)
    return center * lax.rsqrt(spread_tokens + 1e-05) * gain + shift


def slice_attend(weighted_points, masses, triple_maps_rows):
    head_size = triple_maps_rows.shape[0]
    tokens = weighted_points / (masses[..., None] + 1e-05)
    joined = jnp.einsum("imd,de->ime", tokens, triple_maps_rows, precision=exact_arithmetic)
    queries = joined[..., :head_size]
    keys = joined[..., head_size : 2 * head_size]
    values = joined[..., 2 * head_size :]
    scores = jnp.einsum("imd,ind->imn", queries, keys, precision=exact_arithmetic) * head_size ** (
        -0.5
    )
    probs = jax.nn.softmax(scores, -1)
    return jnp.einsum("imn,ind->imd", probs, values, precision=exact_arithmetic)


def slice_front(weight_set, slicer, temper, vec_rows, stream, valid):
    grids_n, points_n, width = stream.shape
    heads = temper.shape[0]
    normed = layer_norm(stream, vec_rows[0], vec_rows[1])
    features = (
        jnp.einsum("gpc,ce->gpe", normed, weight_set[0], precision=exact_arithmetic) + vec_rows[2]
    )
    chip_placement_list = (
        jnp.einsum("gpc,ce->gpe", normed, weight_set[1], precision=exact_arithmetic) + vec_rows[3]
    )
    partition_scores = (
        jnp.einsum(
            "gphd,dm->gphm",
            chip_placement_list.reshape(grids_n, points_n, heads, -1),
            slicer,
            precision=exact_arithmetic,
        )
        / temper[:, None]
    )
    slice_weights = jax.nn.softmax(partition_scores, -1) * valid[:, :, None, None]
    return (slice_weights, features.reshape(grids_n, points_n, heads, -1))


def slice_rest(weight_set, vec_rows, stream, spread_tokens):
    stream = (
        stream
        + jnp.einsum("gpc,ce->gpe", spread_tokens, weight_set[2], precision=exact_arithmetic)
        + vec_rows[4]
    )
    inner = (
        jnp.einsum(
            "gpc,ce->gpe",
            layer_norm(stream, vec_rows[5], vec_rows[6]),
            weight_set[3],
            precision=exact_arithmetic,
        )
        + vec_rows[7]
    )
    hidden = jax.nn.gelu(inner, approximate=False)
    return (
        stream
        + jnp.einsum("gpc,ce->gpe", hidden, weight_set[4], precision=exact_arithmetic)
        + vec_rows[8]
    )


def slice_mix(weighted_points, masses, qkv):
    grids_n, heads, slices, head_size = weighted_points.shape
    items = grids_n * heads
    flat_weighted = weighted_points.reshape(items, slices, head_size)
    flat_masses = masses.reshape(items, slices)
    own_weighted, own_masses = (
        lax.psum_scatter(flat_weighted, "pts", scatter_dimension=0, tiled=True),
        lax.psum_scatter(flat_masses, "pts", scatter_dimension=0, tiled=True),
    )
    mixed_tokens = lax.all_gather(
        slice_attend(own_weighted, own_masses, qkv), "pts", axis=0, tiled=True
    )
    kept = (own_weighted, own_masses)
    return (mixed_tokens.reshape(weighted_points.shape), kept)


def slice_mix_back(grad_mixed, kept, qkv):
    grids_n, heads, slices, head_size = grad_mixed.shape
    flat = grad_mixed.reshape(grids_n * heads, slices, head_size)
    _, pullback = jax.vjp(slice_attend, kept[0], kept[1], qkv)
    own_grad = lax.psum_scatter(flat, "pts", scatter_dimension=0, tiled=True)
    grad_weighted, grad_masses, grad_qkv = pullback(own_grad)
    grad_weighted, grad_masses = (
        lax.all_gather(grad_weighted, "pts", axis=0, tiled=True),
        lax.all_gather(grad_masses, "pts", axis=0, tiled=True),
    )
    return (
        grad_weighted.reshape(grad_mixed.shape),
        grad_masses.reshape(grids_n, heads, slices),
        grad_qkv,
    )


def layer_forward(stream, layer_set, valid):
    weight_set, slicer, qkv, temper, vec_rows = layer_set
    slice_weights, features = slice_front(weight_set, slicer, temper, vec_rows, stream, valid)
    weighted_points = jnp.einsum(
        "gphm,gphd->ghmd", slice_weights, features, precision=exact_arithmetic
    )
    masses = jnp.sum(slice_weights, 1)
    mixed_tokens, kept = slice_mix(weighted_points, masses, qkv)
    spread_tokens = jnp.einsum(
        "gphm,ghmd->gphd", slice_weights, mixed_tokens, precision=exact_arithmetic
    ).reshape(stream.shape)
    return (slice_rest(weight_set, vec_rows, stream, spread_tokens), (stream, mixed_tokens, kept))


def layer_backward(grad_out, layer_set, saved, valid):
    weight_set, slicer, qkv, temper, vec_rows = layer_set
    stream, mixed_tokens, kept = saved
    (slice_weights, features), pull_front = jax.vjp(
        lambda w_set, s_set, t_set, v_set, s_in: slice_front(
            w_set, s_set, t_set, v_set, s_in, valid
        ),
        weight_set,
        slicer,
        temper,
        vec_rows,
        stream,
    )
    spread_tokens = jnp.einsum(
        "gphm,ghmd->gphd", slice_weights, mixed_tokens, precision=exact_arithmetic
    ).reshape(stream.shape)
    _, pull_rest = jax.vjp(slice_rest, weight_set, vec_rows, stream, spread_tokens)
    grad_set_rest, grad_vec_rest, grad_stream, grad_spread = pull_rest(grad_out)
    grad_spread = grad_spread.reshape(features.shape)
    grad_weights = jnp.einsum(
        "gphd,ghmd->gphm", grad_spread, mixed_tokens, precision=exact_arithmetic
    )
    grad_mixed = jnp.einsum(
        "gphm,gphd->ghmd", slice_weights, grad_spread, precision=exact_arithmetic
    )
    grad_weighted, grad_masses, grad_qkv = slice_mix_back(grad_mixed, kept, qkv)
    grad_weights = (
        grad_weights
        + jnp.einsum("ghmd,gphd->gphm", grad_weighted, features, precision=exact_arithmetic)
        + grad_masses[:, None]
    )
    grad_features = jnp.einsum(
        "gphm,ghmd->gphd", slice_weights, grad_weighted, precision=exact_arithmetic
    )
    grad_set_front, grad_slicer, grad_temper, grad_vec_front, grad_stream_front = pull_front(
        (grad_weights, grad_features)
    )
    grads = (
        grad_set_rest + grad_set_front,
        grad_slicer,
        grad_qkv,
        grad_temper,
        grad_vec_rest + grad_vec_front,
    )
    return (grad_stream + grad_stream_front, grads)


def head_loss(head_rows, tail_rows, stream, goals, on_surface, off_surface, inv_surf, inv_vol):
    final = layer_norm(stream, tail_rows[0], tail_rows[1])
    pred = jnp.einsum("oc,gpc->gop", head_rows, final, precision=exact_arithmetic)
    errors = (pred - goals) ** 2
    return inv_surf * jnp.sum(on_surface * errors[:, 0]) + inv_vol * jnp.sum(
        off_surface * (errors[:, 1] + errors[:, 2])
    )


def layer_params(network_state, block_number):
    (
        lifting_readout_rows,
        block_projections,
        partition_maps,
        triple_maps_rows,
        sharpness_factors,
        gain_bias_rows,
    ) = network_state
    return (
        block_projections[block_number],
        partition_maps[block_number],
        triple_maps_rows[block_number],
        sharpness_factors[block_number],
        gain_bias_rows[9 * block_number : 9 * block_number + 9],
    )


def one_batch(network_state, coords, goals, valid, on_surface, off_surface, inv_surf, inv_vol):
    (
        lifting_readout_rows,
        block_projections,
        partition_maps,
        triple_maps_rows,
        sharpness_factors,
        gain_bias_rows,
    ) = network_state
    fin = coords.shape[1]
    layers_n = block_projections.shape[0]
    stream = jnp.einsum(
        "gfp,fc->gpc", coords, lifting_readout_rows[:fin], precision=exact_arithmetic
    )
    saved = []
    for block_number in range(layers_n):
        stream, keep_set = layer_forward(stream, layer_params(network_state, block_number), valid)
        saved.append(keep_set)
    batch_loss, pull_head = jax.vjp(
        lambda h_rows, t_rows, s_in: head_loss(
            h_rows, t_rows, s_in, goals, on_surface, off_surface, inv_surf, inv_vol
        ),
        lifting_readout_rows[fin:],
        gain_bias_rows[9 * layers_n :],
        stream,
    )
    grad_head, grad_tail, grad_stream = pull_head(jnp.ones_like(batch_loss))
    layer_grads = [None] * layers_n
    for block_number in reversed(range(layers_n)):
        grad_stream, layer_grads[block_number] = layer_backward(
            grad_stream, layer_params(network_state, block_number), saved[block_number], valid
        )
    grad_embed = jnp.einsum("gfp,gpc->fc", coords, grad_stream, precision=exact_arithmetic)
    grads = (
        jnp.concatenate([grad_embed, grad_head], 0),
        jnp.stack([entry[0] for entry in layer_grads]),
        jnp.stack([entry[1] for entry in layer_grads]),
        jnp.stack([entry[2] for entry in layer_grads]),
        jnp.stack([entry[3] for entry in layer_grads]),
        jnp.concatenate([entry[4] for entry in layer_grads] + [grad_tail], 0),
    )
    return (batch_loss, grads)


def adamw_update(weight, grad, first, second):
    first_new = beta_one * first + (1.0 - beta_one) * grad
    second_new = beta_two * second + (1.0 - beta_two) * grad * grad
    first_hat = first_new / (1.0 - beta_one**STEP)
    second_hat = second_new / (1.0 - beta_two**STEP)
    weight_new = weight - learn_rate * (
        first_hat / (jnp.sqrt(second_hat) + adam_epsilon) + weight_decay * weight
    )
    return (first_new, second_new, weight_new)


def body_points(
    input_positions,
    flow_labels,
    airfoil_boundary,
    valid_sizes,
    lifting_readout_rows,
    block_projections,
    partition_maps,
    triple_maps_rows,
    sharpness_factors,
    gain_bias_rows,
    lifting_readout_mean,
    projection_running_mean,
    partition_map_mean,
    triple_maps_mean,
    sharpness_mean,
    gain_bias_mean,
    lifting_readout_square,
    projection_running_square,
    partition_map_square,
    triple_maps_square,
    sharpness_square,
    gain_bias_square,
):
    batches = input_positions.shape[0]
    points_n = input_positions.shape[3]
    slots = lax.axis_index("pts") * points_n + jnp.arange(points_n, dtype=jnp.int32)
    valid = (slots[None, None, :] < valid_sizes[:, :, None]).astype(jnp.float32)
    on_surface = valid * airfoil_boundary.astype(jnp.float32)
    off_surface = valid - on_surface
    count_surf, count_vol = lax.psum((jnp.sum(on_surface), jnp.sum(off_surface)), ("pts", "grp"))
    inv_surf = 1.0 / jnp.maximum(count_surf, 1.0)
    inv_vol = 1.0 / jnp.maximum(count_vol, 1.0)
    network_state = (
        lifting_readout_rows,
        block_projections,
        partition_maps,
        triple_maps_rows,
        sharpness_factors,
        gain_bias_rows,
    )
    loss_value = jnp.zeros((), jnp.float32)
    grads = tuple((jnp.zeros_like(entry) for entry in network_state))
    for batch in range(batches):
        batch_loss, batch_set = one_batch(
            network_state,
            input_positions[batch],
            flow_labels[batch],
            valid[batch],
            on_surface[batch],
            off_surface[batch],
            inv_surf,
            inv_vol,
        )
        loss_value = loss_value + batch_loss
        grads = tuple((total + entry for total, entry in zip(grads, batch_set)))
    running_means = (
        lifting_readout_mean,
        projection_running_mean,
        partition_map_mean,
        triple_maps_mean,
        sharpness_mean,
        gain_bias_mean,
    )
    running_squares = (
        lifting_readout_square,
        projection_running_square,
        partition_map_square,
        triple_maps_square,
        sharpness_square,
        gain_bias_square,
    )
    return finish(loss_value, grads, network_state, running_means, running_squares)


def finish(loss_value, grads, network_state, running_means, running_squares):
    summed = lax.psum((loss_value,) + grads, ("pts", "grp"))
    loss_value = summed[0]
    grads = summed[1:]
    grad_norm = jnp.sqrt(sum((jnp.sum(entry * entry) for entry in grads)))
    factor = jnp.minimum(1.0, clip_limit / grad_norm)
    results = []
    for weight, grad, first, second in zip(network_state, grads, running_means, running_squares):
        results.extend(adamw_update(weight, grad * factor, first, second))
    return tuple([loss_value, grad_norm] + results)


def _split(x):
    high = x.astype(bf16)
    return high, (x - high.astype(f32)).astype(bf16)


def _dot(a, b, dims, precision=None):
    return lax.dot_general(a, b, (dims, ((), ())), precision=precision, preferred_element_type=f32)


def _dot3(a, b, dims):
    return _dot(a[0], b[0], dims) + _dot(a[0], b[1], dims) + _dot(a[1], b[0], dims)


def _dotx(a, b, dims):
    return _dot(a, b, dims, lax.Precision.HIGHEST)


def _wide(col, lanes):
    return jnp.concatenate([col] * (lanes // LANES), 1) if lanes > LANES else col


def _fold(x):
    total = x[:, :LANES]
    for start in range(LANES, x.shape[1], LANES):
        total = total + x[:, start : start + LANES]
    return total


def _lockstep(makers):
    running = list(makers)
    while running:
        alive = []
        for entry in running:
            try:
                next(entry)
                alive.append(entry)
            except StopIteration:
                pass
        running = alive


def _diag_heads(full, depth, slices):
    heads = full.shape[0] // depth
    lane = lax.broadcasted_iota(jnp.int32, (depth, full.shape[1]), 1)
    picked = full[:depth]
    for head in range(1, heads):
        picked = jnp.where(lane >= head * slices, full[head * depth : (head + 1) * depth], picked)
    return picked


def _block_heads(flat, heads, slices):
    lane = lax.broadcasted_iota(jnp.int32, flat.shape, 1)
    return jnp.concatenate(
        [
            jnp.where((lane >= head * slices) & (lane < (head + 1) * slices), flat, 0.0)
            for head in range(heads)
        ],
        0,
    )


def _norm(x):
    inv_width = 1.0 / x.shape[0]
    center = x - jnp.sum(x, 0, keepdims=True) * inv_width
    rstd = lax.rsqrt(jnp.sum(center * center, 0, keepdims=True) * inv_width + 1e-05)
    return center * rstd, rstd


def _norm_back(grad, xhat, rstd):
    inv_width = 1.0 / grad.shape[0]
    mean_grad = jnp.sum(grad, 0, keepdims=True) * inv_width
    mean_proj = jnp.sum(grad * xhat, 0, keepdims=True) * inv_width
    return (grad - mean_grad - xhat * mean_proj) * rstd


def grids_kernel(dims, *refs):
    (
        grids,
        points,
        width,
        heads,
        head_size,
        slices,
        layers,
        fin,
        outc,
        tile,
        members,
        groups,
        places,
    ) = dims
    (
        sizes_ref,
        sharp_ref,
        coords_ref,
        goals_ref,
        bound_ref,
        io_ref,
        mats_ref,
        maps_ref,
        qkv_ref,
        vecs_ref,
        packed,
        stream,
        xh1h,
        xh1l,
        rs1,
        feath,
        featl,
        placeh,
        placel,
        wgth,
        wgtl,
        sprh,
        sprl,
        xh2h,
        xh2l,
        rs2,
        hidh,
        hidl,
        gslope,
        upmh,
        upml,
        cols,
        bdmh,
        bdml,
        bdth,
        bdtl,
        accw,
        accf,
        tok,
        rmass,
        qkvs,
        probs,
        mbdh,
        mbdl,
        dbdh,
        dbdl,
        cmbh,
        cmbl,
        dmcol,
        vacc,
        gmacc,
        headacc,
        embacc,
        lossacc,
        qkvacc,
        points_ref,
        outbox,
        inbox,
        tally,
        send_sems,
        recv_sems,
        tally_send,
        tally_recv,
    ) = refs
    half = heads // 2
    span = half * slices
    group = half * head_size
    pairs = heads // 2
    all_slices = heads * slices
    steps = points // tile
    scale = head_size ** (-0.5)
    ones_rows = jnp.ones((8, LANES), f32)
    me, mine = lax.axis_index("pts"), lax.axis_index("grp")
    own_points = points // members

    def peer_points(hop):
        return lax.rem(me + hop, members)

    def peer_group(hop):
        return lax.rem(mine + hop, groups)

    barrier = pltpu.get_barrier_semaphore()
    for hop in range(1, members):
        pl.semaphore_signal(
            barrier, inc=1, device_id=(peer_points(hop), mine), device_id_type=MESH
        )
    for hop in range(1, groups):
        pl.semaphore_signal(
            barrier, inc=1, device_id=(me, peer_group(hop)), device_id_type=MESH
        )

    slots = lax.broadcasted_iota(jnp.int32, (1, own_points), 1) + me * own_points
    surf_total = jnp.zeros((1, own_points), f32)
    vol_total = jnp.zeros((1, own_points), f32)
    blank = jnp.zeros((8 - fin - outc - 1, own_points), f32)
    for dest in range(members):
        for batch in range(grids):
            surf = bound_ref[batch, dest : dest + 1, :].astype(f32)
            outbox[dest, batch * 8 : batch * 8 + 8, :] = jnp.concatenate(
                [coords_ref[batch, dest], goals_ref[batch, dest], surf, blank], 0
            )
            valid = jnp.where(slots < sizes_ref[batch, dest], 1.0, 0.0)
            surf_total = surf_total + valid * surf
            vol_total = vol_total + (valid - valid * surf)
    totals = jnp.concatenate(
        [surf_total, vol_total, jnp.zeros((6, own_points), f32)], 0
    )
    for dest in range(members):
        outbox[dest, grids * 8 :, :] = totals
    pl.semaphore_wait(barrier, members + groups - 2)

    def piece(hop):
        other = peer_points(hop)
        return pltpu.make_async_remote_copy(
            src_ref=outbox.at[other],
            dst_ref=inbox.at[hop - 1],
            send_sem=send_sems.at[hop - 1],
            recv_sem=recv_sems.at[hop - 1],
            device_id=(other, mine),
            device_id_type=MESH,
        )

    def share(hop):
        return pltpu.make_async_remote_copy(
            src_ref=tally.at[0],
            dst_ref=tally.at[hop],
            send_sem=tally_send.at[hop - 1],
            recv_sem=tally_recv.at[hop - 1],
            device_id=(me, peer_group(hop)),
            device_id_type=MESH,
        )

    for hop in range(1, members):
        piece(hop).start()

    def matrix_rows(layer, slot, half_index):
        start = ((layer * 5 + slot) * (width // LANES) + half_index) * width
        return pl.ds(pl.multiple_of(start, width), width)

    def add_matrix(layer, slot, value):
        for index in range(width // LANES):
            packed[matrix_rows(layer, slot, index), :] += value[
                :, index * LANES : (index + 1) * LANES
            ]

    def read_matrix(layer, slot):
        return jnp.concatenate(
            [packed[matrix_rows(layer, slot, index), :] for index in range(width // LANES)], 1
        )

    def split_to(high_ref, low_ref, index, value):
        high, low = _split(value)
        high_ref[index] = high
        low_ref[index] = low
        return high, low

    vecs = vecs_ref[...]
    row_id = lax.broadcasted_iota(jnp.int32, (vecs.shape[0], LANES), 0)

    def column(row):
        return _dotx(vecs, jnp.where(row_id == row, 1.0, 0.0), TN)

    for layer in range(layers):
        base = 9 * layer
        gain_a, shift_a = column(base), column(base + 1)
        gain_b, shift_b = column(base + 5), column(base + 6)
        cols[layer, 0] = gain_a
        cols[layer, 1] = shift_a
        cols[layer, 2] = gain_b
        cols[layer, 3] = shift_b
        for slot in range(5):
            flipped = mats_ref[layer, slot].T
            bias = column(base + (2, 3, 4, 7, 8)[slot])
            if slot in (0, 1, 3):
                gain, shift, row = (gain_b, shift_b, 5) if slot == 3 else (gain_a, shift_a, 0)
                bias = bias + _dotx(flipped, shift, NN)
                flipped = flipped * vecs[base + row : base + row + 1]
            cols[layer, 4 + slot] = bias
            split_to(upmh, upml, (layer, slot), flipped)
        tiled = jnp.concatenate([maps_ref[layer]] * half, 1)
        for part in range(2):
            lane = lax.broadcasted_iota(jnp.int32, (1, span), 1)
            sharp = jnp.full((1, span), 0.0, f32) + sharp_ref[layer, part * half]
            for head in range(1, half):
                sharp = jnp.where(lane >= head * slices, sharp_ref[layer, part * half + head], sharp)
            block = _block_heads(tiled / sharp, half, slices)
            split_to(bdth, bdtl, (layer, part), block)
            split_to(bdmh, bdml, (layer, part), block.T)

    vacc[...] = jnp.zeros_like(vacc)
    gmacc[...] = jnp.zeros_like(gmacc)
    headacc[...] = jnp.zeros_like(headacc)
    embacc[...] = jnp.zeros_like(embacc)
    lossacc[...] = jnp.zeros_like(lossacc)
    packed[...] = jnp.zeros_like(packed)
    qkvacc[...] = jnp.zeros_like(qkvacc)

    io_all = io_ref[...]
    io_id = lax.broadcasted_iota(jnp.int32, (io_all.shape[0], LANES), 0)
    lift = [_dotx(io_all, jnp.where(io_id == row, 1.0, 0.0), TN) for row in range(fin)]

    def window(step):
        return pl.ds(pl.multiple_of(step * tile, tile), tile)

    def pair_of(high_ref, low_ref, index):
        return high_ref[index], low_ref[index]

    def settle(source, block):
        at = pl.ds(pl.multiple_of(source * own_points, own_points), own_points)
        for grid in range(grids):
            points_ref[grid, :, at] = block[grid * 8 : grid * 8 + 8]
        return block[grids * 8 :]

    held = settle(me, outbox[me])
    for hop in range(1, members):
        piece(hop).wait()
        held = held + settle(lax.rem(me + members - hop, members), inbox[hop - 1])
    tally[0] = held
    for hop in range(1, groups):
        share(hop).start()

    @pl.loop(0, steps)
    def _(step):
        at = window(step)
        for grid in range(grids):
            x = jnp.zeros((width, tile), f32)
            for row in range(fin):
                x = x + _wide(lift[row], tile) * points_ref[grid, row : row + 1, at]
            stream[grid, :, at] = x

    def front(layer, grid, at, step):
        xhat, rstd = _norm(stream[grid, :, at])
        xhat = split_to(xh1h, xh1l, (layer, grid, slice(None), at), xhat)
        rs1[layer, grid, :, at] = rstd
        yield
        feat = _dot3(pair_of(upmh, upml, (layer, 0)), xhat, NN) + _wide(cols[layer, 4], tile)
        place = _dot3(pair_of(upmh, upml, (layer, 1)), xhat, NN) + _wide(cols[layer, 5], tile)
        feat = split_to(feath, featl, (layer, grid, slice(None), at), feat)
        place = split_to(placeh, placel, (layer, grid, slice(None), at), place)
        yield
        slots = lax.broadcasted_iota(jnp.int32, (1, tile), 1) + step * tile
        valid = jnp.where(slots < sizes_ref[grid, me], 1.0, 0.0)
        for part in range(2):
            rows = slice(part * group, (part + 1) * group)
            scores = _dot3(
                pair_of(bdmh, bdml, (layer, part)), (place[0][rows], place[1][rows]), NN
            ).reshape(half, slices, tile)
            expo = jnp.exp(scores - jnp.max(scores, 1, keepdims=True))
            ratio = valid[None] / jnp.sum(expo, 1, keepdims=True)
            weight = (expo * ratio).reshape(span, tile)
            wrows = slice(part * span, (part + 1) * span)
            weight = split_to(wgth, wgtl, (layer, grid, wrows, at), weight)
            yield
            lead = jnp.concatenate([feat[0][rows], jnp.ones((16, tile), bf16)], 0)
            accw[grid, part] += _dot(lead, weight[0], NT) + _dot(lead, weight[1], NT)
            accf[grid, part] += _dot(feat[1][rows], weight[0], NT)
            yield

    def attend(layer, grid):
        parts, masses = [], []
        for part in range(2):
            total = accw[grid, part]
            parts.append(_diag_heads(total[:group] + accf[grid, part], head_size, slices))
            masses.append(total[group : group + 1])
        rate = 1.0 / (jnp.concatenate(masses, 1) + 1e-05)
        tokens = jnp.concatenate(parts, 1) * rate
        tok[layer, grid] = tokens
        rmass[layer, grid] = rate
        yield
        joined = _dotx(qkv_ref[layer], tokens, TN)
        qkvs[layer, grid] = joined
        yield
        lane = lax.broadcasted_iota(jnp.int32, (slices, 2 * slices), 1)
        mixed = []
        for pair in range(pairs):
            at = slice(pair * 2 * slices, (pair + 1) * 2 * slices)
            query = joined[:head_size, at]
            key = joined[head_size : 2 * head_size, at]
            value = joined[2 * head_size :, at]
            full = _dotx(key, query, TN)
            scores = jnp.where(lane < slices, full[:slices], full[slices:]) * scale
            expo = jnp.exp(scores - jnp.max(scores, 0, keepdims=True))
            prob = expo / jnp.sum(expo, 0, keepdims=True)
            probs[layer, grid, pair] = prob
            mixed.append(_dotx(value, _block_heads(prob, 2, slices), NN))
        for part in range(2):
            flat = jnp.concatenate(mixed[part * (pairs // 2) : (part + 1) * (pairs // 2)], 1)
            block = _block_heads(flat, half, slices)
            split_to(mbdh, mbdl, (layer, grid, part), block)
        yield

    def rest(layer, grid, at):
        spread = []
        for part in range(2):
            wrows = slice(part * span, (part + 1) * span)
            weight = pair_of(wgth, wgtl, (layer, grid, wrows, at))
            spread.append(_dot3(pair_of(mbdh, mbdl, (layer, grid, part)), weight, NN))
        spread = split_to(
            sprh, sprl, (layer, grid, slice(None), at), jnp.concatenate(spread, 0)
        )
        yield
        x = (
            stream[grid, :, at]
            + _dot3(pair_of(upmh, upml, (layer, 2)), spread, NN)
            + _wide(cols[layer, 6], tile)
        )
        xhat, rstd = _norm(x)
        xhat = split_to(xh2h, xh2l, (layer, grid, slice(None), at), xhat)
        rs2[layer, grid, :, at] = rstd
        yield
        inner = _dot3(pair_of(upmh, upml, (layer, 3)), xhat, NN) + _wide(cols[layer, 7], tile)
        cdf = 0.5 + 0.5 * lax.erf(inner * (0.5**0.5))
        gslope[layer, grid, :, at] = cdf + inner * jnp.exp(-0.5 * inner * inner) * (
            (2.0 * math.pi) ** -0.5
        )
        hidden = split_to(hidh, hidl, (layer, grid, slice(None), at), inner * cdf)
        yield
        stream[grid, :, at] = (
            x
            + _dot3(pair_of(upmh, upml, (layer, 4)), hidden, NN)
            + _wide(cols[layer, 8], tile)
        )
        yield

    @pl.loop(0, layers)
    def _(layer):
        accw[...] = jnp.zeros_like(accw)
        accf[...] = jnp.zeros_like(accf)

        @pl.loop(0, steps)
        def _(step):
            at = window(step)
            _lockstep([front(layer, grid, at, step) for grid in range(grids)])

        _lockstep([attend(layer, grid) for grid in range(grids)])

        @pl.loop(0, steps)
        def _(step):
            at = window(step)
            _lockstep([rest(layer, grid, at) for grid in range(grids)])

    tail = 9 * layers
    head_rows = jnp.concatenate(
        [io_ref[fin:, :], jnp.zeros((8 - outc, width), f32)], 0
    )
    head_gain = head_rows * vecs[tail : tail + 1]
    head_pair = _split(head_gain)
    head_bias = _dotx(head_rows, column(tail + 1), NN)
    counted = tally[0]
    for hop in range(1, groups):
        share(hop).wait()
        counted = counted + tally[hop]
    counted = jnp.broadcast_to(jnp.sum(counted, 1, keepdims=True), counted.shape)
    counted = 1.0 / jnp.maximum(counted, 1.0)
    inv_surf, inv_vol = _wide(counted[:1], tile), _wide(counted[1:2], tile)

    def crown(grid, at, step):
        xhat, rstd = _norm(stream[grid, :, at])
        halves = _split(xhat)
        pred = _dot3(head_pair, halves, NN) + _wide(head_bias, tile)
        slots = lax.broadcasted_iota(jnp.int32, (1, tile), 1) + step * tile
        valid = jnp.where(slots < sizes_ref[grid, me], 1.0, 0.0)
        surf = valid * points_ref[grid, fin + outc : fin + outc + 1, at]
        vol = (valid - surf) * inv_vol
        surf = surf * inv_surf
        row = lax.broadcasted_iota(jnp.int32, (8, tile), 0)
        factor = jnp.where(row == 0, surf, jnp.where(row < outc, vol, 0.0))
        goals = jnp.concatenate(
            [points_ref[grid, fin : fin + outc, at], jnp.zeros((8 - outc, tile), f32)], 0
        )
        error = pred - goals
        scaled = factor * error
        lossacc[...] += _fold(scaled * error)
        dpred = scaled + scaled
        headacc[0] += _fold(dpred)
        dhalves = _split(dpred)
        headacc_rows = _dot3(dhalves, halves, NT)
        for start in range(0, width, LANES):
            headacc[1 + start // LANES] += headacc_rows[:, start : start + LANES]
        yield
        grad = _dot3(head_pair, dhalves, TN)
        stream[grid, :, at] = _norm_back(grad, xhat, rstd)
        yield

    @pl.loop(0, steps)
    def _(step):
        at = window(step)
        _lockstep([crown(grid, at, step) for grid in range(grids)])

    for layer in range(layers):
        for slot in range(5):
            mat = mats_ref[layer, slot]
            if slot in (0, 1, 3):
                mat = mat * _wide(cols[layer, 2 if slot == 3 else 0], width)
            split_to(upmh, upml, (layer, slot), mat)

    def back_rest(layer, grid, at):
        grad = stream[grid, :, at]
        vacc[layer, 4] += _fold(grad)
        pieces = _split(grad)
        dhid = _dot3(pair_of(upmh, upml, (layer, 4)), pieces, NN)
        hidden = pair_of(hidh, hidl, (layer, grid, slice(None), at))
        add_matrix(layer, 4, _dot3(hidden, pieces, NT))
        yield
        dinner = dhid * gslope[layer, grid, :, at]
        vacc[layer, 3] += _fold(dinner)
        pieces = _split(dinner)
        xhat = pair_of(xh2h, xh2l, (layer, grid, slice(None), at))
        dxhat = _dot3(pair_of(upmh, upml, (layer, 3)), pieces, NN)
        add_matrix(layer, 3, _dot3(xhat, pieces, NT))
        yield
        grad = grad + _norm_back(
            dxhat, xhat[0].astype(f32) + xhat[1].astype(f32), rs2[layer, grid, :, at]
        )
        stream[grid, :, at] = grad
        vacc[layer, 2] += _fold(grad)
        pieces = _split(grad)
        dspread = _dot3(pair_of(upmh, upml, (layer, 2)), pieces, NN)
        add_matrix(layer, 2, _dot3(pair_of(sprh, sprl, (layer, grid, slice(None), at)), pieces, NT))
        dspread = split_to(sprh, sprl, (layer, grid, slice(None), at), dspread)
        yield
        for part in range(2):
            rows = slice(part * group, (part + 1) * group)
            wrows = slice(part * span, (part + 1) * span)
            weight = pair_of(wgth, wgtl, (layer, grid, wrows, at))
            accf[grid, part] += _dot3((dspread[0][rows], dspread[1][rows]), weight, NT)
        yield

    def back_attend(layer, grid):
        joined = qkvs[layer, grid]
        tokens = tok[layer, grid]
        rate = rmass[layer, grid]
        lane = lax.broadcasted_iota(jnp.int32, (slices, 2 * slices), 1)
        dmixed = jnp.concatenate(
            [_diag_heads(accf[grid, part], head_size, slices) for part in range(2)], 1
        )
        yield
        dqs, dks, dvs = [], [], []
        for pair in range(pairs):
            at = slice(pair * 2 * slices, (pair + 1) * 2 * slices)
            query = joined[:head_size, at]
            key = joined[head_size : 2 * head_size, at]
            value = joined[2 * head_size :, at]
            prob = probs[layer, grid, pair]
            dmix = dmixed[:, at]
            full = _dotx(value, dmix, TN)
            dprob = jnp.where(lane < slices, full[:slices], full[slices:])
            dscore = (
                prob * (dprob - jnp.sum(prob * dprob, 0, keepdims=True)) * scale
            )
            dblock = _block_heads(dscore, 2, slices)
            dvs.append(_dotx(dmix, _block_heads(prob, 2, slices), NT))
            dqs.append(_dotx(key, dblock, NN))
            dks.append(_dotx(query, dblock, NT))
        dqkv = jnp.concatenate(
            [jnp.concatenate(part, 1) for part in (dqs, dks, dvs)], 0
        )
        yield
        dtok = _dotx(qkv_ref[layer], dqkv, NN)
        qkvacc[layer] += _dotx(tokens, dqkv, NT)
        dweighted = dtok * rate
        dmass = -jnp.sum(dweighted * tokens, 0, keepdims=True)
        yield
        dmass = jnp.broadcast_to(dmass, (8, all_slices))
        row_one = jnp.where(
            lax.broadcasted_iota(jnp.int32, (8, LANES), 0) == 0, 1.0, 0.0
        )
        dmcol[grid] = _dotx(dmass, row_one, TN)
        for part in range(2):
            block = _block_heads(dweighted[:, part * span : (part + 1) * span], half, slices)
            split_to(dbdh, dbdl, (grid, part), block)
            mix = mbdh[layer, grid, part].astype(f32) + mbdl[layer, grid, part].astype(f32)
            both = jnp.concatenate([mix, block], 0)
            split_to(cmbh, cmbl, (grid, part), both.T)
        yield

    def back_front(layer, grid, at):
        feat = pair_of(feath, featl, (layer, grid, slice(None), at))
        place = pair_of(placeh, placel, (layer, grid, slice(None), at))
        dfeats, dplaces = [], []
        for part in range(2):
            rows = slice(part * group, (part + 1) * group)
            wrows = slice(part * span, (part + 1) * span)
            weight = pair_of(wgth, wgtl, (layer, grid, wrows, at))
            dspread = pair_of(sprh, sprl, (layer, grid, rows, at))
            both = tuple(
                jnp.concatenate([one, two[rows]], 0) for one, two in zip(dspread, feat)
            )
            dweight = _dot3(pair_of(cmbh, cmbl, (grid, part)), both, NN)
            dweight = dweight + _wide(dmcol[grid, wrows], tile)
            full = weight[0].astype(f32) + weight[1].astype(f32)
            prod = full * dweight
            total = jnp.sum(prod.reshape(half, slices, tile), 1, keepdims=True)
            dscore = (
                prod.reshape(half, slices, tile) - full.reshape(half, slices, tile) * total
            ).reshape(span, tile)
            pieces = _split(dscore)
            yield
            dplaces.append(_dot3(pair_of(bdth, bdtl, (layer, part)), pieces, NN))
            gmacc[layer, part] += _dot3((place[0][rows], place[1][rows]), pieces, NT)
            dfeats.append(_dot3(pair_of(dbdh, dbdl, (grid, part)), weight, NN))
            yield
        dfeat = jnp.concatenate(dfeats, 0)
        dplace = jnp.concatenate(dplaces, 0)
        vacc[layer, 0] += _fold(dfeat)
        vacc[layer, 1] += _fold(dplace)
        dfeat, dplace = _split(dfeat), _split(dplace)
        xhat = pair_of(xh1h, xh1l, (layer, grid, slice(None), at))
        dxhat = _dot3(pair_of(upmh, upml, (layer, 0)), dfeat, NN) + _dot3(
            pair_of(upmh, upml, (layer, 1)), dplace, NN
        )
        add_matrix(layer, 0, _dot3(xhat, dfeat, NT))
        add_matrix(layer, 1, _dot3(xhat, dplace, NT))
        yield
        grad = stream[grid, :, at] + _norm_back(
            dxhat, xhat[0].astype(f32) + xhat[1].astype(f32), rs1[layer, grid, :, at]
        )
        stream[grid, :, at] = grad
        yield

    @pl.loop(0, layers)
    def _(index):
        layer = layers - 1 - index
        accf[...] = jnp.zeros_like(accf)

        @pl.loop(0, steps)
        def _(step):
            at = window(step)
            _lockstep([back_rest(layer, grid, at) for grid in range(grids)])

        _lockstep([back_attend(layer, grid) for grid in range(grids)])

        @pl.loop(0, steps)
        def _(step):
            at = window(step)
            _lockstep([back_front(layer, grid, at) for grid in range(grids)])

    @pl.loop(0, steps)
    def _(step):
        at = window(step)
        for grid in range(grids):
            coords = jnp.concatenate(
                [points_ref[grid, :fin, at], jnp.zeros((8 - fin, tile), f32)], 0
            )
            embacc[...] += _dot3(_split(coords), _split(stream[grid, :, at]), NT)

    def to_row(folded):
        return _dotx(ones_rows, folded, NT)[:1]

    def put_vector(row, value):
        for index in range(width // LANES):
            start = places["vecs"] + index * places["vecs_stride"] + row
            packed[start : start + 1, :] = value[:, index * LANES : (index + 1) * LANES]

    ones_wide = jnp.ones((8, width), f32)
    for layer in range(layers):
        base = 9 * layer
        sums = [to_row(vacc[layer, slot]) for slot in range(5)]
        gain_rows = []
        for slot in (0, 1, 3):
            gain, shift = (2, 3) if slot == 3 else (0, 1)
            gram = read_matrix(layer, slot)
            mat = mats_ref[layer, slot]
            gain_rows.append(_dotx(ones_wide, gram * mat, NT)[:1])
            value = (
                _wide(cols[layer, gain], width) * gram + _wide(cols[layer, shift], width) * sums[slot]
            )
            for index in range(width // LANES):
                packed[matrix_rows(layer, slot, index), :] = value[
                    :, index * LANES : (index + 1) * LANES
                ]
        def shift_row(slot):
            return _dotx(jnp.broadcast_to(sums[slot], (8, width)), mats_ref[layer, slot], NT)[:1]
        rows = [
            gain_rows[0] + gain_rows[1],
            shift_row(0) + shift_row(1),
            sums[0],
            sums[1],
            sums[2],
            gain_rows[2],
            shift_row(3),
            sums[3],
            sums[4],
        ]
        for slot, row in enumerate(rows):
            put_vector(base + slot, row)
        tiled = jnp.concatenate([maps_ref[layer]] * half, 1)
        total = None
        sharp_total = None
        for part in range(2):
            lane = lax.broadcasted_iota(jnp.int32, (1, span), 1)
            sharp = jnp.full((1, span), 0.0, f32) + sharp_ref[layer, part * half]
            for head in range(1, half):
                sharp = jnp.where(lane >= head * slices, sharp_ref[layer, part * half + head], sharp)
            picked = _diag_heads(gmacc[layer, part], head_size, slices) / sharp
            total = picked if total is None else total + picked
            share = -jnp.sum(picked * tiled, 0, keepdims=True) / sharp
            chosen = jnp.where(
                lax.broadcasted_iota(jnp.int32, (span, LANES), 0) // slices + part * half
                == lax.broadcasted_iota(jnp.int32, (span, LANES), 1),
                1.0,
                0.0,
            )
            share = _dotx(jnp.broadcast_to(share, (8, span)), chosen, NN)
            sharp_total = share if sharp_total is None else sharp_total + share
        packed[places["sharp"] + layer : places["sharp"] + layer + 1, :heads] = sharp_total[:1, :heads]
        total = _fold(total)
        total = total + pltpu.roll(total, slices, 1)
        start = places["maps"] + layer * head_size
        packed[start : start + head_size, :slices] = total[:, :slices]
        start = places["qkv"] + layer * head_size
        packed[start : start + head_size, : 3 * head_size] = qkvacc[layer]

    spread_dpred = _dotx(headacc[0], jnp.ones((LANES, LANES), f32), NN)
    gram = jnp.concatenate([headacc[1 + k] for k in range(width // LANES)], 1)
    gain_row, shift_row = vecs[tail : tail + 1], vecs[tail + 1 : tail + 2]
    head_grad = gram * gain_row + _wide(spread_dpred, width) * shift_row
    for index in range(width // LANES):
        at = slice(index * LANES, (index + 1) * LANES)
        start = places["io"] + index * places["io_stride"]
        packed[start : start + fin, :] = embacc[:fin, at]
        packed[start + fin : start + fin + outc, :] = head_grad[:outc, at]
    put_vector(tail, jnp.sum(gram * head_rows, 0, keepdims=True))
    put_vector(
        tail + 1, jnp.sum(_wide(spread_dpred, width) * head_rows, 0, keepdims=True)
    )
    packed[places["loss"] : places["loss"] + 1, :] = jnp.broadcast_to(
        jnp.sum(jnp.sum(lossacc[...], 0, keepdims=True), 1, keepdims=True), (1, LANES)
    )


def _round_up(value, unit):
    return (value + unit - 1) // unit * unit


def packed_places(layers, width, io_rows, vec_rows, head_size):
    halves = width // LANES
    places = {"io_stride": _round_up(io_rows, 8), "vecs_stride": _round_up(vec_rows, 8)}
    row = layers * 5 * halves * width
    for name, rows in (
        ("io", halves * places["io_stride"]),
        ("vecs", halves * places["vecs_stride"]),
        ("maps", layers * head_size),
        ("qkv", layers * head_size),
        ("sharp", _round_up(layers, 8)),
        ("loss", 8),
    ):
        places[name] = row
        row += rows
    places["rows"] = _round_up(row, 256)
    return places


def sum_kernel(dims, packed, out, squares, core_in, summed, a_one, a_mid, a_two, b_one, b_mid, b_two, send_sems, recv_sems):
    loss_row, depth, floors = dims
    rows = packed.shape[0]
    point, group = lax.axis_index("pts"), lax.axis_index("grp")
    y, z = lax.rem(point, 2), lax.div(point, 2)
    core, x = lax.rem(group, 2), lax.div(group, 2)
    plane = x + 2 * y
    half = rows // 2
    a_rows = a_one.shape[1] * 4
    a_four, b_four = a_one.shape[1], b_one.shape[1]
    a_all, b_all = a_two.shape[1], b_two.shape[1]
    base = core * half

    def plane_peer(hop):
        other_x, other_y = lax.rem(x + hop % 2, 2), lax.rem(y + hop // 2, 2)
        return (z * 2 + other_y, other_x * 2 + core), other_x + 2 * other_y

    def line_peer(hop):
        other = lax.rem(z + hop, floors)
        return (other * 2 + y, group), other

    partner = (point, x * 2 + (1 - core))

    def rows_at(start, count):
        return pl.ds(pl.multiple_of(start, 8), count)

    def send(number, source, target, device):
        return pltpu.make_async_remote_copy(
            src_ref=source,
            dst_ref=target,
            send_sem=send_sems.at[number],
            recv_sem=recv_sems.at[number],
            device_id=device,
            device_id_type=MESH,
        )

    barrier = pltpu.get_barrier_semaphore()
    pl.semaphore_signal(barrier, inc=1, device_id=partner, device_id_type=MESH)
    for hop in range(1, 4):
        pl.semaphore_signal(
            barrier, inc=1, device_id=plane_peer(hop)[0], device_id_type=MESH
        )
        pl.semaphore_signal(
            barrier, inc=1, device_id=line_peer(hop)[0], device_id_type=MESH
        )
    pl.semaphore_wait(barrier, 7)

    cross = send(0, packed.at[rows_at((1 - core) * half, half)], core_in, partner)
    cross.start()
    cross.wait_recv()
    summed[...] = packed[rows_at(base, half), :] + core_in[...]
    a1, b1, a2, b2, a3, b3, a4, b4 = [], [], [], [], [], [], [], []
    for hop in range(1, 4):
        device, spot = plane_peer(hop)
        a1.append(send(hop, summed.at[rows_at(spot * a_four, a_four)], a_one.at[hop - 1], device))
        a1[-1].start()
        device, spot = line_peer(hop)
        b1.append(
            send(3 + hop, summed.at[rows_at(a_rows + spot * b_four, b_four)], b_one.at[hop - 1], device)
        )
        b1[-1].start()
    for copy in a1:
        copy.wait_recv()
    a_mid[...] = (
        summed[rows_at(plane * a_four, a_four), :] + a_one[0] + a_one[1] + a_one[2]
    )
    for hop in range(1, 4):
        device, spot = line_peer(hop)
        a2.append(send(6 + hop, a_mid.at[rows_at(spot * a_all, a_all)], a_two.at[hop - 1], device))
        a2[-1].start()
    for copy in b1:
        copy.wait_recv()
    b_mid[...] = (
        summed[rows_at(a_rows + z * b_four, b_four), :] + b_one[0] + b_one[1] + b_one[2]
    )
    for hop in range(1, 4):
        device, spot = plane_peer(hop)
        b2.append(send(9 + hop, b_mid.at[rows_at(spot * b_all, b_all)], b_two.at[hop - 1], device))
        b2[-1].start()
    for copy in a2:
        copy.wait_recv()
    a_piece = rows_at(base + plane * a_four + z * a_all, a_all)
    out[a_piece, :] = a_mid[rows_at(z * a_all, a_all), :] + a_two[0] + a_two[1] + a_two[2]
    for hop in range(1, 4):
        a3.append(send(12 + hop, out.at[a_piece], out.at[a_piece], line_peer(hop)[0]))
        a3[-1].start()
    for copy in b2:
        copy.wait_recv()
    b_piece = rows_at(base + a_rows + z * b_four + plane * b_all, b_all)
    out[b_piece, :] = b_mid[rows_at(plane * b_all, b_all), :] + b_two[0] + b_two[1] + b_two[2]
    for hop in range(1, 4):
        b3.append(send(15 + hop, out.at[b_piece], out.at[b_piece], plane_peer(hop)[0]))
        b3[-1].start()
    for copy in a3:
        copy.wait_recv()
    a_part = rows_at(base + plane * a_four, a_four)
    for hop in range(1, 4):
        a4.append(send(18 + hop, out.at[a_part], out.at[a_part], plane_peer(hop)[0]))
        a4[-1].start()
    for copy in b3:
        copy.wait_recv()
    b_part = rows_at(base + a_rows + z * b_four, b_four)
    for hop in range(1, 4):
        b4.append(send(21 + hop, out.at[b_part], out.at[b_part], line_peer(hop)[0]))
        b4[-1].start()
    for copy in a4 + b4:
        copy.wait_recv()
    last = send(25, out.at[rows_at(base, half)], out.at[rows_at(base, half)], partner)
    last.start()
    last.wait_recv()
    for copy in [cross, last] + a1 + b1 + a2 + b2 + a3 + b3 + a4 + b4:
        copy.wait_send()

    squares[...] = jnp.zeros_like(squares)

    @pl.loop(0, rows // 256)
    def _(step):
        block = out[pl.ds(pl.multiple_of(step * 256, 256), 256), :]
        row = lax.broadcasted_iota(jnp.int32, block.shape, 0) + step * 256
        block = jnp.where(row == loss_row, 0.0, block)
        squares[...] += jnp.sum((block * block).reshape(32, 8, LANES), 0)


def sum_over_devices(packed, places, members):
    rows = packed.shape[0]
    half = rows // 2
    a_rows = half // 384 * 256
    b_rows = half - a_rows
    floors = members // 2
    vmem = pl.BlockSpec(memory_space=pltpu.VMEM)
    return pl.pallas_call(
        functools.partial(sum_kernel, (places["loss"], 0, floors)),
        out_shape=[
            jax.ShapeDtypeStruct((rows, LANES), f32),
            jax.ShapeDtypeStruct((8, LANES), f32),
        ],
        in_specs=[vmem],
        out_specs=[vmem, vmem],
        scratch_shapes=[
            pltpu.VMEM((half, LANES), f32),
            pltpu.VMEM((half, LANES), f32),
            pltpu.VMEM((3, a_rows // 4, LANES), f32),
            pltpu.VMEM((a_rows // 4, LANES), f32),
            pltpu.VMEM((3, a_rows // 16, LANES), f32),
            pltpu.VMEM((3, b_rows // 4, LANES), f32),
            pltpu.VMEM((b_rows // 4, LANES), f32),
            pltpu.VMEM((3, b_rows // 16, LANES), f32),
            pltpu.SemaphoreType.DMA((26,)),
            pltpu.SemaphoreType.DMA((26,)),
        ],
        compiler_params=pltpu.CompilerParams(
            collective_id=1, has_side_effects=True, vmem_limit_bytes=32 << 20
        ),
    )(packed)


def update_kernel(dims, *refs):
    layers, width, places, first_small = dims
    big, small, squares = refs[:3]
    inputs, outputs = refs[3:21], refs[21:]
    loss_out, norm_out = outputs[:2]
    weights, means, seconds = inputs[:6], inputs[6:12], inputs[12:]
    halves = width // LANES
    total = jnp.sum(jnp.sum(squares[...], 0, keepdims=True), 1, keepdims=True)
    norm = jnp.sqrt(total)
    factor = jnp.minimum(1.0, clip_limit / norm)

    def apply(index, grad):
        weight, mean, second = weights[index], means[index], seconds[index]
        first_new, second_new, weight_new = adamw_update(
            weight[...], grad * factor, mean[...], second[...]
        )
        outputs[2 + 3 * index][...] = first_new
        outputs[3 + 3 * index][...] = second_new
        outputs[4 + 3 * index][...] = weight_new

    grad = jnp.concatenate([big[k * width : (k + 1) * width, :] for k in range(halves)], 1)
    apply(1, grad[None, None])

    @pl.when(pl.program_id(0) == 0)
    def _():
        def rows(name, start, count):
            first = places[name] - first_small + start
            return small[first : first + count, :]

        loss_out[...] = rows("loss", 0, 1)[:, :1]
        norm_out[...] = norm
        for index, name in ((0, "io"), (5, "vecs")):
            stride, count = places[name + "_stride"], weights[index].shape[0]
            apply(
                index,
                jnp.concatenate([rows(name, k * stride, count) for k in range(halves)], 1),
            )
        for index, name in ((2, "maps"), (3, "qkv")):
            _, count, lanes = weights[index].shape
            apply(
                index,
                jnp.stack([rows(name, k * count, count)[:, :lanes] for k in range(layers)]),
            )
        count, lanes = weights[4].shape
        apply(4, rows("sharp", 0, count)[:, :lanes])


def update_all(summed, squares, network_state, running_means, running_squares, places):
    layers, slots, width, _ = network_state[1].shape
    rows_each = width // LANES * width
    first_small = layers * slots * rows_each
    small_rows = summed.shape[0] - first_small

    def whole(entry):
        return pl.BlockSpec(entry.shape, lambda i: (0,) * entry.ndim)

    def spec(index, entry):
        if index == 1:
            return pl.BlockSpec((1, 1, width, width), lambda i: (i // slots, i % slots, 0, 0))
        return whole(entry)

    state_specs = [spec(index, entry) for index, entry in enumerate(network_state)]
    shapes = [jax.ShapeDtypeStruct((1, 1), f32)] * 2
    specs = [pl.BlockSpec((1, 1), lambda i: (0, 0))] * 2
    for index, entry in enumerate(network_state):
        shapes += [jax.ShapeDtypeStruct(entry.shape, f32)] * 3
        specs += [spec(index, entry)] * 3
    results = pl.pallas_call(
        functools.partial(update_kernel, (layers, width, places, first_small)),
        grid=(layers * slots,),
        out_shape=shapes,
        in_specs=[
            pl.BlockSpec((rows_each, LANES), lambda i: (i, 0)),
            pl.BlockSpec((small_rows, LANES), lambda i: (first_small // small_rows, 0)),
            pl.BlockSpec((8, LANES), lambda i: (0, 0)),
        ]
        + state_specs * 3,
        out_specs=specs,
        compiler_params=pltpu.CompilerParams(vmem_limit_bytes=32 << 20),
    )(summed, summed, squares, *network_state, *running_means, *running_squares)
    return (results[0].reshape(()), results[1].reshape(()), *results[2:])


def whole_grid_grads(network_state, coords, goals, bound, sizes, places, mesh_sizes):
    io_rows, mats, maps, qkv, sharp, vecs = network_state
    members, groups = mesh_sizes
    grids, own, _, own_points = coords.shape
    points = own_points * members
    layers, _, width, _ = mats.shape
    heads = sharp.shape[1]
    head_size, slices = maps.shape[1:]
    outc = io_rows.shape[0] - FIN
    tile = TILE
    half, span, group = heads // 2, heads // 2 * slices, heads // 2 * head_size
    dims = (grids, points, width, heads, head_size, slices, layers, FIN, outc, tile)
    dims = dims + (members, groups, places)

    def both(*shape):
        return [pltpu.VMEM(shape, bf16), pltpu.VMEM(shape, bf16)]

    def single(*shape):
        return [pltpu.VMEM(shape, f32)]

    kept = (layers, grids, width, points)
    box = (members, grids * 8 + 8, own_points)
    scratch = (
        single(grids, width, points)
        + both(*kept)
        + single(layers, grids, 1, points)
        + both(*kept)
        + both(*kept)
        + both(layers, grids, 2 * span, points)
        + both(*kept)
        + both(*kept)
        + single(layers, grids, 1, points)
        + both(*kept)
        + single(*kept)
        + both(layers, 5, width, width)
        + single(layers, 9, width, LANES)
        + both(layers, 2, span, group)
        + both(layers, 2, group, span)
        + single(grids, 2, group + 16, span)
        + single(grids, 2, group, span)
        + single(layers, grids, head_size, 2 * span)
        + single(layers, grids, 1, 2 * span)
        + single(layers, grids, 3 * head_size, 2 * span)
        + single(layers, grids, half, slices, 2 * slices)
        + both(layers, grids, 2, group, span)
        + both(grids, 2, group, span)
        + both(grids, 2, span, 2 * group)
        + single(grids, 2 * span, LANES)
        + single(layers, 5, width, LANES)
        + single(layers, 2, group, span)
        + single(1 + width // LANES, 8, LANES)
        + single(8, width)
        + single(8, LANES)
        + single(layers, head_size, 3 * head_size)
        + single(grids, 8, points)
        + single(*box)
        + single(members - 1, *box[1:])
        + single(groups, 8, own_points)
        + [pltpu.SemaphoreType.DMA((members - 1,))] * 2
        + [pltpu.SemaphoreType.DMA((groups - 1,))] * 2
    )
    vmem = pl.BlockSpec(memory_space=pltpu.VMEM)
    smem = pl.BlockSpec(memory_space=pltpu.SMEM)
    return pl.pallas_call(
        functools.partial(grids_kernel, dims),
        out_shape=jax.ShapeDtypeStruct((places["rows"], LANES), f32),
        in_specs=[smem] * 2 + [vmem] * 8,
        out_specs=vmem,
        scratch_shapes=scratch,
        compiler_params=pltpu.CompilerParams(
            collective_id=0, has_side_effects=True, vmem_limit_bytes=VMEM_BYTES
        ),
    )(sizes, sharp, coords, goals, bound, io_rows, mats, maps, qkv, vecs)


def body_grids(mesh_sizes, *arrays):
    network_state = arrays[4:10]
    io_rows, mats, maps, _, _, vecs = network_state
    places = packed_places(
        mats.shape[0], mats.shape[2], io_rows.shape[0], vecs.shape[0], maps.shape[1]
    )
    packed = whole_grid_grads(network_state, *arrays[:4], places, mesh_sizes)
    summed, squares = sum_over_devices(packed, places, mesh_sizes[0])
    return update_all(
        summed, squares, network_state, arrays[10:16], arrays[16:22], places
    )


def solution(mesh):
    in_specs = (
        P(None, "grp", None, "pts"),
        P(None, "grp", None, "pts"),
        P(None, "grp", "pts"),
        P(None, "grp"),
        P(),
        P(),
        P(),
        P(),
        P(),
        P(),
        P(),
        P(),
        P(),
        P(),
        P(),
        P(),
        P(),
        P(),
        P(),
        P(),
        P(),
        P(),
    )
    out_specs = (
        P(),
        P(),
        P(),
        P(),
        P(),
        P(),
        P(),
        P(),
        P(),
        P(),
        P(),
        P(),
        P(),
        P(),
        P(),
        P(),
        P(),
        P(),
        P(),
        P(),
    )
    members, groups = mesh.shape["pts"], mesh.shape["grp"]

    def body(*arrays):
        batches, own, _, own_points = arrays[0].shape
        fits = own == members and batches * own_points * members <= 2048
        if fits and own_points == LANES and (members, groups) == (8, 4):
            return body_grids((members, groups), *arrays)
        return body_points(*arrays)

    return jax.shard_map(body, mesh=mesh, in_specs=in_specs, out_specs=out_specs, check_vma=False)
```

```python
import functools
import math

import jax
import jax.numpy as jnp
from jax import lax
from jax.experimental import pallas as pl
from jax.experimental.pallas import tpu as pltpu
from jax.sharding import PartitionSpec as P

STEP = 10
LANES = 128
FIN = 2
TILE = 512
REST_PLAN = (((), ((2, 1),)), ((), (), ((2, 2),)))
ATTEND_PLAN = ((), ((2, 3),), ((1, 1),))
FRONT_PLAN = (((), ((2, 4),), (), ((1, 2),)), (((2, 5),), (), ((1, 3),), (), ((2, 6),)))
END_PLAN = ((1, 4), (0, 1), (1, 5), (0, 2), (0, 3), (1, 6), (0, 4), (0, 5), (0, 6))
VMEM_BYTES = 63 << 20
f32, bf16 = jnp.float32, jnp.bfloat16
MESH = pl.DeviceIdType.MESH
NN, NT, TN = ((1,), (0,)), ((1,), (1,)), ((0,), (0,))


exact_arithmetic = lax.Precision.HIGHEST
clip_limit = 0.02
learn_rate = 0.1
beta_one = 0.9
beta_two = 0.999
adam_epsilon = 1e-08
weight_decay = 0.01


def layer_norm(values, gain, shift):
    center = values - jnp.mean(values, -1, keepdims=True)
    spread_tokens = jnp.mean(center * center, -1, keepdims=True)
    return center * lax.rsqrt(spread_tokens + 1e-05) * gain + shift


def slice_attend(weighted_points, masses, triple_maps_rows):
    head_size = triple_maps_rows.shape[0]
    tokens = weighted_points / (masses[..., None] + 1e-05)
    joined = jnp.einsum("imd,de->ime", tokens, triple_maps_rows, precision=exact_arithmetic)
    queries = joined[..., :head_size]
    keys = joined[..., head_size : 2 * head_size]
    values = joined[..., 2 * head_size :]
    scores = jnp.einsum("imd,ind->imn", queries, keys, precision=exact_arithmetic) * head_size ** (
        -0.5
    )
    probs = jax.nn.softmax(scores, -1)
    return jnp.einsum("imn,ind->imd", probs, values, precision=exact_arithmetic)


def slice_front(weight_set, slicer, temper, vec_rows, stream, valid):
    grids_n, points_n, width = stream.shape
    heads = temper.shape[0]
    normed = layer_norm(stream, vec_rows[0], vec_rows[1])
    features = (
        jnp.einsum("gpc,ce->gpe", normed, weight_set[0], precision=exact_arithmetic) + vec_rows[2]
    )
    chip_placement_list = (
        jnp.einsum("gpc,ce->gpe", normed, weight_set[1], precision=exact_arithmetic) + vec_rows[3]
    )
    partition_scores = (
        jnp.einsum(
            "gphd,dm->gphm",
            chip_placement_list.reshape(grids_n, points_n, heads, -1),
            slicer,
            precision=exact_arithmetic,
        )
        / temper[:, None]
    )
    slice_weights = jax.nn.softmax(partition_scores, -1) * valid[:, :, None, None]
    return (slice_weights, features.reshape(grids_n, points_n, heads, -1))


def slice_rest(weight_set, vec_rows, stream, spread_tokens):
    stream = (
        stream
        + jnp.einsum("gpc,ce->gpe", spread_tokens, weight_set[2], precision=exact_arithmetic)
        + vec_rows[4]
    )
    inner = (
        jnp.einsum(
            "gpc,ce->gpe",
            layer_norm(stream, vec_rows[5], vec_rows[6]),
            weight_set[3],
            precision=exact_arithmetic,
        )
        + vec_rows[7]
    )
    hidden = jax.nn.gelu(inner, approximate=False)
    return (
        stream
        + jnp.einsum("gpc,ce->gpe", hidden, weight_set[4], precision=exact_arithmetic)
        + vec_rows[8]
    )


def slice_mix(weighted_points, masses, qkv):
    grids_n, heads, slices, head_size = weighted_points.shape
    items = grids_n * heads
    flat_weighted = weighted_points.reshape(items, slices, head_size)
    flat_masses = masses.reshape(items, slices)
    own_weighted, own_masses = (
        lax.psum_scatter(flat_weighted, "pts", scatter_dimension=0, tiled=True),
        lax.psum_scatter(flat_masses, "pts", scatter_dimension=0, tiled=True),
    )
    mixed_tokens = lax.all_gather(
        slice_attend(own_weighted, own_masses, qkv), "pts", axis=0, tiled=True
    )
    kept = (own_weighted, own_masses)
    return (mixed_tokens.reshape(weighted_points.shape), kept)


def slice_mix_back(grad_mixed, kept, qkv):
    grids_n, heads, slices, head_size = grad_mixed.shape
    flat = grad_mixed.reshape(grids_n * heads, slices, head_size)
    _, pullback = jax.vjp(slice_attend, kept[0], kept[1], qkv)
    own_grad = lax.psum_scatter(flat, "pts", scatter_dimension=0, tiled=True)
    grad_weighted, grad_masses, grad_qkv = pullback(own_grad)
    grad_weighted, grad_masses = (
        lax.all_gather(grad_weighted, "pts", axis=0, tiled=True),
        lax.all_gather(grad_masses, "pts", axis=0, tiled=True),
    )
    return (
        grad_weighted.reshape(grad_mixed.shape),
        grad_masses.reshape(grids_n, heads, slices),
        grad_qkv,
    )


def layer_forward(stream, layer_set, valid):
    weight_set, slicer, qkv, temper, vec_rows = layer_set
    slice_weights, features = slice_front(weight_set, slicer, temper, vec_rows, stream, valid)
    weighted_points = jnp.einsum(
        "gphm,gphd->ghmd", slice_weights, features, precision=exact_arithmetic
    )
    masses = jnp.sum(slice_weights, 1)
    mixed_tokens, kept = slice_mix(weighted_points, masses, qkv)
    spread_tokens = jnp.einsum(
        "gphm,ghmd->gphd", slice_weights, mixed_tokens, precision=exact_arithmetic
    ).reshape(stream.shape)
    return (slice_rest(weight_set, vec_rows, stream, spread_tokens), (stream, mixed_tokens, kept))


def layer_backward(grad_out, layer_set, saved, valid):
    weight_set, slicer, qkv, temper, vec_rows = layer_set
    stream, mixed_tokens, kept = saved
    (slice_weights, features), pull_front = jax.vjp(
        lambda w_set, s_set, t_set, v_set, s_in: slice_front(
            w_set, s_set, t_set, v_set, s_in, valid
        ),
        weight_set,
        slicer,
        temper,
        vec_rows,
        stream,
    )
    spread_tokens = jnp.einsum(
        "gphm,ghmd->gphd", slice_weights, mixed_tokens, precision=exact_arithmetic
    ).reshape(stream.shape)
    _, pull_rest = jax.vjp(slice_rest, weight_set, vec_rows, stream, spread_tokens)
    grad_set_rest, grad_vec_rest, grad_stream, grad_spread = pull_rest(grad_out)
    grad_spread = grad_spread.reshape(features.shape)
    grad_weights = jnp.einsum(
        "gphd,ghmd->gphm", grad_spread, mixed_tokens, precision=exact_arithmetic
    )
    grad_mixed = jnp.einsum(
        "gphm,gphd->ghmd", slice_weights, grad_spread, precision=exact_arithmetic
    )
    grad_weighted, grad_masses, grad_qkv = slice_mix_back(grad_mixed, kept, qkv)
    grad_weights = (
        grad_weights
        + jnp.einsum("ghmd,gphd->gphm", grad_weighted, features, precision=exact_arithmetic)
        + grad_masses[:, None]
    )
    grad_features = jnp.einsum(
        "gphm,ghmd->gphd", slice_weights, grad_weighted, precision=exact_arithmetic
    )
    grad_set_front, grad_slicer, grad_temper, grad_vec_front, grad_stream_front = pull_front(
        (grad_weights, grad_features)
    )
    grads = (
        grad_set_rest + grad_set_front,
        grad_slicer,
        grad_qkv,
        grad_temper,
        grad_vec_rest + grad_vec_front,
    )
    return (grad_stream + grad_stream_front, grads)


def head_loss(head_rows, tail_rows, stream, goals, on_surface, off_surface, inv_surf, inv_vol):
    final = layer_norm(stream, tail_rows[0], tail_rows[1])
    pred = jnp.einsum("oc,gpc->gop", head_rows, final, precision=exact_arithmetic)
    errors = (pred - goals) ** 2
    return inv_surf * jnp.sum(on_surface * errors[:, 0]) + inv_vol * jnp.sum(
        off_surface * (errors[:, 1] + errors[:, 2])
    )


def layer_params(network_state, block_number):
    (
        lifting_readout_rows,
        block_projections,
        partition_maps,
        triple_maps_rows,
        sharpness_factors,
        gain_bias_rows,
    ) = network_state
    return (
        block_projections[block_number],
        partition_maps[block_number],
        triple_maps_rows[block_number],
        sharpness_factors[block_number],
        gain_bias_rows[9 * block_number : 9 * block_number + 9],
    )


def one_batch(network_state, coords, goals, valid, on_surface, off_surface, inv_surf, inv_vol):
    (
        lifting_readout_rows,
        block_projections,
        partition_maps,
        triple_maps_rows,
        sharpness_factors,
        gain_bias_rows,
    ) = network_state
    fin = coords.shape[1]
    layers_n = block_projections.shape[0]
    stream = jnp.einsum(
        "gfp,fc->gpc", coords, lifting_readout_rows[:fin], precision=exact_arithmetic
    )
    saved = []
    for block_number in range(layers_n):
        stream, keep_set = layer_forward(stream, layer_params(network_state, block_number), valid)
        saved.append(keep_set)
    batch_loss, pull_head = jax.vjp(
        lambda h_rows, t_rows, s_in: head_loss(
            h_rows, t_rows, s_in, goals, on_surface, off_surface, inv_surf, inv_vol
        ),
        lifting_readout_rows[fin:],
        gain_bias_rows[9 * layers_n :],
        stream,
    )
    grad_head, grad_tail, grad_stream = pull_head(jnp.ones_like(batch_loss))
    layer_grads = [None] * layers_n
    for block_number in reversed(range(layers_n)):
        grad_stream, layer_grads[block_number] = layer_backward(
            grad_stream, layer_params(network_state, block_number), saved[block_number], valid
        )
    grad_embed = jnp.einsum("gfp,gpc->fc", coords, grad_stream, precision=exact_arithmetic)
    grads = (
        jnp.concatenate([grad_embed, grad_head], 0),
        jnp.stack([entry[0] for entry in layer_grads]),
        jnp.stack([entry[1] for entry in layer_grads]),
        jnp.stack([entry[2] for entry in layer_grads]),
        jnp.stack([entry[3] for entry in layer_grads]),
        jnp.concatenate([entry[4] for entry in layer_grads] + [grad_tail], 0),
    )
    return (batch_loss, grads)


def adamw_update(weight, grad, first, second):
    first_new = beta_one * first + (1.0 - beta_one) * grad
    second_new = beta_two * second + (1.0 - beta_two) * grad * grad
    first_hat = first_new / (1.0 - beta_one**STEP)
    second_hat = second_new / (1.0 - beta_two**STEP)
    weight_new = weight - learn_rate * (
        first_hat / (jnp.sqrt(second_hat) + adam_epsilon) + weight_decay * weight
    )
    return (first_new, second_new, weight_new)


def body_points(
    input_positions,
    flow_labels,
    airfoil_boundary,
    valid_sizes,
    lifting_readout_rows,
    block_projections,
    partition_maps,
    triple_maps_rows,
    sharpness_factors,
    gain_bias_rows,
    lifting_readout_mean,
    projection_running_mean,
    partition_map_mean,
    triple_maps_mean,
    sharpness_mean,
    gain_bias_mean,
    lifting_readout_square,
    projection_running_square,
    partition_map_square,
    triple_maps_square,
    sharpness_square,
    gain_bias_square,
):
    batches = input_positions.shape[0]
    points_n = input_positions.shape[3]
    slots = lax.axis_index("pts") * points_n + jnp.arange(points_n, dtype=jnp.int32)
    valid = (slots[None, None, :] < valid_sizes[:, :, None]).astype(jnp.float32)
    on_surface = valid * airfoil_boundary.astype(jnp.float32)
    off_surface = valid - on_surface
    count_surf, count_vol = lax.psum((jnp.sum(on_surface), jnp.sum(off_surface)), ("pts", "grp"))
    inv_surf = 1.0 / jnp.maximum(count_surf, 1.0)
    inv_vol = 1.0 / jnp.maximum(count_vol, 1.0)
    network_state = (
        lifting_readout_rows,
        block_projections,
        partition_maps,
        triple_maps_rows,
        sharpness_factors,
        gain_bias_rows,
    )
    loss_value = jnp.zeros((), jnp.float32)
    grads = tuple((jnp.zeros_like(entry) for entry in network_state))
    for batch in range(batches):
        batch_loss, batch_set = one_batch(
            network_state,
            input_positions[batch],
            flow_labels[batch],
            valid[batch],
            on_surface[batch],
            off_surface[batch],
            inv_surf,
            inv_vol,
        )
        loss_value = loss_value + batch_loss
        grads = tuple((total + entry for total, entry in zip(grads, batch_set)))
    running_means = (
        lifting_readout_mean,
        projection_running_mean,
        partition_map_mean,
        triple_maps_mean,
        sharpness_mean,
        gain_bias_mean,
    )
    running_squares = (
        lifting_readout_square,
        projection_running_square,
        partition_map_square,
        triple_maps_square,
        sharpness_square,
        gain_bias_square,
    )
    return finish(loss_value, grads, network_state, running_means, running_squares)


def finish(loss_value, grads, network_state, running_means, running_squares):
    summed = lax.psum((loss_value,) + grads, ("pts", "grp"))
    loss_value = summed[0]
    grads = summed[1:]
    grad_norm = jnp.sqrt(sum((jnp.sum(entry * entry) for entry in grads)))
    factor = jnp.minimum(1.0, clip_limit / grad_norm)
    results = []
    for weight, grad, first, second in zip(network_state, grads, running_means, running_squares):
        results.extend(adamw_update(weight, grad * factor, first, second))
    return tuple([loss_value, grad_norm] + results)


def _split(x):
    high = x.astype(bf16)
    return high, (x - high.astype(f32)).astype(bf16)


def _dot(a, b, dims, precision=None):
    return lax.dot_general(a, b, (dims, ((), ())), precision=precision, preferred_element_type=f32)


def _dot3(a, b, dims):
    return _dot(a[0], b[0], dims) + _dot(a[0], b[1], dims) + _dot(a[1], b[0], dims)


def _dotx(a, b, dims):
    return _dot(a, b, dims, lax.Precision.HIGHEST)


def _wide(col, lanes):
    return jnp.concatenate([col] * (lanes // LANES), 1) if lanes > LANES else col


def _fold(x):
    total = x[:, :LANES]
    for start in range(LANES, x.shape[1], LANES):
        total = total + x[:, start : start + LANES]
    return total


def _lockstep(makers, hooks=()):
    running = list(makers)
    turn = 0
    while running:
        for hook in hooks[turn : turn + 1]:
            for stage in hook:
                stage()
        turn += 1
        alive = []
        for entry in running:
            try:
                next(entry)
                alive.append(entry)
            except StopIteration:
                pass
        running = alive


def _diag_heads(full, depth, slices):
    heads = full.shape[0] // depth
    lane = lax.broadcasted_iota(jnp.int32, (depth, full.shape[1]), 1)
    picked = full[:depth]
    for head in range(1, heads):
        picked = jnp.where(lane >= head * slices, full[head * depth : (head + 1) * depth], picked)
    return picked


def _block_heads(flat, heads, slices):
    lane = lax.broadcasted_iota(jnp.int32, flat.shape, 1)
    return jnp.concatenate(
        [
            jnp.where((lane >= head * slices) & (lane < (head + 1) * slices), flat, 0.0)
            for head in range(heads)
        ],
        0,
    )


def _norm(x):
    inv_width = 1.0 / x.shape[0]
    center = x - jnp.sum(x, 0, keepdims=True) * inv_width
    rstd = lax.rsqrt(jnp.sum(center * center, 0, keepdims=True) * inv_width + 1e-05)
    return center * rstd, rstd


def _norm_back(grad, xhat, rstd):
    inv_width = 1.0 / grad.shape[0]
    mean_grad = jnp.sum(grad, 0, keepdims=True) * inv_width
    mean_proj = jnp.sum(grad * xhat, 0, keepdims=True) * inv_width
    return (grad - mean_grad - xhat * mean_proj) * rstd


def grids_kernel(dims, *refs):
    (
        grids,
        points,
        width,
        heads,
        head_size,
        slices,
        layers,
        fin,
        outc,
        tile,
        members,
        groups,
        places,
    ) = dims
    (
        sizes_ref,
        sharp_ref,
        coords_ref,
        goals_ref,
        bound_ref,
        io_ref,
        mats_ref,
        maps_ref,
        qkv_ref,
        vecs_ref,
        summed,
        squares,
        packed,
        stream,
        xh1h,
        rs1,
        feath,
        featl,
        placeh,
        placel,
        wgth,
        wgtl,
        sprh,
        sprl,
        xh2h,
        rs2,
        hidh,
        gslope,
        upmh,
        upml,
        cols,
        bdmh,
        bdml,
        bdth,
        bdtl,
        accw,
        accf,
        tok,
        rmass,
        qkvs,
        probs,
        mbdh,
        mbdl,
        dbdh,
        dbdl,
        cmbh,
        cmbl,
        dmcol,
        vacc,
        gmacc,
        headacc,
        embacc,
        lossacc,
        qkvacc,
        points_ref,
        outbox,
        inbox,
        tally,
        send_sems,
        recv_sems,
        tally_send,
        tally_recv,
        sum_send,
        sum_recv,
    ) = refs[: -5 * len(places["groups"])]
    boxes = refs[-5 * len(places["groups"]) :]
    half = heads // 2
    span = half * slices
    group = half * head_size
    pairs = heads // 2
    all_slices = heads * slices
    steps = points // tile
    scale = head_size ** (-0.5)
    ones_rows = jnp.ones((8, LANES), f32)
    me, mine = lax.axis_index("pts"), lax.axis_index("grp")
    own_points = points // members

    def peer_points(hop):
        return lax.rem(me + hop, members)

    def peer_group(hop):
        return lax.rem(mine + hop, groups)

    barrier = pltpu.get_barrier_semaphore()
    for hop in range(1, members):
        pl.semaphore_signal(
            barrier, inc=1, device_id=(peer_points(hop), mine), device_id_type=MESH
        )
    for hop in range(1, groups):
        pl.semaphore_signal(
            barrier, inc=1, device_id=(me, peer_group(hop)), device_id_type=MESH
        )

    def same_plane(hop):
        other_y = lax.rem(lax.rem(me, 2) + hop // 2, 2)
        other_x = lax.rem(lax.div(mine, 2) + hop % 2, 2)
        return (lax.div(me, 2) * 2 + other_y, other_x * 2 + lax.rem(mine, 2))

    pl.semaphore_signal(barrier, inc=1, device_id=same_plane(3), device_id_type=MESH)

    slots = lax.broadcasted_iota(jnp.int32, (1, own_points), 1) + me * own_points
    surf_total = jnp.zeros((1, own_points), f32)
    vol_total = jnp.zeros((1, own_points), f32)
    blank = jnp.zeros((8 - fin - outc - 1, own_points), f32)
    for dest in range(members):
        for batch in range(grids):
            surf = bound_ref[batch, dest : dest + 1, :].astype(f32)
            goals = [goals_ref[batch, field, dest : dest + 1, :] for field in range(outc)]
            outbox[dest, batch * 8 : batch * 8 + 8, :] = jnp.concatenate(
                [coords_ref[batch, dest], *goals, surf, blank], 0
            )
            valid = jnp.where(slots < sizes_ref[batch, dest], 1.0, 0.0)
            surf_total = surf_total + valid * surf
            vol_total = vol_total + (valid - valid * surf)
    totals = jnp.concatenate(
        [surf_total, vol_total, jnp.zeros((6, own_points), f32)], 0
    )
    for dest in range(members):
        outbox[dest, grids * 8 :, :] = totals
    pl.semaphore_wait(barrier, members + groups - 1)

    def piece(hop):
        other = peer_points(hop)
        return pltpu.make_async_remote_copy(
            src_ref=outbox.at[other],
            dst_ref=inbox.at[hop - 1],
            send_sem=send_sems.at[hop - 1],
            recv_sem=recv_sems.at[hop - 1],
            device_id=(other, mine),
            device_id_type=MESH,
        )

    def share(hop):
        return pltpu.make_async_remote_copy(
            src_ref=tally.at[0],
            dst_ref=tally.at[hop],
            send_sem=tally_send.at[hop - 1],
            recv_sem=tally_recv.at[hop - 1],
            device_id=(me, peer_group(hop)),
            device_id_type=MESH,
        )

    for hop in range(1, members):
        piece(hop).start()

    def matrix_rows(layer, slot, half_index):
        start = places["mats"] + ((layer * 5 + slot) * (width // LANES) + half_index) * width
        return pl.ds(pl.multiple_of(start, width), width)

    def add_matrix(layer, slot, value):
        for index in range(width // LANES):
            packed[matrix_rows(layer, slot, index), :] += value[
                :, index * LANES : (index + 1) * LANES
            ]

    def read_matrix(layer, slot):
        return jnp.concatenate(
            [packed[matrix_rows(layer, slot, index), :] for index in range(width // LANES)], 1
        )

    def split_to(high_ref, low_ref, index, value):
        high, low = _split(value)
        high_ref[index] = high
        low_ref[index] = low
        return high, low

    vecs = vecs_ref[...]
    row_id = lax.broadcasted_iota(jnp.int32, (vecs.shape[0], LANES), 0)

    def column(row):
        return _dotx(vecs, jnp.where(row_id == row, 1.0, 0.0), TN)

    for layer in range(layers):
        base = 9 * layer
        gain_a, shift_a = column(base), column(base + 1)
        gain_b, shift_b = column(base + 5), column(base + 6)
        cols[layer, 0] = gain_a
        cols[layer, 1] = shift_a
        cols[layer, 2] = gain_b
        cols[layer, 3] = shift_b
        for slot in range(5):
            flipped = mats_ref[layer, slot].T
            bias = column(base + (2, 3, 4, 7, 8)[slot])
            if slot in (0, 1, 3):
                gain, shift, row = (gain_b, shift_b, 5) if slot == 3 else (gain_a, shift_a, 0)
                bias = bias + _dotx(flipped, shift, NN)
                flipped = flipped * vecs[base + row : base + row + 1]
            cols[layer, 4 + slot] = bias
            split_to(upmh, upml, (layer, slot), flipped)
        tiled = jnp.concatenate([maps_ref[layer]] * half, 1)
        for part in range(2):
            lane = lax.broadcasted_iota(jnp.int32, (1, span), 1)
            sharp = jnp.full((1, span), 0.0, f32) + sharp_ref[layer, part * half]
            for head in range(1, half):
                sharp = jnp.where(lane >= head * slices, sharp_ref[layer, part * half + head], sharp)
            block = _block_heads(tiled / sharp, half, slices)
            split_to(bdth, bdtl, (layer, part), block)
            split_to(bdmh, bdml, (layer, part), block.T)

    vacc[...] = jnp.zeros_like(vacc)
    gmacc[...] = jnp.zeros_like(gmacc)
    headacc[...] = jnp.zeros_like(headacc)
    embacc[...] = jnp.zeros_like(embacc)
    lossacc[...] = jnp.zeros_like(lossacc)
    packed[...] = jnp.zeros_like(packed)
    qkvacc[...] = jnp.zeros_like(qkvacc)

    io_all = io_ref[...]
    io_id = lax.broadcasted_iota(jnp.int32, (io_all.shape[0], LANES), 0)
    lift = [_dotx(io_all, jnp.where(io_id == row, 1.0, 0.0), TN) for row in range(fin)]

    def window(step):
        return pl.ds(pl.multiple_of(step * tile, tile), tile)

    def pair_of(high_ref, low_ref, index):
        return high_ref[index], low_ref[index]

    def settle(source, block):
        at = pl.ds(pl.multiple_of(source * own_points, own_points), own_points)
        for grid in range(grids):
            points_ref[grid, :, at] = block[grid * 8 : grid * 8 + 8]
        return block[grids * 8 :]

    held = settle(me, outbox[me])
    for hop in range(1, members):
        piece(hop).wait()
        held = held + settle(lax.rem(me + members - hop, members), inbox[hop - 1])
    tally[0] = held
    for hop in range(1, groups):
        share(hop).start()

    @pl.loop(0, steps)
    def _(step):
        at = window(step)
        for grid in range(grids):
            x = jnp.zeros((width, tile), f32)
            for row in range(fin):
                x = x + _wide(lift[row], tile) * points_ref[grid, row : row + 1, at]
            stream[grid, :, at] = x

    def front(layer, grid, at, step):
        xhat, rstd = _norm(stream[grid, :, at])
        xhat = _split(xhat)
        xh1h[layer, grid, :, at] = xhat[0]
        rs1[layer, grid, :, at] = rstd
        yield
        feat = _dot3(pair_of(upmh, upml, (layer, 0)), xhat, NN) + _wide(cols[layer, 4], tile)
        place = _dot3(pair_of(upmh, upml, (layer, 1)), xhat, NN) + _wide(cols[layer, 5], tile)
        feat = split_to(feath, featl, (layer, grid, slice(None), at), feat)
        place = split_to(placeh, placel, (layer, grid, slice(None), at), place)
        yield
        slots = lax.broadcasted_iota(jnp.int32, (1, tile), 1) + step * tile
        valid = jnp.where(slots < sizes_ref[grid, me], 1.0, 0.0)
        for part in range(2):
            rows = slice(part * group, (part + 1) * group)
            scores = _dot3(
                pair_of(bdmh, bdml, (layer, part)), (place[0][rows], place[1][rows]), NN
            ).reshape(half, slices, tile)
            expo = jnp.exp(scores - jnp.max(scores, 1, keepdims=True))
            ratio = valid[None] / jnp.sum(expo, 1, keepdims=True)
            weight = (expo * ratio).reshape(span, tile)
            wrows = slice(part * span, (part + 1) * span)
            weight = split_to(wgth, wgtl, (layer, grid, wrows, at), weight)
            yield
            lead = jnp.concatenate([feat[0][rows], jnp.ones((16, tile), bf16)], 0)
            accw[grid, part] += _dot(lead, weight[0], NT) + _dot(lead, weight[1], NT)
            accf[grid, part] += _dot(feat[1][rows], weight[0], NT)
            yield

    def attend(layer, grid):
        parts, masses = [], []
        for part in range(2):
            total = accw[grid, part]
            parts.append(_diag_heads(total[:group] + accf[grid, part], head_size, slices))
            masses.append(total[group : group + 1])
        rate = 1.0 / (jnp.concatenate(masses, 1) + 1e-05)
        tokens = jnp.concatenate(parts, 1) * rate
        tok[layer, grid] = tokens
        rmass[layer, grid] = rate
        yield
        joined = _dotx(qkv_ref[layer], tokens, TN)
        qkvs[layer, grid] = joined
        yield
        lane = lax.broadcasted_iota(jnp.int32, (slices, 2 * slices), 1)
        mixed = []
        for pair in range(pairs):
            at = slice(pair * 2 * slices, (pair + 1) * 2 * slices)
            query = joined[:head_size, at]
            key = joined[head_size : 2 * head_size, at]
            value = joined[2 * head_size :, at]
            full = _dotx(key, query, TN)
            scores = jnp.where(lane < slices, full[:slices], full[slices:]) * scale
            expo = jnp.exp(scores - jnp.max(scores, 0, keepdims=True))
            prob = expo / jnp.sum(expo, 0, keepdims=True)
            probs[layer, grid, pair] = prob
            mixed.append(_dotx(value, _block_heads(prob, 2, slices), NN))
        for part in range(2):
            flat = jnp.concatenate(mixed[part * (pairs // 2) : (part + 1) * (pairs // 2)], 1)
            block = _block_heads(flat, half, slices)
            split_to(mbdh, mbdl, (layer, grid, part), block)
        yield

    def rest(layer, grid, at):
        spread = []
        for part in range(2):
            wrows = slice(part * span, (part + 1) * span)
            weight = pair_of(wgth, wgtl, (layer, grid, wrows, at))
            spread.append(_dot3(pair_of(mbdh, mbdl, (layer, grid, part)), weight, NN))
        spread = split_to(
            sprh, sprl, (layer, grid, slice(None), at), jnp.concatenate(spread, 0)
        )
        yield
        x = (
            stream[grid, :, at]
            + _dot3(pair_of(upmh, upml, (layer, 2)), spread, NN)
            + _wide(cols[layer, 6], tile)
        )
        xhat, rstd = _norm(x)
        xhat = _split(xhat)
        xh2h[layer, grid, :, at] = xhat[0]
        rs2[layer, grid, :, at] = rstd
        yield
        inner = _dot3(pair_of(upmh, upml, (layer, 3)), xhat, NN) + _wide(cols[layer, 7], tile)
        cdf = 0.5 + 0.5 * lax.erf(inner * (0.5**0.5))
        slope = cdf + inner * jnp.exp(-0.5 * inner * inner) * ((2.0 * math.pi) ** -0.5)
        gslope[layer, grid, :, at] = slope.astype(bf16)
        hidden = _split(inner * cdf)
        hidh[layer, grid, :, at] = hidden[0]
        yield
        stream[grid, :, at] = (
            x
            + _dot3(pair_of(upmh, upml, (layer, 4)), hidden, NN)
            + _wide(cols[layer, 8], tile)
        )
        yield

    @pl.loop(0, layers)
    def _(layer):
        accw[...] = jnp.zeros_like(accw)
        accf[...] = jnp.zeros_like(accf)

        @pl.loop(0, steps)
        def _(step):
            at = window(step)
            _lockstep([front(layer, grid, at, step) for grid in range(grids)])

        _lockstep([attend(layer, grid) for grid in range(grids)])

        @pl.loop(0, steps)
        def _(step):
            at = window(step)
            _lockstep([rest(layer, grid, at) for grid in range(grids)])

    tail = 9 * layers
    head_rows = jnp.concatenate(
        [io_ref[fin:, :], jnp.zeros((8 - outc, width), f32)], 0
    )
    head_gain = head_rows * vecs[tail : tail + 1]
    head_pair = _split(head_gain)
    head_bias = _dotx(head_rows, column(tail + 1), NN)
    counted = tally[0]
    for hop in range(1, groups):
        share(hop).wait()
        counted = counted + tally[hop]
    counted = jnp.broadcast_to(jnp.sum(counted, 1, keepdims=True), counted.shape)
    counted = 1.0 / jnp.maximum(counted, 1.0)
    inv_surf, inv_vol = _wide(counted[:1], tile), _wide(counted[1:2], tile)

    def crown(grid, at, step):
        xhat, rstd = _norm(stream[grid, :, at])
        halves = _split(xhat)
        pred = _dot3(head_pair, halves, NN) + _wide(head_bias, tile)
        slots = lax.broadcasted_iota(jnp.int32, (1, tile), 1) + step * tile
        valid = jnp.where(slots < sizes_ref[grid, me], 1.0, 0.0)
        surf = valid * points_ref[grid, fin + outc : fin + outc + 1, at]
        vol = (valid - surf) * inv_vol
        surf = surf * inv_surf
        row = lax.broadcasted_iota(jnp.int32, (8, tile), 0)
        factor = jnp.where(row == 0, surf, jnp.where(row < outc, vol, 0.0))
        goals = jnp.concatenate(
            [points_ref[grid, fin : fin + outc, at], jnp.zeros((8 - outc, tile), f32)], 0
        )
        error = pred - goals
        scaled = factor * error
        lossacc[...] += _fold(scaled * error)
        dpred = scaled + scaled
        headacc[0] += _fold(dpred)
        dhalves = _split(dpred)
        headacc_rows = _dot3(dhalves, halves, NT)
        for start in range(0, width, LANES):
            headacc[1 + start // LANES] += headacc_rows[:, start : start + LANES]
        yield
        grad = _dot3(head_pair, dhalves, TN)
        stream[grid, :, at] = _norm_back(grad, xhat, rstd)
        yield

    @pl.loop(0, steps)
    def _(step):
        at = window(step)
        _lockstep([crown(grid, at, step) for grid in range(grids)])

    for layer in range(layers):
        for slot in range(5):
            mat = mats_ref[layer, slot]
            if slot in (0, 1, 3):
                mat = mat * _wide(cols[layer, 2 if slot == 3 else 0], width)
            split_to(upmh, upml, (layer, slot), mat)

    def back_rest(layer, grid, at):
        grad = stream[grid, :, at]
        vacc[layer, 4] += _fold(grad)
        pieces = _split(grad)
        dhid = _dot(upmh[layer, 4], pieces[0], NN)
        add_matrix(layer, 4, _dot(hidh[layer, grid, :, at], pieces[0], NT))
        yield
        dinner = dhid * gslope[layer, grid, :, at].astype(f32)
        vacc[layer, 3] += _fold(dinner)
        dinner = dinner.astype(bf16)
        xhat = xh2h[layer, grid, :, at]
        dxhat = _dot(upmh[layer, 3], dinner, NN)
        add_matrix(layer, 3, _dot(xhat, dinner, NT))
        yield
        grad = grad + _norm_back(
            dxhat, xhat.astype(f32), rs2[layer, grid, :, at]
        )
        stream[grid, :, at] = grad
        vacc[layer, 2] += _fold(grad)
        pieces = _split(grad)
        dspread = _dot3(pair_of(upmh, upml, (layer, 2)), pieces, NN)
        add_matrix(layer, 2, _dot3(pair_of(sprh, sprl, (layer, grid, slice(None), at)), pieces, NT))
        dspread = split_to(sprh, sprl, (layer, grid, slice(None), at), dspread)
        yield
        for part in range(2):
            rows = slice(part * group, (part + 1) * group)
            wrows = slice(part * span, (part + 1) * span)
            weight = pair_of(wgth, wgtl, (layer, grid, wrows, at))
            accf[grid, part] += _dot3((dspread[0][rows], dspread[1][rows]), weight, NT)
        yield

    def back_attend(layer, grid):
        joined = qkvs[layer, grid]
        tokens = tok[layer, grid]
        rate = rmass[layer, grid]
        lane = lax.broadcasted_iota(jnp.int32, (slices, 2 * slices), 1)
        dmixed = jnp.concatenate(
            [_diag_heads(accf[grid, part], head_size, slices) for part in range(2)], 1
        )
        yield
        dqs, dks, dvs = [], [], []
        for pair in range(pairs):
            at = slice(pair * 2 * slices, (pair + 1) * 2 * slices)
            query = joined[:head_size, at]
            key = joined[head_size : 2 * head_size, at]
            value = joined[2 * head_size :, at]
            prob = probs[layer, grid, pair]
            dmix = dmixed[:, at]
            full = _dotx(value, dmix, TN)
            dprob = jnp.where(lane < slices, full[:slices], full[slices:])
            dscore = (
                prob * (dprob - jnp.sum(prob * dprob, 0, keepdims=True)) * scale
            )
            dblock = _block_heads(dscore, 2, slices)
            dvs.append(_dotx(dmix, _block_heads(prob, 2, slices), NT))
            dqs.append(_dotx(key, dblock, NN))
            dks.append(_dotx(query, dblock, NT))
        dqkv = jnp.concatenate(
            [jnp.concatenate(part, 1) for part in (dqs, dks, dvs)], 0
        )
        yield
        dtok = _dotx(qkv_ref[layer], dqkv, NN)
        qkvacc[layer] += _dotx(tokens, dqkv, NT)
        dweighted = dtok * rate
        dmass = -jnp.sum(dweighted * tokens, 0, keepdims=True)
        yield
        dmass = jnp.broadcast_to(dmass, (8, all_slices))
        row_one = jnp.where(
            lax.broadcasted_iota(jnp.int32, (8, LANES), 0) == 0, 1.0, 0.0
        )
        dmcol[grid] = _dotx(dmass, row_one, TN)
        for part in range(2):
            block = _block_heads(dweighted[:, part * span : (part + 1) * span], half, slices)
            split_to(dbdh, dbdl, (grid, part), block)
            mix = mbdh[layer, grid, part].astype(f32) + mbdl[layer, grid, part].astype(f32)
            both = jnp.concatenate([mix, block], 0)
            split_to(cmbh, cmbl, (grid, part), both.T)
        yield

    def back_front(layer, grid, at):
        feat = pair_of(feath, featl, (layer, grid, slice(None), at))
        place = pair_of(placeh, placel, (layer, grid, slice(None), at))
        dfeats, dplaces = [], []
        for part in range(2):
            rows = slice(part * group, (part + 1) * group)
            wrows = slice(part * span, (part + 1) * span)
            weight = pair_of(wgth, wgtl, (layer, grid, wrows, at))
            dspread = pair_of(sprh, sprl, (layer, grid, rows, at))
            both = tuple(
                jnp.concatenate([one, two[rows]], 0) for one, two in zip(dspread, feat)
            )
            dweight = _dot3(pair_of(cmbh, cmbl, (grid, part)), both, NN)
            dweight = dweight + _wide(dmcol[grid, wrows], tile)
            full = weight[0].astype(f32) + weight[1].astype(f32)
            prod = full * dweight
            total = jnp.sum(prod.reshape(half, slices, tile), 1, keepdims=True)
            dscore = (
                prod.reshape(half, slices, tile) - full.reshape(half, slices, tile) * total
            ).reshape(span, tile)
            pieces = _split(dscore)
            yield
            dplaces.append(_dot3(pair_of(bdth, bdtl, (layer, part)), pieces, NN))
            gmacc[layer, part] += _dot3((place[0][rows], place[1][rows]), pieces, NT)
            dfeats.append(_dot3(pair_of(dbdh, dbdl, (grid, part)), weight, NN))
            yield
        dfeat = jnp.concatenate(dfeats, 0)
        dplace = jnp.concatenate(dplaces, 0)
        vacc[layer, 0] += _fold(dfeat)
        vacc[layer, 1] += _fold(dplace)
        dfeat, dplace = _split(dfeat), _split(dplace)
        xhat = xh1h[layer, grid, :, at]
        dxhat = _dot3(pair_of(upmh, upml, (layer, 0)), dfeat, NN) + _dot3(
            pair_of(upmh, upml, (layer, 1)), dplace, NN
        )
        add_matrix(layer, 0, _dot(xhat, dfeat[0], NT))
        add_matrix(layer, 1, _dot(xhat, dplace[0], NT))
        yield
        grad = stream[grid, :, at] + _norm_back(
            dxhat, xhat.astype(f32), rs1[layer, grid, :, at]
        )
        if isinstance(layer, int) and layer == 0:
            coords = jnp.concatenate(
                [points_ref[grid, :fin, at], jnp.zeros((8 - fin, tile), f32)], 0
            )
            embacc[...] += _dot3(_split(coords), _split(grad), NT)
        else:
            stream[grid, :, at] = grad
        yield

    def to_row(folded):
        return _dotx(ones_rows, folded, NT)[:1]

    ones_wide = jnp.ones((8, width), f32)

    def put_vector(row, value):
        for index in range(width // LANES):
            start = places["vecs"] + index * places["vecs_stride"] + row
            packed[start : start + 1, :] = value[:, index * LANES : (index + 1) * LANES]

    def close_matrix(layer, slot, bias_sum):
        gain, shift = (2, 3) if slot == 3 else (0, 1)
        gram = read_matrix(layer, slot)
        mat = mats_ref[layer, slot]
        value = (
            _wide(cols[layer, gain], width) * gram + _wide(cols[layer, shift], width) * bias_sum
        )
        for index in range(width // LANES):
            packed[matrix_rows(layer, slot, index), :] = value[
                :, index * LANES : (index + 1) * LANES
            ]
        shift_row = _dotx(jnp.broadcast_to(bias_sum, (8, width)), mat, NT)[:1]
        return _dotx(ones_wide, gram * mat, NT)[:1], shift_row

    def close_rest(layer):
        base = 9 * layer
        middle, inner, final = [to_row(vacc[layer, slot]) for slot in (2, 3, 4)]
        gain_row, shift_row = close_matrix(layer, 3, inner)
        for offset, row in ((4, middle), (5, gain_row), (6, shift_row), (7, inner), (8, final)):
            put_vector(base + offset, row)

    def close_front(layer):
        base = 9 * layer
        feat_sum, place_sum = [to_row(vacc[layer, slot]) for slot in (0, 1)]
        feat_gain, feat_shift = close_matrix(layer, 0, feat_sum)
        place_gain, place_shift = close_matrix(layer, 1, place_sum)
        put_vector(base, feat_gain + place_gain)
        put_vector(base + 1, feat_shift + place_shift)
        put_vector(base + 2, feat_sum)
        put_vector(base + 3, place_sum)
        tiled = jnp.concatenate([maps_ref[layer]] * half, 1)
        total = None
        sharp_total = None
        for part in range(2):
            lane = lax.broadcasted_iota(jnp.int32, (1, span), 1)
            sharp = jnp.full((1, span), 0.0, f32) + sharp_ref[layer, part * half]
            for head in range(1, half):
                sharp = jnp.where(
                    lane >= head * slices, sharp_ref[layer, part * half + head], sharp
                )
            picked = _diag_heads(gmacc[layer, part], head_size, slices) / sharp
            total = picked if total is None else total + picked
            share = -jnp.sum(picked * tiled, 0, keepdims=True) / sharp
            chosen = jnp.where(
                lax.broadcasted_iota(jnp.int32, (span, LANES), 0) // slices + part * half
                == lax.broadcasted_iota(jnp.int32, (span, LANES), 1),
                1.0,
                0.0,
            )
            share = _dotx(jnp.broadcast_to(share, (8, span)), chosen, NN)
            sharp_total = share if sharp_total is None else sharp_total + share
        start = places["sharp"] + layer
        packed[start : start + 1, :heads] = sharp_total[:1, :heads]
        total = _fold(total)
        total = total + pltpu.roll(total, slices, 1)
        start = places["maps"] + layer * head_size
        packed[start : start + head_size, :slices] = total[:, :slices]
        start = places["qkv"] + layer * head_size
        packed[start : start + head_size, : 3 * head_size] = qkvacc[layer]

    def close_head():
        spread_dpred = _dotx(headacc[0], jnp.ones((LANES, LANES), f32), NN)
        gram = jnp.concatenate([headacc[1 + k] for k in range(width // LANES)], 1)
        gain_row, shift_row = vecs[tail : tail + 1], vecs[tail + 1 : tail + 2]
        head_grad = gram * gain_row + _wide(spread_dpred, width) * shift_row
        for index in range(width // LANES):
            at = slice(index * LANES, (index + 1) * LANES)
            start = places["io"] + index * places["io_stride"]
            packed[start + fin : start + fin + outc, :] = head_grad[:outc, at]
        put_vector(tail, jnp.sum(gram * head_rows, 0, keepdims=True))
        put_vector(
            tail + 1, jnp.sum(_wide(spread_dpred, width) * head_rows, 0, keepdims=True)
        )
        packed[places["loss"] : places["loss"] + 1, :] = jnp.broadcast_to(
            jnp.sum(jnp.sum(lossacc[...], 0, keepdims=True), 1, keepdims=True), (1, LANES)
        )

    def close_embed():
        for index in range(width // LANES):
            at = slice(index * LANES, (index + 1) * LANES)
            start = places["io"] + index * places["io_stride"]
            packed[start : start + fin, :] = embacc[:fin, at]

    stages = [
        sum_stages(
            packed,
            summed,
            entry,
            boxes[5 * index : 5 * index + 5],
            sum_send.at[index],
            sum_recv.at[index],
            members // 2,
        )
        for index, entry in enumerate(places["groups"])
    ]
    tail_set, lower_set, upper_set = stages

    for layer in range(layers - 1, -1, -1):
        accf[...] = jnp.zeros_like(accf)
        if layer:

            @pl.loop(0, steps)
            def _(step):
                at = window(step)
                _lockstep([back_rest(layer, grid, at) for grid in range(grids)])

            _lockstep([back_attend(layer, grid) for grid in range(grids)])

            @pl.loop(0, steps)
            def _(step):
                at = window(step)
                _lockstep([back_front(layer, grid, at) for grid in range(grids)])

            close_rest(layer)
            close_front(layer)
            upper_set[0]()
            close_head()
            continue
        for step in range(steps):
            at = slice(step * tile, (step + 1) * tile)
            _lockstep(
                [back_rest(layer, grid, at) for grid in range(grids)],
                [[stages[s][n] for s, n in spot] for spot in REST_PLAN[step]],
            )
        close_rest(layer)
        lower_set[0]()
        _lockstep(
            [back_attend(layer, grid) for grid in range(grids)],
            [[stages[s][n] for s, n in spot] for spot in ATTEND_PLAN],
        )
        for step in range(steps):
            at = slice(step * tile, (step + 1) * tile)
            _lockstep(
                [back_front(layer, grid, at) for grid in range(grids)],
                [[stages[s][n] for s, n in spot] for spot in FRONT_PLAN[step]],
            )
        close_front(layer)
        close_embed()
    tail_set[0]()
    for set_index, number in END_PLAN:
        stages[set_index][number]()

    squares[...] = jnp.zeros_like(squares)

    @pl.loop(0, places["rows"] // 256)
    def _(step):
        block = summed[pl.ds(pl.multiple_of(step * 256, 256), 256), :]
        row = lax.broadcasted_iota(jnp.int32, block.shape, 0) + step * 256
        block = jnp.where(row == places["loss"], 0.0, block)
        squares[...] += jnp.sum((block * block).reshape(32, 8, LANES), 0)


def _round_up(value, unit):
    return (value + unit - 1) // unit * unit


def packed_places(layers, width, io_rows, vec_rows, head_size):
    halves = width // LANES
    places = {"io_stride": _round_up(io_rows, 8), "vecs_stride": _round_up(vec_rows, 8)}
    row = 0
    for name, rows in (
        ("io", halves * places["io_stride"]),
        ("vecs", halves * places["vecs_stride"]),
        ("maps", layers * head_size),
        ("qkv", layers * head_size),
        ("sharp", _round_up(layers, 8)),
        ("loss", 8),
    ):
        places[name] = row
        row += rows
    places["mats"] = _round_up(row, 256)
    each = halves * width
    first = places["mats"] + 2 * each
    groups = [(0, first), (first, 3 * each)]
    for layer in range(1, layers):
        groups.append((places["mats"] + layer * 5 * each, 5 * each))
    places["groups"] = groups
    places["rows"] = places["mats"] + layers * 5 * each
    return places


def group_parts(rows):
    half = rows // 2
    a_rows = (half * 2 // 3 + 64) // 128 * 128
    return half, a_rows, half - a_rows


def sum_stages(packed, out, span, boxes, send_sems, recv_sems, floors):
    first, rows = span
    half, a_rows, b_rows = group_parts(rows)
    core_in, a_one, a_two, b_one, b_two = boxes
    a_four, b_four, a_all, b_all = a_rows // 4, b_rows // 4, a_rows // 16, b_rows // 16
    point, group = lax.axis_index("pts"), lax.axis_index("grp")
    y, z = lax.rem(point, 2), lax.div(point, 2)
    core, x = lax.rem(group, 2), lax.div(group, 2)
    plane = x + 2 * y
    base = first + core * half
    hops = (1, 2, 3)

    def plane_peer(hop):
        other_x, other_y = lax.rem(x + hop % 2, 2), lax.rem(y + hop // 2, 2)
        return (z * 2 + other_y, other_x * 2 + core), other_x + 2 * other_y

    def line_peer(hop):
        other = lax.rem(z + hop, floors)
        return (other * 2 + y, group), other

    partner = (point, x * 2 + (1 - core))

    def rows_at(start, count):
        return pl.ds(pl.multiple_of(start, 8), count)

    def send(number, source, target, device):
        return pltpu.make_async_remote_copy(
            src_ref=source,
            dst_ref=target,
            send_sem=send_sems.at[number],
            recv_sem=recv_sems.at[number],
            device_id=device,
            device_id_type=MESH,
        )

    def place(start, count):
        return packed.at[rows_at(start, count)]

    def cross():
        return send(0, place(first + (1 - core) * half, half), core_in, partner)

    def a1(hop):
        device, spot = plane_peer(hop)
        return send(hop, place(base + spot * a_four, a_four), a_one.at[hop - 1], device)

    def b1(hop):
        device, spot = line_peer(hop)
        source = place(base + a_rows + spot * b_four, b_four)
        return send(3 + hop, source, b_one.at[hop - 1], device)

    a_part = rows_at(base + plane * a_four, a_four)
    b_part = rows_at(base + a_rows + z * b_four, b_four)
    a_piece = rows_at(base + plane * a_four + z * a_all, a_all)
    b_piece = rows_at(base + a_rows + z * b_four + plane * b_all, b_all)

    def a2(hop):
        device, spot = line_peer(hop)
        source = place(base + plane * a_four + spot * a_all, a_all)
        return send(6 + hop, source, a_two.at[hop - 1], device)

    def b2(hop):
        device, spot = plane_peer(hop)
        source = place(base + a_rows + z * b_four + spot * b_all, b_all)
        return send(9 + hop, source, b_two.at[hop - 1], device)

    def a3(hop):
        return send(12 + hop, out.at[a_piece], out.at[a_piece], line_peer(hop)[0])

    def b3(hop):
        return send(15 + hop, out.at[b_piece], out.at[b_piece], plane_peer(hop)[0])

    def a4(hop):
        return send(18 + hop, out.at[a_part], out.at[a_part], plane_peer(hop)[0])

    def b4(hop):
        return send(21 + hop, out.at[b_part], out.at[b_part], line_peer(hop)[0])

    def last():
        own = out.at[rows_at(base, half)]
        return send(25, own, own, partner)

    def arrive(make):
        for hop in hops:
            make(hop).wait_recv()

    def depart(make):
        for hop in hops:
            make(hop).start()

    def stage_cross():
        cross().start()

    def stage_first():
        cross().wait_recv()
        own = rows_at(base, half)
        packed[own, :] = packed[own, :] + core_in[...]
        depart(a1)
        depart(b1)

    def stage_second():
        arrive(a1)
        packed[a_part, :] = packed[a_part, :] + a_one[0] + a_one[1] + a_one[2]
        depart(a2)
        arrive(b1)
        packed[b_part, :] = packed[b_part, :] + b_one[0] + b_one[1] + b_one[2]
        depart(b2)

    def stage_third():
        arrive(a2)
        out[a_piece, :] = packed[a_piece, :] + a_two[0] + a_two[1] + a_two[2]
        depart(a3)
        arrive(b2)
        out[b_piece, :] = packed[b_piece, :] + b_two[0] + b_two[1] + b_two[2]
        depart(b3)

    def stage_fourth():
        arrive(a3)
        depart(a4)
        arrive(b3)
        depart(b4)

    def stage_fifth():
        arrive(a4)
        arrive(b4)
        last().start()

    def stage_end():
        last().wait_recv()
        cross().wait_send()
        last().wait_send()
        for make in (a1, b1, a2, b2, a3, b3, a4, b4):
            for hop in hops:
                make(hop).wait_send()

    return (
        stage_cross,
        stage_first,
        stage_second,
        stage_third,
        stage_fourth,
        stage_fifth,
        stage_end,
    )


def update_kernel(dims, *refs):
    layers, width, places = dims
    halves = width // LANES
    bigs, small, squares = refs[:halves], refs[halves], refs[halves + 1]
    inputs, outputs = refs[halves + 2 : halves + 20], refs[halves + 20 :]
    loss_out, norm_out = outputs[:2]
    weights, means, seconds = inputs[:6], inputs[6:12], inputs[12:]
    total = jnp.sum(jnp.sum(squares[...], 0, keepdims=True), 1, keepdims=True)
    norm = jnp.sqrt(total)
    factor = jnp.minimum(1.0, clip_limit / norm)

    def apply(index, grad):
        weight, mean, second = weights[index], means[index], seconds[index]
        first_new, second_new, weight_new = adamw_update(
            weight[...], grad * factor, mean[...], second[...]
        )
        outputs[2 + 3 * index][...] = first_new
        outputs[3 + 3 * index][...] = second_new
        outputs[4 + 3 * index][...] = weight_new

    grad = jnp.concatenate([big[...] for big in bigs], 1)
    apply(1, grad[None, None])

    @pl.when(pl.program_id(0) == 0)
    def _():
        def rows(name, start, count):
            first = places[name] + start
            return small[first : first + count, :]

        loss_out[...] = rows("loss", 0, 1)[:, :1]
        norm_out[...] = norm
        for index, name in ((0, "io"), (5, "vecs")):
            stride, count = places[name + "_stride"], weights[index].shape[0]
            apply(
                index,
                jnp.concatenate([rows(name, k * stride, count) for k in range(halves)], 1),
            )
        for index, name in ((2, "maps"), (3, "qkv")):
            _, count, lanes = weights[index].shape
            apply(
                index,
                jnp.stack([rows(name, k * count, count)[:, :lanes] for k in range(layers)]),
            )
        count, lanes = weights[4].shape
        apply(4, rows("sharp", 0, count)[:, :lanes])


def update_all(summed, squares, network_state, running_means, running_squares, places):
    layers, slots, width, _ = network_state[1].shape
    halves = width // LANES
    skip = places["mats"] // width

    def half_spec(index):
        return pl.BlockSpec((width, LANES), lambda i: (skip + i * halves + index, 0))

    def whole(entry):
        return pl.BlockSpec(entry.shape, lambda i: (0,) * entry.ndim)

    def spec(index, entry):
        if index == 1:
            return pl.BlockSpec((1, 1, width, width), lambda i: (i // slots, i % slots, 0, 0))
        return whole(entry)

    state_specs = [spec(index, entry) for index, entry in enumerate(network_state)]
    shapes = [jax.ShapeDtypeStruct((1, 1), f32)] * 2
    specs = [pl.BlockSpec((1, 1), lambda i: (0, 0))] * 2
    for index, entry in enumerate(network_state):
        shapes += [jax.ShapeDtypeStruct(entry.shape, f32)] * 3
        specs += [spec(index, entry)] * 3
    results = pl.pallas_call(
        functools.partial(update_kernel, (layers, width, places)),
        grid=(layers * slots,),
        out_shape=shapes,
        in_specs=[
            *[half_spec(index) for index in range(halves)],
            pl.BlockSpec((places["mats"], LANES), lambda i: (0, 0)),
            pl.BlockSpec((8, LANES), lambda i: (0, 0)),
        ]
        + state_specs * 3,
        out_specs=specs,
        compiler_params=pltpu.CompilerParams(vmem_limit_bytes=VMEM_BYTES),
    )(*[summed] * (halves + 1), squares, *network_state, *running_means, *running_squares)
    return (results[0].reshape(()), results[1].reshape(()), *results[2:])


def whole_grid_grads(network_state, coords, goals, bound, sizes, places, mesh_sizes):
    io_rows, mats, maps, qkv, sharp, vecs = network_state
    members, groups = mesh_sizes
    grids, own, _, own_points = coords.shape
    points = own_points * members
    layers, _, width, _ = mats.shape
    heads = sharp.shape[1]
    head_size, slices = maps.shape[1:]
    outc = io_rows.shape[0] - FIN
    tile = TILE
    half, span, group = heads // 2, heads // 2 * slices, heads // 2 * head_size
    dims = (grids, points, width, heads, head_size, slices, layers, FIN, outc, tile)
    dims = dims + (members, groups, places)

    def both(*shape):
        return [pltpu.VMEM(shape, bf16), pltpu.VMEM(shape, bf16)]

    def single(*shape):
        return [pltpu.VMEM(shape, f32)]

    kept = (layers, grids, width, points)
    box = (members, grids * 8 + 8, own_points)
    scratch = (
        single(places["rows"], LANES)
        + single(grids, width, points)
        + [pltpu.VMEM(kept, bf16)]
        + single(layers, grids, 1, points)
        + both(*kept)
        + both(*kept)
        + both(layers, grids, 2 * span, points)
        + both(*kept)
        + [pltpu.VMEM(kept, bf16)]
        + single(layers, grids, 1, points)
        + [pltpu.VMEM(kept, bf16)] * 2
        + both(layers, 5, width, width)
        + single(layers, 9, width, LANES)
        + both(layers, 2, span, group)
        + both(layers, 2, group, span)
        + single(grids, 2, group + 16, span)
        + single(grids, 2, group, span)
        + single(layers, grids, head_size, 2 * span)
        + single(layers, grids, 1, 2 * span)
        + single(layers, grids, 3 * head_size, 2 * span)
        + single(layers, grids, half, slices, 2 * slices)
        + both(layers, grids, 2, group, span)
        + both(grids, 2, group, span)
        + both(grids, 2, span, 2 * group)
        + single(grids, 2 * span, LANES)
        + single(layers, 5, width, LANES)
        + single(layers, 2, group, span)
        + single(1 + width // LANES, 8, LANES)
        + single(8, width)
        + single(8, LANES)
        + single(layers, head_size, 3 * head_size)
        + single(grids, 8, points)
        + single(*box)
        + single(members - 1, *box[1:])
        + single(groups, 8, own_points)
        + [pltpu.SemaphoreType.DMA((members - 1,))] * 2
        + [pltpu.SemaphoreType.DMA((groups - 1,))] * 2
        + [pltpu.SemaphoreType.DMA((len(places["groups"]), 26))] * 2
    )
    for _, rows in places["groups"]:
        half_rows, a_rows, b_rows = group_parts(rows)
        scratch += single(half_rows, LANES)
        for part_rows in (a_rows, b_rows):
            scratch += single(3, part_rows // 4, LANES) + single(3, part_rows // 16, LANES)
    vmem = pl.BlockSpec(memory_space=pltpu.VMEM)
    smem = pl.BlockSpec(memory_space=pltpu.SMEM)
    return pl.pallas_call(
        functools.partial(grids_kernel, dims),
        out_shape=[
            jax.ShapeDtypeStruct((places["rows"], LANES), f32),
            jax.ShapeDtypeStruct((8, LANES), f32),
        ],
        in_specs=[smem] * 2 + [vmem] * 8,
        out_specs=[vmem, vmem],
        scratch_shapes=scratch,
        compiler_params=pltpu.CompilerParams(
            collective_id=0, has_side_effects=True, vmem_limit_bytes=VMEM_BYTES
        ),
    )(sizes, sharp, coords, jnp.swapaxes(goals, 1, 2), bound, io_rows, mats, maps, qkv, vecs)


def body_grids(mesh_sizes, *arrays):
    network_state = arrays[4:10]
    io_rows, mats, maps, _, _, vecs = network_state
    places = packed_places(
        mats.shape[0], mats.shape[2], io_rows.shape[0], vecs.shape[0], maps.shape[1]
    )
    summed, squares = whole_grid_grads(network_state, *arrays[:4], places, mesh_sizes)
    return update_all(
        summed, squares, network_state, arrays[10:16], arrays[16:22], places
    )


def solution(mesh):
    in_specs = (
        P(None, "grp", None, "pts"),
        P(None, "grp", None, "pts"),
        P(None, "grp", "pts"),
        P(None, "grp"),
        P(),
        P(),
        P(),
        P(),
        P(),
        P(),
        P(),
        P(),
        P(),
        P(),
        P(),
        P(),
        P(),
        P(),
        P(),
        P(),
        P(),
        P(),
    )
    out_specs = (
        P(),
        P(),
        P(),
        P(),
        P(),
        P(),
        P(),
        P(),
        P(),
        P(),
        P(),
        P(),
        P(),
        P(),
        P(),
        P(),
        P(),
        P(),
        P(),
        P(),
    )
    members, groups = mesh.shape["pts"], mesh.shape["grp"]

    def body(*arrays):
        batches, own, _, own_points = arrays[0].shape
        fits = own == members and batches * own_points * members <= 2048
        if fits and own_points == LANES and (members, groups) == (8, 4) and arrays[5].shape[0] == 2:
            return body_grids((members, groups), *arrays)
        return body_points(*arrays)

    return jax.shard_map(body, mesh=mesh, in_specs=in_specs, out_specs=out_specs, check_vma=False)
```

```python
import functools
import math

import jax
import jax.numpy as jnp
from jax import lax
from jax.experimental import pallas as pl
from jax.experimental.pallas import tpu as pltpu
from jax.sharding import PartitionSpec as P

STEP = 10
LANES = 128
FIN = 2
TILE = 512
SLOT_ORDER = (1, 0, 2, 3, 4)
PLAN = {
    ("attend", 1, 0): {4: ((4, 1),)},
    ("front", 1, 0): {6: ((4, 2),)},
    ("front", 1, 1): {6: ((4, 3),)},
    ("rest", 0, 0): {8: ((3, 1),)},
    ("rest", 0, 1): {5: ((4, 4),)},
    ("attend", 0, 0): {2: ((3, 2),), 4: ((2, 1),)},
    ("feat", 0, 1): {3: ((4, 5),)},
    ("front", 0, 0): {2: ((1, 1),), 4: ((2, 2),), 6: ((3, 4), (4, 6))},
    ("front", 0, 1): {3: ((1, 2),), 6: ((2, 3),)},
}
AFTER_REST = {1: ((4, 0),), 0: ((2, 0),)}
AFTER_FEAT = {1: (), 0: ((1, 0), (3, 3))}
AFTER_FRONT = {
    1: ((3, 0),),
    0: ((0, 0), (3, 5), (1, 3), (0, 1), (2, 4), (3, 6), (0, 2), (1, 4), (0, 3), (2, 5), (1, 5), (0, 4), (2, 6), (1, 6), (0, 5), (0, 6)),
}
VMEM_BYTES = 65400 << 10
f32, bf16 = jnp.float32, jnp.bfloat16
MESH = pl.DeviceIdType.MESH
NN, NT, TN = ((1,), (0,)), ((1,), (1,)), ((0,), (0,))


exact_arithmetic = lax.Precision.HIGHEST
clip_limit = 0.02
learn_rate = 0.1
beta_one = 0.9
beta_two = 0.999
adam_epsilon = 1e-08
weight_decay = 0.01


def layer_norm(values, gain, shift):
    center = values - jnp.mean(values, -1, keepdims=True)
    spread_tokens = jnp.mean(center * center, -1, keepdims=True)
    return center * lax.rsqrt(spread_tokens + 1e-05) * gain + shift


def slice_attend(weighted_points, masses, triple_maps_rows):
    head_size = triple_maps_rows.shape[0]
    tokens = weighted_points / (masses[..., None] + 1e-05)
    joined = jnp.einsum("imd,de->ime", tokens, triple_maps_rows, precision=exact_arithmetic)
    queries = joined[..., :head_size]
    keys = joined[..., head_size : 2 * head_size]
    values = joined[..., 2 * head_size :]
    scores = jnp.einsum("imd,ind->imn", queries, keys, precision=exact_arithmetic) * head_size ** (
        -0.5
    )
    probs = jax.nn.softmax(scores, -1)
    return jnp.einsum("imn,ind->imd", probs, values, precision=exact_arithmetic)


def slice_front(weight_set, slicer, temper, vec_rows, stream, valid):
    grids_n, points_n, width = stream.shape
    heads = temper.shape[0]
    normed = layer_norm(stream, vec_rows[0], vec_rows[1])
    features = (
        jnp.einsum("gpc,ce->gpe", normed, weight_set[0], precision=exact_arithmetic) + vec_rows[2]
    )
    chip_placement_list = (
        jnp.einsum("gpc,ce->gpe", normed, weight_set[1], precision=exact_arithmetic) + vec_rows[3]
    )
    partition_scores = (
        jnp.einsum(
            "gphd,dm->gphm",
            chip_placement_list.reshape(grids_n, points_n, heads, -1),
            slicer,
            precision=exact_arithmetic,
        )
        / temper[:, None]
    )
    slice_weights = jax.nn.softmax(partition_scores, -1) * valid[:, :, None, None]
    return (slice_weights, features.reshape(grids_n, points_n, heads, -1))


def slice_rest(weight_set, vec_rows, stream, spread_tokens):
    stream = (
        stream
        + jnp.einsum("gpc,ce->gpe", spread_tokens, weight_set[2], precision=exact_arithmetic)
        + vec_rows[4]
    )
    inner = (
        jnp.einsum(
            "gpc,ce->gpe",
            layer_norm(stream, vec_rows[5], vec_rows[6]),
            weight_set[3],
            precision=exact_arithmetic,
        )
        + vec_rows[7]
    )
    hidden = jax.nn.gelu(inner, approximate=False)
    return (
        stream
        + jnp.einsum("gpc,ce->gpe", hidden, weight_set[4], precision=exact_arithmetic)
        + vec_rows[8]
    )


def slice_mix(weighted_points, masses, qkv):
    grids_n, heads, slices, head_size = weighted_points.shape
    items = grids_n * heads
    flat_weighted = weighted_points.reshape(items, slices, head_size)
    flat_masses = masses.reshape(items, slices)
    own_weighted, own_masses = (
        lax.psum_scatter(flat_weighted, "pts", scatter_dimension=0, tiled=True),
        lax.psum_scatter(flat_masses, "pts", scatter_dimension=0, tiled=True),
    )
    mixed_tokens = lax.all_gather(
        slice_attend(own_weighted, own_masses, qkv), "pts", axis=0, tiled=True
    )
    kept = (own_weighted, own_masses)
    return (mixed_tokens.reshape(weighted_points.shape), kept)


def slice_mix_back(grad_mixed, kept, qkv):
    grids_n, heads, slices, head_size = grad_mixed.shape
    flat = grad_mixed.reshape(grids_n * heads, slices, head_size)
    _, pullback = jax.vjp(slice_attend, kept[0], kept[1], qkv)
    own_grad = lax.psum_scatter(flat, "pts", scatter_dimension=0, tiled=True)
    grad_weighted, grad_masses, grad_qkv = pullback(own_grad)
    grad_weighted, grad_masses = (
        lax.all_gather(grad_weighted, "pts", axis=0, tiled=True),
        lax.all_gather(grad_masses, "pts", axis=0, tiled=True),
    )
    return (
        grad_weighted.reshape(grad_mixed.shape),
        grad_masses.reshape(grids_n, heads, slices),
        grad_qkv,
    )


def layer_forward(stream, layer_set, valid):
    weight_set, slicer, qkv, temper, vec_rows = layer_set
    slice_weights, features = slice_front(weight_set, slicer, temper, vec_rows, stream, valid)
    weighted_points = jnp.einsum(
        "gphm,gphd->ghmd", slice_weights, features, precision=exact_arithmetic
    )
    masses = jnp.sum(slice_weights, 1)
    mixed_tokens, kept = slice_mix(weighted_points, masses, qkv)
    spread_tokens = jnp.einsum(
        "gphm,ghmd->gphd", slice_weights, mixed_tokens, precision=exact_arithmetic
    ).reshape(stream.shape)
    return (slice_rest(weight_set, vec_rows, stream, spread_tokens), (stream, mixed_tokens, kept))


def layer_backward(grad_out, layer_set, saved, valid):
    weight_set, slicer, qkv, temper, vec_rows = layer_set
    stream, mixed_tokens, kept = saved
    (slice_weights, features), pull_front = jax.vjp(
        lambda w_set, s_set, t_set, v_set, s_in: slice_front(
            w_set, s_set, t_set, v_set, s_in, valid
        ),
        weight_set,
        slicer,
        temper,
        vec_rows,
        stream,
    )
    spread_tokens = jnp.einsum(
        "gphm,ghmd->gphd", slice_weights, mixed_tokens, precision=exact_arithmetic
    ).reshape(stream.shape)
    _, pull_rest = jax.vjp(slice_rest, weight_set, vec_rows, stream, spread_tokens)
    grad_set_rest, grad_vec_rest, grad_stream, grad_spread = pull_rest(grad_out)
    grad_spread = grad_spread.reshape(features.shape)
    grad_weights = jnp.einsum(
        "gphd,ghmd->gphm", grad_spread, mixed_tokens, precision=exact_arithmetic
    )
    grad_mixed = jnp.einsum(
        "gphm,gphd->ghmd", slice_weights, grad_spread, precision=exact_arithmetic
    )
    grad_weighted, grad_masses, grad_qkv = slice_mix_back(grad_mixed, kept, qkv)
    grad_weights = (
        grad_weights
        + jnp.einsum("ghmd,gphd->gphm", grad_weighted, features, precision=exact_arithmetic)
        + grad_masses[:, None]
    )
    grad_features = jnp.einsum(
        "gphm,ghmd->gphd", slice_weights, grad_weighted, precision=exact_arithmetic
    )
    grad_set_front, grad_slicer, grad_temper, grad_vec_front, grad_stream_front = pull_front(
        (grad_weights, grad_features)
    )
    grads = (
        grad_set_rest + grad_set_front,
        grad_slicer,
        grad_qkv,
        grad_temper,
        grad_vec_rest + grad_vec_front,
    )
    return (grad_stream + grad_stream_front, grads)


def head_loss(head_rows, tail_rows, stream, goals, on_surface, off_surface, inv_surf, inv_vol):
    final = layer_norm(stream, tail_rows[0], tail_rows[1])
    pred = jnp.einsum("oc,gpc->gop", head_rows, final, precision=exact_arithmetic)
    errors = (pred - goals) ** 2
    return inv_surf * jnp.sum(on_surface * errors[:, 0]) + inv_vol * jnp.sum(
        off_surface * (errors[:, 1] + errors[:, 2])
    )


def layer_params(network_state, block_number):
    (
        lifting_readout_rows,
        block_projections,
        partition_maps,
        triple_maps_rows,
        sharpness_factors,
        gain_bias_rows,
    ) = network_state
    return (
        block_projections[block_number],
        partition_maps[block_number],
        triple_maps_rows[block_number],
        sharpness_factors[block_number],
        gain_bias_rows[9 * block_number : 9 * block_number + 9],
    )


def one_batch(network_state, coords, goals, valid, on_surface, off_surface, inv_surf, inv_vol):
    (
        lifting_readout_rows,
        block_projections,
        partition_maps,
        triple_maps_rows,
        sharpness_factors,
        gain_bias_rows,
    ) = network_state
    fin = coords.shape[1]
    layers_n = block_projections.shape[0]
    stream = jnp.einsum(
        "gfp,fc->gpc", coords, lifting_readout_rows[:fin], precision=exact_arithmetic
    )
    saved = []
    for block_number in range(layers_n):
        stream, keep_set = layer_forward(stream, layer_params(network_state, block_number), valid)
        saved.append(keep_set)
    batch_loss, pull_head = jax.vjp(
        lambda h_rows, t_rows, s_in: head_loss(
            h_rows, t_rows, s_in, goals, on_surface, off_surface, inv_surf, inv_vol
        ),
        lifting_readout_rows[fin:],
        gain_bias_rows[9 * layers_n :],
        stream,
    )
    grad_head, grad_tail, grad_stream = pull_head(jnp.ones_like(batch_loss))
    layer_grads = [None] * layers_n
    for block_number in reversed(range(layers_n)):
        grad_stream, layer_grads[block_number] = layer_backward(
            grad_stream, layer_params(network_state, block_number), saved[block_number], valid
        )
    grad_embed = jnp.einsum("gfp,gpc->fc", coords, grad_stream, precision=exact_arithmetic)
    grads = (
        jnp.concatenate([grad_embed, grad_head], 0),
        jnp.stack([entry[0] for entry in layer_grads]),
        jnp.stack([entry[1] for entry in layer_grads]),
        jnp.stack([entry[2] for entry in layer_grads]),
        jnp.stack([entry[3] for entry in layer_grads]),
        jnp.concatenate([entry[4] for entry in layer_grads] + [grad_tail], 0),
    )
    return (batch_loss, grads)


def adamw_update(weight, grad, first, second):
    first_new = beta_one * first + (1.0 - beta_one) * grad
    second_new = beta_two * second + (1.0 - beta_two) * grad * grad
    first_hat = first_new / (1.0 - beta_one**STEP)
    second_hat = second_new / (1.0 - beta_two**STEP)
    weight_new = weight - learn_rate * (
        first_hat / (jnp.sqrt(second_hat) + adam_epsilon) + weight_decay * weight
    )
    return (first_new, second_new, weight_new)


def body_points(
    input_positions,
    flow_labels,
    airfoil_boundary,
    valid_sizes,
    lifting_readout_rows,
    block_projections,
    partition_maps,
    triple_maps_rows,
    sharpness_factors,
    gain_bias_rows,
    lifting_readout_mean,
    projection_running_mean,
    partition_map_mean,
    triple_maps_mean,
    sharpness_mean,
    gain_bias_mean,
    lifting_readout_square,
    projection_running_square,
    partition_map_square,
    triple_maps_square,
    sharpness_square,
    gain_bias_square,
):
    batches = input_positions.shape[0]
    points_n = input_positions.shape[3]
    slots = lax.axis_index("pts") * points_n + jnp.arange(points_n, dtype=jnp.int32)
    valid = (slots[None, None, :] < valid_sizes[:, :, None]).astype(jnp.float32)
    on_surface = valid * airfoil_boundary.astype(jnp.float32)
    off_surface = valid - on_surface
    count_surf, count_vol = lax.psum((jnp.sum(on_surface), jnp.sum(off_surface)), ("pts", "grp"))
    inv_surf = 1.0 / jnp.maximum(count_surf, 1.0)
    inv_vol = 1.0 / jnp.maximum(count_vol, 1.0)
    network_state = (
        lifting_readout_rows,
        block_projections,
        partition_maps,
        triple_maps_rows,
        sharpness_factors,
        gain_bias_rows,
    )
    loss_value = jnp.zeros((), jnp.float32)
    grads = tuple((jnp.zeros_like(entry) for entry in network_state))
    for batch in range(batches):
        batch_loss, batch_set = one_batch(
            network_state,
            input_positions[batch],
            flow_labels[batch],
            valid[batch],
            on_surface[batch],
            off_surface[batch],
            inv_surf,
            inv_vol,
        )
        loss_value = loss_value + batch_loss
        grads = tuple((total + entry for total, entry in zip(grads, batch_set)))
    running_means = (
        lifting_readout_mean,
        projection_running_mean,
        partition_map_mean,
        triple_maps_mean,
        sharpness_mean,
        gain_bias_mean,
    )
    running_squares = (
        lifting_readout_square,
        projection_running_square,
        partition_map_square,
        triple_maps_square,
        sharpness_square,
        gain_bias_square,
    )
    return finish(loss_value, grads, network_state, running_means, running_squares)


def finish(loss_value, grads, network_state, running_means, running_squares):
    summed = lax.psum((loss_value,) + grads, ("pts", "grp"))
    loss_value = summed[0]
    grads = summed[1:]
    grad_norm = jnp.sqrt(sum((jnp.sum(entry * entry) for entry in grads)))
    factor = jnp.minimum(1.0, clip_limit / grad_norm)
    results = []
    for weight, grad, first, second in zip(network_state, grads, running_means, running_squares):
        results.extend(adamw_update(weight, grad * factor, first, second))
    return tuple([loss_value, grad_norm] + results)


def _split(x):
    high = x.astype(bf16)
    return high, (x - high.astype(f32)).astype(bf16)


def _dot(a, b, dims, precision=None):
    return lax.dot_general(a, b, (dims, ((), ())), precision=precision, preferred_element_type=f32)


def _dot3(a, b, dims):
    left = jnp.concatenate([a[0], a[0], a[1]], dims[0][0])
    right = jnp.concatenate([b[0], b[1], b[0]], dims[1][0])
    return _dot(left, right, dims)


def _doth(a, b, dims):
    return _dot3(_split(a), _split(b), dims)


def _row_sums(value):
    high, low = _split(value)
    ones = jnp.ones((8, 2 * value.shape[1]), bf16)
    return _dot(ones, jnp.concatenate([high, low], 1), NT)[:1]


def _dotx(a, b, dims):
    return _dot(a, b, dims, lax.Precision.HIGHEST)


def _wide(col, lanes):
    return jnp.concatenate([col] * (lanes // LANES), 1) if lanes > LANES else col


def _fold(x):
    total = x[:, :LANES]
    for start in range(LANES, x.shape[1], LANES):
        total = total + x[:, start : start + LANES]
    return total


def _lockstep(makers, hooks=()):
    turn = 0
    running = list(makers)
    while running:
        for stage in hooks[turn] if turn < len(hooks) else ():
            stage()
        turn += 1
        alive = []
        for entry in running:
            try:
                next(entry)
                alive.append(entry)
            except StopIteration:
                pass
        running = alive


def _diag_heads(full, depth, slices):
    heads = full.shape[0] // depth
    lane = lax.broadcasted_iota(jnp.int32, (depth, full.shape[1]), 1)
    picked = full[:depth]
    for head in range(1, heads):
        picked = jnp.where(lane >= head * slices, full[head * depth : (head + 1) * depth], picked)
    return picked


def _block_heads(flat, heads, slices):
    lane = lax.broadcasted_iota(jnp.int32, flat.shape, 1)
    return jnp.concatenate(
        [
            jnp.where((lane >= head * slices) & (lane < (head + 1) * slices), flat, 0.0)
            for head in range(heads)
        ],
        0,
    )


def _norm(x):
    inv_width = 1.0 / x.shape[0]
    center = x - jnp.sum(x, 0, keepdims=True) * inv_width
    rstd = lax.rsqrt(jnp.sum(center * center, 0, keepdims=True) * inv_width + 1e-05)
    return center * rstd, rstd


def _norm_back(grad, xhat, rstd):
    inv_width = 1.0 / grad.shape[0]
    mean_grad = jnp.sum(grad, 0, keepdims=True) * inv_width
    mean_proj = jnp.sum(grad * xhat, 0, keepdims=True) * inv_width
    return (grad - mean_grad - xhat * mean_proj) * rstd


def grids_kernel(dims, *refs):
    (
        grids,
        points,
        width,
        heads,
        head_size,
        slices,
        layers,
        fin,
        outc,
        tile,
        members,
        groups,
        places,
    ) = dims
    (
        sizes_ref,
        sharp_ref,
        coords_ref,
        goals_ref,
        bound_ref,
        io_ref,
        mats_ref,
        maps_ref,
        qkv_ref,
        vecs_ref,
        summed,
        squares,
        packed,
        stream,
        xh1h,
        rs1,
        feath,
        featl,
        placeh,
        placel,
        wgth,
        wgtl,
        sprh,
        sprl,
        xh2h,
        rs2,
        hidh,
        gslope,
        upmh,
        upml,
        cols,
        bdmh,
        bdml,
        bdth,
        bdtl,
        accw,
        accf,
        tok,
        rmass,
        qkvs,
        probs,
        mbdh,
        mbdl,
        dbdh,
        dbdl,
        cmbh,
        cmbl,
        dmcol,
        vacc,
        gmacc,
        headacc,
        embacc,
        lossacc,
        qkvacc,
        points_ref,
        outbox,
        inbox,
        tally,
        send_sems,
        recv_sems,
        tally_send,
        tally_recv,
        sum_send,
        sum_recv,
    ) = refs[: -5 * len(places["groups"])]
    boxes = refs[-5 * len(places["groups"]) :]
    half = heads // 2
    span = half * slices
    group = half * head_size
    pairs = heads // 2
    all_slices = heads * slices
    steps = points // tile
    scale = head_size ** (-0.5)
    me, mine = lax.axis_index("pts"), lax.axis_index("grp")
    own_points = points // members

    def peer_points(hop):
        return lax.rem(me + hop, members)

    def peer_group(hop):
        return lax.rem(mine + hop, groups)

    barrier = pltpu.get_barrier_semaphore()
    for hop in range(1, members):
        pl.semaphore_signal(
            barrier, inc=1, device_id=(peer_points(hop), mine), device_id_type=MESH
        )
    for hop in range(1, groups):
        pl.semaphore_signal(
            barrier, inc=1, device_id=(me, peer_group(hop)), device_id_type=MESH
        )

    def same_plane(hop):
        other_y = lax.rem(lax.rem(me, 2) + hop // 2, 2)
        other_x = lax.rem(lax.div(mine, 2) + hop % 2, 2)
        return (lax.div(me, 2) * 2 + other_y, other_x * 2 + lax.rem(mine, 2))

    pl.semaphore_signal(barrier, inc=1, device_id=same_plane(3), device_id_type=MESH)

    slots = lax.broadcasted_iota(jnp.int32, (1, own_points), 1) + me * own_points
    surf_total = jnp.zeros((1, own_points), f32)
    vol_total = jnp.zeros((1, own_points), f32)
    blank = jnp.zeros((8 - fin - outc - 1, own_points), f32)
    for dest in range(members):
        for batch in range(grids):
            surf = bound_ref[batch, dest : dest + 1, :].astype(f32)
            goals = [goals_ref[batch, field, dest : dest + 1, :] for field in range(outc)]
            outbox[dest, batch * 8 : batch * 8 + 8, :] = jnp.concatenate(
                [coords_ref[batch, dest], *goals, surf, blank], 0
            )
            valid = jnp.where(slots < sizes_ref[batch, dest], 1.0, 0.0)
            surf_total = surf_total + valid * surf
            vol_total = vol_total + (valid - valid * surf)
    totals = jnp.concatenate(
        [surf_total, vol_total, jnp.zeros((6, own_points), f32)], 0
    )
    for dest in range(members):
        outbox[dest, grids * 8 :, :] = totals

    def piece(hop):
        other = peer_points(hop)
        return pltpu.make_async_remote_copy(
            src_ref=outbox.at[other],
            dst_ref=inbox.at[hop - 1],
            send_sem=send_sems.at[hop - 1],
            recv_sem=recv_sems.at[hop - 1],
            device_id=(other, mine),
            device_id_type=MESH,
        )

    def share(hop):
        return pltpu.make_async_remote_copy(
            src_ref=tally.at[0],
            dst_ref=tally.at[hop],
            send_sem=tally_send.at[hop - 1],
            recv_sem=tally_recv.at[hop - 1],
            device_id=(me, peer_group(hop)),
            device_id_type=MESH,
        )

    def greet():
        pl.semaphore_wait(barrier, members + groups - 1)
        for hop in range(1, members):
            piece(hop).start()


    def matrix_rows(layer, slot, half_index):
        spot = layer * 5 + SLOT_ORDER[slot]
        start = places["mats"] + (spot * (width // LANES) + half_index) * width
        return pl.ds(pl.multiple_of(start, width), width)

    def add_matrix(layer, slot, value):
        for index in range(width // LANES):
            packed[matrix_rows(layer, slot, index), :] += value[
                :, index * LANES : (index + 1) * LANES
            ]

    def read_matrix(layer, slot):
        return jnp.concatenate(
            [packed[matrix_rows(layer, slot, index), :] for index in range(width // LANES)], 1
        )

    def split_to(high_ref, low_ref, index, value):
        high, low = _split(value)
        high_ref[index] = high
        low_ref[index] = low
        return high, low

    vecs = vecs_ref[...]
    spare = jnp.zeros((LANES - vecs.shape[0], width), f32)
    standing = jnp.concatenate([vecs, spare], 0).T

    def column(row):
        return jnp.broadcast_to(standing[:, row : row + 1], (width, LANES))

    for layer in range(layers):
        if layer == layers - 1:
            greet()
        base = 9 * layer
        gain_a, shift_a = column(base), column(base + 1)
        gain_b, shift_b = column(base + 5), column(base + 6)
        cols[layer, 0] = gain_a
        cols[layer, 1] = shift_a
        cols[layer, 2] = gain_b
        cols[layer, 3] = shift_b
        for slot in range(5):
            flipped = mats_ref[layer, slot].T
            bias = column(base + (2, 3, 4, 7, 8)[slot])
            if slot in (0, 1, 3):
                gain, shift, row = (gain_b, shift_b, 5) if slot == 3 else (gain_a, shift_a, 0)
                bias = bias + _doth(flipped, shift, NN)
                flipped = flipped * vecs[base + row : base + row + 1]
            cols[layer, 4 + slot] = bias
            split_to(upmh, upml, (layer, slot), flipped)
        tiled = jnp.concatenate([maps_ref[layer]] * half, 1)
        for part in range(2):
            lane = lax.broadcasted_iota(jnp.int32, (1, span), 1)
            sharp = jnp.full((1, span), 0.0, f32) + sharp_ref[layer, part * half]
            for head in range(1, half):
                sharp = jnp.where(lane >= head * slices, sharp_ref[layer, part * half + head], sharp)
            block = _block_heads(tiled / sharp, half, slices)
            split_to(bdth, bdtl, (layer, part), block)
            split_to(bdmh, bdml, (layer, part), block.T)

    vacc[...] = jnp.zeros_like(vacc)
    gmacc[...] = jnp.zeros_like(gmacc)
    headacc[...] = jnp.zeros_like(headacc)
    embacc[...] = jnp.zeros_like(embacc)
    lossacc[...] = jnp.zeros_like(lossacc)
    packed[...] = jnp.zeros_like(packed)
    qkvacc[...] = jnp.zeros_like(qkvacc)

    io_all = io_ref[...]
    rising = jnp.concatenate([io_all, jnp.zeros((LANES - io_all.shape[0], width), f32)], 0).T
    lift = [jnp.broadcast_to(rising[:, row : row + 1], (width, LANES)) for row in range(fin)]

    def window(step):
        return pl.ds(pl.multiple_of(step * tile, tile), tile)

    def pair_of(high_ref, low_ref, index):
        return high_ref[index], low_ref[index]

    def settle(source, block):
        at = pl.ds(pl.multiple_of(source * own_points, own_points), own_points)
        for grid in range(grids):
            points_ref[grid, :, at] = block[grid * 8 : grid * 8 + 8]
        return block[grids * 8 :]

    held = settle(me, outbox[me])
    for hop in range(1, members):
        piece(hop).wait()
        held = held + settle(lax.rem(me + members - hop, members), inbox[hop - 1])
    tally[0] = held
    for hop in range(1, groups):
        share(hop).start()

    @pl.loop(0, steps)
    def _(step):
        at = window(step)
        for grid in range(grids):
            x = jnp.zeros((width, tile), f32)
            for row in range(fin):
                x = x + _wide(lift[row], tile) * points_ref[grid, row : row + 1, at]
            stream[grid, :, at] = x

    def front(layer, grid, at, step):
        xhat, rstd = _norm(stream[grid, :, at])
        xhat = _split(xhat)
        xh1h[layer, grid, :, at] = xhat[0]
        rs1[layer, grid, :, at] = rstd
        yield
        feat = _dot3(pair_of(upmh, upml, (layer, 0)), xhat, NN)
        place = _dot3(pair_of(upmh, upml, (layer, 1)), xhat, NN)
        yield
        feat = feat + _wide(cols[layer, 4], tile)
        place = place + _wide(cols[layer, 5], tile)
        feat = split_to(feath, featl, (layer, grid, slice(None), at), feat)
        place = split_to(placeh, placel, (layer, grid, slice(None), at), place)
        slots = lax.broadcasted_iota(jnp.int32, (1, tile), 1) + step * tile
        valid = jnp.where(slots < sizes_ref[grid, me], 1.0, 0.0)
        yield
        rows = [slice(part * group, (part + 1) * group) for part in range(2)]
        scores = [
            _dot3(
                pair_of(bdmh, bdml, (layer, part)), (place[0][rows[part]], place[1][rows[part]]), NN
            )
            for part in range(2)
        ]
        yield
        weights = []
        for part in range(2):
            pieces = []
            for head in range(half):
                score = scores[part][head * slices : (head + 1) * slices]
                expo = jnp.exp(score - jnp.max(score, 0, keepdims=True))
                weight = expo * (valid / jnp.sum(expo, 0, keepdims=True))
                start = part * span + head * slices
                wrows = slice(start, start + slices)
                pieces.append(split_to(wgth, wgtl, (layer, grid, wrows, at), weight))
            weights.append(tuple(jnp.concatenate(list(side), 0) for side in zip(*pieces)))
        yield
        sums = []
        for part in range(2):
            weight = weights[part]
            lead = jnp.concatenate([feat[0][rows[part]], jnp.ones((16, tile), bf16)], 0)
            sums.append(
                (
                    _dot(
                        jnp.concatenate([lead, lead], 1), jnp.concatenate(weight, 1), NT
                    ),
                    _dot(feat[1][rows[part]], weight[0], NT),
                )
            )
        yield
        for part in range(2):
            accw[grid, part] += sums[part][0]
            accf[grid, part] += sums[part][1]
        yield

    def attend(layer, grid):
        parts, masses = [], []
        for part in range(2):
            total = accw[grid, part]
            parts.append(_diag_heads(total[:group] + accf[grid, part], head_size, slices))
            masses.append(total[group : group + 1])
        rate = 1.0 / (jnp.concatenate(masses, 1) + 1e-05)
        tokens = jnp.concatenate(parts, 1) * rate
        tok[layer, grid] = tokens
        rmass[layer, grid] = rate
        yield
        joined = _doth(qkv_ref[layer], tokens, TN)
        qkvs[layer, grid] = joined
        yield
        lane = lax.broadcasted_iota(jnp.int32, (slices, 2 * slices), 1)
        mixed = []
        for pair in range(pairs):
            at = slice(pair * 2 * slices, (pair + 1) * 2 * slices)
            query = joined[:head_size, at]
            key = joined[head_size : 2 * head_size, at]
            value = joined[2 * head_size :, at]
            full = _doth(key, query, TN)
            scores = jnp.where(lane < slices, full[:slices], full[slices:]) * scale
            expo = jnp.exp(scores - jnp.max(scores, 0, keepdims=True))
            prob = expo / jnp.sum(expo, 0, keepdims=True)
            probs[layer, grid, pair] = prob
            mixed.append(_doth(value, _block_heads(prob, 2, slices), NN))
        for part in range(2):
            flat = jnp.concatenate(mixed[part * (pairs // 2) : (part + 1) * (pairs // 2)], 1)
            block = _block_heads(flat, half, slices)
            split_to(mbdh, mbdl, (layer, grid, part), block)
        yield

    def rest(layer, grid, at):
        before = stream[grid, :, at]
        yield
        spread = []
        for part in range(2):
            wrows = slice(part * span, (part + 1) * span)
            weight = pair_of(wgth, wgtl, (layer, grid, wrows, at))
            spread.append(_dot3(pair_of(mbdh, mbdl, (layer, grid, part)), weight, NN))
        yield
        spread = split_to(
            sprh, sprl, (layer, grid, slice(None), at), jnp.concatenate(spread, 0)
        )
        yield
        moved = _dot3(pair_of(upmh, upml, (layer, 2)), spread, NN)
        yield
        x = before + moved + _wide(cols[layer, 6], tile)
        xhat, rstd = _norm(x)
        xhat = _split(xhat)
        xh2h[layer, grid, :, at] = xhat[0]
        rs2[layer, grid, :, at] = rstd
        yield
        inner = _dot3(pair_of(upmh, upml, (layer, 3)), xhat, NN)
        yield
        inner = inner + _wide(cols[layer, 7], tile)
        cdf = 0.5 + 0.5 * lax.erf(inner * (0.5**0.5))
        slope = cdf + inner * jnp.exp(-0.5 * inner * inner) * ((2.0 * math.pi) ** -0.5)
        gslope[layer, grid, :, at] = slope.astype(bf16)
        hidden = _split(inner * cdf)
        hidh[layer, grid, :, at] = hidden[0]
        yield
        moved = _dot3(pair_of(upmh, upml, (layer, 4)), hidden, NN)
        yield
        stream[grid, :, at] = x + moved + _wide(cols[layer, 8], tile)
        yield

    @pl.loop(0, layers)
    def _(layer):
        accw[...] = jnp.zeros_like(accw)
        accf[...] = jnp.zeros_like(accf)

        @pl.loop(0, steps)
        def _(step):
            at = window(step)
            _lockstep([front(layer, grid, at, step) for grid in range(grids)])

        _lockstep([attend(layer, grid) for grid in range(grids)])

        @pl.loop(0, steps)
        def _(step):
            at = window(step)
            _lockstep([rest(layer, grid, at) for grid in range(grids)])

    tail = 9 * layers
    head_rows = jnp.concatenate(
        [io_ref[fin:, :], jnp.zeros((8 - outc, width), f32)], 0
    )
    head_gain = head_rows * vecs[tail : tail + 1]
    head_pair = _split(head_gain)
    head_bias = _dotx(head_rows, column(tail + 1), NN)
    counted = tally[0]
    for hop in range(1, groups):
        share(hop).wait()
        counted = counted + tally[hop]
    counted = jnp.broadcast_to(jnp.sum(counted, 1, keepdims=True), counted.shape)
    counted = 1.0 / jnp.maximum(counted, 1.0)
    inv_surf, inv_vol = _wide(counted[:1], tile), _wide(counted[1:2], tile)

    def crown(grid, at, step):
        xhat, rstd = _norm(stream[grid, :, at])
        halves = _split(xhat)
        pred = _dot3(head_pair, halves, NN) + _wide(head_bias, tile)
        slots = lax.broadcasted_iota(jnp.int32, (1, tile), 1) + step * tile
        valid = jnp.where(slots < sizes_ref[grid, me], 1.0, 0.0)
        surf = valid * points_ref[grid, fin + outc : fin + outc + 1, at]
        vol = (valid - surf) * inv_vol
        surf = surf * inv_surf
        row = lax.broadcasted_iota(jnp.int32, (8, tile), 0)
        factor = jnp.where(row == 0, surf, jnp.where(row < outc, vol, 0.0))
        goals = jnp.concatenate(
            [points_ref[grid, fin : fin + outc, at], jnp.zeros((8 - outc, tile), f32)], 0
        )
        error = pred - goals
        scaled = factor * error
        lossacc[...] += _fold(scaled * error)
        dpred = scaled + scaled
        headacc[0] += _fold(dpred)
        dhalves = _split(dpred)
        headacc_rows = _dot3(dhalves, halves, NT)
        for start in range(0, width, LANES):
            headacc[1 + start // LANES] += headacc_rows[:, start : start + LANES]
        yield
        grad = _dot3(head_pair, dhalves, TN)
        stream[grid, :, at] = _norm_back(grad, xhat, rstd)
        yield

    @pl.loop(0, steps)
    def _(step):
        at = window(step)
        _lockstep([crown(grid, at, step) for grid in range(grids)])

    for layer in range(layers):
        for slot in range(5):
            mat = mats_ref[layer, slot]
            if slot in (0, 1, 3):
                mat = mat * _wide(cols[layer, 2 if slot == 3 else 0], width)
            split_to(upmh, upml, (layer, slot), mat)

    def back_rest(layer, grid, at):
        grad = stream[grid, :, at]
        vacc[layer, 4] += _fold(grad)
        pieces = grad.astype(bf16)
        yield
        dhid = _dot(upmh[layer, 4], pieces, NN)
        gram = _dot(hidh[layer, grid, :, at], pieces, NT)
        yield
        add_matrix(layer, 4, gram)
        dinner = dhid * gslope[layer, grid, :, at].astype(f32)
        vacc[layer, 3] += _fold(dinner)
        dinner = dinner.astype(bf16)
        xhat = xh2h[layer, grid, :, at]
        yield
        dxhat = _dot(upmh[layer, 3], dinner, NN)
        gram = _dot(xhat, dinner, NT)
        yield
        add_matrix(layer, 3, gram)
        grad = grad + _norm_back(dxhat, xhat.astype(f32), rs2[layer, grid, :, at])
        stream[grid, :, at] = grad
        vacc[layer, 2] += _fold(grad)
        pieces = _split(grad)
        yield
        dspread = _dot3(pair_of(upmh, upml, (layer, 2)), pieces, NN)
        gram = _dot3(pair_of(sprh, sprl, (layer, grid, slice(None), at)), pieces, NT)
        yield
        add_matrix(layer, 2, gram)
        dspread = split_to(sprh, sprl, (layer, grid, slice(None), at), dspread)
        yield
        sums = []
        for part in range(2):
            rows = slice(part * group, (part + 1) * group)
            wrows = slice(part * span, (part + 1) * span)
            weight = pair_of(wgth, wgtl, (layer, grid, wrows, at))
            sums.append(_dot3((dspread[0][rows], dspread[1][rows]), weight, NT))
        yield
        for part in range(2):
            accf[grid, part] += sums[part]
        yield

    def back_attend(layer, grid):
        joined = qkvs[layer, grid]
        tokens = tok[layer, grid]
        rate = rmass[layer, grid]
        lane = lax.broadcasted_iota(jnp.int32, (slices, 2 * slices), 1)
        dmixed = jnp.concatenate(
            [_diag_heads(accf[grid, part], head_size, slices) for part in range(2)], 1
        )
        yield
        dqs, dks, dvs = [], [], []
        for pair in range(pairs):
            at = slice(pair * 2 * slices, (pair + 1) * 2 * slices)
            query = joined[:head_size, at]
            key = joined[head_size : 2 * head_size, at]
            value = joined[2 * head_size :, at]
            prob = probs[layer, grid, pair]
            dmix = dmixed[:, at]
            full = _doth(value, dmix, TN)
            dprob = jnp.where(lane < slices, full[:slices], full[slices:])
            dscore = (
                prob * (dprob - jnp.sum(prob * dprob, 0, keepdims=True)) * scale
            )
            dblock = _block_heads(dscore, 2, slices)
            dvs.append(_doth(dmix, _block_heads(prob, 2, slices), NT))
            dqs.append(_doth(key, dblock, NN))
            dks.append(_doth(query, dblock, NT))
        dqkv = jnp.concatenate(
            [jnp.concatenate(part, 1) for part in (dqs, dks, dvs)], 0
        )
        yield
        dtok = _doth(qkv_ref[layer], dqkv, NN)
        qkvacc[layer] += _doth(tokens, dqkv, NT)
        dweighted = dtok * rate
        dmass = -jnp.sum(dweighted * tokens, 0, keepdims=True)
        yield
        dmcol[grid] = jnp.broadcast_to(dmass, (LANES, all_slices)).T
        for part in range(2):
            block = _block_heads(dweighted[:, part * span : (part + 1) * span], half, slices)
            split_to(dbdh, dbdl, (grid, part), block)
            mix = mbdh[layer, grid, part].astype(f32) + mbdl[layer, grid, part].astype(f32)
            both = jnp.concatenate([mix, block], 0)
            split_to(cmbh, cmbl, (grid, part), both.T)
        yield

    def back_feat(layer, grid, at):
        dfeats = []
        for part in range(2):
            wrows = slice(part * span, (part + 1) * span)
            weight = pair_of(wgth, wgtl, (layer, grid, wrows, at))
            dfeats.append(_dot3(pair_of(dbdh, dbdl, (grid, part)), weight, NN))
        yield
        dfeat = jnp.concatenate(dfeats, 0)
        vacc[layer, 0] += _fold(dfeat)
        dfeat = split_to(hidh, gslope, (layer, grid, slice(None), at), dfeat)
        yield
        gram = _dot(xh1h[layer, grid, :, at], dfeat[0], NT)
        yield
        add_matrix(layer, 0, gram)
        yield

    def back_front(layer, grid, at):
        feat = pair_of(feath, featl, (layer, grid, slice(None), at))
        place = pair_of(placeh, placel, (layer, grid, slice(None), at))
        rows = [slice(part * group, (part + 1) * group) for part in range(2)]
        wrows = [slice(part * span, (part + 1) * span) for part in range(2)]
        weights = [pair_of(wgth, wgtl, (layer, grid, wrows[part], at)) for part in range(2)]
        dweights = []
        for part in range(2):
            dspread = pair_of(sprh, sprl, (layer, grid, rows[part], at))
            both = tuple(
                jnp.concatenate([one, two[rows[part]]], 0) for one, two in zip(dspread, feat)
            )
            dweights.append(_dot3(pair_of(cmbh, cmbl, (grid, part)), both, NN))
        yield
        dscores = []
        for part in range(2):
            pieces = []
            for head in range(half):
                at_head = slice(head * slices, (head + 1) * slices)
                start = part * span + head * slices
                dweight = dweights[part][at_head] + _wide(
                    dmcol[grid, start : start + slices], tile
                )
                full = weights[part][0][at_head].astype(f32) + weights[part][1][at_head].astype(f32)
                prod = full * dweight
                pieces.append(_split(prod - full * jnp.sum(prod, 0, keepdims=True)))
            dscores.append(tuple(jnp.concatenate(list(side), 0) for side in zip(*pieces)))
        yield
        dplaces, grams = [], []
        for part in range(2):
            pieces = dscores[part]
            dplaces.append(_dot3(pair_of(bdth, bdtl, (layer, part)), pieces, NN))
            grams.append(_dot3((place[0][rows[part]], place[1][rows[part]]), pieces, NT))
        yield
        for part in range(2):
            gmacc[layer, part] += grams[part]
        dplace = jnp.concatenate(dplaces, 0)
        vacc[layer, 1] += _fold(dplace)
        dplace = _split(dplace)
        yield
        xhat = xh1h[layer, grid, :, at]
        dfeat = pair_of(hidh, gslope, (layer, grid, slice(None), at))
        dxhat = _dot3(pair_of(upmh, upml, (layer, 0)), dfeat, NN) + _dot3(
            pair_of(upmh, upml, (layer, 1)), dplace, NN
        )
        gram = _dot(xhat, dplace[0], NT)
        yield
        add_matrix(layer, 1, gram)
        grad = stream[grid, :, at] + _norm_back(
            dxhat, xhat.astype(f32), rs1[layer, grid, :, at]
        )
        if isinstance(layer, int) and layer == 0:
            coords = jnp.concatenate(
                [points_ref[grid, :fin, at], jnp.zeros((8 - fin, tile), f32)], 0
            )
            embacc[...] += _dot3(_split(coords), _split(grad), NT)
        else:
            stream[grid, :, at] = grad
        yield

    def to_row(folded):
        return _row_sums(folded)

    def put_vector(row, value, add=False):
        for index in range(width // LANES):
            start = places["vecs"] + index * places["vecs_stride"] + row
            piece = value[:, index * LANES : (index + 1) * LANES]
            if add:
                piece = piece + packed[start : start + 1, :]
            packed[start : start + 1, :] = piece

    def close_matrix(layer, slot, bias_sum):
        gain, shift = (2, 3) if slot == 3 else (0, 1)
        gram = read_matrix(layer, slot)
        mat = mats_ref[layer, slot]
        value = (
            _wide(cols[layer, gain], width) * gram + _wide(cols[layer, shift], width) * bias_sum
        )
        for index in range(width // LANES):
            packed[matrix_rows(layer, slot, index), :] = value[
                :, index * LANES : (index + 1) * LANES
            ]
        shift_row = _doth(jnp.broadcast_to(bias_sum, (8, width)), mat, NT)[:1]
        return _row_sums(gram * mat), shift_row

    def close_rest(layer):
        base = 9 * layer
        middle, inner, final = [to_row(vacc[layer, slot]) for slot in (2, 3, 4)]
        gain_row, shift_row = close_matrix(layer, 3, inner)
        for offset, row in ((4, middle), (5, gain_row), (6, shift_row), (7, inner), (8, final)):
            put_vector(base + offset, row)

    def close_feat(layer):
        total = to_row(vacc[layer, 0])
        gain, shift = close_matrix(layer, 0, total)
        put_vector(9 * layer, gain)
        put_vector(9 * layer + 1, shift)
        put_vector(9 * layer + 2, total)

    def close_front(layer):
        base = 9 * layer
        place_sum = to_row(vacc[layer, 1])
        place_gain, place_shift = close_matrix(layer, 1, place_sum)
        put_vector(base, place_gain, True)
        put_vector(base + 1, place_shift, True)
        put_vector(base + 3, place_sum)
        tiled = jnp.concatenate([maps_ref[layer]] * half, 1)
        total = None
        sharp_total = None
        for part in range(2):
            lane = lax.broadcasted_iota(jnp.int32, (1, span), 1)
            sharp = jnp.full((1, span), 0.0, f32) + sharp_ref[layer, part * half]
            for head in range(1, half):
                sharp = jnp.where(
                    lane >= head * slices, sharp_ref[layer, part * half + head], sharp
                )
            picked = _diag_heads(gmacc[layer, part], head_size, slices) / sharp
            total = picked if total is None else total + picked
            share = -jnp.sum(picked * tiled, 0, keepdims=True) / sharp
            chosen = jnp.where(
                lax.broadcasted_iota(jnp.int32, (span, LANES), 0) // slices + part * half
                == lax.broadcasted_iota(jnp.int32, (span, LANES), 1),
                1.0,
                0.0,
            )
            share = _dotx(jnp.broadcast_to(share, (8, span)), chosen, NN)
            sharp_total = share if sharp_total is None else sharp_total + share
        start = places["sharp"] + layer
        packed[start : start + 1, :heads] = sharp_total[:1, :heads]
        total = _fold(total)
        total = total + pltpu.roll(total, slices, 1)
        start = places["maps"] + layer * head_size
        packed[start : start + head_size, :slices] = total[:, :slices]
        start = places["qkv"] + layer * head_size
        packed[start : start + head_size, : 3 * head_size] = qkvacc[layer]

    def close_head():
        spread_dpred = _dotx(headacc[0], jnp.ones((LANES, LANES), f32), NN)
        gram = jnp.concatenate([headacc[1 + k] for k in range(width // LANES)], 1)
        gain_row, shift_row = vecs[tail : tail + 1], vecs[tail + 1 : tail + 2]
        head_grad = gram * gain_row + _wide(spread_dpred, width) * shift_row
        for index in range(width // LANES):
            at = slice(index * LANES, (index + 1) * LANES)
            start = places["io"] + index * places["io_stride"]
            packed[start + fin : start + fin + outc, :] = head_grad[:outc, at]
        put_vector(tail, jnp.sum(gram * head_rows, 0, keepdims=True))
        put_vector(
            tail + 1, jnp.sum(_wide(spread_dpred, width) * head_rows, 0, keepdims=True)
        )
        packed[places["loss"] : places["loss"] + 1, :] = jnp.broadcast_to(
            jnp.sum(jnp.sum(lossacc[...], 0, keepdims=True), 1, keepdims=True), (1, LANES)
        )

    def close_embed():
        for index in range(width // LANES):
            at = slice(index * LANES, (index + 1) * LANES)
            start = places["io"] + index * places["io_stride"]
            packed[start : start + fin, :] = embacc[:fin, at]

    stages = [
        sum_stages(
            packed,
            summed,
            entry,
            boxes[5 * index : 5 * index + 5],
            sum_send.at[index],
            sum_recv.at[index],
            members // 2,
        )
        for index, entry in enumerate(places["groups"])
    ]
    def run(spots):
        for set_index, number in spots:
            stages[set_index][number]()

    def hooks(phase, layer, step):
        found = PLAN.get((phase, layer, step), {})
        return [
            [stages[s][n] for s, n in found.get(turn, ())] for turn in range(max(found, default=-1) + 1)
        ]

    def woven(phase, maker, layer):
        if not any(key[:2] == (phase, layer) for key in PLAN):

            @pl.loop(0, steps)
            def _(step):
                at = window(step)
                _lockstep([maker(layer, grid, at) for grid in range(grids)])

            return
        for step in range(steps):
            at = slice(step * tile, (step + 1) * tile)
            _lockstep(
                [maker(layer, grid, at) for grid in range(grids)], hooks(phase, layer, step)
            )

    for layer in range(layers - 1, -1, -1):
        accf[...] = jnp.zeros_like(accf)
        woven("rest", back_rest, layer)
        close_rest(layer)
        run(AFTER_REST[layer])
        _lockstep(
            [back_attend(layer, grid) for grid in range(grids)], hooks("attend", layer, 0)
        )
        woven("feat", back_feat, layer)
        close_feat(layer)
        run(AFTER_FEAT[layer])
        if layer:
            close_head()
        woven("front", back_front, layer)
        close_front(layer)
        if layer == 0:
            close_embed()
        run(AFTER_FRONT[layer])

    squares[...] = jnp.zeros_like(squares)

    @pl.loop(0, places["rows"] // 256)
    def _(step):
        block = summed[pl.ds(pl.multiple_of(step * 256, 256), 256), :]
        row = lax.broadcasted_iota(jnp.int32, block.shape, 0) + step * 256
        block = jnp.where(row == places["loss"], 0.0, block)
        squares[...] += jnp.sum((block * block).reshape(32, 8, LANES), 0)


def _round_up(value, unit):
    return (value + unit - 1) // unit * unit


def packed_places(layers, width, io_rows, vec_rows, head_size):
    halves = width // LANES
    places = {"io_stride": _round_up(io_rows, 8), "vecs_stride": _round_up(vec_rows, 8)}
    row = 0
    for name, rows in (
        ("io", halves * places["io_stride"]),
        ("vecs", halves * places["vecs_stride"]),
        ("maps", layers * head_size),
        ("qkv", layers * head_size),
        ("sharp", _round_up(layers, 8)),
        ("loss", 8),
    ):
        places[name] = row
        row += rows
    places["mats"] = _round_up(row, 256)
    each = halves * width
    first = places["mats"] + each
    groups = [(0, first), (first, each), (first + each, 3 * each)]
    for layer in range(1, layers):
        start = places["mats"] + layer * 5 * each
        groups += [(start, 2 * each), (start + 2 * each, 3 * each)]
    places["groups"] = groups
    places["rows"] = places["mats"] + layers * 5 * each
    return places


def group_parts(rows):
    half = rows // 2
    a_rows = (half * 2 // 3 + 64) // 128 * 128
    return half, a_rows, half - a_rows


def sum_stages(packed, out, span, boxes, send_sems, recv_sems, floors):
    first, rows = span
    half, a_rows, b_rows = group_parts(rows)
    core_in, a_one, a_two, b_one, b_two = boxes
    a_four, b_four, a_all, b_all = a_rows // 4, b_rows // 4, a_rows // 16, b_rows // 16
    point, group = lax.axis_index("pts"), lax.axis_index("grp")
    y, z = lax.rem(point, 2), lax.div(point, 2)
    core, x = lax.rem(group, 2), lax.div(group, 2)
    plane = x + 2 * y
    base = first + core * half
    hops = (1, 2, 3)

    def plane_peer(hop):
        other_x, other_y = lax.rem(x + hop % 2, 2), lax.rem(y + hop // 2, 2)
        return (z * 2 + other_y, other_x * 2 + core), other_x + 2 * other_y

    def line_peer(hop):
        other = lax.rem(z + hop, floors)
        return (other * 2 + y, group), other

    partner = (point, x * 2 + (1 - core))

    def rows_at(start, count):
        return pl.ds(pl.multiple_of(start, 8), count)

    def send(number, source, target, device):
        return pltpu.make_async_remote_copy(
            src_ref=source,
            dst_ref=target,
            send_sem=send_sems.at[number],
            recv_sem=recv_sems.at[number],
            device_id=device,
            device_id_type=MESH,
        )

    def place(start, count):
        return packed.at[rows_at(start, count)]

    def cross():
        return send(0, place(first + (1 - core) * half, half), core_in, partner)

    def a1(hop):
        device, spot = plane_peer(hop)
        return send(hop, place(base + spot * a_four, a_four), a_one.at[hop - 1], device)

    def b1(hop):
        device, spot = line_peer(hop)
        source = place(base + a_rows + spot * b_four, b_four)
        return send(3 + hop, source, b_one.at[hop - 1], device)

    a_part = rows_at(base + plane * a_four, a_four)
    b_part = rows_at(base + a_rows + z * b_four, b_four)
    a_piece = rows_at(base + plane * a_four + z * a_all, a_all)
    b_piece = rows_at(base + a_rows + z * b_four + plane * b_all, b_all)

    def a2(hop):
        device, spot = line_peer(hop)
        source = place(base + plane * a_four + spot * a_all, a_all)
        return send(6 + hop, source, a_two.at[hop - 1], device)

    def b2(hop):
        device, spot = plane_peer(hop)
        source = place(base + a_rows + z * b_four + spot * b_all, b_all)
        return send(9 + hop, source, b_two.at[hop - 1], device)

    def a3(hop):
        return send(12 + hop, out.at[a_piece], out.at[a_piece], line_peer(hop)[0])

    def b3(hop):
        return send(15 + hop, out.at[b_piece], out.at[b_piece], plane_peer(hop)[0])

    def a4(hop):
        return send(18 + hop, out.at[a_part], out.at[a_part], plane_peer(hop)[0])

    def b4(hop):
        return send(21 + hop, out.at[b_part], out.at[b_part], line_peer(hop)[0])

    def last():
        own = out.at[rows_at(base, half)]
        return send(25, own, own, partner)

    def arrive(make):
        for hop in hops:
            make(hop).wait_recv()

    def depart(make):
        for hop in hops:
            make(hop).start()

    def stage_cross():
        cross().start()

    def stage_first():
        cross().wait_recv()
        own = rows_at(base, half)
        packed[own, :] = packed[own, :] + core_in[...]
        depart(a1)
        depart(b1)

    def stage_second():
        arrive(a1)
        packed[a_part, :] = packed[a_part, :] + a_one[0] + a_one[1] + a_one[2]
        depart(a2)
        arrive(b1)
        packed[b_part, :] = packed[b_part, :] + b_one[0] + b_one[1] + b_one[2]
        depart(b2)

    def stage_third():
        arrive(a2)
        out[a_piece, :] = packed[a_piece, :] + a_two[0] + a_two[1] + a_two[2]
        depart(a3)
        arrive(b2)
        out[b_piece, :] = packed[b_piece, :] + b_two[0] + b_two[1] + b_two[2]
        depart(b3)

    def stage_fourth():
        arrive(a3)
        depart(a4)
        arrive(b3)
        depart(b4)

    def stage_fifth():
        arrive(a4)
        arrive(b4)
        last().start()

    def stage_end():
        last().wait_recv()
        cross().wait_send()
        last().wait_send()
        for make in (a1, b1, a2, b2, a3, b3, a4, b4):
            for hop in hops:
                make(hop).wait_send()

    return (
        stage_cross,
        stage_first,
        stage_second,
        stage_third,
        stage_fourth,
        stage_fifth,
        stage_end,
    )


def update_kernel(dims, *refs):
    layers, width, places = dims
    halves = width // LANES
    bigs, small, squares = refs[:halves], refs[halves], refs[halves + 1]
    inputs, outputs = refs[halves + 2 : halves + 20], refs[halves + 20 :]
    loss_out, norm_out = outputs[:2]
    weights, means, seconds = inputs[:6], inputs[6:12], inputs[12:]
    total = jnp.sum(jnp.sum(squares[...], 0, keepdims=True), 1, keepdims=True)
    norm = jnp.sqrt(total)
    factor = jnp.minimum(1.0, clip_limit / norm)

    def apply(index, grad):
        weight, mean, second = weights[index], means[index], seconds[index]
        first_new, second_new, weight_new = adamw_update(
            weight[...], grad * factor, mean[...], second[...]
        )
        outputs[2 + 3 * index][...] = first_new
        outputs[3 + 3 * index][...] = second_new
        outputs[4 + 3 * index][...] = weight_new

    grad = jnp.concatenate([big[...] for big in bigs], 1)
    apply(1, grad[None, None])

    @pl.when(pl.program_id(0) == 0)
    def _():
        def rows(name, start, count):
            first = places[name] + start
            return small[first : first + count, :]

        loss_out[...] = rows("loss", 0, 1)[:, :1]
        norm_out[...] = norm
        for index, name in ((0, "io"), (5, "vecs")):
            stride, count = places[name + "_stride"], weights[index].shape[0]
            apply(
                index,
                jnp.concatenate([rows(name, k * stride, count) for k in range(halves)], 1),
            )
        for index, name in ((2, "maps"), (3, "qkv")):
            _, count, lanes = weights[index].shape
            apply(
                index,
                jnp.stack([rows(name, k * count, count)[:, :lanes] for k in range(layers)]),
            )
        count, lanes = weights[4].shape
        apply(4, rows("sharp", 0, count)[:, :lanes])


def update_all(summed, squares, network_state, running_means, running_squares, places):
    layers, slots, width, _ = network_state[1].shape
    halves = width // LANES
    skip = places["mats"] // width

    def half_spec(index):
        def spot(i):
            slot = i % slots
            return i - slot + jnp.where(slot < 2, 1 - slot, slot)

        return pl.BlockSpec((width, LANES), lambda i: (skip + spot(i) * halves + index, 0))

    def whole(entry):
        return pl.BlockSpec(entry.shape, lambda i: (0,) * entry.ndim)

    def spec(index, entry):
        if index == 1:
            return pl.BlockSpec((1, 1, width, width), lambda i: (i // slots, i % slots, 0, 0))
        return whole(entry)

    state_specs = [spec(index, entry) for index, entry in enumerate(network_state)]
    shapes = [jax.ShapeDtypeStruct((1, 1), f32)] * 2
    specs = [pl.BlockSpec((1, 1), lambda i: (0, 0))] * 2
    for index, entry in enumerate(network_state):
        shapes += [jax.ShapeDtypeStruct(entry.shape, f32)] * 3
        specs += [spec(index, entry)] * 3
    results = pl.pallas_call(
        functools.partial(update_kernel, (layers, width, places)),
        grid=(layers * slots,),
        out_shape=shapes,
        in_specs=[
            *[half_spec(index) for index in range(halves)],
            pl.BlockSpec((places["mats"], LANES), lambda i: (0, 0)),
            pl.BlockSpec((8, LANES), lambda i: (0, 0)),
        ]
        + state_specs * 3,
        out_specs=specs,
        compiler_params=pltpu.CompilerParams(vmem_limit_bytes=VMEM_BYTES),
    )(*[summed] * (halves + 1), squares, *network_state, *running_means, *running_squares)
    return (results[0].reshape(()), results[1].reshape(()), *results[2:])


def whole_grid_grads(network_state, coords, goals, bound, sizes, places, mesh_sizes):
    io_rows, mats, maps, qkv, sharp, vecs = network_state
    members, groups = mesh_sizes
    grids, own, _, own_points = coords.shape
    points = own_points * members
    layers, _, width, _ = mats.shape
    heads = sharp.shape[1]
    head_size, slices = maps.shape[1:]
    outc = io_rows.shape[0] - FIN
    tile = TILE
    half, span, group = heads // 2, heads // 2 * slices, heads // 2 * head_size
    dims = (grids, points, width, heads, head_size, slices, layers, FIN, outc, tile)
    dims = dims + (members, groups, places)

    def both(*shape):
        return [pltpu.VMEM(shape, bf16), pltpu.VMEM(shape, bf16)]

    def single(*shape):
        return [pltpu.VMEM(shape, f32)]

    kept = (layers, grids, width, points)
    box = (members, grids * 8 + 8, own_points)
    scratch = (
        single(places["rows"], LANES)
        + single(grids, width, points)
        + [pltpu.VMEM(kept, bf16)]
        + single(layers, grids, 1, points)
        + both(*kept)
        + both(*kept)
        + both(layers, grids, 2 * span, points)
        + both(*kept)
        + [pltpu.VMEM(kept, bf16)]
        + single(layers, grids, 1, points)
        + [pltpu.VMEM(kept, bf16)] * 2
        + both(layers, 5, width, width)
        + single(layers, 9, width, LANES)
        + both(layers, 2, span, group)
        + both(layers, 2, group, span)
        + single(grids, 2, group + 16, span)
        + single(grids, 2, group, span)
        + single(layers, grids, head_size, 2 * span)
        + single(layers, grids, 1, 2 * span)
        + single(layers, grids, 3 * head_size, 2 * span)
        + single(layers, grids, half, slices, 2 * slices)
        + both(layers, grids, 2, group, span)
        + both(grids, 2, group, span)
        + both(grids, 2, span, 2 * group)
        + single(grids, 2 * span, LANES)
        + single(layers, 5, width, LANES)
        + single(layers, 2, group, span)
        + single(1 + width // LANES, 8, LANES)
        + single(8, width)
        + single(8, LANES)
        + single(layers, head_size, 3 * head_size)
        + single(grids, 8, points)
        + single(*box)
        + single(members - 1, *box[1:])
        + single(groups, 8, own_points)
        + [pltpu.SemaphoreType.DMA((members - 1,))] * 2
        + [pltpu.SemaphoreType.DMA((groups - 1,))] * 2
        + [pltpu.SemaphoreType.DMA((len(places["groups"]), 26))] * 2
    )
    for _, rows in places["groups"]:
        half_rows, a_rows, b_rows = group_parts(rows)
        scratch += single(half_rows, LANES)
        for part_rows in (a_rows, b_rows):
            scratch += single(3, part_rows // 4, LANES) + single(3, part_rows // 16, LANES)
    vmem = pl.BlockSpec(memory_space=pltpu.VMEM)
    smem = pl.BlockSpec(memory_space=pltpu.SMEM)
    return pl.pallas_call(
        functools.partial(grids_kernel, dims),
        out_shape=[
            jax.ShapeDtypeStruct((places["rows"], LANES), f32),
            jax.ShapeDtypeStruct((8, LANES), f32),
        ],
        in_specs=[smem] * 2 + [vmem] * 8,
        out_specs=[vmem, vmem],
        scratch_shapes=scratch,
        compiler_params=pltpu.CompilerParams(
            collective_id=0, has_side_effects=True, vmem_limit_bytes=VMEM_BYTES
        ),
    )(sizes, sharp, coords, jnp.swapaxes(goals, 1, 2), bound, io_rows, mats, maps, qkv, vecs)


def body_grids(mesh_sizes, *arrays):
    network_state = arrays[4:10]
    io_rows, mats, maps, _, _, vecs = network_state
    places = packed_places(
        mats.shape[0], mats.shape[2], io_rows.shape[0], vecs.shape[0], maps.shape[1]
    )
    summed, squares = whole_grid_grads(network_state, *arrays[:4], places, mesh_sizes)
    return update_all(
        summed, squares, network_state, arrays[10:16], arrays[16:22], places
    )


def solution(mesh):
    in_specs = (
        P(None, "grp", None, "pts"),
        P(None, "grp", None, "pts"),
        P(None, "grp", "pts"),
        P(None, "grp"),
        P(),
        P(),
        P(),
        P(),
        P(),
        P(),
        P(),
        P(),
        P(),
        P(),
        P(),
        P(),
        P(),
        P(),
        P(),
        P(),
        P(),
        P(),
    )
    out_specs = (
        P(),
        P(),
        P(),
        P(),
        P(),
        P(),
        P(),
        P(),
        P(),
        P(),
        P(),
        P(),
        P(),
        P(),
        P(),
        P(),
        P(),
        P(),
        P(),
        P(),
    )
    members, groups = mesh.shape["pts"], mesh.shape["grp"]

    def body(*arrays):
        batches, own, _, own_points = arrays[0].shape
        fits = own == members and batches * own_points * members <= 2048
        if fits and own_points == LANES and (members, groups) == (8, 4) and arrays[5].shape[0] == 2:
            return body_grids((members, groups), *arrays)
        return body_points(*arrays)

    return jax.shard_map(body, mesh=mesh, in_specs=in_specs, out_specs=out_specs, check_vma=False)
```

```python
import functools
import math

import jax
import jax.numpy as jnp
from jax import lax
from jax.experimental import pallas as pl
from jax.experimental.pallas import tpu as pltpu
from jax.sharding import PartitionSpec as P

STEP = 10
LANES = 128
FIN = 2
TILE = 512
SLOT_ORDER = (1, 0, 2, 3, 4)
BLOCK = 64
PLAN = {
    ("attend", 1, 0): {4: ((4, 1),)},
    ("front", 1, 0): {3: ((4, 2),), 5: ((4, 3),)},
    ("rest", 0, 0): {3: ((3, 1),), 5: ((4, 4),)},
    ("attend", 0, 0): {2: ((3, 2),), 4: ((2, 1),)},
    ("feat", 0, 0): {2: ((4, 5),)},
    ("front", 0, 0): {1: ((1, 1),), 2: ((2, 2),), 3: ((3, 4), (4, 6)), 4: ((1, 2),), 5: ((2, 3),)},
}
AFTER_REST = {1: ((4, 0),), 0: ((2, 0),)}
AFTER_FEAT = {1: (), 0: ((1, 0), (3, 3))}
AFTER_FRONT = {
    1: ((3, 0),),
    0: ((0, 0), (3, 5), (1, 3), (0, 1), (2, 4), (3, 6), (0, 2), (1, 4), (0, 3), (2, 5), (1, 5), (0, 4), (2, 6), (1, 6), (0, 5), (0, 6)),
}
VMEM_BYTES = 65400 << 10
f32, bf16 = jnp.float32, jnp.bfloat16
MESH = pl.DeviceIdType.MESH
NN, NT, TN = ((1,), (0,)), ((1,), (1,)), ((0,), (0,))


exact_arithmetic = lax.Precision.HIGHEST
clip_limit = 0.02
learn_rate = 0.1
beta_one = 0.9
beta_two = 0.999
adam_epsilon = 1e-08
weight_decay = 0.01


def layer_norm(values, gain, shift):
    center = values - jnp.mean(values, -1, keepdims=True)
    spread_tokens = jnp.mean(center * center, -1, keepdims=True)
    return center * lax.rsqrt(spread_tokens + 1e-05) * gain + shift


def slice_attend(weighted_points, masses, triple_maps_rows):
    head_size = triple_maps_rows.shape[0]
    tokens = weighted_points / (masses[..., None] + 1e-05)
    joined = jnp.einsum("imd,de->ime", tokens, triple_maps_rows, precision=exact_arithmetic)
    queries = joined[..., :head_size]
    keys = joined[..., head_size : 2 * head_size]
    values = joined[..., 2 * head_size :]
    scores = jnp.einsum("imd,ind->imn", queries, keys, precision=exact_arithmetic) * head_size ** (
        -0.5
    )
    probs = jax.nn.softmax(scores, -1)
    return jnp.einsum("imn,ind->imd", probs, values, precision=exact_arithmetic)


def slice_front(weight_set, slicer, temper, vec_rows, stream, valid):
    grids_n, points_n, width = stream.shape
    heads = temper.shape[0]
    normed = layer_norm(stream, vec_rows[0], vec_rows[1])
    features = (
        jnp.einsum("gpc,ce->gpe", normed, weight_set[0], precision=exact_arithmetic) + vec_rows[2]
    )
    chip_placement_list = (
        jnp.einsum("gpc,ce->gpe", normed, weight_set[1], precision=exact_arithmetic) + vec_rows[3]
    )
    partition_scores = (
        jnp.einsum(
            "gphd,dm->gphm",
            chip_placement_list.reshape(grids_n, points_n, heads, -1),
            slicer,
            precision=exact_arithmetic,
        )
        / temper[:, None]
    )
    slice_weights = jax.nn.softmax(partition_scores, -1) * valid[:, :, None, None]
    return (slice_weights, features.reshape(grids_n, points_n, heads, -1))


def slice_rest(weight_set, vec_rows, stream, spread_tokens):
    stream = (
        stream
        + jnp.einsum("gpc,ce->gpe", spread_tokens, weight_set[2], precision=exact_arithmetic)
        + vec_rows[4]
    )
    inner = (
        jnp.einsum(
            "gpc,ce->gpe",
            layer_norm(stream, vec_rows[5], vec_rows[6]),
            weight_set[3],
            precision=exact_arithmetic,
        )
        + vec_rows[7]
    )
    hidden = jax.nn.gelu(inner, approximate=False)
    return (
        stream
        + jnp.einsum("gpc,ce->gpe", hidden, weight_set[4], precision=exact_arithmetic)
        + vec_rows[8]
    )


def slice_mix(weighted_points, masses, qkv):
    grids_n, heads, slices, head_size = weighted_points.shape
    items = grids_n * heads
    flat_weighted = weighted_points.reshape(items, slices, head_size)
    flat_masses = masses.reshape(items, slices)
    own_weighted, own_masses = (
        lax.psum_scatter(flat_weighted, "pts", scatter_dimension=0, tiled=True),
        lax.psum_scatter(flat_masses, "pts", scatter_dimension=0, tiled=True),
    )
    mixed_tokens = lax.all_gather(
        slice_attend(own_weighted, own_masses, qkv), "pts", axis=0, tiled=True
    )
    kept = (own_weighted, own_masses)
    return (mixed_tokens.reshape(weighted_points.shape), kept)


def slice_mix_back(grad_mixed, kept, qkv):
    grids_n, heads, slices, head_size = grad_mixed.shape
    flat = grad_mixed.reshape(grids_n * heads, slices, head_size)
    _, pullback = jax.vjp(slice_attend, kept[0], kept[1], qkv)
    own_grad = lax.psum_scatter(flat, "pts", scatter_dimension=0, tiled=True)
    grad_weighted, grad_masses, grad_qkv = pullback(own_grad)
    grad_weighted, grad_masses = (
        lax.all_gather(grad_weighted, "pts", axis=0, tiled=True),
        lax.all_gather(grad_masses, "pts", axis=0, tiled=True),
    )
    return (
        grad_weighted.reshape(grad_mixed.shape),
        grad_masses.reshape(grids_n, heads, slices),
        grad_qkv,
    )


def layer_forward(stream, layer_set, valid):
    weight_set, slicer, qkv, temper, vec_rows = layer_set
    slice_weights, features = slice_front(weight_set, slicer, temper, vec_rows, stream, valid)
    weighted_points = jnp.einsum(
        "gphm,gphd->ghmd", slice_weights, features, precision=exact_arithmetic
    )
    masses = jnp.sum(slice_weights, 1)
    mixed_tokens, kept = slice_mix(weighted_points, masses, qkv)
    spread_tokens = jnp.einsum(
        "gphm,ghmd->gphd", slice_weights, mixed_tokens, precision=exact_arithmetic
    ).reshape(stream.shape)
    return (slice_rest(weight_set, vec_rows, stream, spread_tokens), (stream, mixed_tokens, kept))


def layer_backward(grad_out, layer_set, saved, valid):
    weight_set, slicer, qkv, temper, vec_rows = layer_set
    stream, mixed_tokens, kept = saved
    (slice_weights, features), pull_front = jax.vjp(
        lambda w_set, s_set, t_set, v_set, s_in: slice_front(
            w_set, s_set, t_set, v_set, s_in, valid
        ),
        weight_set,
        slicer,
        temper,
        vec_rows,
        stream,
    )
    spread_tokens = jnp.einsum(
        "gphm,ghmd->gphd", slice_weights, mixed_tokens, precision=exact_arithmetic
    ).reshape(stream.shape)
    _, pull_rest = jax.vjp(slice_rest, weight_set, vec_rows, stream, spread_tokens)
    grad_set_rest, grad_vec_rest, grad_stream, grad_spread = pull_rest(grad_out)
    grad_spread = grad_spread.reshape(features.shape)
    grad_weights = jnp.einsum(
        "gphd,ghmd->gphm", grad_spread, mixed_tokens, precision=exact_arithmetic
    )
    grad_mixed = jnp.einsum(
        "gphm,gphd->ghmd", slice_weights, grad_spread, precision=exact_arithmetic
    )
    grad_weighted, grad_masses, grad_qkv = slice_mix_back(grad_mixed, kept, qkv)
    grad_weights = (
        grad_weights
        + jnp.einsum("ghmd,gphd->gphm", grad_weighted, features, precision=exact_arithmetic)
        + grad_masses[:, None]
    )
    grad_features = jnp.einsum(
        "gphm,ghmd->gphd", slice_weights, grad_weighted, precision=exact_arithmetic
    )
    grad_set_front, grad_slicer, grad_temper, grad_vec_front, grad_stream_front = pull_front(
        (grad_weights, grad_features)
    )
    grads = (
        grad_set_rest + grad_set_front,
        grad_slicer,
        grad_qkv,
        grad_temper,
        grad_vec_rest + grad_vec_front,
    )
    return (grad_stream + grad_stream_front, grads)


def head_loss(head_rows, tail_rows, stream, goals, on_surface, off_surface, inv_surf, inv_vol):
    final = layer_norm(stream, tail_rows[0], tail_rows[1])
    pred = jnp.einsum("oc,gpc->gop", head_rows, final, precision=exact_arithmetic)
    errors = (pred - goals) ** 2
    return inv_surf * jnp.sum(on_surface * errors[:, 0]) + inv_vol * jnp.sum(
        off_surface * (errors[:, 1] + errors[:, 2])
    )


def layer_params(network_state, block_number):
    (
        lifting_readout_rows,
        block_projections,
        partition_maps,
        triple_maps_rows,
        sharpness_factors,
        gain_bias_rows,
    ) = network_state
    return (
        block_projections[block_number],
        partition_maps[block_number],
        triple_maps_rows[block_number],
        sharpness_factors[block_number],
        gain_bias_rows[9 * block_number : 9 * block_number + 9],
    )


def one_batch(network_state, coords, goals, valid, on_surface, off_surface, inv_surf, inv_vol):
    (
        lifting_readout_rows,
        block_projections,
        partition_maps,
        triple_maps_rows,
        sharpness_factors,
        gain_bias_rows,
    ) = network_state
    fin = coords.shape[1]
    layers_n = block_projections.shape[0]
    stream = jnp.einsum(
        "gfp,fc->gpc", coords, lifting_readout_rows[:fin], precision=exact_arithmetic
    )
    saved = []
    for block_number in range(layers_n):
        stream, keep_set = layer_forward(stream, layer_params(network_state, block_number), valid)
        saved.append(keep_set)
    batch_loss, pull_head = jax.vjp(
        lambda h_rows, t_rows, s_in: head_loss(
            h_rows, t_rows, s_in, goals, on_surface, off_surface, inv_surf, inv_vol
        ),
        lifting_readout_rows[fin:],
        gain_bias_rows[9 * layers_n :],
        stream,
    )
    grad_head, grad_tail, grad_stream = pull_head(jnp.ones_like(batch_loss))
    layer_grads = [None] * layers_n
    for block_number in reversed(range(layers_n)):
        grad_stream, layer_grads[block_number] = layer_backward(
            grad_stream, layer_params(network_state, block_number), saved[block_number], valid
        )
    grad_embed = jnp.einsum("gfp,gpc->fc", coords, grad_stream, precision=exact_arithmetic)
    grads = (
        jnp.concatenate([grad_embed, grad_head], 0),
        jnp.stack([entry[0] for entry in layer_grads]),
        jnp.stack([entry[1] for entry in layer_grads]),
        jnp.stack([entry[2] for entry in layer_grads]),
        jnp.stack([entry[3] for entry in layer_grads]),
        jnp.concatenate([entry[4] for entry in layer_grads] + [grad_tail], 0),
    )
    return (batch_loss, grads)


def adamw_update(weight, grad, first, second):
    first_new = beta_one * first + (1.0 - beta_one) * grad
    second_new = beta_two * second + (1.0 - beta_two) * grad * grad
    first_hat = first_new / (1.0 - beta_one**STEP)
    second_hat = second_new / (1.0 - beta_two**STEP)
    weight_new = weight - learn_rate * (
        first_hat / (jnp.sqrt(second_hat) + adam_epsilon) + weight_decay * weight
    )
    return (first_new, second_new, weight_new)


def body_points(
    input_positions,
    flow_labels,
    airfoil_boundary,
    valid_sizes,
    lifting_readout_rows,
    block_projections,
    partition_maps,
    triple_maps_rows,
    sharpness_factors,
    gain_bias_rows,
    lifting_readout_mean,
    projection_running_mean,
    partition_map_mean,
    triple_maps_mean,
    sharpness_mean,
    gain_bias_mean,
    lifting_readout_square,
    projection_running_square,
    partition_map_square,
    triple_maps_square,
    sharpness_square,
    gain_bias_square,
):
    batches = input_positions.shape[0]
    points_n = input_positions.shape[3]
    slots = lax.axis_index("pts") * points_n + jnp.arange(points_n, dtype=jnp.int32)
    valid = (slots[None, None, :] < valid_sizes[:, :, None]).astype(jnp.float32)
    on_surface = valid * airfoil_boundary.astype(jnp.float32)
    off_surface = valid - on_surface
    count_surf, count_vol = lax.psum((jnp.sum(on_surface), jnp.sum(off_surface)), ("pts", "grp"))
    inv_surf = 1.0 / jnp.maximum(count_surf, 1.0)
    inv_vol = 1.0 / jnp.maximum(count_vol, 1.0)
    network_state = (
        lifting_readout_rows,
        block_projections,
        partition_maps,
        triple_maps_rows,
        sharpness_factors,
        gain_bias_rows,
    )
    loss_value = jnp.zeros((), jnp.float32)
    grads = tuple((jnp.zeros_like(entry) for entry in network_state))
    for batch in range(batches):
        batch_loss, batch_set = one_batch(
            network_state,
            input_positions[batch],
            flow_labels[batch],
            valid[batch],
            on_surface[batch],
            off_surface[batch],
            inv_surf,
            inv_vol,
        )
        loss_value = loss_value + batch_loss
        grads = tuple((total + entry for total, entry in zip(grads, batch_set)))
    running_means = (
        lifting_readout_mean,
        projection_running_mean,
        partition_map_mean,
        triple_maps_mean,
        sharpness_mean,
        gain_bias_mean,
    )
    running_squares = (
        lifting_readout_square,
        projection_running_square,
        partition_map_square,
        triple_maps_square,
        sharpness_square,
        gain_bias_square,
    )
    return finish(loss_value, grads, network_state, running_means, running_squares)


def finish(loss_value, grads, network_state, running_means, running_squares):
    summed = lax.psum((loss_value,) + grads, ("pts", "grp"))
    loss_value = summed[0]
    grads = summed[1:]
    grad_norm = jnp.sqrt(sum((jnp.sum(entry * entry) for entry in grads)))
    factor = jnp.minimum(1.0, clip_limit / grad_norm)
    results = []
    for weight, grad, first, second in zip(network_state, grads, running_means, running_squares):
        results.extend(adamw_update(weight, grad * factor, first, second))
    return tuple([loss_value, grad_norm] + results)


def _split(x):
    high = x.astype(bf16)
    return high, (x - high.astype(f32)).astype(bf16)


def _dot(a, b, dims, precision=None):
    return lax.dot_general(a, b, (dims, ((), ())), precision=precision, preferred_element_type=f32)


def _dot3(a, b, dims):
    left = jnp.concatenate([a[0], a[0], a[1]], dims[0][0])
    right = jnp.concatenate([b[0], b[1], b[0]], dims[1][0])
    return _dot(left, right, dims)


def _doth(a, b, dims):
    return _dot3(_split(a), _split(b), dims)


def _row_sums(value):
    high, low = _split(value)
    ones = jnp.ones((8, 2 * value.shape[1]), bf16)
    return _dot(ones, jnp.concatenate([high, low], 1), NT)[:1]


def _dotx(a, b, dims):
    return _dot(a, b, dims, lax.Precision.HIGHEST)


def _wide(col, lanes):
    return jnp.concatenate([col] * (lanes // LANES), 1) if lanes > LANES else col


def _fold(x):
    total = x[:, :LANES]
    for start in range(LANES, x.shape[1], LANES):
        total = total + x[:, start : start + LANES]
    return total


def _lockstep(makers, hooks=()):
    turn = 0
    running = list(makers)
    while running:
        for stage in hooks[turn] if turn < len(hooks) else ():
            stage()
        turn += 1
        alive = []
        for entry in running:
            try:
                next(entry)
                alive.append(entry)
            except StopIteration:
                pass
        running = alive


def _diag_heads(full, depth, slices):
    heads = full.shape[0] // depth
    lane = lax.broadcasted_iota(jnp.int32, (depth, full.shape[1]), 1)
    picked = full[:depth]
    for head in range(1, heads):
        picked = jnp.where(lane >= head * slices, full[head * depth : (head + 1) * depth], picked)
    return picked


def _block_heads(flat, heads, slices):
    lane = lax.broadcasted_iota(jnp.int32, flat.shape, 1)
    return jnp.concatenate(
        [
            jnp.where((lane >= head * slices) & (lane < (head + 1) * slices), flat, 0.0)
            for head in range(heads)
        ],
        0,
    )


def _norm(x):
    inv_width = 1.0 / x.shape[0]
    center = x - jnp.sum(x, 0, keepdims=True) * inv_width
    rstd = lax.rsqrt(jnp.sum(center * center, 0, keepdims=True) * inv_width + 1e-05)
    return center * rstd, rstd


def _norm_back(grad, xhat, rstd):
    inv_width = 1.0 / grad.shape[0]
    mean_grad = jnp.sum(grad, 0, keepdims=True) * inv_width
    mean_proj = jnp.sum(grad * xhat, 0, keepdims=True) * inv_width
    return (grad - mean_grad - xhat * mean_proj) * rstd


def grids_kernel(dims, *refs):
    (
        grids,
        points,
        width,
        heads,
        head_size,
        slices,
        layers,
        fin,
        outc,
        tile,
        members,
        groups,
        places,
    ) = dims
    (
        sizes_ref,
        sharp_ref,
        coords_ref,
        goals_ref,
        bound_ref,
        io_ref,
        mats_hbm,
        maps_ref,
        qkv_ref,
        vecs_ref,
        summed_hbm,
        squares,
        mats_ref,
        summed,
        packed,
        stream,
        xh1h,
        rs1,
        feath,
        featl,
        placeh,
        placel,
        wgth,
        wgtl,
        sprh,
        sprl,
        xh2h,
        rs2,
        hidh,
        gslope,
        upmh,
        upml,
        cols,
        bdmh,
        bdml,
        bdth,
        bdtl,
        accw,
        accf,
        tok,
        rmass,
        qkvs,
        probs,
        mbdh,
        mbdl,
        dbdh,
        dbdl,
        cmbh,
        cmbl,
        dmcol,
        vacc,
        gmacc,
        headacc,
        embacc,
        lossacc,
        qkvacc,
        points_ref,
        outbox,
        inbox,
        tally,
        send_sems,
        recv_sems,
        tally_send,
        tally_recv,
        sum_send,
        sum_recv,
        mats_sem,
        out_sems,
    ) = refs[: -5 * len(places["groups"])]
    boxes = refs[-5 * len(places["groups"]) :]
    half = heads // 2
    span = half * slices
    group = half * head_size
    pairs = heads // 2
    all_slices = heads * slices
    steps = points // tile
    scale = head_size ** (-0.5)
    mats_copy = pltpu.make_async_copy(mats_hbm, mats_ref, mats_sem)
    mats_copy.start()
    me, mine = lax.axis_index("pts"), lax.axis_index("grp")
    own_points = points // members

    def peer_points(hop):
        return lax.rem(me + hop, members)

    def peer_group(hop):
        return lax.rem(mine + hop, groups)

    barrier = pltpu.get_barrier_semaphore()
    for hop in range(1, members):
        pl.semaphore_signal(
            barrier, inc=1, device_id=(peer_points(hop), mine), device_id_type=MESH
        )
    for hop in range(1, groups):
        pl.semaphore_signal(
            barrier, inc=1, device_id=(me, peer_group(hop)), device_id_type=MESH
        )

    def same_plane(hop):
        other_y = lax.rem(lax.rem(me, 2) + hop // 2, 2)
        other_x = lax.rem(lax.div(mine, 2) + hop % 2, 2)
        return (lax.div(me, 2) * 2 + other_y, other_x * 2 + lax.rem(mine, 2))

    pl.semaphore_signal(barrier, inc=1, device_id=same_plane(3), device_id_type=MESH)

    slots = lax.broadcasted_iota(jnp.int32, (1, own_points), 1) + me * own_points
    surf_total = jnp.zeros((1, own_points), f32)
    vol_total = jnp.zeros((1, own_points), f32)
    blank = jnp.zeros((8 - fin - outc - 1, own_points), f32)
    for dest in range(members):
        for batch in range(grids):
            surf = bound_ref[batch, dest : dest + 1, :].astype(f32)
            goals = [goals_ref[batch, field, dest : dest + 1, :] for field in range(outc)]
            outbox[dest, batch * 8 : batch * 8 + 8, :] = jnp.concatenate(
                [coords_ref[batch, dest], *goals, surf, blank], 0
            )
            valid = jnp.where(slots < sizes_ref[batch, dest], 1.0, 0.0)
            surf_total = surf_total + valid * surf
            vol_total = vol_total + (valid - valid * surf)
    totals = jnp.concatenate(
        [surf_total, vol_total, jnp.zeros((6, own_points), f32)], 0
    )
    for dest in range(members):
        outbox[dest, grids * 8 :, :] = totals

    def piece(hop):
        other = peer_points(hop)
        return pltpu.make_async_remote_copy(
            src_ref=outbox.at[other],
            dst_ref=inbox.at[hop - 1],
            send_sem=send_sems.at[hop - 1],
            recv_sem=recv_sems.at[hop - 1],
            device_id=(other, mine),
            device_id_type=MESH,
        )

    def share(hop):
        return pltpu.make_async_remote_copy(
            src_ref=tally.at[0],
            dst_ref=tally.at[hop],
            send_sem=tally_send.at[hop - 1],
            recv_sem=tally_recv.at[hop - 1],
            device_id=(me, peer_group(hop)),
            device_id_type=MESH,
        )

    def greet():
        pl.semaphore_wait(barrier, members + groups - 1)
        for hop in range(1, members):
            piece(hop).start()


    def matrix_rows(layer, slot, half_index):
        spot = layer * 5 + SLOT_ORDER[slot]
        start = places["mats"] + (spot * (width // LANES) + half_index) * width
        return pl.ds(pl.multiple_of(start, width), width)

    def add_matrix(layer, slot, value):
        for index in range(width // LANES):
            packed[matrix_rows(layer, slot, index), :] += value[
                :, index * LANES : (index + 1) * LANES
            ]

    def read_matrix(layer, slot):
        return jnp.concatenate(
            [packed[matrix_rows(layer, slot, index), :] for index in range(width // LANES)], 1
        )

    def split_to(high_ref, low_ref, index, value):
        high, low = _split(value)
        high_ref[index] = high
        low_ref[index] = low
        return high, low

    vecs = vecs_ref[...]
    spare = jnp.zeros((LANES - vecs.shape[0], width), f32)
    standing = jnp.concatenate([vecs, spare], 0).T

    def column(row):
        return jnp.broadcast_to(standing[:, row : row + 1], (width, LANES))

    mats_copy.wait()
    for layer in range(layers):
        if layer == layers - 1:
            greet()
        base = 9 * layer
        gain_a, shift_a = column(base), column(base + 1)
        gain_b, shift_b = column(base + 5), column(base + 6)
        cols[layer, 0] = gain_a
        cols[layer, 1] = shift_a
        cols[layer, 2] = gain_b
        cols[layer, 3] = shift_b
        for slot in range(5):
            flipped = mats_ref[layer, slot].T
            bias = column(base + (2, 3, 4, 7, 8)[slot])
            if slot in (0, 1, 3):
                gain, shift, row = (gain_b, shift_b, 5) if slot == 3 else (gain_a, shift_a, 0)
                bias = bias + _doth(flipped, shift, NN)
                flipped = flipped * vecs[base + row : base + row + 1]
            cols[layer, 4 + slot] = bias
            split_to(upmh, upml, (layer, slot), flipped)
        tiled = jnp.concatenate([maps_ref[layer]] * half, 1)
        for part in range(2):
            lane = lax.broadcasted_iota(jnp.int32, (1, span), 1)
            sharp = jnp.full((1, span), 0.0, f32) + sharp_ref[layer, part * half]
            for head in range(1, half):
                sharp = jnp.where(lane >= head * slices, sharp_ref[layer, part * half + head], sharp)
            block = _block_heads(tiled / sharp, half, slices)
            split_to(bdth, bdtl, (layer, part), block)
            split_to(bdmh, bdml, (layer, part), block.T)

    vacc[...] = jnp.zeros_like(vacc)
    gmacc[...] = jnp.zeros_like(gmacc)
    headacc[...] = jnp.zeros_like(headacc)
    embacc[...] = jnp.zeros_like(embacc)
    lossacc[...] = jnp.zeros_like(lossacc)
    packed[...] = jnp.zeros_like(packed)
    qkvacc[...] = jnp.zeros_like(qkvacc)

    io_all = io_ref[...]
    rising = jnp.concatenate([io_all, jnp.zeros((LANES - io_all.shape[0], width), f32)], 0).T
    lift = [jnp.broadcast_to(rising[:, row : row + 1], (width, LANES)) for row in range(fin)]

    def window(step):
        return pl.ds(pl.multiple_of(step * tile, tile), tile)

    spots = [
        (grid, slice(step * tile, (step + 1) * tile), step)
        for step in range(steps)
        for grid in range(grids)
    ]

    def pair_of(high_ref, low_ref, index):
        return high_ref[index], low_ref[index]

    def settle(source, block):
        at = pl.ds(pl.multiple_of(source * own_points, own_points), own_points)
        for grid in range(grids):
            points_ref[grid, :, at] = block[grid * 8 : grid * 8 + 8]
        return block[grids * 8 :]

    held = settle(me, outbox[me])
    for hop in range(1, members):
        piece(hop).wait()
        held = held + settle(lax.rem(me + members - hop, members), inbox[hop - 1])
    tally[0] = held
    for hop in range(1, groups):
        share(hop).start()

    @pl.loop(0, steps)
    def _(step):
        at = window(step)
        for grid in range(grids):
            x = jnp.zeros((width, tile), f32)
            for row in range(fin):
                x = x + _wide(lift[row], tile) * points_ref[grid, row : row + 1, at]
            stream[grid, :, at] = x

    def front(layer, grid, at, step):
        xhat, rstd = _norm(stream[grid, :, at])
        xhat = _split(xhat)
        xh1h[layer, grid, :, at] = xhat[0]
        rs1[layer, grid, :, at] = rstd
        yield
        place = _dot3(pair_of(upmh, upml, (layer, 1)), xhat, NN)
        place = place + _wide(cols[layer, 5], tile)
        place = split_to(placeh, placel, (layer, grid, slice(None), at), place)
        feat = _dot3(pair_of(upmh, upml, (layer, 0)), xhat, NN)
        feat = feat + _wide(cols[layer, 4], tile)
        feat = split_to(feath, featl, (layer, grid, slice(None), at), feat)
        slots = lax.broadcasted_iota(jnp.int32, (1, tile), 1) + step * tile
        valid = jnp.where(slots < sizes_ref[grid, me], 1.0, 0.0)
        rows = [slice(part * group, (part + 1) * group) for part in range(2)]
        yield
        for part in range(2):
            here = (place[0][rows[part]], place[1][rows[part]])
            scores = _dot3(pair_of(bdmh, bdml, (layer, part)), here, NN)
            pieces = []
            for head in range(half):
                score = scores[head * slices : (head + 1) * slices]
                expo = jnp.exp(score - jnp.max(score, 0, keepdims=True))
                weight = expo * (valid / jnp.sum(expo, 0, keepdims=True))
                start = part * span + head * slices
                wrows = slice(start, start + slices)
                pieces.append(split_to(wgth, wgtl, (layer, grid, wrows, at), weight))
            yield
            weight = tuple(jnp.concatenate(list(side), 0) for side in zip(*pieces))
            lead = jnp.concatenate([feat[0][rows[part]], jnp.ones((16, tile), bf16)], 0)
            accw[grid, part] += _dot(
                jnp.concatenate([lead, lead], 1), jnp.concatenate(weight, 1), NT
            )
            accf[grid, part] += _dot(feat[1][rows[part]], weight[0], NT)
        yield

    def attend(layer, grid):
        parts, masses = [], []
        for part in range(2):
            total = accw[grid, part]
            parts.append(_diag_heads(total[:group] + accf[grid, part], head_size, slices))
            masses.append(total[group : group + 1])
        rate = 1.0 / (jnp.concatenate(masses, 1) + 1e-05)
        tokens = jnp.concatenate(parts, 1) * rate
        tok[layer, grid] = tokens
        rmass[layer, grid] = rate
        yield
        joined = _doth(qkv_ref[layer], tokens, TN)
        qkvs[layer, grid] = joined
        yield
        lane = lax.broadcasted_iota(jnp.int32, (slices, 2 * slices), 1)
        mixed = []
        for pair in range(pairs):
            at = slice(pair * 2 * slices, (pair + 1) * 2 * slices)
            query = joined[:head_size, at]
            key = joined[head_size : 2 * head_size, at]
            value = joined[2 * head_size :, at]
            full = _doth(key, query, TN)
            scores = jnp.where(lane < slices, full[:slices], full[slices:]) * scale
            expo = jnp.exp(scores - jnp.max(scores, 0, keepdims=True))
            prob = expo / jnp.sum(expo, 0, keepdims=True)
            probs[layer, grid, pair] = prob
            mixed.append(_doth(value, _block_heads(prob, 2, slices), NN))
        for part in range(2):
            flat = jnp.concatenate(mixed[part * (pairs // 2) : (part + 1) * (pairs // 2)], 1)
            block = _block_heads(flat, half, slices)
            split_to(mbdh, mbdl, (layer, grid, part), block)
        yield

    def rest(layer, grid, at):
        pieces = []
        for part in range(2):
            rows = slice(part * group, (part + 1) * group)
            wrows = slice(part * span, (part + 1) * span)
            weight = pair_of(wgth, wgtl, (layer, grid, wrows, at))
            spread = _dot3(pair_of(mbdh, mbdl, (layer, grid, part)), weight, NN)
            pieces.append(split_to(sprh, sprl, (layer, grid, rows, at), spread))
        spread = tuple(jnp.concatenate(list(side), 0) for side in zip(*pieces))
        yield
        moved = _dot3(pair_of(upmh, upml, (layer, 2)), spread, NN)
        x = stream[grid, :, at] + moved + _wide(cols[layer, 6], tile)
        stream[grid, :, at] = x
        xhat, rstd = _norm(x)
        xhat = _split(xhat)
        xh2h[layer, grid, :, at] = xhat[0]
        rs2[layer, grid, :, at] = rstd
        yield
        inner = _dot3(pair_of(upmh, upml, (layer, 3)), xhat, NN)
        pieces = []
        for start in range(0, width, BLOCK):
            rows = slice(start, start + BLOCK)
            value = inner[rows] + _wide(cols[layer, 7, rows], tile)
            cdf = 0.5 + 0.5 * lax.erf(value * (0.5**0.5))
            slope = cdf + value * jnp.exp(-0.5 * value * value) * ((2.0 * math.pi) ** -0.5)
            gslope[layer, grid, rows, at] = slope.astype(bf16)
            pieces.append(_split(value * cdf))
            hidh[layer, grid, rows, at] = pieces[-1][0]
        hidden = tuple(jnp.concatenate(list(side), 0) for side in zip(*pieces))
        yield
        moved = _dot3(pair_of(upmh, upml, (layer, 4)), hidden, NN)
        stream[grid, :, at] = stream[grid, :, at] + moved + _wide(cols[layer, 8], tile)
        yield

    @pl.loop(0, layers)
    def _(layer):
        accw[...] = jnp.zeros_like(accw)
        accf[...] = jnp.zeros_like(accf)

        _lockstep([front(layer, *spot) for spot in spots])

        _lockstep([attend(layer, grid) for grid in range(grids)])

        _lockstep([rest(layer, *spot[:2]) for spot in spots])

    tail = 9 * layers
    head_rows = jnp.concatenate(
        [io_ref[fin:, :], jnp.zeros((8 - outc, width), f32)], 0
    )
    head_gain = head_rows * vecs[tail : tail + 1]
    head_pair = _split(head_gain)
    head_bias = _dotx(head_rows, column(tail + 1), NN)
    counted = tally[0]
    for hop in range(1, groups):
        share(hop).wait()
        counted = counted + tally[hop]
    counted = jnp.broadcast_to(jnp.sum(counted, 1, keepdims=True), counted.shape)
    counted = 1.0 / jnp.maximum(counted, 1.0)
    inv_surf, inv_vol = _wide(counted[:1], tile), _wide(counted[1:2], tile)

    def crown(grid, at, step):
        xhat, rstd = _norm(stream[grid, :, at])
        halves = _split(xhat)
        pred = _dot3(head_pair, halves, NN) + _wide(head_bias, tile)
        slots = lax.broadcasted_iota(jnp.int32, (1, tile), 1) + step * tile
        valid = jnp.where(slots < sizes_ref[grid, me], 1.0, 0.0)
        surf = valid * points_ref[grid, fin + outc : fin + outc + 1, at]
        vol = (valid - surf) * inv_vol
        surf = surf * inv_surf
        row = lax.broadcasted_iota(jnp.int32, (8, tile), 0)
        factor = jnp.where(row == 0, surf, jnp.where(row < outc, vol, 0.0))
        goals = jnp.concatenate(
            [points_ref[grid, fin : fin + outc, at], jnp.zeros((8 - outc, tile), f32)], 0
        )
        error = pred - goals
        scaled = factor * error
        lossacc[...] += _fold(scaled * error)
        dpred = scaled + scaled
        headacc[0] += _fold(dpred)
        dhalves = _split(dpred)
        headacc_rows = _dot3(dhalves, halves, NT)
        for start in range(0, width, LANES):
            headacc[1 + start // LANES] += headacc_rows[:, start : start + LANES]
        yield
        grad = _dot3(head_pair, dhalves, TN)
        stream[grid, :, at] = _norm_back(grad, xhat, rstd)
        yield

    _lockstep([crown(*spot) for spot in spots])

    for layer in range(layers):
        for slot in range(5):
            mat = mats_ref[layer, slot]
            if slot in (0, 1, 3):
                mat = mat * _wide(cols[layer, 2 if slot == 3 else 0], width)
            split_to(upmh, upml, (layer, slot), mat)

    def back_rest(layer, grid, at):
        grad = stream[grid, :, at]
        vacc[layer, 4] += _fold(grad)
        pieces = grad.astype(bf16)
        yield
        dhid = _dot(upmh[layer, 4], pieces, NN)
        dinner = dhid * gslope[layer, grid, :, at].astype(f32)
        vacc[layer, 3] += _fold(dinner)
        dinner = dinner.astype(bf16)
        add_matrix(layer, 4, _dot(hidh[layer, grid, :, at], pieces, NT))
        yield
        xhat = xh2h[layer, grid, :, at]
        dxhat = _dot(upmh[layer, 3], dinner, NN)
        grad = grad + _norm_back(dxhat, xhat.astype(f32), rs2[layer, grid, :, at])
        stream[grid, :, at] = grad
        vacc[layer, 2] += _fold(grad)
        pieces = _split(grad)
        add_matrix(layer, 3, _dot(xhat, dinner, NT))
        yield
        dspread = _dot3(pair_of(upmh, upml, (layer, 2)), pieces, NN)
        spread = pair_of(sprh, sprl, (layer, grid, slice(None), at))
        gram = _dot3(spread, pieces, NT)
        dspread = split_to(sprh, sprl, (layer, grid, slice(None), at), dspread)
        add_matrix(layer, 2, gram)
        yield
        for part in range(2):
            rows = slice(part * group, (part + 1) * group)
            wrows = slice(part * span, (part + 1) * span)
            weight = pair_of(wgth, wgtl, (layer, grid, wrows, at))
            accf[grid, part] += _dot3((dspread[0][rows], dspread[1][rows]), weight, NT)
        yield

    def back_attend(layer, grid):
        joined = qkvs[layer, grid]
        tokens = tok[layer, grid]
        rate = rmass[layer, grid]
        lane = lax.broadcasted_iota(jnp.int32, (slices, 2 * slices), 1)
        dmixed = jnp.concatenate(
            [_diag_heads(accf[grid, part], head_size, slices) for part in range(2)], 1
        )
        yield
        dqs, dks, dvs = [], [], []
        for pair in range(pairs):
            at = slice(pair * 2 * slices, (pair + 1) * 2 * slices)
            query = joined[:head_size, at]
            key = joined[head_size : 2 * head_size, at]
            value = joined[2 * head_size :, at]
            prob = probs[layer, grid, pair]
            dmix = dmixed[:, at]
            full = _doth(value, dmix, TN)
            dprob = jnp.where(lane < slices, full[:slices], full[slices:])
            dscore = (
                prob * (dprob - jnp.sum(prob * dprob, 0, keepdims=True)) * scale
            )
            dblock = _block_heads(dscore, 2, slices)
            dvs.append(_doth(dmix, _block_heads(prob, 2, slices), NT))
            dqs.append(_doth(key, dblock, NN))
            dks.append(_doth(query, dblock, NT))
        dqkv = jnp.concatenate(
            [jnp.concatenate(part, 1) for part in (dqs, dks, dvs)], 0
        )
        yield
        dtok = _doth(qkv_ref[layer], dqkv, NN)
        qkvacc[layer] += _doth(tokens, dqkv, NT)
        dweighted = dtok * rate
        dmass = -jnp.sum(dweighted * tokens, 0, keepdims=True)
        yield
        dmcol[grid] = jnp.broadcast_to(dmass, (LANES, all_slices)).T
        for part in range(2):
            block = _block_heads(dweighted[:, part * span : (part + 1) * span], half, slices)
            split_to(dbdh, dbdl, (grid, part), block)
            mix = mbdh[layer, grid, part].astype(f32) + mbdl[layer, grid, part].astype(f32)
            both = jnp.concatenate([mix, block], 0)
            split_to(cmbh, cmbl, (grid, part), both.T)
        yield

    def back_feat(layer, grid, at):
        pieces = []
        for part in range(2):
            rows = slice(part * group, (part + 1) * group)
            wrows = slice(part * span, (part + 1) * span)
            weight = pair_of(wgth, wgtl, (layer, grid, wrows, at))
            dfeat = _dot3(pair_of(dbdh, dbdl, (grid, part)), weight, NN)
            vacc[layer, 0, rows] += _fold(dfeat)
            pieces.append(split_to(hidh, gslope, (layer, grid, rows, at), dfeat)[0])
        yield
        gram = _dot(xh1h[layer, grid, :, at], jnp.concatenate(pieces, 0), NT)
        add_matrix(layer, 0, gram)
        yield

    def back_front(layer, grid, at):
        feat = pair_of(feath, featl, (layer, grid, slice(None), at))
        place = pair_of(placeh, placel, (layer, grid, slice(None), at))
        dplaces = []
        for part in range(2):
            rows = slice(part * group, (part + 1) * group)
            wrows = slice(part * span, (part + 1) * span)
            weight = pair_of(wgth, wgtl, (layer, grid, wrows, at))
            dspread = pair_of(sprh, sprl, (layer, grid, rows, at))
            both = tuple(
                jnp.concatenate([one, two[rows]], 0) for one, two in zip(dspread, feat)
            )
            dweights = _dot3(pair_of(cmbh, cmbl, (grid, part)), both, NN)
            pieces = []
            for head in range(half):
                at_head = slice(head * slices, (head + 1) * slices)
                start = part * span + head * slices
                dweight = dweights[at_head] + _wide(dmcol[grid, start : start + slices], tile)
                full = weight[0][at_head].astype(f32) + weight[1][at_head].astype(f32)
                prod = full * dweight
                pieces.append(_split(prod - full * jnp.sum(prod, 0, keepdims=True)))
            pieces = tuple(jnp.concatenate(list(side), 0) for side in zip(*pieces))
            yield
            dplace = _dot3(pair_of(bdth, bdtl, (layer, part)), pieces, NN)
            vacc[layer, 1, rows] += _fold(dplace)
            dplaces.append(_split(dplace))
            gmacc[layer, part] += _dot3((place[0][rows], place[1][rows]), pieces, NT)
        dplace = tuple(jnp.concatenate(list(side), 0) for side in zip(*dplaces))
        yield
        xhat = xh1h[layer, grid, :, at]
        dfeat = pair_of(hidh, gslope, (layer, grid, slice(None), at))
        dxhat = _dot3(pair_of(upmh, upml, (layer, 0)), dfeat, NN) + _dot3(
            pair_of(upmh, upml, (layer, 1)), dplace, NN
        )
        grad = stream[grid, :, at] + _norm_back(
            dxhat, xhat.astype(f32), rs1[layer, grid, :, at]
        )
        first = isinstance(layer, int) and layer == 0
        if not first:
            stream[grid, :, at] = grad
        add_matrix(layer, 1, _dot(xhat, dplace[0], NT))
        yield
        if first:
            coords = jnp.concatenate(
                [points_ref[grid, :fin, at], jnp.zeros((8 - fin, tile), f32)], 0
            )
            embacc[...] += _dot3(_split(coords), _split(grad), NT)
        yield

    def to_row(folded):
        return _row_sums(folded)

    def put_vector(row, value, add=False):
        for index in range(width // LANES):
            start = places["vecs"] + index * places["vecs_stride"] + row
            piece = value[:, index * LANES : (index + 1) * LANES]
            if add:
                piece = piece + packed[start : start + 1, :]
            packed[start : start + 1, :] = piece

    def close_matrix(layer, slot, bias_sum):
        gain, shift = (2, 3) if slot == 3 else (0, 1)
        gram = read_matrix(layer, slot)
        mat = mats_ref[layer, slot]
        value = (
            _wide(cols[layer, gain], width) * gram + _wide(cols[layer, shift], width) * bias_sum
        )
        for index in range(width // LANES):
            packed[matrix_rows(layer, slot, index), :] = value[
                :, index * LANES : (index + 1) * LANES
            ]
        shift_row = _doth(jnp.broadcast_to(bias_sum, (8, width)), mat, NT)[:1]
        return _row_sums(gram * mat), shift_row

    def close_rest(layer):
        base = 9 * layer
        middle, inner, final = [to_row(vacc[layer, slot]) for slot in (2, 3, 4)]
        gain_row, shift_row = close_matrix(layer, 3, inner)
        for offset, row in ((4, middle), (5, gain_row), (6, shift_row), (7, inner), (8, final)):
            put_vector(base + offset, row)

    def close_feat(layer):
        total = to_row(vacc[layer, 0])
        gain, shift = close_matrix(layer, 0, total)
        put_vector(9 * layer, gain)
        put_vector(9 * layer + 1, shift)
        put_vector(9 * layer + 2, total)

    def close_front(layer):
        base = 9 * layer
        place_sum = to_row(vacc[layer, 1])
        place_gain, place_shift = close_matrix(layer, 1, place_sum)
        put_vector(base, place_gain, True)
        put_vector(base + 1, place_shift, True)
        put_vector(base + 3, place_sum)
        tiled = jnp.concatenate([maps_ref[layer]] * half, 1)
        total = None
        sharp_total = None
        for part in range(2):
            lane = lax.broadcasted_iota(jnp.int32, (1, span), 1)
            sharp = jnp.full((1, span), 0.0, f32) + sharp_ref[layer, part * half]
            for head in range(1, half):
                sharp = jnp.where(
                    lane >= head * slices, sharp_ref[layer, part * half + head], sharp
                )
            picked = _diag_heads(gmacc[layer, part], head_size, slices) / sharp
            total = picked if total is None else total + picked
            share = -jnp.sum(picked * tiled, 0, keepdims=True) / sharp
            chosen = jnp.where(
                lax.broadcasted_iota(jnp.int32, (span, LANES), 0) // slices + part * half
                == lax.broadcasted_iota(jnp.int32, (span, LANES), 1),
                1.0,
                0.0,
            )
            share = _dotx(jnp.broadcast_to(share, (8, span)), chosen, NN)
            sharp_total = share if sharp_total is None else sharp_total + share
        start = places["sharp"] + layer
        packed[start : start + 1, :heads] = sharp_total[:1, :heads]
        total = _fold(total)
        total = total + pltpu.roll(total, slices, 1)
        start = places["maps"] + layer * head_size
        packed[start : start + head_size, :slices] = total[:, :slices]
        start = places["qkv"] + layer * head_size
        packed[start : start + head_size, : 3 * head_size] = qkvacc[layer]

    def close_head():
        spread_dpred = _dotx(headacc[0], jnp.ones((LANES, LANES), f32), NN)
        gram = jnp.concatenate([headacc[1 + k] for k in range(width // LANES)], 1)
        gain_row, shift_row = vecs[tail : tail + 1], vecs[tail + 1 : tail + 2]
        head_grad = gram * gain_row + _wide(spread_dpred, width) * shift_row
        for index in range(width // LANES):
            at = slice(index * LANES, (index + 1) * LANES)
            start = places["io"] + index * places["io_stride"]
            packed[start + fin : start + fin + outc, :] = head_grad[:outc, at]
        put_vector(tail, jnp.sum(gram * head_rows, 0, keepdims=True))
        put_vector(
            tail + 1, jnp.sum(_wide(spread_dpred, width) * head_rows, 0, keepdims=True)
        )
        packed[places["loss"] : places["loss"] + 1, :] = jnp.broadcast_to(
            jnp.sum(jnp.sum(lossacc[...], 0, keepdims=True), 1, keepdims=True), (1, LANES)
        )

    def close_embed():
        for index in range(width // LANES):
            at = slice(index * LANES, (index + 1) * LANES)
            start = places["io"] + index * places["io_stride"]
            packed[start : start + fin, :] = embacc[:fin, at]

    stages = [
        sum_stages(
            packed,
            summed,
            entry,
            boxes[5 * index : 5 * index + 5],
            sum_send.at[index],
            sum_recv.at[index],
            members // 2,
        )
        for index, entry in enumerate(places["groups"])
    ]
    squares[...] = jnp.zeros_like(squares)

    def handed(index):
        start, number = places["groups"][index]
        rows = slice(start, start + number)
        return pltpu.make_async_copy(summed.at[rows], summed_hbm.at[rows], out_sems.at[index])

    def hand_over(index):
        start, number = places["groups"][index]
        handed(index).start()

        @pl.loop(0, number // 256)
        def _(step):
            block = summed[pl.ds(pl.multiple_of(start + step * 256, 256), 256), :]
            if index == 0:
                row = lax.broadcasted_iota(jnp.int32, block.shape, 0) + step * 256
                block = jnp.where(row == places["loss"], 0.0, block)
            squares[...] += jnp.sum((block * block).reshape(32, 8, LANES), 0)

    def wrapped(index):
        def finish_group():
            stages_end[index]()
            hand_over(index)

        return finish_group

    stages_end = [entry[6] for entry in stages]
    stages = [(*entry[:6], wrapped(index)) for index, entry in enumerate(stages)]

    def run(spots):
        for set_index, number in spots:
            stages[set_index][number]()

    def hooks(phase, layer, step):
        found = PLAN.get((phase, layer, step), {})
        return [
            [stages[s][n] for s, n in found.get(turn, ())] for turn in range(max(found, default=-1) + 1)
        ]

    def woven(phase, maker, layer):
        _lockstep([maker(layer, *spot[:2]) for spot in spots], hooks(phase, layer, 0))

    for layer in range(layers - 1, -1, -1):
        accf[...] = jnp.zeros_like(accf)
        woven("rest", back_rest, layer)
        close_rest(layer)
        run(AFTER_REST[layer])
        _lockstep(
            [back_attend(layer, grid) for grid in range(grids)], hooks("attend", layer, 0)
        )
        woven("feat", back_feat, layer)
        close_feat(layer)
        run(AFTER_FEAT[layer])
        if layer:
            close_head()
        woven("front", back_front, layer)
        close_front(layer)
        if layer == 0:
            close_embed()
        run(AFTER_FRONT[layer])

    for index in range(len(stages)):
        handed(index).wait()


def _round_up(value, unit):
    return (value + unit - 1) // unit * unit


def packed_places(layers, width, io_rows, vec_rows, head_size):
    halves = width // LANES
    places = {"io_stride": _round_up(io_rows, 8), "vecs_stride": _round_up(vec_rows, 8)}
    row = 0
    for name, rows in (
        ("io", halves * places["io_stride"]),
        ("vecs", halves * places["vecs_stride"]),
        ("maps", layers * head_size),
        ("qkv", layers * head_size),
        ("sharp", _round_up(layers, 8)),
        ("loss", 8),
    ):
        places[name] = row
        row += rows
    places["mats"] = _round_up(row, 256)
    each = halves * width
    first = places["mats"] + each
    groups = [(0, first), (first, each), (first + each, 3 * each)]
    for layer in range(1, layers):
        start = places["mats"] + layer * 5 * each
        groups += [(start, 2 * each), (start + 2 * each, 3 * each)]
    places["groups"] = groups
    places["rows"] = places["mats"] + layers * 5 * each
    return places


def group_parts(rows):
    half = rows // 2
    a_rows = (half * 2 // 3 + 64) // 128 * 128
    return half, a_rows, half - a_rows


def sum_stages(packed, out, span, boxes, send_sems, recv_sems, floors):
    first, rows = span
    half, a_rows, b_rows = group_parts(rows)
    core_in, a_one, a_two, b_one, b_two = boxes
    a_four, b_four, a_all, b_all = a_rows // 4, b_rows // 4, a_rows // 16, b_rows // 16
    point, group = lax.axis_index("pts"), lax.axis_index("grp")
    y, z = lax.rem(point, 2), lax.div(point, 2)
    core, x = lax.rem(group, 2), lax.div(group, 2)
    plane = x + 2 * y
    base = first + core * half
    hops = (1, 2, 3)

    def plane_peer(hop):
        other_x, other_y = lax.rem(x + hop % 2, 2), lax.rem(y + hop // 2, 2)
        return (z * 2 + other_y, other_x * 2 + core), other_x + 2 * other_y

    def line_peer(hop):
        other = lax.rem(z + hop, floors)
        return (other * 2 + y, group), other

    partner = (point, x * 2 + (1 - core))

    def rows_at(start, count):
        return pl.ds(pl.multiple_of(start, 8), count)

    def send(number, source, target, device):
        return pltpu.make_async_remote_copy(
            src_ref=source,
            dst_ref=target,
            send_sem=send_sems.at[number],
            recv_sem=recv_sems.at[number],
            device_id=device,
            device_id_type=MESH,
        )

    def place(start, count):
        return packed.at[rows_at(start, count)]

    def cross():
        return send(0, place(first + (1 - core) * half, half), core_in, partner)

    def a1(hop):
        device, spot = plane_peer(hop)
        return send(hop, place(base + spot * a_four, a_four), a_one.at[hop - 1], device)

    def b1(hop):
        device, spot = line_peer(hop)
        source = place(base + a_rows + spot * b_four, b_four)
        return send(3 + hop, source, b_one.at[hop - 1], device)

    a_part = rows_at(base + plane * a_four, a_four)
    b_part = rows_at(base + a_rows + z * b_four, b_four)
    a_piece = rows_at(base + plane * a_four + z * a_all, a_all)
    b_piece = rows_at(base + a_rows + z * b_four + plane * b_all, b_all)

    def a2(hop):
        device, spot = line_peer(hop)
        source = place(base + plane * a_four + spot * a_all, a_all)
        return send(6 + hop, source, a_two.at[hop - 1], device)

    def b2(hop):
        device, spot = plane_peer(hop)
        source = place(base + a_rows + z * b_four + spot * b_all, b_all)
        return send(9 + hop, source, b_two.at[hop - 1], device)

    def a3(hop):
        return send(12 + hop, out.at[a_piece], out.at[a_piece], line_peer(hop)[0])

    def b3(hop):
        return send(15 + hop, out.at[b_piece], out.at[b_piece], plane_peer(hop)[0])

    def a4(hop):
        return send(18 + hop, out.at[a_part], out.at[a_part], plane_peer(hop)[0])

    def b4(hop):
        return send(21 + hop, out.at[b_part], out.at[b_part], line_peer(hop)[0])

    def last():
        own = out.at[rows_at(base, half)]
        return send(25, own, own, partner)

    def arrive(make):
        for hop in hops:
            make(hop).wait_recv()

    def depart(make):
        for hop in hops:
            make(hop).start()

    def stage_cross():
        cross().start()

    def stage_first():
        cross().wait_recv()
        own = rows_at(base, half)
        packed[own, :] = packed[own, :] + core_in[...]
        depart(a1)
        depart(b1)

    def stage_second():
        arrive(a1)
        packed[a_part, :] = packed[a_part, :] + a_one[0] + a_one[1] + a_one[2]
        depart(a2)
        arrive(b1)
        packed[b_part, :] = packed[b_part, :] + b_one[0] + b_one[1] + b_one[2]
        depart(b2)

    def stage_third():
        arrive(a2)
        out[a_piece, :] = packed[a_piece, :] + a_two[0] + a_two[1] + a_two[2]
        depart(a3)
        arrive(b2)
        out[b_piece, :] = packed[b_piece, :] + b_two[0] + b_two[1] + b_two[2]
        depart(b3)

    def stage_fourth():
        arrive(a3)
        depart(a4)
        arrive(b3)
        depart(b4)

    def stage_fifth():
        arrive(a4)
        arrive(b4)
        last().start()

    def stage_end():
        last().wait_recv()
        cross().wait_send()
        last().wait_send()
        for make in (a1, b1, a2, b2, a3, b3, a4, b4):
            for hop in hops:
                make(hop).wait_send()

    return (
        stage_cross,
        stage_first,
        stage_second,
        stage_third,
        stage_fourth,
        stage_fifth,
        stage_end,
    )


def update_kernel(dims, *refs):
    layers, slots, width, places = dims
    summed, squares = refs[:2]
    weights, means, seconds = refs[2:8], refs[8:14], refs[14:20]
    loss_out, norm_out = refs[20:22]
    firsts, news, fresh = refs[22:40:3], refs[23:40:3], refs[24:40:3]
    grads, state, results, in_sems, out_sems = refs[40:]
    halves = width // LANES
    each = halves * width
    count = layers * slots

    def incoming(index):
        layer, slot = index // slots, index % slots
        start = places["mats"] + (layer * slots + SLOT_ORDER[slot]) * each
        sources = [summed.at[start : start + each]]
        targets = [grads.at[places["mats"] + index * each : places["mats"] + (index + 1) * each]]
        for kind, array in enumerate((weights[1], means[1], seconds[1])):
            sources.append(array.at[layer, slot])
            targets.append(state.at[kind, index])
        return [
            pltpu.make_async_copy(source, target, in_sems.at[index, number])
            for number, (source, target) in enumerate(zip(sources, targets))
        ]

    def outgoing(index):
        layer, slot = index // slots, index % slots
        return [
            pltpu.make_async_copy(
                results.at[kind, index], array.at[layer, slot], out_sems.at[index, kind]
            )
            for kind, array in enumerate((firsts[1], news[1], fresh[1]))
        ]

    small = pltpu.make_async_copy(
        summed.at[: places["mats"]], grads.at[: places["mats"]], in_sems.at[count, 0]
    )
    for index in range(count):
        for copy in incoming(index):
            copy.start()
    small.start()
    total = jnp.sum(jnp.sum(squares[...], 0, keepdims=True), 1, keepdims=True)
    norm = jnp.sqrt(total)
    factor = jnp.minimum(1.0, clip_limit / norm)
    norm_out[...] = norm
    for index in range(count):
        for copy in incoming(index):
            copy.wait()
        start = places["mats"] + index * each
        grad = jnp.concatenate(
            [grads[start + k * width : start + (k + 1) * width, :] for k in range(halves)], 1
        )
        first_new, second_new, weight_new = adamw_update(
            state[0, index], grad * factor, state[1, index], state[2, index]
        )
        results[0, index] = first_new
        results[1, index] = second_new
        results[2, index] = weight_new
        for copy in outgoing(index):
            copy.start()
    small.wait()

    def apply(index, grad):
        first_new, second_new, weight_new = adamw_update(
            weights[index][...], grad * factor, means[index][...], seconds[index][...]
        )
        firsts[index][...] = first_new
        news[index][...] = second_new
        fresh[index][...] = weight_new

    def rows(name, start, number):
        first = places[name] + start
        return grads[first : first + number, :]

    loss_out[...] = rows("loss", 0, 1)[:, :1]
    for index, name in ((0, "io"), (5, "vecs")):
        stride, number = places[name + "_stride"], weights[index].shape[0]
        apply(
            index,
            jnp.concatenate([rows(name, k * stride, number) for k in range(halves)], 1),
        )
    for index, name in ((2, "maps"), (3, "qkv")):
        _, number, lanes = weights[index].shape
        apply(
            index,
            jnp.stack([rows(name, k * number, number)[:, :lanes] for k in range(layers)]),
        )
    number, lanes = weights[4].shape
    apply(4, rows("sharp", 0, number)[:, :lanes])
    for index in range(count):
        for copy in outgoing(index):
            copy.wait()


def update_all(summed, squares, network_state, running_means, running_squares, places):
    layers, slots, width, _ = network_state[1].shape
    vmem = pl.BlockSpec(memory_space=pltpu.VMEM)
    hbm = pl.BlockSpec(memory_space=pl.ANY)
    state_specs = [hbm if index == 1 else vmem for index in range(6)]
    shapes = [jax.ShapeDtypeStruct((1, 1), f32)] * 2
    specs = [vmem] * 2
    for index, entry in enumerate(network_state):
        shapes += [jax.ShapeDtypeStruct(entry.shape, f32)] * 3
        specs += [hbm if index == 1 else vmem] * 3
    count = layers * slots
    kept = pltpu.VMEM((3, count, width, width), f32)
    results = pl.pallas_call(
        functools.partial(update_kernel, (layers, slots, width, places)),
        out_shape=shapes,
        in_specs=[hbm, vmem] + state_specs * 3,
        out_specs=specs,
        scratch_shapes=[
            pltpu.VMEM((places["rows"], LANES), f32),
            kept,
            kept,
            pltpu.SemaphoreType.DMA((count + 1, 4)),
            pltpu.SemaphoreType.DMA((count, 3)),
        ],
        compiler_params=pltpu.CompilerParams(vmem_limit_bytes=VMEM_BYTES),
    )(summed, squares, *network_state, *running_means, *running_squares)
    return (results[0].reshape(()), results[1].reshape(()), *results[2:])


def whole_grid_grads(network_state, coords, goals, bound, sizes, places, mesh_sizes):
    io_rows, mats, maps, qkv, sharp, vecs = network_state
    members, groups = mesh_sizes
    grids, own, _, own_points = coords.shape
    points = own_points * members
    layers, _, width, _ = mats.shape
    heads = sharp.shape[1]
    head_size, slices = maps.shape[1:]
    outc = io_rows.shape[0] - FIN
    tile = TILE
    half, span, group = heads // 2, heads // 2 * slices, heads // 2 * head_size
    dims = (grids, points, width, heads, head_size, slices, layers, FIN, outc, tile)
    dims = dims + (members, groups, places)

    def both(*shape):
        return [pltpu.VMEM(shape, bf16), pltpu.VMEM(shape, bf16)]

    def single(*shape):
        return [pltpu.VMEM(shape, f32)]

    kept = (layers, grids, width, points)
    box = (members, grids * 8 + 8, own_points)
    scratch = (
        single(layers, 5, width, width)
        + single(places["rows"], LANES)
        + single(places["rows"], LANES)
        + single(grids, width, points)
        + [pltpu.VMEM(kept, bf16)]
        + single(layers, grids, 1, points)
        + both(*kept)
        + both(*kept)
        + both(layers, grids, 2 * span, points)
        + both(*kept)
        + [pltpu.VMEM(kept, bf16)]
        + single(layers, grids, 1, points)
        + [pltpu.VMEM(kept, bf16)] * 2
        + both(layers, 5, width, width)
        + single(layers, 9, width, LANES)
        + both(layers, 2, span, group)
        + both(layers, 2, group, span)
        + single(grids, 2, group + 16, span)
        + single(grids, 2, group, span)
        + single(layers, grids, head_size, 2 * span)
        + single(layers, grids, 1, 2 * span)
        + single(layers, grids, 3 * head_size, 2 * span)
        + single(layers, grids, half, slices, 2 * slices)
        + both(layers, grids, 2, group, span)
        + both(grids, 2, group, span)
        + both(grids, 2, span, 2 * group)
        + single(grids, 2 * span, LANES)
        + single(layers, 5, width, LANES)
        + single(layers, 2, group, span)
        + single(1 + width // LANES, 8, LANES)
        + single(8, width)
        + single(8, LANES)
        + single(layers, head_size, 3 * head_size)
        + single(grids, 8, points)
        + single(*box)
        + single(members - 1, *box[1:])
        + single(groups, 8, own_points)
        + [pltpu.SemaphoreType.DMA((members - 1,))] * 2
        + [pltpu.SemaphoreType.DMA((groups - 1,))] * 2
        + [pltpu.SemaphoreType.DMA((len(places["groups"]), 26))] * 2
        + [pltpu.SemaphoreType.DMA, pltpu.SemaphoreType.DMA((len(places["groups"]),))]
    )
    for _, rows in places["groups"]:
        half_rows, a_rows, b_rows = group_parts(rows)
        scratch += single(half_rows, LANES)
        for part_rows in (a_rows, b_rows):
            scratch += single(3, part_rows // 4, LANES) + single(3, part_rows // 16, LANES)
    vmem = pl.BlockSpec(memory_space=pltpu.VMEM)
    smem = pl.BlockSpec(memory_space=pltpu.SMEM)
    hbm = pl.BlockSpec(memory_space=pl.ANY)
    return pl.pallas_call(
        functools.partial(grids_kernel, dims),
        out_shape=[
            jax.ShapeDtypeStruct((places["rows"], LANES), f32),
            jax.ShapeDtypeStruct((8, LANES), f32),
        ],
        in_specs=[smem] * 2 + [vmem] * 4 + [hbm] + [vmem] * 3,
        out_specs=[hbm, vmem],
        scratch_shapes=scratch,
        compiler_params=pltpu.CompilerParams(
            collective_id=0, has_side_effects=True, vmem_limit_bytes=VMEM_BYTES
        ),
    )(sizes, sharp, coords, jnp.swapaxes(goals, 1, 2), bound, io_rows, mats, maps, qkv, vecs)


def body_grids(mesh_sizes, *arrays):
    network_state = arrays[4:10]
    io_rows, mats, maps, _, _, vecs = network_state
    places = packed_places(
        mats.shape[0], mats.shape[2], io_rows.shape[0], vecs.shape[0], maps.shape[1]
    )
    summed, squares = whole_grid_grads(network_state, *arrays[:4], places, mesh_sizes)
    return update_all(
        summed, squares, network_state, arrays[10:16], arrays[16:22], places
    )


def solution(mesh):
    in_specs = (
        P(None, "grp", None, "pts"),
        P(None, "grp", None, "pts"),
        P(None, "grp", "pts"),
        P(None, "grp"),
        P(),
        P(),
        P(),
        P(),
        P(),
        P(),
        P(),
        P(),
        P(),
        P(),
        P(),
        P(),
        P(),
        P(),
        P(),
        P(),
        P(),
        P(),
    )
    out_specs = (
        P(),
        P(),
        P(),
        P(),
        P(),
        P(),
        P(),
        P(),
        P(),
        P(),
        P(),
        P(),
        P(),
        P(),
        P(),
        P(),
        P(),
        P(),
        P(),
        P(),
    )
    members, groups = mesh.shape["pts"], mesh.shape["grp"]

    def body(*arrays):
        batches, own, _, own_points = arrays[0].shape
        fits = own == members and batches * own_points * members <= 2048
        if fits and own_points == LANES and (members, groups) == (8, 4) and arrays[5].shape[0] == 2:
            return body_grids((members, groups), *arrays)
        return body_points(*arrays)

    return jax.shard_map(body, mesh=mesh, in_specs=in_specs, out_specs=out_specs, check_vma=False)
```

```python
import functools
import math

import jax
import jax.numpy as jnp
from jax import lax
from jax.experimental import pallas as pl
from jax.experimental.pallas import tpu as pltpu
from jax.sharding import PartitionSpec as P

STEP = 10
LANES = 128
FIN = 2
TILE = 512
SLOT_ORDER = (1, 0, 2, 3, 4)
BLOCK = 64
PLAN = {
    ("attend", 0, 0): {4: ((2, 1),)},
    ("front", 0, 0): {3: ((1, 1), (2, 2), (3, 3))},
}
AFTER_REST = {1: ((4, 0),), 0: ((2, 0), (4, 3), (3, 1))}
AFTER_FEAT = {1: ((4, 1),), 0: ((1, 0), (3, 2), (4, 4))}
AFTER_FRONT = {
    1: ((3, 0), (4, 2)),
    0: (
        *((0, 0), (4, 5), (3, 4), (0, 1), (1, 2), (2, 3), (4, 6), (0, 2), (3, 5), (1, 3)),
        *((2, 4), (3, 6), (0, 3), (1, 4), (2, 5), (1, 5), (0, 4), (2, 6), (1, 6), (0, 5)),
        (0, 6),
    ),
}
VMEM_BYTES = 65400 << 10
f32, bf16 = jnp.float32, jnp.bfloat16
MESH = pl.DeviceIdType.MESH
NN, NT, TN = ((1,), (0,)), ((1,), (1,)), ((0,), (0,))


exact_arithmetic = lax.Precision.HIGHEST
clip_limit = 0.02
learn_rate = 0.1
beta_one = 0.9
beta_two = 0.999
adam_epsilon = 1e-08
weight_decay = 0.01


def layer_norm(values, gain, shift):
    center = values - jnp.mean(values, -1, keepdims=True)
    spread_tokens = jnp.mean(center * center, -1, keepdims=True)
    return center * lax.rsqrt(spread_tokens + 1e-05) * gain + shift


def slice_attend(weighted_points, masses, triple_maps_rows):
    head_size = triple_maps_rows.shape[0]
    tokens = weighted_points / (masses[..., None] + 1e-05)
    joined = jnp.einsum("imd,de->ime", tokens, triple_maps_rows, precision=exact_arithmetic)
    queries = joined[..., :head_size]
    keys = joined[..., head_size : 2 * head_size]
    values = joined[..., 2 * head_size :]
    scores = jnp.einsum("imd,ind->imn", queries, keys, precision=exact_arithmetic) * head_size ** (
        -0.5
    )
    probs = jax.nn.softmax(scores, -1)
    return jnp.einsum("imn,ind->imd", probs, values, precision=exact_arithmetic)


def slice_front(weight_set, slicer, temper, vec_rows, stream, valid):
    grids_n, points_n, width = stream.shape
    heads = temper.shape[0]
    normed = layer_norm(stream, vec_rows[0], vec_rows[1])
    features = (
        jnp.einsum("gpc,ce->gpe", normed, weight_set[0], precision=exact_arithmetic) + vec_rows[2]
    )
    chip_placement_list = (
        jnp.einsum("gpc,ce->gpe", normed, weight_set[1], precision=exact_arithmetic) + vec_rows[3]
    )
    partition_scores = (
        jnp.einsum(
            "gphd,dm->gphm",
            chip_placement_list.reshape(grids_n, points_n, heads, -1),
            slicer,
            precision=exact_arithmetic,
        )
        / temper[:, None]
    )
    slice_weights = jax.nn.softmax(partition_scores, -1) * valid[:, :, None, None]
    return (slice_weights, features.reshape(grids_n, points_n, heads, -1))


def slice_rest(weight_set, vec_rows, stream, spread_tokens):
    stream = (
        stream
        + jnp.einsum("gpc,ce->gpe", spread_tokens, weight_set[2], precision=exact_arithmetic)
        + vec_rows[4]
    )
    inner = (
        jnp.einsum(
            "gpc,ce->gpe",
            layer_norm(stream, vec_rows[5], vec_rows[6]),
            weight_set[3],
            precision=exact_arithmetic,
        )
        + vec_rows[7]
    )
    hidden = jax.nn.gelu(inner, approximate=False)
    return (
        stream
        + jnp.einsum("gpc,ce->gpe", hidden, weight_set[4], precision=exact_arithmetic)
        + vec_rows[8]
    )


def slice_mix(weighted_points, masses, qkv):
    grids_n, heads, slices, head_size = weighted_points.shape
    items = grids_n * heads
    flat_weighted = weighted_points.reshape(items, slices, head_size)
    flat_masses = masses.reshape(items, slices)
    own_weighted, own_masses = (
        lax.psum_scatter(flat_weighted, "pts", scatter_dimension=0, tiled=True),
        lax.psum_scatter(flat_masses, "pts", scatter_dimension=0, tiled=True),
    )
    mixed_tokens = lax.all_gather(
        slice_attend(own_weighted, own_masses, qkv), "pts", axis=0, tiled=True
    )
    kept = (own_weighted, own_masses)
    return (mixed_tokens.reshape(weighted_points.shape), kept)


def slice_mix_back(grad_mixed, kept, qkv):
    grids_n, heads, slices, head_size = grad_mixed.shape
    flat = grad_mixed.reshape(grids_n * heads, slices, head_size)
    _, pullback = jax.vjp(slice_attend, kept[0], kept[1], qkv)
    own_grad = lax.psum_scatter(flat, "pts", scatter_dimension=0, tiled=True)
    grad_weighted, grad_masses, grad_qkv = pullback(own_grad)
    grad_weighted, grad_masses = (
        lax.all_gather(grad_weighted, "pts", axis=0, tiled=True),
        lax.all_gather(grad_masses, "pts", axis=0, tiled=True),
    )
    return (
        grad_weighted.reshape(grad_mixed.shape),
        grad_masses.reshape(grids_n, heads, slices),
        grad_qkv,
    )


def layer_forward(stream, layer_set, valid):
    weight_set, slicer, qkv, temper, vec_rows = layer_set
    slice_weights, features = slice_front(weight_set, slicer, temper, vec_rows, stream, valid)
    weighted_points = jnp.einsum(
        "gphm,gphd->ghmd", slice_weights, features, precision=exact_arithmetic
    )
    masses = jnp.sum(slice_weights, 1)
    mixed_tokens, kept = slice_mix(weighted_points, masses, qkv)
    spread_tokens = jnp.einsum(
        "gphm,ghmd->gphd", slice_weights, mixed_tokens, precision=exact_arithmetic
    ).reshape(stream.shape)
    return (slice_rest(weight_set, vec_rows, stream, spread_tokens), (stream, mixed_tokens, kept))


def layer_backward(grad_out, layer_set, saved, valid):
    weight_set, slicer, qkv, temper, vec_rows = layer_set
    stream, mixed_tokens, kept = saved
    (slice_weights, features), pull_front = jax.vjp(
        lambda w_set, s_set, t_set, v_set, s_in: slice_front(
            w_set, s_set, t_set, v_set, s_in, valid
        ),
        weight_set,
        slicer,
        temper,
        vec_rows,
        stream,
    )
    spread_tokens = jnp.einsum(
        "gphm,ghmd->gphd", slice_weights, mixed_tokens, precision=exact_arithmetic
    ).reshape(stream.shape)
    _, pull_rest = jax.vjp(slice_rest, weight_set, vec_rows, stream, spread_tokens)
    grad_set_rest, grad_vec_rest, grad_stream, grad_spread = pull_rest(grad_out)
    grad_spread = grad_spread.reshape(features.shape)
    grad_weights = jnp.einsum(
        "gphd,ghmd->gphm", grad_spread, mixed_tokens, precision=exact_arithmetic
    )
    grad_mixed = jnp.einsum(
        "gphm,gphd->ghmd", slice_weights, grad_spread, precision=exact_arithmetic
    )
    grad_weighted, grad_masses, grad_qkv = slice_mix_back(grad_mixed, kept, qkv)
    grad_weights = (
        grad_weights
        + jnp.einsum("ghmd,gphd->gphm", grad_weighted, features, precision=exact_arithmetic)
        + grad_masses[:, None]
    )
    grad_features = jnp.einsum(
        "gphm,ghmd->gphd", slice_weights, grad_weighted, precision=exact_arithmetic
    )
    grad_set_front, grad_slicer, grad_temper, grad_vec_front, grad_stream_front = pull_front(
        (grad_weights, grad_features)
    )
    grads = (
        grad_set_rest + grad_set_front,
        grad_slicer,
        grad_qkv,
        grad_temper,
        grad_vec_rest + grad_vec_front,
    )
    return (grad_stream + grad_stream_front, grads)


def head_loss(head_rows, tail_rows, stream, goals, on_surface, off_surface, inv_surf, inv_vol):
    final = layer_norm(stream, tail_rows[0], tail_rows[1])
    pred = jnp.einsum("oc,gpc->gop", head_rows, final, precision=exact_arithmetic)
    errors = (pred - goals) ** 2
    return inv_surf * jnp.sum(on_surface * errors[:, 0]) + inv_vol * jnp.sum(
        off_surface * (errors[:, 1] + errors[:, 2])
    )


def layer_params(network_state, block_number):
    (
        lifting_readout_rows,
        block_projections,
        partition_maps,
        triple_maps_rows,
        sharpness_factors,
        gain_bias_rows,
    ) = network_state
    return (
        block_projections[block_number],
        partition_maps[block_number],
        triple_maps_rows[block_number],
        sharpness_factors[block_number],
        gain_bias_rows[9 * block_number : 9 * block_number + 9],
    )


def one_batch(network_state, coords, goals, valid, on_surface, off_surface, inv_surf, inv_vol):
    (
        lifting_readout_rows,
        block_projections,
        partition_maps,
        triple_maps_rows,
        sharpness_factors,
        gain_bias_rows,
    ) = network_state
    fin = coords.shape[1]
    layers_n = block_projections.shape[0]
    stream = jnp.einsum(
        "gfp,fc->gpc", coords, lifting_readout_rows[:fin], precision=exact_arithmetic
    )
    saved = []
    for block_number in range(layers_n):
        stream, keep_set = layer_forward(stream, layer_params(network_state, block_number), valid)
        saved.append(keep_set)
    batch_loss, pull_head = jax.vjp(
        lambda h_rows, t_rows, s_in: head_loss(
            h_rows, t_rows, s_in, goals, on_surface, off_surface, inv_surf, inv_vol
        ),
        lifting_readout_rows[fin:],
        gain_bias_rows[9 * layers_n :],
        stream,
    )
    grad_head, grad_tail, grad_stream = pull_head(jnp.ones_like(batch_loss))
    layer_grads = [None] * layers_n
    for block_number in reversed(range(layers_n)):
        grad_stream, layer_grads[block_number] = layer_backward(
            grad_stream, layer_params(network_state, block_number), saved[block_number], valid
        )
    grad_embed = jnp.einsum("gfp,gpc->fc", coords, grad_stream, precision=exact_arithmetic)
    grads = (
        jnp.concatenate([grad_embed, grad_head], 0),
        jnp.stack([entry[0] for entry in layer_grads]),
        jnp.stack([entry[1] for entry in layer_grads]),
        jnp.stack([entry[2] for entry in layer_grads]),
        jnp.stack([entry[3] for entry in layer_grads]),
        jnp.concatenate([entry[4] for entry in layer_grads] + [grad_tail], 0),
    )
    return (batch_loss, grads)


def adamw_update(weight, grad, first, second):
    first_new = beta_one * first + (1.0 - beta_one) * grad
    second_new = beta_two * second + (1.0 - beta_two) * grad * grad
    first_hat = first_new / (1.0 - beta_one**STEP)
    second_hat = second_new / (1.0 - beta_two**STEP)
    weight_new = weight - learn_rate * (
        first_hat / (jnp.sqrt(second_hat) + adam_epsilon) + weight_decay * weight
    )
    return (first_new, second_new, weight_new)


def body_points(
    input_positions,
    flow_labels,
    airfoil_boundary,
    valid_sizes,
    lifting_readout_rows,
    block_projections,
    partition_maps,
    triple_maps_rows,
    sharpness_factors,
    gain_bias_rows,
    lifting_readout_mean,
    projection_running_mean,
    partition_map_mean,
    triple_maps_mean,
    sharpness_mean,
    gain_bias_mean,
    lifting_readout_square,
    projection_running_square,
    partition_map_square,
    triple_maps_square,
    sharpness_square,
    gain_bias_square,
):
    batches = input_positions.shape[0]
    points_n = input_positions.shape[3]
    slots = lax.axis_index("pts") * points_n + jnp.arange(points_n, dtype=jnp.int32)
    valid = (slots[None, None, :] < valid_sizes[:, :, None]).astype(jnp.float32)
    on_surface = valid * airfoil_boundary.astype(jnp.float32)
    off_surface = valid - on_surface
    count_surf, count_vol = lax.psum((jnp.sum(on_surface), jnp.sum(off_surface)), ("pts", "grp"))
    inv_surf = 1.0 / jnp.maximum(count_surf, 1.0)
    inv_vol = 1.0 / jnp.maximum(count_vol, 1.0)
    network_state = (
        lifting_readout_rows,
        block_projections,
        partition_maps,
        triple_maps_rows,
        sharpness_factors,
        gain_bias_rows,
    )
    loss_value = jnp.zeros((), jnp.float32)
    grads = tuple((jnp.zeros_like(entry) for entry in network_state))
    for batch in range(batches):
        batch_loss, batch_set = one_batch(
            network_state,
            input_positions[batch],
            flow_labels[batch],
            valid[batch],
            on_surface[batch],
            off_surface[batch],
            inv_surf,
            inv_vol,
        )
        loss_value = loss_value + batch_loss
        grads = tuple((total + entry for total, entry in zip(grads, batch_set)))
    running_means = (
        lifting_readout_mean,
        projection_running_mean,
        partition_map_mean,
        triple_maps_mean,
        sharpness_mean,
        gain_bias_mean,
    )
    running_squares = (
        lifting_readout_square,
        projection_running_square,
        partition_map_square,
        triple_maps_square,
        sharpness_square,
        gain_bias_square,
    )
    return finish(loss_value, grads, network_state, running_means, running_squares)


def finish(loss_value, grads, network_state, running_means, running_squares):
    summed = lax.psum((loss_value,) + grads, ("pts", "grp"))
    loss_value = summed[0]
    grads = summed[1:]
    grad_norm = jnp.sqrt(sum((jnp.sum(entry * entry) for entry in grads)))
    factor = jnp.minimum(1.0, clip_limit / grad_norm)
    results = []
    for weight, grad, first, second in zip(network_state, grads, running_means, running_squares):
        results.extend(adamw_update(weight, grad * factor, first, second))
    return tuple([loss_value, grad_norm] + results)


def _split(x):
    high = x.astype(bf16)
    return high, (x - high.astype(f32)).astype(bf16)


def _dot(a, b, dims, precision=None):
    return lax.dot_general(a, b, (dims, ((), ())), precision=precision, preferred_element_type=f32)


def _dot3(a, b, dims):
    left = jnp.concatenate([a[0], a[0], a[1]], dims[0][0])
    right = jnp.concatenate([b[0], b[1], b[0]], dims[1][0])
    return _dot(left, right, dims)


def _doth(a, b, dims):
    return _dot3(_split(a), _split(b), dims)


def _row_sums(value):
    high, low = _split(value)
    ones = jnp.ones((8, 2 * value.shape[1]), bf16)
    return _dot(ones, jnp.concatenate([high, low], 1), NT)[:1]


def _dotx(a, b, dims):
    return _dot(a, b, dims, lax.Precision.HIGHEST)


def _wide(col, lanes):
    return jnp.concatenate([col] * (lanes // LANES), 1) if lanes > LANES else col


def _fold(x):
    total = x[:, :LANES]
    for start in range(LANES, x.shape[1], LANES):
        total = total + x[:, start : start + LANES]
    return total


def _lockstep(makers, hooks=()):
    turn = 0
    running = list(makers)
    while running:
        for stage in hooks[turn] if turn < len(hooks) else ():
            stage()
        turn += 1
        alive = []
        for entry in running:
            try:
                next(entry)
                alive.append(entry)
            except StopIteration:
                pass
        running = alive


def _diag_heads(full, depth, slices):
    heads = full.shape[0] // depth
    lane = lax.broadcasted_iota(jnp.int32, (depth, full.shape[1]), 1)
    picked = full[:depth]
    for head in range(1, heads):
        picked = jnp.where(lane >= head * slices, full[head * depth : (head + 1) * depth], picked)
    return picked


def _block_heads(flat, heads, slices):
    lane = lax.broadcasted_iota(jnp.int32, flat.shape, 1)
    return jnp.concatenate(
        [
            jnp.where((lane >= head * slices) & (lane < (head + 1) * slices), flat, 0.0)
            for head in range(heads)
        ],
        0,
    )


def _norm(x):
    inv_width = 1.0 / x.shape[0]
    center = x - jnp.sum(x, 0, keepdims=True) * inv_width
    rstd = lax.rsqrt(jnp.sum(center * center, 0, keepdims=True) * inv_width + 1e-05)
    return center * rstd, rstd


def _norm_back(grad, xhat, rstd):
    inv_width = 1.0 / grad.shape[0]
    mean_grad = jnp.sum(grad, 0, keepdims=True) * inv_width
    mean_proj = jnp.sum(grad * xhat, 0, keepdims=True) * inv_width
    return (grad - mean_grad - xhat * mean_proj) * rstd


def grids_kernel(dims, *refs):
    (
        grids,
        points,
        width,
        heads,
        head_size,
        slices,
        layers,
        fin,
        outc,
        tile,
        members,
        groups,
        places,
    ) = dims
    (
        sizes_ref,
        sharp_ref,
        coords_ref,
        goals_ref,
        bound_ref,
        io_ref,
        mats_hbm,
        maps_ref,
        qkv_ref,
        vecs_ref,
        summed_hbm,
        squares,
        mats_ref,
        summed,
        packed,
        stream,
        xh1h,
        rs1,
        feath,
        featl,
        placeh,
        placel,
        wgth,
        wgtl,
        sprh,
        sprl,
        xh2h,
        rs2,
        hidh,
        gslope,
        upmh,
        upml,
        cols,
        bdmh,
        bdml,
        bdth,
        bdtl,
        accw,
        accf,
        tok,
        rmass,
        qkvs,
        probs,
        mbdh,
        mbdl,
        dbdh,
        dbdl,
        cmbh,
        cmbl,
        dmcol,
        vacc,
        gmacc,
        headacc,
        embacc,
        lossacc,
        qkvacc,
        points_ref,
        outbox,
        inbox,
        tally,
        send_sems,
        recv_sems,
        tally_send,
        tally_recv,
        sum_send,
        sum_recv,
        mats_sem,
        out_sems,
    ) = refs[: -3 * len(places["groups"])]
    boxes = refs[-3 * len(places["groups"]) :]
    half = heads // 2
    span = half * slices
    group = half * head_size
    pairs = heads // 2
    all_slices = heads * slices
    steps = points // tile
    scale = head_size ** (-0.5)
    mats_copy = pltpu.make_async_copy(mats_hbm, mats_ref, mats_sem)
    mats_copy.start()
    me, mine = lax.axis_index("pts"), lax.axis_index("grp")
    own_points = points // members

    def peer_points(hop):
        return lax.rem(me + hop, members)

    def peer_group(hop):
        return lax.rem(mine + hop, groups)

    barrier = pltpu.get_barrier_semaphore()
    for hop in range(1, members):
        pl.semaphore_signal(
            barrier, inc=1, device_id=(peer_points(hop), mine), device_id_type=MESH
        )
    for hop in range(1, groups):
        pl.semaphore_signal(
            barrier, inc=1, device_id=(me, peer_group(hop)), device_id_type=MESH
        )

    def same_plane(hop):
        other_y = lax.rem(lax.rem(me, 2) + hop // 2, 2)
        other_x = lax.rem(lax.div(mine, 2) + hop % 2, 2)
        return (lax.div(me, 2) * 2 + other_y, other_x * 2 + lax.rem(mine, 2))

    pl.semaphore_signal(barrier, inc=1, device_id=same_plane(3), device_id_type=MESH)

    slots = lax.broadcasted_iota(jnp.int32, (1, own_points), 1) + me * own_points
    surf_total = jnp.zeros((1, own_points), f32)
    vol_total = jnp.zeros((1, own_points), f32)
    blank = jnp.zeros((8 - fin - outc - 1, own_points), f32)
    for dest in range(members):
        for batch in range(grids):
            surf = bound_ref[batch, dest : dest + 1, :].astype(f32)
            goals = [goals_ref[batch, field, dest : dest + 1, :] for field in range(outc)]
            outbox[dest, batch * 8 : batch * 8 + 8, :] = jnp.concatenate(
                [coords_ref[batch, dest], *goals, surf, blank], 0
            )
            valid = jnp.where(slots < sizes_ref[batch, dest], 1.0, 0.0)
            surf_total = surf_total + valid * surf
            vol_total = vol_total + (valid - valid * surf)
    totals = jnp.concatenate(
        [surf_total, vol_total, jnp.zeros((6, own_points), f32)], 0
    )
    for dest in range(members):
        outbox[dest, grids * 8 :, :] = totals

    def piece(hop):
        other = peer_points(hop)
        return pltpu.make_async_remote_copy(
            src_ref=outbox.at[other],
            dst_ref=inbox.at[hop - 1],
            send_sem=send_sems.at[hop - 1],
            recv_sem=recv_sems.at[hop - 1],
            device_id=(other, mine),
            device_id_type=MESH,
        )

    def share(hop):
        return pltpu.make_async_remote_copy(
            src_ref=tally.at[0],
            dst_ref=tally.at[hop],
            send_sem=tally_send.at[hop - 1],
            recv_sem=tally_recv.at[hop - 1],
            device_id=(me, peer_group(hop)),
            device_id_type=MESH,
        )

    def greet():
        pl.semaphore_wait(barrier, members + groups - 1)
        for hop in range(1, members):
            piece(hop).start()


    def matrix_rows(layer, slot, half_index):
        spot = layer * 5 + SLOT_ORDER[slot]
        start = places["mats"] + (spot * (width // LANES) + half_index) * width
        return pl.ds(pl.multiple_of(start, width), width)

    def add_matrix(layer, slot, value):
        for index in range(width // LANES):
            packed[matrix_rows(layer, slot, index), :] += value[
                :, index * LANES : (index + 1) * LANES
            ]

    def read_matrix(layer, slot):
        return jnp.concatenate(
            [packed[matrix_rows(layer, slot, index), :] for index in range(width // LANES)], 1
        )

    def split_to(high_ref, low_ref, index, value):
        high, low = _split(value)
        high_ref[index] = high
        low_ref[index] = low
        return high, low

    vecs = vecs_ref[...]
    spare = jnp.zeros((LANES - vecs.shape[0], width), f32)
    standing = jnp.concatenate([vecs, spare], 0).T

    def column(row):
        return jnp.broadcast_to(standing[:, row : row + 1], (width, LANES))

    mats_copy.wait()
    for layer in range(layers):
        if layer == layers - 1:
            greet()
        base = 9 * layer
        gain_a, shift_a = column(base), column(base + 1)
        gain_b, shift_b = column(base + 5), column(base + 6)
        cols[layer, 0] = gain_a
        cols[layer, 1] = shift_a
        cols[layer, 2] = gain_b
        cols[layer, 3] = shift_b
        for slot in range(5):
            flipped = mats_ref[layer, slot].T
            bias = column(base + (2, 3, 4, 7, 8)[slot])
            if slot in (0, 1, 3):
                gain, shift, row = (gain_b, shift_b, 5) if slot == 3 else (gain_a, shift_a, 0)
                bias = bias + _doth(flipped, shift, NN)
                flipped = flipped * vecs[base + row : base + row + 1]
            cols[layer, 4 + slot] = bias
            split_to(upmh, upml, (layer, slot), flipped)
        tiled = jnp.concatenate([maps_ref[layer]] * half, 1)
        for part in range(2):
            lane = lax.broadcasted_iota(jnp.int32, (1, span), 1)
            sharp = jnp.full((1, span), 0.0, f32) + sharp_ref[layer, part * half]
            for head in range(1, half):
                sharp = jnp.where(lane >= head * slices, sharp_ref[layer, part * half + head], sharp)
            block = _block_heads(tiled / sharp, half, slices)
            split_to(bdth, bdtl, (layer, part), block)
            split_to(bdmh, bdml, (layer, part), block.T)

    vacc[...] = jnp.zeros_like(vacc)
    gmacc[...] = jnp.zeros_like(gmacc)
    headacc[...] = jnp.zeros_like(headacc)
    embacc[...] = jnp.zeros_like(embacc)
    lossacc[...] = jnp.zeros_like(lossacc)
    packed[...] = jnp.zeros_like(packed)
    qkvacc[...] = jnp.zeros_like(qkvacc)

    io_all = io_ref[...]
    rising = jnp.concatenate([io_all, jnp.zeros((LANES - io_all.shape[0], width), f32)], 0).T
    lift = [jnp.broadcast_to(rising[:, row : row + 1], (width, LANES)) for row in range(fin)]

    def window(step):
        return pl.ds(pl.multiple_of(step * tile, tile), tile)

    spots = [
        (grid, slice(step * tile, (step + 1) * tile), step)
        for step in range(steps)
        for grid in range(grids)
    ]

    def pair_of(high_ref, low_ref, index):
        return high_ref[index], low_ref[index]

    def settle(source, block):
        at = pl.ds(pl.multiple_of(source * own_points, own_points), own_points)
        for grid in range(grids):
            points_ref[grid, :, at] = block[grid * 8 : grid * 8 + 8]
        return block[grids * 8 :]

    held = settle(me, outbox[me])
    for hop in range(1, members):
        piece(hop).wait()
        held = held + settle(lax.rem(me + members - hop, members), inbox[hop - 1])
    tally[0] = held
    for hop in range(1, groups):
        share(hop).start()

    @pl.loop(0, steps)
    def _(step):
        at = window(step)
        for grid in range(grids):
            x = jnp.zeros((width, tile), f32)
            for row in range(fin):
                x = x + _wide(lift[row], tile) * points_ref[grid, row : row + 1, at]
            stream[grid, :, at] = x

    def front(layer, grid, at, step):
        xhat, rstd = _norm(stream[grid, :, at])
        xhat = _split(xhat)
        xh1h[layer, grid, :, at] = xhat[0]
        rs1[layer, grid, :, at] = rstd
        yield
        place = _dot3(pair_of(upmh, upml, (layer, 1)), xhat, NN)
        place = place + _wide(cols[layer, 5], tile)
        place = split_to(placeh, placel, (layer, grid, slice(None), at), place)
        feat = _dot3(pair_of(upmh, upml, (layer, 0)), xhat, NN)
        feat = feat + _wide(cols[layer, 4], tile)
        feat = split_to(feath, featl, (layer, grid, slice(None), at), feat)
        slots = lax.broadcasted_iota(jnp.int32, (1, tile), 1) + step * tile
        valid = jnp.where(slots < sizes_ref[grid, me], 1.0, 0.0)
        rows = [slice(part * group, (part + 1) * group) for part in range(2)]
        yield
        for part in range(2):
            here = (place[0][rows[part]], place[1][rows[part]])
            scores = _dot3(pair_of(bdmh, bdml, (layer, part)), here, NN)
            pieces = []
            for head in range(half):
                score = scores[head * slices : (head + 1) * slices]
                expo = jnp.exp(score - jnp.max(score, 0, keepdims=True))
                weight = expo * (valid / jnp.sum(expo, 0, keepdims=True))
                start = part * span + head * slices
                wrows = slice(start, start + slices)
                pieces.append(split_to(wgth, wgtl, (layer, grid, wrows, at), weight))
            yield
            weight = tuple(jnp.concatenate(list(side), 0) for side in zip(*pieces))
            lead = jnp.concatenate([feat[0][rows[part]], jnp.ones((16, tile), bf16)], 0)
            accw[grid, part] += _dot(
                jnp.concatenate([lead, lead], 1), jnp.concatenate(weight, 1), NT
            )
            accf[grid, part] += _dot(feat[1][rows[part]], weight[0], NT)
        yield

    def attend(layer, grid):
        parts, masses = [], []
        for part in range(2):
            total = accw[grid, part]
            parts.append(_diag_heads(total[:group] + accf[grid, part], head_size, slices))
            masses.append(total[group : group + 1])
        rate = 1.0 / (jnp.concatenate(masses, 1) + 1e-05)
        tokens = jnp.concatenate(parts, 1) * rate
        tok[layer, grid] = tokens
        rmass[layer, grid] = rate
        yield
        joined = _doth(qkv_ref[layer], tokens, TN)
        qkvs[layer, grid] = joined
        yield
        lane = lax.broadcasted_iota(jnp.int32, (slices, 2 * slices), 1)
        mixed = []
        for pair in range(pairs):
            at = slice(pair * 2 * slices, (pair + 1) * 2 * slices)
            query = joined[:head_size, at]
            key = joined[head_size : 2 * head_size, at]
            value = joined[2 * head_size :, at]
            full = _doth(key, query, TN)
            scores = jnp.where(lane < slices, full[:slices], full[slices:]) * scale
            expo = jnp.exp(scores - jnp.max(scores, 0, keepdims=True))
            prob = expo / jnp.sum(expo, 0, keepdims=True)
            probs[layer, grid, pair] = prob
            mixed.append(_doth(value, _block_heads(prob, 2, slices), NN))
        for part in range(2):
            flat = jnp.concatenate(mixed[part * (pairs // 2) : (part + 1) * (pairs // 2)], 1)
            block = _block_heads(flat, half, slices)
            split_to(mbdh, mbdl, (layer, grid, part), block)
        yield

    def rest(layer, grid, at):
        pieces = []
        for part in range(2):
            rows = slice(part * group, (part + 1) * group)
            wrows = slice(part * span, (part + 1) * span)
            weight = pair_of(wgth, wgtl, (layer, grid, wrows, at))
            spread = _dot3(pair_of(mbdh, mbdl, (layer, grid, part)), weight, NN)
            pieces.append(split_to(sprh, sprl, (layer, grid, rows, at), spread))
        spread = tuple(jnp.concatenate(list(side), 0) for side in zip(*pieces))
        yield
        moved = _dot3(pair_of(upmh, upml, (layer, 2)), spread, NN)
        x = stream[grid, :, at] + moved + _wide(cols[layer, 6], tile)
        stream[grid, :, at] = x
        xhat, rstd = _norm(x)
        xhat = _split(xhat)
        xh2h[layer, grid, :, at] = xhat[0]
        rs2[layer, grid, :, at] = rstd
        yield
        inner = _dot3(pair_of(upmh, upml, (layer, 3)), xhat, NN)
        pieces = []
        for start in range(0, width, BLOCK):
            rows = slice(start, start + BLOCK)
            value = inner[rows] + _wide(cols[layer, 7, rows], tile)
            cdf = 0.5 + 0.5 * lax.erf(value * (0.5**0.5))
            slope = cdf + value * jnp.exp(-0.5 * value * value) * ((2.0 * math.pi) ** -0.5)
            gslope[layer, grid, rows, at] = slope.astype(bf16)
            pieces.append(_split(value * cdf))
            hidh[layer, grid, rows, at] = pieces[-1][0]
        hidden = tuple(jnp.concatenate(list(side), 0) for side in zip(*pieces))
        yield
        moved = _dot3(pair_of(upmh, upml, (layer, 4)), hidden, NN)
        stream[grid, :, at] = stream[grid, :, at] + moved + _wide(cols[layer, 8], tile)
        yield

    @pl.loop(0, layers)
    def _(layer):
        accw[...] = jnp.zeros_like(accw)
        accf[...] = jnp.zeros_like(accf)

        _lockstep([front(layer, *spot) for spot in spots])

        _lockstep([attend(layer, grid) for grid in range(grids)])

        _lockstep([rest(layer, *spot[:2]) for spot in spots])

    tail = 9 * layers
    head_rows = jnp.concatenate(
        [io_ref[fin:, :], jnp.zeros((8 - outc, width), f32)], 0
    )
    head_gain = head_rows * vecs[tail : tail + 1]
    head_pair = _split(head_gain)
    head_bias = _dotx(head_rows, column(tail + 1), NN)
    counted = tally[0]
    for hop in range(1, groups):
        share(hop).wait()
        counted = counted + tally[hop]
    counted = jnp.broadcast_to(jnp.sum(counted, 1, keepdims=True), counted.shape)
    counted = 1.0 / jnp.maximum(counted, 1.0)
    inv_surf, inv_vol = _wide(counted[:1], tile), _wide(counted[1:2], tile)

    def crown(grid, at, step):
        xhat, rstd = _norm(stream[grid, :, at])
        halves = _split(xhat)
        pred = _dot3(head_pair, halves, NN) + _wide(head_bias, tile)
        slots = lax.broadcasted_iota(jnp.int32, (1, tile), 1) + step * tile
        valid = jnp.where(slots < sizes_ref[grid, me], 1.0, 0.0)
        surf = valid * points_ref[grid, fin + outc : fin + outc + 1, at]
        vol = (valid - surf) * inv_vol
        surf = surf * inv_surf
        row = lax.broadcasted_iota(jnp.int32, (8, tile), 0)
        factor = jnp.where(row == 0, surf, jnp.where(row < outc, vol, 0.0))
        goals = jnp.concatenate(
            [points_ref[grid, fin : fin + outc, at], jnp.zeros((8 - outc, tile), f32)], 0
        )
        error = pred - goals
        scaled = factor * error
        lossacc[...] += _fold(scaled * error)
        dpred = scaled + scaled
        headacc[0] += _fold(dpred)
        dhalves = _split(dpred)
        headacc_rows = _dot3(dhalves, halves, NT)
        for start in range(0, width, LANES):
            headacc[1 + start // LANES] += headacc_rows[:, start : start + LANES]
        yield
        grad = _dot3(head_pair, dhalves, TN)
        stream[grid, :, at] = _norm_back(grad, xhat, rstd)
        yield

    _lockstep([crown(*spot) for spot in spots])

    for layer in range(layers):
        for slot in range(5):
            mat = mats_ref[layer, slot]
            if slot in (0, 1, 3):
                mat = mat * _wide(cols[layer, 2 if slot == 3 else 0], width)
            split_to(upmh, upml, (layer, slot), mat)

    def back_rest(layer, grid, at):
        grad = stream[grid, :, at]
        vacc[layer, 4] += _fold(grad)
        pieces = grad.astype(bf16)
        yield
        dhid = _dot(upmh[layer, 4], pieces, NN)
        dinner = dhid * gslope[layer, grid, :, at].astype(f32)
        vacc[layer, 3] += _fold(dinner)
        dinner = dinner.astype(bf16)
        add_matrix(layer, 4, _dot(hidh[layer, grid, :, at], pieces, NT))
        yield
        xhat = xh2h[layer, grid, :, at]
        dxhat = _dot(upmh[layer, 3], dinner, NN)
        grad = grad + _norm_back(dxhat, xhat.astype(f32), rs2[layer, grid, :, at])
        stream[grid, :, at] = grad
        vacc[layer, 2] += _fold(grad)
        pieces = _split(grad)
        add_matrix(layer, 3, _dot(xhat, dinner, NT))
        yield
        dspread = _dot3(pair_of(upmh, upml, (layer, 2)), pieces, NN)
        spread = pair_of(sprh, sprl, (layer, grid, slice(None), at))
        gram = _dot3(spread, pieces, NT)
        dspread = split_to(sprh, sprl, (layer, grid, slice(None), at), dspread)
        add_matrix(layer, 2, gram)
        yield
        for part in range(2):
            rows = slice(part * group, (part + 1) * group)
            wrows = slice(part * span, (part + 1) * span)
            weight = pair_of(wgth, wgtl, (layer, grid, wrows, at))
            accf[grid, part] += _dot3((dspread[0][rows], dspread[1][rows]), weight, NT)
        yield

    def back_attend(layer, grid):
        joined = qkvs[layer, grid]
        tokens = tok[layer, grid]
        rate = rmass[layer, grid]
        lane = lax.broadcasted_iota(jnp.int32, (slices, 2 * slices), 1)
        dmixed = jnp.concatenate(
            [_diag_heads(accf[grid, part], head_size, slices) for part in range(2)], 1
        )
        yield
        dqs, dks, dvs = [], [], []
        for pair in range(pairs):
            at = slice(pair * 2 * slices, (pair + 1) * 2 * slices)
            query = joined[:head_size, at]
            key = joined[head_size : 2 * head_size, at]
            value = joined[2 * head_size :, at]
            prob = probs[layer, grid, pair]
            dmix = dmixed[:, at]
            full = _doth(value, dmix, TN)
            dprob = jnp.where(lane < slices, full[:slices], full[slices:])
            dscore = (
                prob * (dprob - jnp.sum(prob * dprob, 0, keepdims=True)) * scale
            )
            dblock = _block_heads(dscore, 2, slices)
            dvs.append(_doth(dmix, _block_heads(prob, 2, slices), NT))
            dqs.append(_doth(key, dblock, NN))
            dks.append(_doth(query, dblock, NT))
        dqkv = jnp.concatenate(
            [jnp.concatenate(part, 1) for part in (dqs, dks, dvs)], 0
        )
        yield
        dtok = _doth(qkv_ref[layer], dqkv, NN)
        qkvacc[layer] += _doth(tokens, dqkv, NT)
        dweighted = dtok * rate
        dmass = -jnp.sum(dweighted * tokens, 0, keepdims=True)
        yield
        dmcol[grid] = jnp.broadcast_to(dmass, (LANES, all_slices)).T
        for part in range(2):
            block = _block_heads(dweighted[:, part * span : (part + 1) * span], half, slices)
            split_to(dbdh, dbdl, (grid, part), block)
            mix = mbdh[layer, grid, part].astype(f32) + mbdl[layer, grid, part].astype(f32)
            both = jnp.concatenate([mix, block], 0)
            split_to(cmbh, cmbl, (grid, part), both.T)
        yield

    def back_feat(layer, grid, at):
        pieces = []
        for part in range(2):
            rows = slice(part * group, (part + 1) * group)
            wrows = slice(part * span, (part + 1) * span)
            weight = pair_of(wgth, wgtl, (layer, grid, wrows, at))
            dfeat = _dot3(pair_of(dbdh, dbdl, (grid, part)), weight, NN)
            vacc[layer, 0, rows] += _fold(dfeat)
            pieces.append(split_to(hidh, gslope, (layer, grid, rows, at), dfeat)[0])
        yield
        gram = _dot(xh1h[layer, grid, :, at], jnp.concatenate(pieces, 0), NT)
        add_matrix(layer, 0, gram)
        yield

    def back_front(layer, grid, at):
        feat = pair_of(feath, featl, (layer, grid, slice(None), at))
        place = pair_of(placeh, placel, (layer, grid, slice(None), at))
        dplaces = []
        for part in range(2):
            rows = slice(part * group, (part + 1) * group)
            wrows = slice(part * span, (part + 1) * span)
            weight = pair_of(wgth, wgtl, (layer, grid, wrows, at))
            dspread = pair_of(sprh, sprl, (layer, grid, rows, at))
            both = tuple(
                jnp.concatenate([one, two[rows]], 0) for one, two in zip(dspread, feat)
            )
            dweights = _dot3(pair_of(cmbh, cmbl, (grid, part)), both, NN)
            pieces = []
            for head in range(half):
                at_head = slice(head * slices, (head + 1) * slices)
                start = part * span + head * slices
                dweight = dweights[at_head] + _wide(dmcol[grid, start : start + slices], tile)
                full = weight[0][at_head].astype(f32) + weight[1][at_head].astype(f32)
                prod = full * dweight
                pieces.append(_split(prod - full * jnp.sum(prod, 0, keepdims=True)))
            pieces = tuple(jnp.concatenate(list(side), 0) for side in zip(*pieces))
            yield
            dplace = _dot3(pair_of(bdth, bdtl, (layer, part)), pieces, NN)
            vacc[layer, 1, rows] += _fold(dplace)
            dplaces.append(_split(dplace))
            gmacc[layer, part] += _dot3((place[0][rows], place[1][rows]), pieces, NT)
        dplace = tuple(jnp.concatenate(list(side), 0) for side in zip(*dplaces))
        yield
        xhat = xh1h[layer, grid, :, at]
        dfeat = pair_of(hidh, gslope, (layer, grid, slice(None), at))
        dxhat = _dot3(pair_of(upmh, upml, (layer, 0)), dfeat, NN) + _dot3(
            pair_of(upmh, upml, (layer, 1)), dplace, NN
        )
        grad = stream[grid, :, at] + _norm_back(
            dxhat, xhat.astype(f32), rs1[layer, grid, :, at]
        )
        first = isinstance(layer, int) and layer == 0
        if not first:
            stream[grid, :, at] = grad
        add_matrix(layer, 1, _dot(xhat, dplace[0], NT))
        yield
        if first:
            coords = jnp.concatenate(
                [points_ref[grid, :fin, at], jnp.zeros((8 - fin, tile), f32)], 0
            )
            embacc[...] += _dot3(_split(coords), _split(grad), NT)
        yield

    def to_row(folded):
        return _row_sums(folded)

    def put_vector(row, value, add=False):
        for index in range(width // LANES):
            start = places["vecs"] + index * places["vecs_stride"] + row
            piece = value[:, index * LANES : (index + 1) * LANES]
            if add:
                piece = piece + packed[start : start + 1, :]
            packed[start : start + 1, :] = piece

    def close_matrix(layer, slot, bias_sum):
        gain, shift = (2, 3) if slot == 3 else (0, 1)
        gram = read_matrix(layer, slot)
        mat = mats_ref[layer, slot]
        value = (
            _wide(cols[layer, gain], width) * gram + _wide(cols[layer, shift], width) * bias_sum
        )
        for index in range(width // LANES):
            packed[matrix_rows(layer, slot, index), :] = value[
                :, index * LANES : (index + 1) * LANES
            ]
        shift_row = _doth(jnp.broadcast_to(bias_sum, (8, width)), mat, NT)[:1]
        return _row_sums(gram * mat), shift_row

    def close_rest(layer):
        base = 9 * layer
        middle, inner, final = [to_row(vacc[layer, slot]) for slot in (2, 3, 4)]
        gain_row, shift_row = close_matrix(layer, 3, inner)
        for offset, row in ((4, middle), (5, gain_row), (6, shift_row), (7, inner), (8, final)):
            put_vector(base + offset, row)

    def close_feat(layer):
        total = to_row(vacc[layer, 0])
        gain, shift = close_matrix(layer, 0, total)
        put_vector(9 * layer, gain)
        put_vector(9 * layer + 1, shift)
        put_vector(9 * layer + 2, total)

    def close_front(layer):
        base = 9 * layer
        place_sum = to_row(vacc[layer, 1])
        place_gain, place_shift = close_matrix(layer, 1, place_sum)
        put_vector(base, place_gain, True)
        put_vector(base + 1, place_shift, True)
        put_vector(base + 3, place_sum)
        tiled = jnp.concatenate([maps_ref[layer]] * half, 1)
        total = None
        sharp_total = None
        for part in range(2):
            lane = lax.broadcasted_iota(jnp.int32, (1, span), 1)
            sharp = jnp.full((1, span), 0.0, f32) + sharp_ref[layer, part * half]
            for head in range(1, half):
                sharp = jnp.where(
                    lane >= head * slices, sharp_ref[layer, part * half + head], sharp
                )
            picked = _diag_heads(gmacc[layer, part], head_size, slices) / sharp
            total = picked if total is None else total + picked
            share = -jnp.sum(picked * tiled, 0, keepdims=True) / sharp
            chosen = jnp.where(
                lax.broadcasted_iota(jnp.int32, (span, LANES), 0) // slices + part * half
                == lax.broadcasted_iota(jnp.int32, (span, LANES), 1),
                1.0,
                0.0,
            )
            share = _dotx(jnp.broadcast_to(share, (8, span)), chosen, NN)
            sharp_total = share if sharp_total is None else sharp_total + share
        start = places["sharp"] + layer
        packed[start : start + 1, :heads] = sharp_total[:1, :heads]
        total = _fold(total)
        total = total + pltpu.roll(total, slices, 1)
        start = places["maps"] + layer * head_size
        packed[start : start + head_size, :slices] = total[:, :slices]
        start = places["qkv"] + layer * head_size
        packed[start : start + head_size, : 3 * head_size] = qkvacc[layer]

    def close_head():
        spread_dpred = _dotx(headacc[0], jnp.ones((LANES, LANES), f32), NN)
        gram = jnp.concatenate([headacc[1 + k] for k in range(width // LANES)], 1)
        gain_row, shift_row = vecs[tail : tail + 1], vecs[tail + 1 : tail + 2]
        head_grad = gram * gain_row + _wide(spread_dpred, width) * shift_row
        for index in range(width // LANES):
            at = slice(index * LANES, (index + 1) * LANES)
            start = places["io"] + index * places["io_stride"]
            packed[start + fin : start + fin + outc, :] = head_grad[:outc, at]
        put_vector(tail, jnp.sum(gram * head_rows, 0, keepdims=True))
        put_vector(
            tail + 1, jnp.sum(_wide(spread_dpred, width) * head_rows, 0, keepdims=True)
        )
        packed[places["loss"] : places["loss"] + 1, :] = jnp.broadcast_to(
            jnp.sum(jnp.sum(lossacc[...], 0, keepdims=True), 1, keepdims=True), (1, LANES)
        )

    def close_embed():
        for index in range(width // LANES):
            at = slice(index * LANES, (index + 1) * LANES)
            start = places["io"] + index * places["io_stride"]
            packed[start : start + fin, :] = embacc[:fin, at]

    stages = [
        sum_stages(
            packed,
            summed,
            entry,
            boxes[3 * index : 3 * index + 3],
            sum_send.at[index],
            sum_recv.at[index],
            members // 2,
        )
        for index, entry in enumerate(places["groups"])
    ]
    squares[...] = jnp.zeros_like(squares)

    def handed(index):
        start, number = places["groups"][index]
        rows = slice(start, start + number)
        return pltpu.make_async_copy(summed.at[rows], summed_hbm.at[rows], out_sems.at[index])

    def hand_over(index):
        start, number = places["groups"][index]
        handed(index).start()

        @pl.loop(0, number // 256)
        def _(step):
            block = summed[pl.ds(pl.multiple_of(start + step * 256, 256), 256), :]
            if index == 0:
                row = lax.broadcasted_iota(jnp.int32, block.shape, 0) + step * 256
                block = jnp.where(row == places["loss"], 0.0, block)
            squares[...] += jnp.sum((block * block).reshape(32, 8, LANES), 0)

    def wrapped(index):
        def finish_group():
            stages_end[index]()
            hand_over(index)

        return finish_group

    stages_end = [entry[6] for entry in stages]
    stages = [(*entry[:6], wrapped(index)) for index, entry in enumerate(stages)]

    def run(spots):
        for set_index, number in spots:
            stages[set_index][number]()

    def hooks(phase, layer, step):
        found = PLAN.get((phase, layer, step), {})
        return [
            [stages[s][n] for s, n in found.get(turn, ())] for turn in range(max(found, default=-1) + 1)
        ]

    def woven(phase, maker, layer):
        _lockstep([maker(layer, *spot[:2]) for spot in spots], hooks(phase, layer, 0))

    for layer in range(layers - 1, -1, -1):
        accf[...] = jnp.zeros_like(accf)
        woven("rest", back_rest, layer)
        close_rest(layer)
        run(AFTER_REST[layer])
        _lockstep(
            [back_attend(layer, grid) for grid in range(grids)], hooks("attend", layer, 0)
        )
        woven("feat", back_feat, layer)
        close_feat(layer)
        run(AFTER_FEAT[layer])
        if layer:
            close_head()
        woven("front", back_front, layer)
        close_front(layer)
        if layer == 0:
            close_embed()
        run(AFTER_FRONT[layer])

    for index in range(len(stages)):
        handed(index).wait()


def _round_up(value, unit):
    return (value + unit - 1) // unit * unit


def packed_places(layers, width, io_rows, vec_rows, head_size):
    halves = width // LANES
    places = {"io_stride": _round_up(io_rows, 8), "vecs_stride": _round_up(vec_rows, 8)}
    row = 0
    for name, rows in (
        ("io", halves * places["io_stride"]),
        ("vecs", halves * places["vecs_stride"]),
        ("maps", layers * head_size),
        ("qkv", layers * head_size),
        ("sharp", _round_up(layers, 8)),
        ("loss", 8),
    ):
        places[name] = row
        row += rows
    places["mats"] = _round_up(row, 256)
    each = halves * width
    first = places["mats"] + each
    groups = [(0, first), (first, each), (first + each, 3 * each)]
    for layer in range(1, layers):
        start = places["mats"] + layer * 5 * each
        groups += [(start, 2 * each), (start + 2 * each, 3 * each)]
    places["groups"] = groups
    places["rows"] = places["mats"] + layers * 5 * each
    return places


def group_parts(rows):
    half = rows // 2
    return half, half // 4, half // 16


def sum_stages(packed, out, span, boxes, send_sems, recv_sems, floors):
    first, rows = span
    half, a_four, a_all = group_parts(rows)
    core_in, a_one, a_two = boxes
    point, group = lax.axis_index("pts"), lax.axis_index("grp")
    y, z = lax.rem(point, 2), lax.div(point, 2)
    core, x = lax.rem(group, 2), lax.div(group, 2)
    plane = x + 2 * y
    base = first + core * half
    hops = (1, 2, 3)

    def plane_peer(hop):
        other_x, other_y = lax.rem(x + hop % 2, 2), lax.rem(y + hop // 2, 2)
        return (z * 2 + other_y, other_x * 2 + core), other_x + 2 * other_y

    def line_peer(hop):
        other = lax.rem(z + hop, floors)
        return (other * 2 + y, group), other

    partner = (point, x * 2 + (1 - core))

    def rows_at(start, count):
        return pl.ds(pl.multiple_of(start, 8), count)

    def send(number, source, target, device):
        return pltpu.make_async_remote_copy(
            src_ref=source,
            dst_ref=target,
            send_sem=send_sems.at[number],
            recv_sem=recv_sems.at[number],
            device_id=device,
            device_id_type=MESH,
        )

    def place(start, count):
        return packed.at[rows_at(start, count)]

    def cross():
        return send(0, place(first + (1 - core) * half, half), core_in, partner)

    def a1(hop):
        device, spot = plane_peer(hop)
        return send(hop, place(base + spot * a_four, a_four), a_one.at[hop - 1], device)

    a_part = rows_at(base + plane * a_four, a_four)
    a_piece = rows_at(base + plane * a_four + z * a_all, a_all)
    def a2(hop):
        device, spot = line_peer(hop)
        source = place(base + plane * a_four + spot * a_all, a_all)
        return send(3 + hop, source, a_two.at[hop - 1], device)

    def a3(hop):
        return send(6 + hop, out.at[a_piece], out.at[a_piece], line_peer(hop)[0])

    def a4(hop):
        return send(9 + hop, out.at[a_part], out.at[a_part], plane_peer(hop)[0])

    def last():
        own = out.at[rows_at(base, half)]
        return send(13, own, own, partner)

    def arrive(make):
        for hop in hops:
            make(hop).wait_recv()

    def depart(make):
        for hop in hops:
            make(hop).start()

    def stage_cross():
        cross().start()

    def stage_first():
        cross().wait_recv()
        own = rows_at(base, half)
        packed[own, :] = packed[own, :] + core_in[...]
        depart(a1)

    def stage_second():
        arrive(a1)
        packed[a_part, :] = packed[a_part, :] + a_one[0] + a_one[1] + a_one[2]
        depart(a2)

    def stage_third():
        arrive(a2)
        out[a_piece, :] = packed[a_piece, :] + a_two[0] + a_two[1] + a_two[2]
        depart(a3)

    def stage_fourth():
        arrive(a3)
        depart(a4)

    def stage_fifth():
        arrive(a4)
        last().start()

    def stage_end():
        last().wait_recv()
        cross().wait_send()
        last().wait_send()
        for make in (a1, a2, a3, a4):
            for hop in hops:
                make(hop).wait_send()

    return (
        stage_cross,
        stage_first,
        stage_second,
        stage_third,
        stage_fourth,
        stage_fifth,
        stage_end,
    )


def update_kernel(dims, *refs):
    layers, slots, width, places = dims
    summed, squares = refs[:2]
    weights, means, seconds = refs[2:8], refs[8:14], refs[14:20]
    loss_out, norm_out = refs[20:22]
    firsts, news, fresh = refs[22:40:3], refs[23:40:3], refs[24:40:3]
    grads, state, results, in_sems, out_sems = refs[40:]
    halves = width // LANES
    each = halves * width
    count = layers * slots

    def incoming(index):
        layer, slot = index // slots, index % slots
        start = places["mats"] + (layer * slots + SLOT_ORDER[slot]) * each
        sources = [summed.at[start : start + each]]
        targets = [grads.at[places["mats"] + index * each : places["mats"] + (index + 1) * each]]
        for kind, array in enumerate((weights[1], means[1], seconds[1])):
            sources.append(array.at[layer, slot])
            targets.append(state.at[kind, index])
        return [
            pltpu.make_async_copy(source, target, in_sems.at[index, number])
            for number, (source, target) in enumerate(zip(sources, targets))
        ]

    def outgoing(index):
        layer, slot = index // slots, index % slots
        return [
            pltpu.make_async_copy(
                results.at[kind, index], array.at[layer, slot], out_sems.at[index, kind]
            )
            for kind, array in enumerate((firsts[1], news[1], fresh[1]))
        ]

    small = pltpu.make_async_copy(
        summed.at[: places["mats"]], grads.at[: places["mats"]], in_sems.at[count, 0]
    )
    for index in range(count):
        for copy in incoming(index):
            copy.start()
    small.start()
    total = jnp.sum(jnp.sum(squares[...], 0, keepdims=True), 1, keepdims=True)
    norm = jnp.sqrt(total)
    factor = jnp.minimum(1.0, clip_limit / norm)
    norm_out[...] = norm
    for index in range(count):
        for copy in incoming(index):
            copy.wait()
        start = places["mats"] + index * each
        grad = jnp.concatenate(
            [grads[start + k * width : start + (k + 1) * width, :] for k in range(halves)], 1
        )
        first_new, second_new, weight_new = adamw_update(
            state[0, index], grad * factor, state[1, index], state[2, index]
        )
        results[0, index] = first_new
        results[1, index] = second_new
        results[2, index] = weight_new
        for copy in outgoing(index):
            copy.start()
    small.wait()

    def apply(index, grad):
        first_new, second_new, weight_new = adamw_update(
            weights[index][...], grad * factor, means[index][...], seconds[index][...]
        )
        firsts[index][...] = first_new
        news[index][...] = second_new
        fresh[index][...] = weight_new

    def rows(name, start, number):
        first = places[name] + start
        return grads[first : first + number, :]

    loss_out[...] = rows("loss", 0, 1)[:, :1]
    for index, name in ((0, "io"), (5, "vecs")):
        stride, number = places[name + "_stride"], weights[index].shape[0]
        apply(
            index,
            jnp.concatenate([rows(name, k * stride, number) for k in range(halves)], 1),
        )
    for index, name in ((2, "maps"), (3, "qkv")):
        _, number, lanes = weights[index].shape
        apply(
            index,
            jnp.stack([rows(name, k * number, number)[:, :lanes] for k in range(layers)]),
        )
    number, lanes = weights[4].shape
    apply(4, rows("sharp", 0, number)[:, :lanes])
    for index in range(count):
        for copy in outgoing(index):
            copy.wait()


def update_all(summed, squares, network_state, running_means, running_squares, places):
    layers, slots, width, _ = network_state[1].shape
    vmem = pl.BlockSpec(memory_space=pltpu.VMEM)
    hbm = pl.BlockSpec(memory_space=pl.ANY)
    state_specs = [hbm if index == 1 else vmem for index in range(6)]
    shapes = [jax.ShapeDtypeStruct((1, 1), f32)] * 2
    specs = [vmem] * 2
    for index, entry in enumerate(network_state):
        shapes += [jax.ShapeDtypeStruct(entry.shape, f32)] * 3
        specs += [hbm if index == 1 else vmem] * 3
    count = layers * slots
    kept = pltpu.VMEM((3, count, width, width), f32)
    results = pl.pallas_call(
        functools.partial(update_kernel, (layers, slots, width, places)),
        out_shape=shapes,
        in_specs=[hbm, vmem] + state_specs * 3,
        out_specs=specs,
        scratch_shapes=[
            pltpu.VMEM((places["rows"], LANES), f32),
            kept,
            kept,
            pltpu.SemaphoreType.DMA((count + 1, 4)),
            pltpu.SemaphoreType.DMA((count, 3)),
        ],
        compiler_params=pltpu.CompilerParams(vmem_limit_bytes=VMEM_BYTES),
    )(summed, squares, *network_state, *running_means, *running_squares)
    return (results[0].reshape(()), results[1].reshape(()), *results[2:])


def whole_grid_grads(network_state, coords, goals, bound, sizes, places, mesh_sizes):
    io_rows, mats, maps, qkv, sharp, vecs = network_state
    members, groups = mesh_sizes
    grids, own, _, own_points = coords.shape
    points = own_points * members
    layers, _, width, _ = mats.shape
    heads = sharp.shape[1]
    head_size, slices = maps.shape[1:]
    outc = io_rows.shape[0] - FIN
    tile = TILE
    half, span, group = heads // 2, heads // 2 * slices, heads // 2 * head_size
    dims = (grids, points, width, heads, head_size, slices, layers, FIN, outc, tile)
    dims = dims + (members, groups, places)

    def both(*shape):
        return [pltpu.VMEM(shape, bf16), pltpu.VMEM(shape, bf16)]

    def single(*shape):
        return [pltpu.VMEM(shape, f32)]

    kept = (layers, grids, width, points)
    box = (members, grids * 8 + 8, own_points)
    scratch = (
        single(layers, 5, width, width)
        + single(places["rows"], LANES)
        + single(places["rows"], LANES)
        + single(grids, width, points)
        + [pltpu.VMEM(kept, bf16)]
        + single(layers, grids, 1, points)
        + both(*kept)
        + both(*kept)
        + both(layers, grids, 2 * span, points)
        + both(*kept)
        + [pltpu.VMEM(kept, bf16)]
        + single(layers, grids, 1, points)
        + [pltpu.VMEM(kept, bf16)] * 2
        + both(layers, 5, width, width)
        + single(layers, 9, width, LANES)
        + both(layers, 2, span, group)
        + both(layers, 2, group, span)
        + single(grids, 2, group + 16, span)
        + single(grids, 2, group, span)
        + single(layers, grids, head_size, 2 * span)
        + single(layers, grids, 1, 2 * span)
        + single(layers, grids, 3 * head_size, 2 * span)
        + single(layers, grids, half, slices, 2 * slices)
        + both(layers, grids, 2, group, span)
        + both(grids, 2, group, span)
        + both(grids, 2, span, 2 * group)
        + single(grids, 2 * span, LANES)
        + single(layers, 5, width, LANES)
        + single(layers, 2, group, span)
        + single(1 + width // LANES, 8, LANES)
        + single(8, width)
        + single(8, LANES)
        + single(layers, head_size, 3 * head_size)
        + single(grids, 8, points)
        + single(*box)
        + single(members - 1, *box[1:])
        + single(groups, 8, own_points)
        + [pltpu.SemaphoreType.DMA((members - 1,))] * 2
        + [pltpu.SemaphoreType.DMA((groups - 1,))] * 2
        + [pltpu.SemaphoreType.DMA((len(places["groups"]), 14))] * 2
        + [pltpu.SemaphoreType.DMA, pltpu.SemaphoreType.DMA((len(places["groups"]),))]
    )
    for _, rows in places["groups"]:
        half_rows, quarter, piece = group_parts(rows)
        scratch += single(half_rows, LANES)
        scratch += single(3, quarter, LANES) + single(3, piece, LANES)
    vmem = pl.BlockSpec(memory_space=pltpu.VMEM)
    smem = pl.BlockSpec(memory_space=pltpu.SMEM)
    hbm = pl.BlockSpec(memory_space=pl.ANY)
    return pl.pallas_call(
        functools.partial(grids_kernel, dims),
        out_shape=[
            jax.ShapeDtypeStruct((places["rows"], LANES), f32),
            jax.ShapeDtypeStruct((8, LANES), f32),
        ],
        in_specs=[smem] * 2 + [vmem] * 4 + [hbm] + [vmem] * 3,
        out_specs=[hbm, vmem],
        scratch_shapes=scratch,
        compiler_params=pltpu.CompilerParams(
            collective_id=0, has_side_effects=True, vmem_limit_bytes=VMEM_BYTES
        ),
    )(sizes, sharp, coords, jnp.swapaxes(goals, 1, 2), bound, io_rows, mats, maps, qkv, vecs)


def body_grids(mesh_sizes, *arrays):
    network_state = arrays[4:10]
    io_rows, mats, maps, _, _, vecs = network_state
    places = packed_places(
        mats.shape[0], mats.shape[2], io_rows.shape[0], vecs.shape[0], maps.shape[1]
    )
    summed, squares = whole_grid_grads(network_state, *arrays[:4], places, mesh_sizes)
    return update_all(
        summed, squares, network_state, arrays[10:16], arrays[16:22], places
    )


def solution(mesh):
    in_specs = (
        P(None, "grp", None, "pts"),
        P(None, "grp", None, "pts"),
        P(None, "grp", "pts"),
        P(None, "grp"),
        P(),
        P(),
        P(),
        P(),
        P(),
        P(),
        P(),
        P(),
        P(),
        P(),
        P(),
        P(),
        P(),
        P(),
        P(),
        P(),
        P(),
        P(),
    )
    out_specs = (
        P(),
        P(),
        P(),
        P(),
        P(),
        P(),
        P(),
        P(),
        P(),
        P(),
        P(),
        P(),
        P(),
        P(),
        P(),
        P(),
        P(),
        P(),
        P(),
        P(),
    )
    members, groups = mesh.shape["pts"], mesh.shape["grp"]

    def body(*arrays):
        batches, own, _, own_points = arrays[0].shape
        fits = own == members and batches * own_points * members <= 2048
        if fits and own_points == LANES and (members, groups) == (8, 4) and arrays[5].shape[0] == 2:
            return body_grids((members, groups), *arrays)
        return body_points(*arrays)

    return jax.shard_map(body, mesh=mesh, in_specs=in_specs, out_specs=out_specs, check_vma=False)
```

```python
import functools
import math

import jax
import jax.numpy as jnp
from jax import lax
from jax.experimental import pallas as pl
from jax.experimental.pallas import tpu as pltpu
from jax.sharding import PartitionSpec as P

STEP = 10
LANES = 128
FIN = 2
TILE = 512
SLOT_ORDER = (1, 0, 2, 3, 4)
BLOCK = 64
PLAN = {
    ("attend", 0, 0): {4: ((2, 1),)},
    ("front", 0, 0): {3: ((1, 1), (2, 2), (3, 3))},
}
AFTER_REST = {1: ((4, 0),), 0: ((2, 0), (4, 3), (3, 1))}
AFTER_FEAT = {1: ((4, 1),), 0: ((1, 0), (3, 2), (4, 4))}
AFTER_FRONT = {
    1: ((3, 0), (4, 2)),
    0: (
        *((0, 0), (4, 5), (3, 4), (0, 1), (1, 2), (2, 3), (4, 6), (0, 2), (3, 5), (1, 3)),
        *((2, 4), (3, 6), (0, 3), (1, 4), (2, 5), (1, 5), (0, 4), (2, 6), (1, 6), (0, 5)),
        (0, 6),
    ),
}
VMEM_BYTES = 65400 << 10
f32, bf16 = jnp.float32, jnp.bfloat16
MESH = pl.DeviceIdType.MESH
NN, NT, TN = ((1,), (0,)), ((1,), (1,)), ((0,), (0,))


exact_arithmetic = lax.Precision.HIGHEST
clip_limit = 0.02
learn_rate = 0.1
beta_one = 0.9
beta_two = 0.999
adam_epsilon = 1e-08
weight_decay = 0.01


def layer_norm(values, gain, shift):
    center = values - jnp.mean(values, -1, keepdims=True)
    spread_tokens = jnp.mean(center * center, -1, keepdims=True)
    return center * lax.rsqrt(spread_tokens + 1e-05) * gain + shift


def slice_attend(weighted_points, masses, triple_maps_rows):
    head_size = triple_maps_rows.shape[0]
    tokens = weighted_points / (masses[..., None] + 1e-05)
    joined = jnp.einsum("imd,de->ime", tokens, triple_maps_rows, precision=exact_arithmetic)
    queries = joined[..., :head_size]
    keys = joined[..., head_size : 2 * head_size]
    values = joined[..., 2 * head_size :]
    scores = jnp.einsum("imd,ind->imn", queries, keys, precision=exact_arithmetic) * head_size ** (
        -0.5
    )
    probs = jax.nn.softmax(scores, -1)
    return jnp.einsum("imn,ind->imd", probs, values, precision=exact_arithmetic)


def slice_front(weight_set, slicer, temper, vec_rows, stream, valid):
    grids_n, points_n, width = stream.shape
    heads = temper.shape[0]
    normed = layer_norm(stream, vec_rows[0], vec_rows[1])
    features = (
        jnp.einsum("gpc,ce->gpe", normed, weight_set[0], precision=exact_arithmetic) + vec_rows[2]
    )
    chip_placement_list = (
        jnp.einsum("gpc,ce->gpe", normed, weight_set[1], precision=exact_arithmetic) + vec_rows[3]
    )
    partition_scores = (
        jnp.einsum(
            "gphd,dm->gphm",
            chip_placement_list.reshape(grids_n, points_n, heads, -1),
            slicer,
            precision=exact_arithmetic,
        )
        / temper[:, None]
    )
    slice_weights = jax.nn.softmax(partition_scores, -1) * valid[:, :, None, None]
    return (slice_weights, features.reshape(grids_n, points_n, heads, -1))


def slice_rest(weight_set, vec_rows, stream, spread_tokens):
    stream = (
        stream
        + jnp.einsum("gpc,ce->gpe", spread_tokens, weight_set[2], precision=exact_arithmetic)
        + vec_rows[4]
    )
    inner = (
        jnp.einsum(
            "gpc,ce->gpe",
            layer_norm(stream, vec_rows[5], vec_rows[6]),
            weight_set[3],
            precision=exact_arithmetic,
        )
        + vec_rows[7]
    )
    hidden = jax.nn.gelu(inner, approximate=False)
    return (
        stream
        + jnp.einsum("gpc,ce->gpe", hidden, weight_set[4], precision=exact_arithmetic)
        + vec_rows[8]
    )


def slice_mix(weighted_points, masses, qkv):
    grids_n, heads, slices, head_size = weighted_points.shape
    items = grids_n * heads
    flat_weighted = weighted_points.reshape(items, slices, head_size)
    flat_masses = masses.reshape(items, slices)
    own_weighted, own_masses = (
        lax.psum_scatter(flat_weighted, "pts", scatter_dimension=0, tiled=True),
        lax.psum_scatter(flat_masses, "pts", scatter_dimension=0, tiled=True),
    )
    mixed_tokens = lax.all_gather(
        slice_attend(own_weighted, own_masses, qkv), "pts", axis=0, tiled=True
    )
    kept = (own_weighted, own_masses)
    return (mixed_tokens.reshape(weighted_points.shape), kept)


def slice_mix_back(grad_mixed, kept, qkv):
    grids_n, heads, slices, head_size = grad_mixed.shape
    flat = grad_mixed.reshape(grids_n * heads, slices, head_size)
    _, pullback = jax.vjp(slice_attend, kept[0], kept[1], qkv)
    own_grad = lax.psum_scatter(flat, "pts", scatter_dimension=0, tiled=True)
    grad_weighted, grad_masses, grad_qkv = pullback(own_grad)
    grad_weighted, grad_masses = (
        lax.all_gather(grad_weighted, "pts", axis=0, tiled=True),
        lax.all_gather(grad_masses, "pts", axis=0, tiled=True),
    )
    return (
        grad_weighted.reshape(grad_mixed.shape),
        grad_masses.reshape(grids_n, heads, slices),
        grad_qkv,
    )


def layer_forward(stream, layer_set, valid):
    weight_set, slicer, qkv, temper, vec_rows = layer_set
    slice_weights, features = slice_front(weight_set, slicer, temper, vec_rows, stream, valid)
    weighted_points = jnp.einsum(
        "gphm,gphd->ghmd", slice_weights, features, precision=exact_arithmetic
    )
    masses = jnp.sum(slice_weights, 1)
    mixed_tokens, kept = slice_mix(weighted_points, masses, qkv)
    spread_tokens = jnp.einsum(
        "gphm,ghmd->gphd", slice_weights, mixed_tokens, precision=exact_arithmetic
    ).reshape(stream.shape)
    return (slice_rest(weight_set, vec_rows, stream, spread_tokens), (stream, mixed_tokens, kept))


def layer_backward(grad_out, layer_set, saved, valid):
    weight_set, slicer, qkv, temper, vec_rows = layer_set
    stream, mixed_tokens, kept = saved
    (slice_weights, features), pull_front = jax.vjp(
        lambda w_set, s_set, t_set, v_set, s_in: slice_front(
            w_set, s_set, t_set, v_set, s_in, valid
        ),
        weight_set,
        slicer,
        temper,
        vec_rows,
        stream,
    )
    spread_tokens = jnp.einsum(
        "gphm,ghmd->gphd", slice_weights, mixed_tokens, precision=exact_arithmetic
    ).reshape(stream.shape)
    _, pull_rest = jax.vjp(slice_rest, weight_set, vec_rows, stream, spread_tokens)
    grad_set_rest, grad_vec_rest, grad_stream, grad_spread = pull_rest(grad_out)
    grad_spread = grad_spread.reshape(features.shape)
    grad_weights = jnp.einsum(
        "gphd,ghmd->gphm", grad_spread, mixed_tokens, precision=exact_arithmetic
    )
    grad_mixed = jnp.einsum(
        "gphm,gphd->ghmd", slice_weights, grad_spread, precision=exact_arithmetic
    )
    grad_weighted, grad_masses, grad_qkv = slice_mix_back(grad_mixed, kept, qkv)
    grad_weights = (
        grad_weights
        + jnp.einsum("ghmd,gphd->gphm", grad_weighted, features, precision=exact_arithmetic)
        + grad_masses[:, None]
    )
    grad_features = jnp.einsum(
        "gphm,ghmd->gphd", slice_weights, grad_weighted, precision=exact_arithmetic
    )
    grad_set_front, grad_slicer, grad_temper, grad_vec_front, grad_stream_front = pull_front(
        (grad_weights, grad_features)
    )
    grads = (
        grad_set_rest + grad_set_front,
        grad_slicer,
        grad_qkv,
        grad_temper,
        grad_vec_rest + grad_vec_front,
    )
    return (grad_stream + grad_stream_front, grads)


def head_loss(head_rows, tail_rows, stream, goals, on_surface, off_surface, inv_surf, inv_vol):
    final = layer_norm(stream, tail_rows[0], tail_rows[1])
    pred = jnp.einsum("oc,gpc->gop", head_rows, final, precision=exact_arithmetic)
    errors = (pred - goals) ** 2
    return inv_surf * jnp.sum(on_surface * errors[:, 0]) + inv_vol * jnp.sum(
        off_surface * (errors[:, 1] + errors[:, 2])
    )


def layer_params(network_state, block_number):
    (
        lifting_readout_rows,
        block_projections,
        partition_maps,
        triple_maps_rows,
        sharpness_factors,
        gain_bias_rows,
    ) = network_state
    return (
        block_projections[block_number],
        partition_maps[block_number],
        triple_maps_rows[block_number],
        sharpness_factors[block_number],
        gain_bias_rows[9 * block_number : 9 * block_number + 9],
    )


def one_batch(network_state, coords, goals, valid, on_surface, off_surface, inv_surf, inv_vol):
    (
        lifting_readout_rows,
        block_projections,
        partition_maps,
        triple_maps_rows,
        sharpness_factors,
        gain_bias_rows,
    ) = network_state
    fin = coords.shape[1]
    layers_n = block_projections.shape[0]
    stream = jnp.einsum(
        "gfp,fc->gpc", coords, lifting_readout_rows[:fin], precision=exact_arithmetic
    )
    saved = []
    for block_number in range(layers_n):
        stream, keep_set = layer_forward(stream, layer_params(network_state, block_number), valid)
        saved.append(keep_set)
    batch_loss, pull_head = jax.vjp(
        lambda h_rows, t_rows, s_in: head_loss(
            h_rows, t_rows, s_in, goals, on_surface, off_surface, inv_surf, inv_vol
        ),
        lifting_readout_rows[fin:],
        gain_bias_rows[9 * layers_n :],
        stream,
    )
    grad_head, grad_tail, grad_stream = pull_head(jnp.ones_like(batch_loss))
    layer_grads = [None] * layers_n
    for block_number in reversed(range(layers_n)):
        grad_stream, layer_grads[block_number] = layer_backward(
            grad_stream, layer_params(network_state, block_number), saved[block_number], valid
        )
    grad_embed = jnp.einsum("gfp,gpc->fc", coords, grad_stream, precision=exact_arithmetic)
    grads = (
        jnp.concatenate([grad_embed, grad_head], 0),
        jnp.stack([entry[0] for entry in layer_grads]),
        jnp.stack([entry[1] for entry in layer_grads]),
        jnp.stack([entry[2] for entry in layer_grads]),
        jnp.stack([entry[3] for entry in layer_grads]),
        jnp.concatenate([entry[4] for entry in layer_grads] + [grad_tail], 0),
    )
    return (batch_loss, grads)


def adamw_update(weight, grad, first, second):
    first_new = beta_one * first + (1.0 - beta_one) * grad
    second_new = beta_two * second + (1.0 - beta_two) * grad * grad
    first_hat = first_new / (1.0 - beta_one**STEP)
    second_hat = second_new / (1.0 - beta_two**STEP)
    weight_new = weight - learn_rate * (
        first_hat / (jnp.sqrt(second_hat) + adam_epsilon) + weight_decay * weight
    )
    return (first_new, second_new, weight_new)


def body_points(
    input_positions,
    flow_labels,
    airfoil_boundary,
    valid_sizes,
    lifting_readout_rows,
    block_projections,
    partition_maps,
    triple_maps_rows,
    sharpness_factors,
    gain_bias_rows,
    lifting_readout_mean,
    projection_running_mean,
    partition_map_mean,
    triple_maps_mean,
    sharpness_mean,
    gain_bias_mean,
    lifting_readout_square,
    projection_running_square,
    partition_map_square,
    triple_maps_square,
    sharpness_square,
    gain_bias_square,
):
    batches = input_positions.shape[0]
    points_n = input_positions.shape[3]
    slots = lax.axis_index("pts") * points_n + jnp.arange(points_n, dtype=jnp.int32)
    valid = (slots[None, None, :] < valid_sizes[:, :, None]).astype(jnp.float32)
    on_surface = valid * airfoil_boundary.astype(jnp.float32)
    off_surface = valid - on_surface
    count_surf, count_vol = lax.psum((jnp.sum(on_surface), jnp.sum(off_surface)), ("pts", "grp"))
    inv_surf = 1.0 / jnp.maximum(count_surf, 1.0)
    inv_vol = 1.0 / jnp.maximum(count_vol, 1.0)
    network_state = (
        lifting_readout_rows,
        block_projections,
        partition_maps,
        triple_maps_rows,
        sharpness_factors,
        gain_bias_rows,
    )
    loss_value = jnp.zeros((), jnp.float32)
    grads = tuple((jnp.zeros_like(entry) for entry in network_state))
    for batch in range(batches):
        batch_loss, batch_set = one_batch(
            network_state,
            input_positions[batch],
            flow_labels[batch],
            valid[batch],
            on_surface[batch],
            off_surface[batch],
            inv_surf,
            inv_vol,
        )
        loss_value = loss_value + batch_loss
        grads = tuple((total + entry for total, entry in zip(grads, batch_set)))
    running_means = (
        lifting_readout_mean,
        projection_running_mean,
        partition_map_mean,
        triple_maps_mean,
        sharpness_mean,
        gain_bias_mean,
    )
    running_squares = (
        lifting_readout_square,
        projection_running_square,
        partition_map_square,
        triple_maps_square,
        sharpness_square,
        gain_bias_square,
    )
    return finish(loss_value, grads, network_state, running_means, running_squares)


def finish(loss_value, grads, network_state, running_means, running_squares):
    summed = lax.psum((loss_value,) + grads, ("pts", "grp"))
    loss_value = summed[0]
    grads = summed[1:]
    grad_norm = jnp.sqrt(sum((jnp.sum(entry * entry) for entry in grads)))
    factor = jnp.minimum(1.0, clip_limit / grad_norm)
    results = []
    for weight, grad, first, second in zip(network_state, grads, running_means, running_squares):
        results.extend(adamw_update(weight, grad * factor, first, second))
    return tuple([loss_value, grad_norm] + results)


def _split(x):
    high = x.astype(bf16)
    return high, (x - high.astype(f32)).astype(bf16)


def _dot(a, b, dims, precision=None):
    return lax.dot_general(a, b, (dims, ((), ())), precision=precision, preferred_element_type=f32)


def _dot3(a, b, dims):
    left = jnp.concatenate([a[0], a[0], a[1]], dims[0][0])
    right = jnp.concatenate([b[0], b[1], b[0]], dims[1][0])
    return _dot(left, right, dims)


def _dot_wide(weight, value, dims):
    return _dot(
        jnp.concatenate(weight, dims[0][0]), jnp.concatenate([value, value], dims[1][0]), dims
    )


def _doth(a, b, dims):
    return _dot3(_split(a), _split(b), dims)


def _row_sums(value):
    high, low = _split(value)
    ones = jnp.ones((8, 2 * value.shape[1]), bf16)
    return _dot(ones, jnp.concatenate([high, low], 1), NT)[:1]


def _dotx(a, b, dims):
    return _dot(a, b, dims, lax.Precision.HIGHEST)


def _wide(col, lanes):
    return jnp.concatenate([col] * (lanes // LANES), 1) if lanes > LANES else col


def _fold(x):
    total = x[:, :LANES]
    for start in range(LANES, x.shape[1], LANES):
        total = total + x[:, start : start + LANES]
    return total


def _lockstep(makers, hooks=()):
    turn = 0
    running = list(makers)
    while running:
        for stage in hooks[turn] if turn < len(hooks) else ():
            stage()
        turn += 1
        alive = []
        for entry in running:
            try:
                next(entry)
                alive.append(entry)
            except StopIteration:
                pass
        running = alive


def _diag_heads(full, depth, slices):
    heads = full.shape[0] // depth
    lane = lax.broadcasted_iota(jnp.int32, (depth, full.shape[1]), 1)
    picked = full[:depth]
    for head in range(1, heads):
        picked = jnp.where(lane >= head * slices, full[head * depth : (head + 1) * depth], picked)
    return picked


def _block_heads(flat, heads, slices):
    lane = lax.broadcasted_iota(jnp.int32, flat.shape, 1)
    return jnp.concatenate(
        [
            jnp.where((lane >= head * slices) & (lane < (head + 1) * slices), flat, 0.0)
            for head in range(heads)
        ],
        0,
    )


def _norm(x):
    inv_width = 1.0 / x.shape[0]
    center = x - jnp.sum(x, 0, keepdims=True) * inv_width
    rstd = lax.rsqrt(jnp.sum(center * center, 0, keepdims=True) * inv_width + 1e-05)
    return center * rstd, rstd


def _norm_back(grad, xhat, rstd):
    inv_width = 1.0 / grad.shape[0]
    mean_grad = jnp.sum(grad, 0, keepdims=True) * inv_width
    mean_proj = jnp.sum(grad * xhat, 0, keepdims=True) * inv_width
    return (grad - mean_grad - xhat * mean_proj) * rstd


def grids_kernel(dims, *refs):
    (
        grids,
        points,
        width,
        heads,
        head_size,
        slices,
        layers,
        fin,
        outc,
        tile,
        members,
        groups,
        places,
    ) = dims
    (
        sizes_ref,
        sharp_ref,
        coords_ref,
        goals_ref,
        bound_ref,
        io_ref,
        mats_hbm,
        maps_ref,
        qkv_ref,
        vecs_ref,
        summed_hbm,
        squares,
        mats_ref,
        summed,
        packed,
        stream,
        xh1h,
        rs1,
        feath,
        featl,
        placeh,
        placel,
        wgth,
        wgtl,
        sprh,
        sprl,
        xh2h,
        rs2,
        hidh,
        gslope,
        upmh,
        upml,
        cols,
        bdmh,
        bdml,
        bdth,
        bdtl,
        accw,
        accf,
        tok,
        rmass,
        qkvs,
        probs,
        mbdh,
        mbdl,
        dbdh,
        dbdl,
        cmbh,
        cmbl,
        dmcol,
        vacc,
        gmacc,
        headacc,
        embacc,
        lossacc,
        qkvacc,
        points_ref,
        outbox,
        inbox,
        tally,
        send_sems,
        recv_sems,
        tally_send,
        tally_recv,
        sum_send,
        sum_recv,
        mats_sem,
        out_sems,
    ) = refs[: -3 * len(places["groups"])]
    boxes = refs[-3 * len(places["groups"]) :]
    half = heads // 2
    span = half * slices
    group = half * head_size
    pairs = heads // 2
    all_slices = heads * slices
    steps = points // tile
    scale = head_size ** (-0.5)
    mats_copy = pltpu.make_async_copy(mats_hbm, mats_ref, mats_sem)
    mats_copy.start()
    me, mine = lax.axis_index("pts"), lax.axis_index("grp")
    own_points = points // members

    def peer_points(hop):
        return lax.rem(me + hop, members)

    def peer_group(hop):
        return lax.rem(mine + hop, groups)

    barrier = pltpu.get_barrier_semaphore()
    for hop in range(1, members):
        pl.semaphore_signal(
            barrier, inc=1, device_id=(peer_points(hop), mine), device_id_type=MESH
        )
    for hop in range(1, groups):
        pl.semaphore_signal(
            barrier, inc=1, device_id=(me, peer_group(hop)), device_id_type=MESH
        )

    def same_plane(hop):
        other_y = lax.rem(lax.rem(me, 2) + hop // 2, 2)
        other_x = lax.rem(lax.div(mine, 2) + hop % 2, 2)
        return (lax.div(me, 2) * 2 + other_y, other_x * 2 + lax.rem(mine, 2))

    pl.semaphore_signal(barrier, inc=1, device_id=same_plane(3), device_id_type=MESH)

    slots = lax.broadcasted_iota(jnp.int32, (1, own_points), 1) + me * own_points
    surf_total = jnp.zeros((1, own_points), f32)
    vol_total = jnp.zeros((1, own_points), f32)
    blank = jnp.zeros((8 - fin - outc - 1, own_points), f32)
    for dest in range(members):
        for batch in range(grids):
            surf = bound_ref[batch, dest : dest + 1, :].astype(f32)
            goals = [goals_ref[batch, field, dest : dest + 1, :] for field in range(outc)]
            outbox[dest, batch * 8 : batch * 8 + 8, :] = jnp.concatenate(
                [coords_ref[batch, dest], *goals, surf, blank], 0
            )
            valid = jnp.where(slots < sizes_ref[batch, dest], 1.0, 0.0)
            surf_total = surf_total + valid * surf
            vol_total = vol_total + (valid - valid * surf)
    totals = jnp.concatenate(
        [surf_total, vol_total, jnp.zeros((6, own_points), f32)], 0
    )
    for dest in range(members):
        outbox[dest, grids * 8 :, :] = totals

    def piece(hop):
        other = peer_points(hop)
        return pltpu.make_async_remote_copy(
            src_ref=outbox.at[other],
            dst_ref=inbox.at[hop - 1],
            send_sem=send_sems.at[hop - 1],
            recv_sem=recv_sems.at[hop - 1],
            device_id=(other, mine),
            device_id_type=MESH,
        )

    def share(hop):
        return pltpu.make_async_remote_copy(
            src_ref=tally.at[0],
            dst_ref=tally.at[hop],
            send_sem=tally_send.at[hop - 1],
            recv_sem=tally_recv.at[hop - 1],
            device_id=(me, peer_group(hop)),
            device_id_type=MESH,
        )

    def greet():
        pl.semaphore_wait(barrier, members + groups - 1)
        for hop in range(1, members):
            piece(hop).start()


    def matrix_rows(layer, slot, half_index):
        spot = layer * 5 + SLOT_ORDER[slot]
        start = places["mats"] + (spot * (width // LANES) + half_index) * width
        return pl.ds(pl.multiple_of(start, width), width)

    def add_matrix(layer, slot, value):
        for index in range(width // LANES):
            packed[matrix_rows(layer, slot, index), :] += value[
                :, index * LANES : (index + 1) * LANES
            ]

    def read_matrix(layer, slot):
        return jnp.concatenate(
            [packed[matrix_rows(layer, slot, index), :] for index in range(width // LANES)], 1
        )

    def split_to(high_ref, low_ref, index, value):
        high, low = _split(value)
        high_ref[index] = high
        low_ref[index] = low
        return high, low

    vecs = vecs_ref[...]
    spare = jnp.zeros((LANES - vecs.shape[0], width), f32)
    standing = jnp.concatenate([vecs, spare], 0).T

    def column(row):
        return jnp.broadcast_to(standing[:, row : row + 1], (width, LANES))

    mats_copy.wait()
    for layer in range(layers):
        if layer == layers - 1:
            greet()
        base = 9 * layer
        gain_a, shift_a = column(base), column(base + 1)
        gain_b, shift_b = column(base + 5), column(base + 6)
        cols[layer, 0] = gain_a
        cols[layer, 1] = shift_a
        cols[layer, 2] = gain_b
        cols[layer, 3] = shift_b
        for slot in range(5):
            flipped = mats_ref[layer, slot].T
            bias = column(base + (2, 3, 4, 7, 8)[slot])
            if slot in (0, 1, 3):
                gain, shift, row = (gain_b, shift_b, 5) if slot == 3 else (gain_a, shift_a, 0)
                bias = bias + _doth(flipped, shift, NN)
                flipped = flipped * vecs[base + row : base + row + 1]
            cols[layer, 4 + slot] = bias
            split_to(upmh, upml, (layer, slot), flipped)
        tiled = jnp.concatenate([maps_ref[layer]] * half, 1)
        for part in range(2):
            lane = lax.broadcasted_iota(jnp.int32, (1, span), 1)
            sharp = jnp.full((1, span), 0.0, f32) + sharp_ref[layer, part * half]
            for head in range(1, half):
                sharp = jnp.where(lane >= head * slices, sharp_ref[layer, part * half + head], sharp)
            block = _block_heads(tiled / sharp, half, slices)
            split_to(bdth, bdtl, (layer, part), block)
            split_to(bdmh, bdml, (layer, part), block.T)

    vacc[...] = jnp.zeros_like(vacc)
    gmacc[...] = jnp.zeros_like(gmacc)
    headacc[...] = jnp.zeros_like(headacc)
    embacc[...] = jnp.zeros_like(embacc)
    lossacc[...] = jnp.zeros_like(lossacc)
    packed[...] = jnp.zeros_like(packed)
    qkvacc[...] = jnp.zeros_like(qkvacc)

    io_all = io_ref[...]
    rising = jnp.concatenate([io_all, jnp.zeros((LANES - io_all.shape[0], width), f32)], 0).T
    lift = [jnp.broadcast_to(rising[:, row : row + 1], (width, LANES)) for row in range(fin)]

    def window(step):
        return pl.ds(pl.multiple_of(step * tile, tile), tile)

    spots = [
        (grid, slice(step * tile, (step + 1) * tile), step)
        for step in range(steps)
        for grid in range(grids)
    ]

    def pair_of(high_ref, low_ref, index):
        return high_ref[index], low_ref[index]

    def settle(source, block):
        at = pl.ds(pl.multiple_of(source * own_points, own_points), own_points)
        for grid in range(grids):
            points_ref[grid, :, at] = block[grid * 8 : grid * 8 + 8]
        return block[grids * 8 :]

    held = settle(me, outbox[me])
    for hop in range(1, members):
        piece(hop).wait()
        held = held + settle(lax.rem(me + members - hop, members), inbox[hop - 1])
    tally[0] = held
    for hop in range(1, groups):
        share(hop).start()

    @pl.loop(0, steps)
    def _(step):
        at = window(step)
        for grid in range(grids):
            x = jnp.zeros((width, tile), f32)
            for row in range(fin):
                x = x + _wide(lift[row], tile) * points_ref[grid, row : row + 1, at]
            stream[grid, :, at] = x

    def front(layer, grid, at, step):
        xhat, rstd = _norm(stream[grid, :, at])
        xhat = _split(xhat)
        xh1h[layer, grid, :, at] = xhat[0]
        rs1[layer, grid, :, at] = rstd
        yield
        place = _dot3(pair_of(upmh, upml, (layer, 1)), xhat, NN)
        place = place + _wide(cols[layer, 5], tile)
        place = split_to(placeh, placel, (layer, grid, slice(None), at), place)
        feat = _dot3(pair_of(upmh, upml, (layer, 0)), xhat, NN)
        feat = feat + _wide(cols[layer, 4], tile)
        feat = split_to(feath, featl, (layer, grid, slice(None), at), feat)
        slots = lax.broadcasted_iota(jnp.int32, (1, tile), 1) + step * tile
        valid = jnp.where(slots < sizes_ref[grid, me], 1.0, 0.0)
        rows = [slice(part * group, (part + 1) * group) for part in range(2)]
        yield
        for part in range(2):
            here = (place[0][rows[part]], place[1][rows[part]])
            scores = _dot3(pair_of(bdmh, bdml, (layer, part)), here, NN)
            pieces = []
            for head in range(half):
                score = scores[head * slices : (head + 1) * slices]
                expo = jnp.exp(score - jnp.max(score, 0, keepdims=True))
                weight = expo * (valid / jnp.sum(expo, 0, keepdims=True))
                start = part * span + head * slices
                wrows = slice(start, start + slices)
                pieces.append(split_to(wgth, wgtl, (layer, grid, wrows, at), weight))
            yield
            weight = tuple(jnp.concatenate(list(side), 0) for side in zip(*pieces))
            lead = jnp.concatenate([feat[0][rows[part]], jnp.ones((16, tile), bf16)], 0)
            accw[grid, part] += _dot(
                jnp.concatenate([lead, lead], 1), jnp.concatenate(weight, 1), NT
            )
            accf[grid, part] += _dot(feat[1][rows[part]], weight[0], NT)
        yield

    def attend(layer, grid):
        parts, masses = [], []
        for part in range(2):
            total = accw[grid, part]
            parts.append(_diag_heads(total[:group] + accf[grid, part], head_size, slices))
            masses.append(total[group : group + 1])
        rate = 1.0 / (jnp.concatenate(masses, 1) + 1e-05)
        tokens = jnp.concatenate(parts, 1) * rate
        tok[layer, grid] = tokens
        rmass[layer, grid] = rate
        yield
        joined = _doth(qkv_ref[layer], tokens, TN)
        qkvs[layer, grid] = joined
        yield
        lane = lax.broadcasted_iota(jnp.int32, (slices, 2 * slices), 1)
        mixed = []
        for pair in range(pairs):
            at = slice(pair * 2 * slices, (pair + 1) * 2 * slices)
            query = joined[:head_size, at]
            key = joined[head_size : 2 * head_size, at]
            value = joined[2 * head_size :, at]
            full = _doth(key, query, TN)
            scores = jnp.where(lane < slices, full[:slices], full[slices:]) * scale
            expo = jnp.exp(scores - jnp.max(scores, 0, keepdims=True))
            prob = expo / jnp.sum(expo, 0, keepdims=True)
            probs[layer, grid, pair] = prob
            mixed.append(_doth(value, _block_heads(prob, 2, slices), NN))
        for part in range(2):
            flat = jnp.concatenate(mixed[part * (pairs // 2) : (part + 1) * (pairs // 2)], 1)
            block = _block_heads(flat, half, slices)
            split_to(mbdh, mbdl, (layer, grid, part), block)
        yield

    def rest(layer, grid, at):
        pieces = []
        for part in range(2):
            rows = slice(part * group, (part + 1) * group)
            wrows = slice(part * span, (part + 1) * span)
            weight = pair_of(wgth, wgtl, (layer, grid, wrows, at))
            spread = _dot3(pair_of(mbdh, mbdl, (layer, grid, part)), weight, NN)
            pieces.append(split_to(sprh, sprl, (layer, grid, rows, at), spread))
        spread = tuple(jnp.concatenate(list(side), 0) for side in zip(*pieces))
        yield
        moved = _dot3(pair_of(upmh, upml, (layer, 2)), spread, NN)
        x = stream[grid, :, at] + moved + _wide(cols[layer, 6], tile)
        stream[grid, :, at] = x
        xhat, rstd = _norm(x)
        xhat = xhat.astype(bf16)
        xh2h[layer, grid, :, at] = xhat
        rs2[layer, grid, :, at] = rstd
        yield
        inner = _dot_wide(pair_of(upmh, upml, (layer, 3)), xhat, NN)
        pieces = []
        for start in range(0, width, BLOCK):
            rows = slice(start, start + BLOCK)
            value = inner[rows] + _wide(cols[layer, 7, rows], tile)
            cdf = 0.5 + 0.5 * lax.erf(value * (0.5**0.5))
            slope = cdf + value * jnp.exp(-0.5 * value * value) * ((2.0 * math.pi) ** -0.5)
            gslope[layer, grid, rows, at] = slope.astype(bf16)
            pieces.append((value * cdf).astype(bf16))
            hidh[layer, grid, rows, at] = pieces[-1]
        hidden = jnp.concatenate(pieces, 0)
        yield
        moved = _dot_wide(pair_of(upmh, upml, (layer, 4)), hidden, NN)
        stream[grid, :, at] = stream[grid, :, at] + moved + _wide(cols[layer, 8], tile)
        yield

    @pl.loop(0, layers)
    def _(layer):
        accw[...] = jnp.zeros_like(accw)
        accf[...] = jnp.zeros_like(accf)

        _lockstep([front(layer, *spot) for spot in spots])

        _lockstep([attend(layer, grid) for grid in range(grids)])

        _lockstep([rest(layer, *spot[:2]) for spot in spots])

    tail = 9 * layers
    head_rows = jnp.concatenate(
        [io_ref[fin:, :], jnp.zeros((8 - outc, width), f32)], 0
    )
    head_gain = head_rows * vecs[tail : tail + 1]
    head_pair = _split(head_gain)
    head_bias = _dotx(head_rows, column(tail + 1), NN)
    counted = tally[0]
    for hop in range(1, groups):
        share(hop).wait()
        counted = counted + tally[hop]
    counted = jnp.broadcast_to(jnp.sum(counted, 1, keepdims=True), counted.shape)
    counted = 1.0 / jnp.maximum(counted, 1.0)
    inv_surf, inv_vol = _wide(counted[:1], tile), _wide(counted[1:2], tile)

    def crown(grid, at, step):
        xhat, rstd = _norm(stream[grid, :, at])
        halves = _split(xhat)
        pred = _dot3(head_pair, halves, NN) + _wide(head_bias, tile)
        slots = lax.broadcasted_iota(jnp.int32, (1, tile), 1) + step * tile
        valid = jnp.where(slots < sizes_ref[grid, me], 1.0, 0.0)
        surf = valid * points_ref[grid, fin + outc : fin + outc + 1, at]
        vol = (valid - surf) * inv_vol
        surf = surf * inv_surf
        row = lax.broadcasted_iota(jnp.int32, (8, tile), 0)
        factor = jnp.where(row == 0, surf, jnp.where(row < outc, vol, 0.0))
        goals = jnp.concatenate(
            [points_ref[grid, fin : fin + outc, at], jnp.zeros((8 - outc, tile), f32)], 0
        )
        error = pred - goals
        scaled = factor * error
        lossacc[...] += _fold(scaled * error)
        dpred = scaled + scaled
        headacc[0] += _fold(dpred)
        dhalves = _split(dpred)
        headacc_rows = _dot3(dhalves, halves, NT)
        for start in range(0, width, LANES):
            headacc[1 + start // LANES] += headacc_rows[:, start : start + LANES]
        yield
        grad = _dot3(head_pair, dhalves, TN)
        stream[grid, :, at] = _norm_back(grad, xhat, rstd)
        yield

    _lockstep([crown(*spot) for spot in spots])

    for layer in range(layers):
        for slot in range(5):
            mat = mats_ref[layer, slot]
            if slot in (0, 1, 3):
                mat = mat * _wide(cols[layer, 2 if slot == 3 else 0], width)
            split_to(upmh, upml, (layer, slot), mat)

    def back_rest(layer, grid, at):
        grad = stream[grid, :, at]
        vacc[layer, 4] += _fold(grad)
        pieces = grad.astype(bf16)
        yield
        dhid = _dot(upmh[layer, 4], pieces, NN)
        dinner = dhid * gslope[layer, grid, :, at].astype(f32)
        vacc[layer, 3] += _fold(dinner)
        dinner = dinner.astype(bf16)
        add_matrix(layer, 4, _dot(hidh[layer, grid, :, at], pieces, NT))
        yield
        xhat = xh2h[layer, grid, :, at]
        dxhat = _dot(upmh[layer, 3], dinner, NN)
        grad = grad + _norm_back(dxhat, xhat.astype(f32), rs2[layer, grid, :, at])
        stream[grid, :, at] = grad
        vacc[layer, 2] += _fold(grad)
        pieces = _split(grad)
        add_matrix(layer, 3, _dot(xhat, dinner, NT))
        yield
        dspread = _dot_wide(pair_of(upmh, upml, (layer, 2)), pieces[0], NN)
        spread = pair_of(sprh, sprl, (layer, grid, slice(None), at))
        gram = _dot3(spread, pieces, NT)
        dspread = split_to(sprh, sprl, (layer, grid, slice(None), at), dspread)
        add_matrix(layer, 2, gram)
        yield
        for part in range(2):
            rows = slice(part * group, (part + 1) * group)
            wrows = slice(part * span, (part + 1) * span)
            weight = pair_of(wgth, wgtl, (layer, grid, wrows, at))
            accf[grid, part] += _dot3((dspread[0][rows], dspread[1][rows]), weight, NT)
        yield

    def back_attend(layer, grid):
        joined = qkvs[layer, grid]
        tokens = tok[layer, grid]
        rate = rmass[layer, grid]
        lane = lax.broadcasted_iota(jnp.int32, (slices, 2 * slices), 1)
        dmixed = jnp.concatenate(
            [_diag_heads(accf[grid, part], head_size, slices) for part in range(2)], 1
        )
        yield
        dqs, dks, dvs = [], [], []
        for pair in range(pairs):
            at = slice(pair * 2 * slices, (pair + 1) * 2 * slices)
            query = joined[:head_size, at]
            key = joined[head_size : 2 * head_size, at]
            value = joined[2 * head_size :, at]
            prob = probs[layer, grid, pair]
            dmix = dmixed[:, at]
            full = _doth(value, dmix, TN)
            dprob = jnp.where(lane < slices, full[:slices], full[slices:])
            dscore = (
                prob * (dprob - jnp.sum(prob * dprob, 0, keepdims=True)) * scale
            )
            dblock = _block_heads(dscore, 2, slices)
            dvs.append(_doth(dmix, _block_heads(prob, 2, slices), NT))
            dqs.append(_doth(key, dblock, NN))
            dks.append(_doth(query, dblock, NT))
        dqkv = jnp.concatenate(
            [jnp.concatenate(part, 1) for part in (dqs, dks, dvs)], 0
        )
        yield
        dtok = _doth(qkv_ref[layer], dqkv, NN)
        qkvacc[layer] += _doth(tokens, dqkv, NT)
        dweighted = dtok * rate
        dmass = -jnp.sum(dweighted * tokens, 0, keepdims=True)
        yield
        dmcol[grid] = jnp.broadcast_to(dmass, (LANES, all_slices)).T
        for part in range(2):
            block = _block_heads(dweighted[:, part * span : (part + 1) * span], half, slices)
            split_to(dbdh, dbdl, (grid, part), block)
            mix = mbdh[layer, grid, part].astype(f32) + mbdl[layer, grid, part].astype(f32)
            both = jnp.concatenate([mix, block], 0)
            split_to(cmbh, cmbl, (grid, part), both.T)
        yield

    def back_feat(layer, grid, at):
        pieces = []
        for part in range(2):
            rows = slice(part * group, (part + 1) * group)
            wrows = slice(part * span, (part + 1) * span)
            weight = pair_of(wgth, wgtl, (layer, grid, wrows, at))
            dfeat = _dot3(pair_of(dbdh, dbdl, (grid, part)), weight, NN)
            vacc[layer, 0, rows] += _fold(dfeat)
            pieces.append(dfeat.astype(bf16))
            hidh[layer, grid, rows, at] = pieces[-1]
        yield
        gram = _dot(xh1h[layer, grid, :, at], jnp.concatenate(pieces, 0), NT)
        add_matrix(layer, 0, gram)
        yield

    def back_front(layer, grid, at):
        feat = pair_of(feath, featl, (layer, grid, slice(None), at))
        place = pair_of(placeh, placel, (layer, grid, slice(None), at))
        dplaces = []
        for part in range(2):
            rows = slice(part * group, (part + 1) * group)
            wrows = slice(part * span, (part + 1) * span)
            weight = pair_of(wgth, wgtl, (layer, grid, wrows, at))
            dspread = pair_of(sprh, sprl, (layer, grid, rows, at))
            both = tuple(
                jnp.concatenate([one, two[rows]], 0) for one, two in zip(dspread, feat)
            )
            dweights = _dot3(pair_of(cmbh, cmbl, (grid, part)), both, NN)
            pieces = []
            for head in range(half):
                at_head = slice(head * slices, (head + 1) * slices)
                start = part * span + head * slices
                dweight = dweights[at_head] + _wide(dmcol[grid, start : start + slices], tile)
                full = weight[0][at_head].astype(f32) + weight[1][at_head].astype(f32)
                prod = full * dweight
                pieces.append(_split(prod - full * jnp.sum(prod, 0, keepdims=True)))
            pieces = tuple(jnp.concatenate(list(side), 0) for side in zip(*pieces))
            yield
            dplace = _dot_wide(pair_of(bdth, bdtl, (layer, part)), pieces[0], NN)
            vacc[layer, 1, rows] += _fold(dplace)
            dplaces.append(dplace.astype(bf16))
            gmacc[layer, part] += _dot3((place[0][rows], place[1][rows]), pieces, NT)
        dplace = jnp.concatenate(dplaces, 0)
        yield
        xhat = xh1h[layer, grid, :, at]
        dfeat = hidh[layer, grid, :, at]
        dxhat = _dot_wide(pair_of(upmh, upml, (layer, 0)), dfeat, NN) + _dot_wide(
            pair_of(upmh, upml, (layer, 1)), dplace, NN
        )
        grad = stream[grid, :, at] + _norm_back(
            dxhat, xhat.astype(f32), rs1[layer, grid, :, at]
        )
        first = isinstance(layer, int) and layer == 0
        if not first:
            stream[grid, :, at] = grad
        add_matrix(layer, 1, _dot(xhat, dplace, NT))
        yield
        if first:
            coords = jnp.concatenate(
                [points_ref[grid, :fin, at], jnp.zeros((8 - fin, tile), f32)], 0
            )
            embacc[...] += _dot3(_split(coords), _split(grad), NT)
        yield

    def to_row(folded):
        return _row_sums(folded)

    def put_vector(row, value, add=False):
        for index in range(width // LANES):
            start = places["vecs"] + index * places["vecs_stride"] + row
            piece = value[:, index * LANES : (index + 1) * LANES]
            if add:
                piece = piece + packed[start : start + 1, :]
            packed[start : start + 1, :] = piece

    def close_matrix(layer, slot, bias_sum):
        gain, shift = (2, 3) if slot == 3 else (0, 1)
        gram = read_matrix(layer, slot)
        mat = mats_ref[layer, slot]
        value = (
            _wide(cols[layer, gain], width) * gram + _wide(cols[layer, shift], width) * bias_sum
        )
        for index in range(width // LANES):
            packed[matrix_rows(layer, slot, index), :] = value[
                :, index * LANES : (index + 1) * LANES
            ]
        shift_row = _doth(jnp.broadcast_to(bias_sum, (8, width)), mat, NT)[:1]
        return _row_sums(gram * mat), shift_row

    def close_rest(layer):
        base = 9 * layer
        middle, inner, final = [to_row(vacc[layer, slot]) for slot in (2, 3, 4)]
        gain_row, shift_row = close_matrix(layer, 3, inner)
        for offset, row in ((4, middle), (5, gain_row), (6, shift_row), (7, inner), (8, final)):
            put_vector(base + offset, row)

    def close_feat(layer):
        total = to_row(vacc[layer, 0])
        gain, shift = close_matrix(layer, 0, total)
        put_vector(9 * layer, gain)
        put_vector(9 * layer + 1, shift)
        put_vector(9 * layer + 2, total)

    def close_front(layer):
        base = 9 * layer
        place_sum = to_row(vacc[layer, 1])
        place_gain, place_shift = close_matrix(layer, 1, place_sum)
        put_vector(base, place_gain, True)
        put_vector(base + 1, place_shift, True)
        put_vector(base + 3, place_sum)
        tiled = jnp.concatenate([maps_ref[layer]] * half, 1)
        total = None
        sharp_total = None
        for part in range(2):
            lane = lax.broadcasted_iota(jnp.int32, (1, span), 1)
            sharp = jnp.full((1, span), 0.0, f32) + sharp_ref[layer, part * half]
            for head in range(1, half):
                sharp = jnp.where(
                    lane >= head * slices, sharp_ref[layer, part * half + head], sharp
                )
            picked = _diag_heads(gmacc[layer, part], head_size, slices) / sharp
            total = picked if total is None else total + picked
            share = -jnp.sum(picked * tiled, 0, keepdims=True) / sharp
            chosen = jnp.where(
                lax.broadcasted_iota(jnp.int32, (span, LANES), 0) // slices + part * half
                == lax.broadcasted_iota(jnp.int32, (span, LANES), 1),
                1.0,
                0.0,
            )
            share = _dotx(jnp.broadcast_to(share, (8, span)), chosen, NN)
            sharp_total = share if sharp_total is None else sharp_total + share
        start = places["sharp"] + layer
        packed[start : start + 1, :heads] = sharp_total[:1, :heads]
        total = _fold(total)
        total = total + pltpu.roll(total, slices, 1)
        start = places["maps"] + layer * head_size
        packed[start : start + head_size, :slices] = total[:, :slices]
        start = places["qkv"] + layer * head_size
        packed[start : start + head_size, : 3 * head_size] = qkvacc[layer]

    def close_head():
        spread_dpred = _dotx(headacc[0], jnp.ones((LANES, LANES), f32), NN)
        gram = jnp.concatenate([headacc[1 + k] for k in range(width // LANES)], 1)
        gain_row, shift_row = vecs[tail : tail + 1], vecs[tail + 1 : tail + 2]
        head_grad = gram * gain_row + _wide(spread_dpred, width) * shift_row
        for index in range(width // LANES):
            at = slice(index * LANES, (index + 1) * LANES)
            start = places["io"] + index * places["io_stride"]
            packed[start + fin : start + fin + outc, :] = head_grad[:outc, at]
        put_vector(tail, jnp.sum(gram * head_rows, 0, keepdims=True))
        put_vector(
            tail + 1, jnp.sum(_wide(spread_dpred, width) * head_rows, 0, keepdims=True)
        )
        packed[places["loss"] : places["loss"] + 1, :] = jnp.broadcast_to(
            jnp.sum(jnp.sum(lossacc[...], 0, keepdims=True), 1, keepdims=True), (1, LANES)
        )

    def close_embed():
        for index in range(width // LANES):
            at = slice(index * LANES, (index + 1) * LANES)
            start = places["io"] + index * places["io_stride"]
            packed[start : start + fin, :] = embacc[:fin, at]

    stages = [
        sum_stages(
            packed,
            summed,
            entry,
            boxes[3 * index : 3 * index + 3],
            sum_send.at[index],
            sum_recv.at[index],
            members // 2,
        )
        for index, entry in enumerate(places["groups"])
    ]
    squares[...] = jnp.zeros_like(squares)

    def handed(index):
        start, number = places["groups"][index]
        rows = slice(start, start + number)
        return pltpu.make_async_copy(summed.at[rows], summed_hbm.at[rows], out_sems.at[index])

    def hand_over(index):
        start, number = places["groups"][index]
        handed(index).start()

        @pl.loop(0, number // 256)
        def _(step):
            block = summed[pl.ds(pl.multiple_of(start + step * 256, 256), 256), :]
            if index == 0:
                row = lax.broadcasted_iota(jnp.int32, block.shape, 0) + step * 256
                block = jnp.where(row == places["loss"], 0.0, block)
            squares[...] += jnp.sum((block * block).reshape(32, 8, LANES), 0)

    def wrapped(index):
        def finish_group():
            stages_end[index]()
            hand_over(index)

        return finish_group

    stages_end = [entry[6] for entry in stages]
    stages = [(*entry[:6], wrapped(index)) for index, entry in enumerate(stages)]

    def run(spots):
        for set_index, number in spots:
            stages[set_index][number]()

    def hooks(phase, layer, step):
        found = PLAN.get((phase, layer, step), {})
        return [
            [stages[s][n] for s, n in found.get(turn, ())] for turn in range(max(found, default=-1) + 1)
        ]

    def woven(phase, maker, layer):
        _lockstep([maker(layer, *spot[:2]) for spot in spots], hooks(phase, layer, 0))

    for layer in range(layers - 1, -1, -1):
        accf[...] = jnp.zeros_like(accf)
        woven("rest", back_rest, layer)
        close_rest(layer)
        run(AFTER_REST[layer])
        _lockstep(
            [back_attend(layer, grid) for grid in range(grids)], hooks("attend", layer, 0)
        )
        woven("feat", back_feat, layer)
        close_feat(layer)
        run(AFTER_FEAT[layer])
        if layer:
            close_head()
        woven("front", back_front, layer)
        close_front(layer)
        if layer == 0:
            close_embed()
        run(AFTER_FRONT[layer])

    for index in range(len(stages)):
        handed(index).wait()


def _round_up(value, unit):
    return (value + unit - 1) // unit * unit


def packed_places(layers, width, io_rows, vec_rows, head_size):
    halves = width // LANES
    places = {"io_stride": _round_up(io_rows, 8), "vecs_stride": _round_up(vec_rows, 8)}
    row = 0
    for name, rows in (
        ("io", halves * places["io_stride"]),
        ("vecs", halves * places["vecs_stride"]),
        ("maps", layers * head_size),
        ("qkv", layers * head_size),
        ("sharp", _round_up(layers, 8)),
        ("loss", 8),
    ):
        places[name] = row
        row += rows
    places["mats"] = _round_up(row, 256)
    each = halves * width
    first = places["mats"] + each
    groups = [(0, first), (first, each), (first + each, 3 * each)]
    for layer in range(1, layers):
        start = places["mats"] + layer * 5 * each
        groups += [(start, 2 * each), (start + 2 * each, 3 * each)]
    places["groups"] = groups
    places["rows"] = places["mats"] + layers * 5 * each
    return places


def group_parts(rows):
    half = rows // 2
    return half, half // 4, half // 16


def sum_stages(packed, out, span, boxes, send_sems, recv_sems, floors):
    first, rows = span
    half, a_four, a_all = group_parts(rows)
    core_in, a_one, a_two = boxes
    point, group = lax.axis_index("pts"), lax.axis_index("grp")
    y, z = lax.rem(point, 2), lax.div(point, 2)
    core, x = lax.rem(group, 2), lax.div(group, 2)
    plane = x + 2 * y
    base = first + core * half
    hops = (1, 2, 3)

    def plane_peer(hop):
        other_x, other_y = lax.rem(x + hop % 2, 2), lax.rem(y + hop // 2, 2)
        return (z * 2 + other_y, other_x * 2 + core), other_x + 2 * other_y

    def line_peer(hop):
        other = lax.rem(z + hop, floors)
        return (other * 2 + y, group), other

    partner = (point, x * 2 + (1 - core))

    def rows_at(start, count):
        return pl.ds(pl.multiple_of(start, 8), count)

    def send(number, source, target, device):
        return pltpu.make_async_remote_copy(
            src_ref=source,
            dst_ref=target,
            send_sem=send_sems.at[number],
            recv_sem=recv_sems.at[number],
            device_id=device,
            device_id_type=MESH,
        )

    def place(start, count):
        return packed.at[rows_at(start, count)]

    def cross():
        return send(0, place(first + (1 - core) * half, half), core_in, partner)

    def a1(hop):
        device, spot = plane_peer(hop)
        return send(hop, place(base + spot * a_four, a_four), a_one.at[hop - 1], device)

    a_part = rows_at(base + plane * a_four, a_four)
    a_piece = rows_at(base + plane * a_four + z * a_all, a_all)
    def a2(hop):
        device, spot = line_peer(hop)
        source = place(base + plane * a_four + spot * a_all, a_all)
        return send(3 + hop, source, a_two.at[hop - 1], device)

    def a3(hop):
        return send(6 + hop, out.at[a_piece], out.at[a_piece], line_peer(hop)[0])

    def a4(hop):
        return send(9 + hop, out.at[a_part], out.at[a_part], plane_peer(hop)[0])

    def last():
        own = out.at[rows_at(base, half)]
        return send(13, own, own, partner)

    def arrive(make):
        for hop in hops:
            make(hop).wait_recv()

    def depart(make):
        for hop in hops:
            make(hop).start()

    def stage_cross():
        cross().start()

    def stage_first():
        cross().wait_recv()
        own = rows_at(base, half)
        packed[own, :] = packed[own, :] + core_in[...]
        depart(a1)

    def stage_second():
        arrive(a1)
        packed[a_part, :] = packed[a_part, :] + a_one[0] + a_one[1] + a_one[2]
        depart(a2)

    def stage_third():
        arrive(a2)
        out[a_piece, :] = packed[a_piece, :] + a_two[0] + a_two[1] + a_two[2]
        depart(a3)

    def stage_fourth():
        arrive(a3)
        depart(a4)

    def stage_fifth():
        arrive(a4)
        last().start()

    def stage_end():
        last().wait_recv()
        cross().wait_send()
        last().wait_send()
        for make in (a1, a2, a3, a4):
            for hop in hops:
                make(hop).wait_send()

    return (
        stage_cross,
        stage_first,
        stage_second,
        stage_third,
        stage_fourth,
        stage_fifth,
        stage_end,
    )


def update_kernel(dims, *refs):
    layers, slots, width, places = dims
    summed, squares = refs[:2]
    weights, means, seconds = refs[2:8], refs[8:14], refs[14:20]
    loss_out, norm_out = refs[20:22]
    firsts, news, fresh = refs[22:40:3], refs[23:40:3], refs[24:40:3]
    grads, state, results, in_sems, out_sems = refs[40:]
    halves = width // LANES
    each = halves * width
    count = layers * slots

    def incoming(index):
        layer, slot = index // slots, index % slots
        start = places["mats"] + (layer * slots + SLOT_ORDER[slot]) * each
        sources = [summed.at[start : start + each]]
        targets = [grads.at[places["mats"] + index * each : places["mats"] + (index + 1) * each]]
        for kind, array in enumerate((weights[1], means[1], seconds[1])):
            sources.append(array.at[layer, slot])
            targets.append(state.at[kind, index])
        return [
            pltpu.make_async_copy(source, target, in_sems.at[index, number])
            for number, (source, target) in enumerate(zip(sources, targets))
        ]

    def outgoing(index):
        layer, slot = index // slots, index % slots
        return [
            pltpu.make_async_copy(
                results.at[kind, index], array.at[layer, slot], out_sems.at[index, kind]
            )
            for kind, array in enumerate((firsts[1], news[1], fresh[1]))
        ]

    small = pltpu.make_async_copy(
        summed.at[: places["mats"]], grads.at[: places["mats"]], in_sems.at[count, 0]
    )
    for index in range(count):
        for copy in incoming(index):
            copy.start()
    small.start()
    total = jnp.sum(jnp.sum(squares[...], 0, keepdims=True), 1, keepdims=True)
    norm = jnp.sqrt(total)
    factor = jnp.minimum(1.0, clip_limit / norm)
    norm_out[...] = norm
    for index in range(count):
        for copy in incoming(index):
            copy.wait()
        start = places["mats"] + index * each
        grad = jnp.concatenate(
            [grads[start + k * width : start + (k + 1) * width, :] for k in range(halves)], 1
        )
        first_new, second_new, weight_new = adamw_update(
            state[0, index], grad * factor, state[1, index], state[2, index]
        )
        results[0, index] = first_new
        results[1, index] = second_new
        results[2, index] = weight_new
        for copy in outgoing(index):
            copy.start()
    small.wait()

    def apply(index, grad):
        first_new, second_new, weight_new = adamw_update(
            weights[index][...], grad * factor, means[index][...], seconds[index][...]
        )
        firsts[index][...] = first_new
        news[index][...] = second_new
        fresh[index][...] = weight_new

    def rows(name, start, number):
        first = places[name] + start
        return grads[first : first + number, :]

    loss_out[...] = rows("loss", 0, 1)[:, :1]
    for index, name in ((0, "io"), (5, "vecs")):
        stride, number = places[name + "_stride"], weights[index].shape[0]
        apply(
            index,
            jnp.concatenate([rows(name, k * stride, number) for k in range(halves)], 1),
        )
    for index, name in ((2, "maps"), (3, "qkv")):
        _, number, lanes = weights[index].shape
        apply(
            index,
            jnp.stack([rows(name, k * number, number)[:, :lanes] for k in range(layers)]),
        )
    number, lanes = weights[4].shape
    apply(4, rows("sharp", 0, number)[:, :lanes])
    for index in range(count):
        for copy in outgoing(index):
            copy.wait()


def update_all(summed, squares, network_state, running_means, running_squares, places):
    layers, slots, width, _ = network_state[1].shape
    vmem = pl.BlockSpec(memory_space=pltpu.VMEM)
    hbm = pl.BlockSpec(memory_space=pl.ANY)
    state_specs = [hbm if index == 1 else vmem for index in range(6)]
    shapes = [jax.ShapeDtypeStruct((1, 1), f32)] * 2
    specs = [vmem] * 2
    for index, entry in enumerate(network_state):
        shapes += [jax.ShapeDtypeStruct(entry.shape, f32)] * 3
        specs += [hbm if index == 1 else vmem] * 3
    count = layers * slots
    kept = pltpu.VMEM((3, count, width, width), f32)
    results = pl.pallas_call(
        functools.partial(update_kernel, (layers, slots, width, places)),
        out_shape=shapes,
        in_specs=[hbm, vmem] + state_specs * 3,
        out_specs=specs,
        scratch_shapes=[
            pltpu.VMEM((places["rows"], LANES), f32),
            kept,
            kept,
            pltpu.SemaphoreType.DMA((count + 1, 4)),
            pltpu.SemaphoreType.DMA((count, 3)),
        ],
        compiler_params=pltpu.CompilerParams(vmem_limit_bytes=VMEM_BYTES),
    )(summed, squares, *network_state, *running_means, *running_squares)
    return (results[0].reshape(()), results[1].reshape(()), *results[2:])


def whole_grid_grads(network_state, coords, goals, bound, sizes, places, mesh_sizes):
    io_rows, mats, maps, qkv, sharp, vecs = network_state
    members, groups = mesh_sizes
    grids, own, _, own_points = coords.shape
    points = own_points * members
    layers, _, width, _ = mats.shape
    heads = sharp.shape[1]
    head_size, slices = maps.shape[1:]
    outc = io_rows.shape[0] - FIN
    tile = TILE
    half, span, group = heads // 2, heads // 2 * slices, heads // 2 * head_size
    dims = (grids, points, width, heads, head_size, slices, layers, FIN, outc, tile)
    dims = dims + (members, groups, places)

    def both(*shape):
        return [pltpu.VMEM(shape, bf16), pltpu.VMEM(shape, bf16)]

    def single(*shape):
        return [pltpu.VMEM(shape, f32)]

    kept = (layers, grids, width, points)
    box = (members, grids * 8 + 8, own_points)
    scratch = (
        single(layers, 5, width, width)
        + single(places["rows"], LANES)
        + single(places["rows"], LANES)
        + single(grids, width, points)
        + [pltpu.VMEM(kept, bf16)]
        + single(layers, grids, 1, points)
        + both(*kept)
        + both(*kept)
        + both(layers, grids, 2 * span, points)
        + both(*kept)
        + [pltpu.VMEM(kept, bf16)]
        + single(layers, grids, 1, points)
        + [pltpu.VMEM(kept, bf16)] * 2
        + both(layers, 5, width, width)
        + single(layers, 9, width, LANES)
        + both(layers, 2, span, group)
        + both(layers, 2, group, span)
        + single(grids, 2, group + 16, span)
        + single(grids, 2, group, span)
        + single(layers, grids, head_size, 2 * span)
        + single(layers, grids, 1, 2 * span)
        + single(layers, grids, 3 * head_size, 2 * span)
        + single(layers, grids, half, slices, 2 * slices)
        + both(layers, grids, 2, group, span)
        + both(grids, 2, group, span)
        + both(grids, 2, span, 2 * group)
        + single(grids, 2 * span, LANES)
        + single(layers, 5, width, LANES)
        + single(layers, 2, group, span)
        + single(1 + width // LANES, 8, LANES)
        + single(8, width)
        + single(8, LANES)
        + single(layers, head_size, 3 * head_size)
        + single(grids, 8, points)
        + single(*box)
        + single(members - 1, *box[1:])
        + single(groups, 8, own_points)
        + [pltpu.SemaphoreType.DMA((members - 1,))] * 2
        + [pltpu.SemaphoreType.DMA((groups - 1,))] * 2
        + [pltpu.SemaphoreType.DMA((len(places["groups"]), 14))] * 2
        + [pltpu.SemaphoreType.DMA, pltpu.SemaphoreType.DMA((len(places["groups"]),))]
    )
    for _, rows in places["groups"]:
        half_rows, quarter, piece = group_parts(rows)
        scratch += single(half_rows, LANES)
        scratch += single(3, quarter, LANES) + single(3, piece, LANES)
    vmem = pl.BlockSpec(memory_space=pltpu.VMEM)
    smem = pl.BlockSpec(memory_space=pltpu.SMEM)
    hbm = pl.BlockSpec(memory_space=pl.ANY)
    return pl.pallas_call(
        functools.partial(grids_kernel, dims),
        out_shape=[
            jax.ShapeDtypeStruct((places["rows"], LANES), f32),
            jax.ShapeDtypeStruct((8, LANES), f32),
        ],
        in_specs=[smem] * 2 + [vmem] * 4 + [hbm] + [vmem] * 3,
        out_specs=[hbm, vmem],
        scratch_shapes=scratch,
        compiler_params=pltpu.CompilerParams(
            collective_id=0, has_side_effects=True, vmem_limit_bytes=VMEM_BYTES
        ),
    )(sizes, sharp, coords, jnp.swapaxes(goals, 1, 2), bound, io_rows, mats, maps, qkv, vecs)


def body_grids(mesh_sizes, *arrays):
    network_state = arrays[4:10]
    io_rows, mats, maps, _, _, vecs = network_state
    places = packed_places(
        mats.shape[0], mats.shape[2], io_rows.shape[0], vecs.shape[0], maps.shape[1]
    )
    summed, squares = whole_grid_grads(network_state, *arrays[:4], places, mesh_sizes)
    return update_all(
        summed, squares, network_state, arrays[10:16], arrays[16:22], places
    )


def solution(mesh):
    in_specs = (
        P(None, "grp", None, "pts"),
        P(None, "grp", None, "pts"),
        P(None, "grp", "pts"),
        P(None, "grp"),
        P(),
        P(),
        P(),
        P(),
        P(),
        P(),
        P(),
        P(),
        P(),
        P(),
        P(),
        P(),
        P(),
        P(),
        P(),
        P(),
        P(),
        P(),
    )
    out_specs = (
        P(),
        P(),
        P(),
        P(),
        P(),
        P(),
        P(),
        P(),
        P(),
        P(),
        P(),
        P(),
        P(),
        P(),
        P(),
        P(),
        P(),
        P(),
        P(),
        P(),
    )
    members, groups = mesh.shape["pts"], mesh.shape["grp"]

    def body(*arrays):
        batches, own, _, own_points = arrays[0].shape
        fits = own == members and batches * own_points * members <= 2048
        if fits and own_points == LANES and (members, groups) == (8, 4) and arrays[5].shape[0] == 2:
            return body_grids((members, groups), *arrays)
        return body_points(*arrays)

    return jax.shard_map(body, mesh=mesh, in_specs=in_specs, out_specs=out_specs, check_vma=False)
```
